32 devices in a mesh: dp: 4 (over z), ctx: 2 (over y), tp: 4 (over x, core).
Axes of the slice: x: 2, y: 2, z: 4, core: 2. Of those that a mesh axis runs over, the one named last changes fastest.
Arguments:
- inputs: bfloat16 [8, 1024, 768], P('dp', ('ctx', 'tp')), may hold values from -6 to 6
- segments: int32 [8, 1024], P('dp', 'ctx'), may hold values from 0 to 4, never falling along the last dimension, each value on 1 to 512 neighbouring positions
- cotangent: bfloat16 [8, 1024, 768], P('dp', ('ctx', 'tp')), may hold values from -6 to 6
- student_first_gain: bfloat16 [768], P('dp'), may hold values from 0.5 to 1.5
- student_first_shift: bfloat16 [768], P('dp'), may hold values from -3 to 3
- student_merged_weight: bfloat16 [768, 3, 768], P('dp', None, 'tp'), may hold values from -0.21875 to 0.21875
- student_merged_bias: bfloat16 [2, 12, 64], P(None, 'tp', 'dp'), may hold values from -3 to 3
- student_output_weight: bfloat16 [768, 768], P('tp', 'dp'), may hold values from -1.25 to 1.25
- student_output_bias: bfloat16 [768], P('dp'), may hold values from -3 to 3
- student_second_gain: bfloat16 [768], P('dp'), may hold values from 0.5 to 1.5
- student_second_shift: bfloat16 [768], P('dp'), may hold values from -3 to 3
- student_expand_weight: bfloat16 [768, 3072], P('dp', 'tp'), may hold values from -0.21875 to 0.21875
- student_expand_bias: bfloat16 [48, 64], P('tp', 'dp'), may hold values from -3 to 3
- student_reduce_weight: bfloat16 [3072, 768], P('tp', 'dp'), may hold values from -0.109375 to 0.109375
- student_reduce_bias: bfloat16 [768], P('dp'), may hold values from -3 to 3
- teacher_first_gain: bfloat16 [768], P('dp'), may hold values from 0.5 to 1.5
- teacher_first_shift: bfloat16 [768], P('dp'), may hold values from -3 to 3
- teacher_merged_weight: bfloat16 [768, 3, 768], P('dp', None, 'tp'), may hold values from -0.21875 to 0.21875
- teacher_merged_bias: bfloat16 [2, 12, 64], P(None, 'tp', 'dp'), may hold values from -3 to 3
- teacher_output_weight: bfloat16 [768, 768], P('tp', 'dp'), may hold values from -1.25 to 1.25
- teacher_output_bias: bfloat16 [768], P('dp'), may hold values from -3 to 3
- teacher_second_gain: bfloat16 [768], P('dp'), may hold values from 0.5 to 1.5
- teacher_second_shift: bfloat16 [768], P('dp'), may hold values from -3 to 3
- teacher_expand_weight: bfloat16 [768, 3072], P('dp', 'tp'), may hold values from -0.21875 to 0.21875
- teacher_expand_bias: bfloat16 [48, 64], P('tp', 'dp'), may hold values from -3 to 3
- teacher_reduce_weight: bfloat16 [3072, 768], P('tp', 'dp'), may hold values from -0.109375 to 0.109375
- teacher_reduce_bias: bfloat16 [768], P('dp'), may hold values from -3 to 3
Outputs:
- output: bfloat16 [8, 1024, 768], P('dp', ('ctx', 'tp'))
- input_grad: float32 [8, 1024, 768], P('dp', ('ctx', 'tp'))
- grad_student_first_gain: float32 [768], P('dp')
- grad_student_first_shift: float32 [768], P('dp')
- grad_student_merged_weight: float32 [768, 3, 768], P('dp', None, 'tp')
- grad_student_merged_bias: float32 [2, 12, 64], P(None, 'tp', 'dp')
- grad_student_output_weight: float32 [768, 768], P('tp', 'dp')
- grad_student_output_bias: float32 [768], P('dp')
- grad_student_second_gain: float32 [768], P('dp')
- grad_student_second_shift: float32 [768], P('dp')
- grad_student_expand_weight: float32 [768, 3072], P('dp', 'tp')
- grad_student_expand_bias: float32 [48, 64], P('tp', 'dp')
- grad_student_reduce_weight: float32 [3072, 768], P('tp', 'dp')
- grad_student_reduce_bias: float32 [768], P('dp')
- grad_teacher_first_gain: float32 [768], P('dp')
- grad_teacher_first_shift: float32 [768], P('dp')
- grad_teacher_merged_weight: float32 [768, 3, 768], P('dp', None, 'tp')
- grad_teacher_merged_bias: float32 [2, 12, 64], P(None, 'tp', 'dp')
- grad_teacher_output_weight: float32 [768, 768], P('tp', 'dp')
- grad_teacher_output_bias: float32 [768], P('dp')
- grad_teacher_second_gain: float32 [768], P('dp')
- grad_teacher_second_shift: float32 [768], P('dp')
- grad_teacher_expand_weight: float32 [768, 3072], P('dp', 'tp')
- grad_teacher_expand_bias: float32 [48, 64], P('tp', 'dp')
- grad_teacher_reduce_weight: float32 [3072, 768], P('tp', 'dp')
- grad_teacher_reduce_bias: float32 [768], P('dp')
The draws below stay inside these ranges and needn't reach their ends.
Inputs may be any that keep to these rules, and one draw needn't show every extreme that they name: `segments`: within a sequence the document numbers never fall from one token to the next; a document holds 1 to 512 consecutive tokens, and each sequence has one of exactly 512.
All inputs are finite; a program needn't handle non-finite values.
Results may differ from the reference program's by a relative error of at most 0.025.
Values may be sent and summed in bfloat16 or wider, within the bound.
No kernel may reach another device: no remote copies, remote signals or barrier semaphores. Data moves between devices by JAX's collectives and lax.ppermute only.
A program may use at most 192 MiB of HBM per device.

```python
import math
import jax
import jax.numpy as jnp
import numpy as np
from jax import lax

D = 768
H = 12
HD = 64
FF = 3072
QBLK = 512
SEQ = 1024
SEQS = 8
DOC_LONG = 512
SEG_COUNT = 5


def steps_of(own_key, dims, split, low, high):
    factor_of, own = 1.0, jax.random.fold_in(own_key, 6)
    for axis_at, shards_of in split:
        draws = jnp.exp(jax.random.uniform(jax.random.fold_in(own, axis_at), (shards_of,), jnp.float32, low / len(split), high / len(split)))
        factor_of = factor_of * jnp.repeat(draws, dims[axis_at] // shards_of).reshape([-1 if axis == axis_at else 1 for axis in range(len(dims))])
    return factor_of


def profile(amount, total, limit, slope):
    portions = [(1 << 20) // math.isqrt(standing ** slope) + 1 for standing in range(2, amount + 1)]
    spare, holding = total - limit - (amount - 1), [1] * (amount - 1)
    while spare > 0:
        candidates = [i for i in range(amount - 1) if holding[i] < limit]
        pool, left = sum([portions[i] for i in candidates]), spare
        for i in candidates:
            addition = min(limit - holding[i], max(1, left * portions[i] // pool), spare)
            holding[i] = holding[i] + addition
            spare = spare - addition
    return np.array([limit] + holding)


def uneven(key, count, total, most, lean):
    if count == 2:
        one = jax.random.randint(key, (), max(1, total - most), min(most, total - 1) + 1)
        return jnp.stack([one, total - one])
    lengths = jnp.asarray(profile(count, total, most, lean), jnp.int32)
    pairs = (count - 1) // 2
    donor, receiver = lengths[1:1 + 2 * pairs:2], lengths[2:2 + 2 * pairs:2]
    room = jnp.minimum(donor - 1, most - receiver)
    passed = jax.random.randint(jax.random.fold_in(key, 1), (pairs,), 0, 1 << 20) % (room + 1)
    lengths = lengths.at[1:1 + 2 * pairs:2].set(donor - passed).at[2:2 + 2 * pairs:2].set(receiver + passed)
    return lengths[jax.random.permutation(jax.random.fold_in(key, 2), count)]


def bell_draw(own_key, shape, scale, most, shards=(), kind=jnp.bfloat16):
    values = scale * jax.random.normal(own_key, shape, jnp.float32)
    if shards:
        values = values * steps_of(own_key, shape, shards, -0.22, 0.18)
    return jnp.clip(values, -most, most).astype(kind)


def setup_inputs(seed: int = 0) -> dict:
    arg_keys = jax.random.split(jax.random.key(seed), 28)
    return {
        "inputs": bell_draw(arg_keys[0], (SEQS, SEQ, D), 1.0, 6.0, ((0, 4), (1, 8))),
        "segments": jax.vmap(lambda own: jnp.searchsorted(jnp.cumsum(uneven(own, SEG_COUNT, SEQ, DOC_LONG, 1)), jnp.arange(SEQ), side="right"))(jax.random.split(arg_keys[1], SEQS)).reshape((SEQS, SEQ)).astype(jnp.int32),
        "cotangent": bell_draw(arg_keys[2], (SEQS, SEQ, D), 1.0, 6.0, ((0, 4), (1, 8))),
        "student_first_gain": jnp.clip(1.0 + 0.1 * jax.random.normal(arg_keys[3], (D,), jnp.float32), 0.5, 1.5).astype(jnp.bfloat16),
        "student_first_shift": bell_draw(arg_keys[4], (D,), 0.3, 3.0, ((0, 4),)),
        "student_merged_weight": bell_draw(arg_keys[5], (D, 3, D), D ** -0.5, 0.21875, ((0, 4), (2, 4))),
        "student_merged_bias": bell_draw(arg_keys[6], (2, H, HD), 0.3, 3.0, ((1, 4), (2, 4))),
        "student_output_weight": bell_draw(arg_keys[7], (D, D), (D // 32) ** -0.5, 1.25, ((0, 4), (1, 4))),
        "student_output_bias": bell_draw(arg_keys[8], (D,), 0.3, 3.0, ((0, 4),)),
        "student_second_gain": jnp.clip(1.0 + 0.1 * jax.random.normal(arg_keys[9], (D,), jnp.float32), 0.5, 1.5).astype(jnp.bfloat16),
        "student_second_shift": bell_draw(arg_keys[10], (D,), 0.3, 3.0, ((0, 4),)),
        "student_expand_weight": bell_draw(arg_keys[11], (D, FF), D ** -0.5, 0.21875, ((0, 4), (1, 4))),
        "student_expand_bias": bell_draw(arg_keys[12], (FF // HD, HD), 0.3, 3.0, ((0, 4), (1, 4))),
        "student_reduce_weight": bell_draw(arg_keys[13], (FF, D), FF ** -0.5, 0.109375, ((0, 4), (1, 4))),
        "student_reduce_bias": bell_draw(arg_keys[14], (D,), 0.3, 3.0, ((0, 4),)),
        "teacher_first_gain": jnp.clip(1.0 + 0.1 * jax.random.normal(arg_keys[15], (D,), jnp.float32), 0.5, 1.5).astype(jnp.bfloat16),
        "teacher_first_shift": bell_draw(arg_keys[16], (D,), 0.3, 3.0, ((0, 4),)),
        "teacher_merged_weight": bell_draw(arg_keys[17], (D, 3, D), D ** -0.5, 0.21875, ((0, 4), (2, 4))),
        "teacher_merged_bias": bell_draw(arg_keys[18], (2, H, HD), 0.3, 3.0, ((1, 4), (2, 4))),
        "teacher_output_weight": bell_draw(arg_keys[19], (D, D), (D // 32) ** -0.5, 1.25, ((0, 4), (1, 4))),
        "teacher_output_bias": bell_draw(arg_keys[20], (D,), 0.3, 3.0, ((0, 4),)),
        "teacher_second_gain": jnp.clip(1.0 + 0.1 * jax.random.normal(arg_keys[21], (D,), jnp.float32), 0.5, 1.5).astype(jnp.bfloat16),
        "teacher_second_shift": bell_draw(arg_keys[22], (D,), 0.3, 3.0, ((0, 4),)),
        "teacher_expand_weight": bell_draw(arg_keys[23], (D, FF), D ** -0.5, 0.21875, ((0, 4), (1, 4))),
        "teacher_expand_bias": bell_draw(arg_keys[24], (FF // HD, HD), 0.3, 3.0, ((0, 4), (1, 4))),
        "teacher_reduce_weight": bell_draw(arg_keys[25], (FF, D), FF ** -0.5, 0.109375, ((0, 4), (1, 4))),
        "teacher_reduce_bias": bell_draw(arg_keys[26], (D,), 0.3, 3.0, ((0, 4),)),
    }


@jax.custom_vjp
def low(v):
    return lax.optimization_barrier(v.astype(jnp.bfloat16)).astype(jnp.float32)

@jax.custom_vjp
def low_back(v):
    return v

def low_keep(v):
    return (low(v), None)

def low_pass(kept, grad):
    return (grad,)

def back_keep(v):
    return (v, None)

def back_low(kept, grad):
    return (low(grad),)
low.defvjp(low_keep, low_pass)
low_back.defvjp(back_keep, back_low)
EPSILON = 1e-05
GELU_SCALE = 0.7978845608028654
HIGHEST = lax.Precision.HIGHEST

def both_ways(values):
    return low(low_back(values))

def layer_norm(values, norm_gain, norm_shift):
    center = values - lax.optimization_barrier(jnp.mean(values, axis=-1, keepdims=True))
    spread = lax.optimization_barrier(jnp.mean(center * center, axis=-1, keepdims=True))
    return center * lax.rsqrt(spread + EPSILON) * norm_gain + norm_shift

def gelu_tanh(values):
    return 0.5 * values * (1.0 + jnp.tanh(GELU_SCALE * (values + 0.044715 * values * values * values)))

def attend(query_all, key_all, value_all, doc_ids):
    reach = QBLK * ((DOC_LONG - 2) // QBLK + 1)
    key_pad = jnp.concatenate([jnp.zeros((reach, H, HD), jnp.float32), key_all], axis=0)
    value_pad = jnp.concatenate([jnp.zeros((reach, H, HD), jnp.float32), value_all], axis=0)
    doc_pad = jnp.concatenate([jnp.full((reach,), -1, jnp.int32), doc_ids.astype(jnp.int32)], axis=0)

    def one_block(start_row):
        query_rows = lax.dynamic_slice_in_dim(query_all, start_row, QBLK, 0)
        query_docs = lax.dynamic_slice_in_dim(doc_ids.astype(jnp.int32), start_row, QBLK, 0)
        key_rows = lax.dynamic_slice_in_dim(key_pad, start_row, reach + QBLK, 0)
        value_rows = lax.dynamic_slice_in_dim(value_pad, start_row, reach + QBLK, 0)
        key_docs = lax.dynamic_slice_in_dim(doc_pad, start_row, reach + QBLK, 0)
        scores = low_back(jnp.einsum('qhd,khd->hqk', query_rows, key_rows, precision=HIGHEST) * 0.125)
        query_place = start_row + jnp.arange(QBLK, dtype=jnp.int32)
        key_place = start_row - reach + jnp.arange(reach + QBLK, dtype=jnp.int32)
        keep_mask = (key_place[None, :] <= query_place[:, None]) & (key_docs[None, :] == query_docs[:, None])
        scores = jnp.where(keep_mask[None], scores, -1e+30)
        row_top = lax.optimization_barrier(jnp.max(scores, axis=-1, keepdims=True))
        raised = jnp.exp(scores - row_top)
        weights = raised / lax.optimization_barrier(jnp.sum(raised, axis=-1, keepdims=True))
        return jnp.einsum('hqk,khd->qhd', low(weights), value_rows, precision=HIGHEST)
    starts = (jnp.arange(SEQ // QBLK, dtype=jnp.int32) * QBLK).astype(jnp.int32)
    blocks = lax.map(jax.checkpoint(one_block), starts)
    return blocks.reshape(SEQ, H * HD)

def block(stream, doc_ids, params):
    first_gain, first_shift, merged_weight, merged_bias, output_weight, output_bias, second_gain, second_shift, expand_weight, expand_bias, reduce_weight, reduce_bias = params
    normed = low(layer_norm(stream, first_gain, first_shift))
    merged_out = jnp.einsum('td,dkf->tkf', normed, merged_weight, precision=HIGHEST)
    query_all = both_ways(merged_out[:, 0] + merged_bias[0].reshape(D))
    key_all = both_ways(merged_out[:, 1])
    value_all = both_ways(merged_out[:, 2] + merged_bias[1].reshape(D))
    mixed = both_ways(attend(query_all.reshape(SEQ, H, HD), key_all.reshape(SEQ, H, HD), value_all.reshape(SEQ, H, HD), doc_ids))
    middle = stream + low_back(jnp.dot(mixed, output_weight, precision=HIGHEST)) + output_bias
    normed_two = low(layer_norm(middle, second_gain, second_shift))
    hidden = low_back(jnp.dot(normed_two, expand_weight, precision=HIGHEST) + expand_bias.reshape(FF))
    activated = low(gelu_tanh(hidden))
    return middle + low_back(jnp.dot(activated, reduce_weight, precision=HIGHEST)) + reduce_bias

def reference(inputs, segments, cotangent, student_first_gain, student_first_shift, student_merged_weight, student_merged_bias, student_output_weight, student_output_bias, student_second_gain, student_second_shift, student_expand_weight, student_expand_bias, student_reduce_weight, student_reduce_bias, teacher_first_gain, teacher_first_shift, teacher_merged_weight, teacher_merged_bias, teacher_output_weight, teacher_output_bias, teacher_second_gain, teacher_second_shift, teacher_expand_weight, teacher_expand_bias, teacher_reduce_weight, teacher_reduce_bias):
    params = [student_first_gain, student_first_shift, student_merged_weight, student_merged_bias, student_output_weight, student_output_bias, student_second_gain, student_second_shift, student_expand_weight, student_expand_bias, student_reduce_weight, student_reduce_bias, teacher_first_gain, teacher_first_shift, teacher_merged_weight, teacher_merged_bias, teacher_output_weight, teacher_output_bias, teacher_second_gain, teacher_second_shift, teacher_expand_weight, teacher_expand_bias, teacher_reduce_weight, teacher_reduce_bias]
    floats = [tensor.astype(jnp.float32) for tensor in params]

    def forward(stream_all, weights):

        def per_sequence(paired):
            stream, doc_ids = paired
            return block(block(stream, doc_ids, weights[:12]), doc_ids, weights[12:])
        return lax.map(jax.checkpoint(per_sequence), (stream_all, segments))
    result, pull = jax.vjp(forward, inputs.astype(jnp.float32), floats)
    input_grad, grads = pull(cotangent.astype(jnp.float32))
    return (result.astype(jnp.bfloat16), input_grad, grads[0], grads[1], grads[2], grads[3], grads[4], grads[5], grads[6], grads[7], grads[8], grads[9], grads[10], grads[11], grads[12], grads[13], grads[14], grads[15], grads[16], grads[17], grads[18], grads[19], grads[20], grads[21], grads[22], grads[23])
```

```python
import jax
import jax.numpy as jnp
from jax import lax
from jax.experimental import pallas as pl
from jax.experimental.pallas import tpu as pltpu
from jax.sharding import PartitionSpec as P

HD = 64
DOC_MAX = 2000


EPSILON = 1e-05
GELU_SCALE = 0.7978845608028654


def from_behind(block, axis, distance):
    devices = range(lax.axis_size(axis))
    route = [(i - distance, i) for i in devices if i - distance in devices]
    return lax.ppermute(block, axis, route)


def layer_norm(values, norm_gain, norm_shift):
    center = values - jnp.mean(values, axis=-1, keepdims=True)
    spread = jnp.mean(center * center, axis=-1, keepdims=True)
    return center * lax.rsqrt(spread + EPSILON) * norm_gain + norm_shift


def gelu_tanh(values):
    return (
        0.5 * values * (1.0 + jnp.tanh(GELU_SCALE * (values + 0.044715 * values * values * values)))
    )


def spread_rows(row_block):
    return lax.all_gather(row_block, "tp", axis=1, tiled=True)


def gather_sums(partial_value):
    return lax.psum_scatter(
        partial_value.astype(jnp.bfloat16), "tp", scatter_dimension=1, tiled=True
    ).astype(jnp.float32)


def to_items(tensor, head_count):
    batches, length, features = tensor.shape
    head_size = features // head_count
    return (
        tensor.reshape(batches, length, head_count, head_size)
        .transpose(0, 2, 1, 3)
        .reshape(batches * head_count, length, head_size)
    )


def from_items(tensor, head_count):
    item_count, length, head_size = tensor.shape
    batches = item_count // head_count
    return (
        tensor.reshape(batches, head_count, length, head_size)
        .transpose(0, 2, 1, 3)
        .reshape(batches, length, head_count * head_size)
    )


def masked_scores(query_rows, key_rows, query_docs, key_docs, allowed):
    raw_scores = (
        jnp.einsum("qd,kd->qk", query_rows, key_rows, preferred_element_type=jnp.float32) * 0.125
    )
    keep_mask = allowed & (key_docs[None, :] == query_docs[:, None])
    return (jnp.where(keep_mask, raw_scores, -1e30), keep_mask)


def attend_forward(allowed):

    def attend_item(packed):
        query_rows, key_rows, value_rows, query_docs, key_docs = packed
        scores, keep_mask = masked_scores(query_rows, key_rows, query_docs, key_docs, allowed)
        row_top = jnp.max(scores, axis=-1, keepdims=True)
        raised = jnp.exp(scores - row_top)
        row_total = jnp.sum(raised, axis=-1, keepdims=True)
        weights = (raised / row_total).astype(jnp.bfloat16)
        mixed_rows = jnp.dot(weights, value_rows, preferred_element_type=jnp.float32).astype(
            jnp.bfloat16
        )
        return (mixed_rows, row_top[:, 0] + jnp.log(row_total[:, 0]))

    return attend_item


def attend_backward(allowed):

    def attend_item(packed):
        query_rows, key_rows, value_rows, query_docs, key_docs, log_total, grad_rows = packed
        scores, keep_mask = masked_scores(query_rows, key_rows, query_docs, key_docs, allowed)
        weights = jnp.where(keep_mask, jnp.exp(scores - log_total[:, None]), 0.0)
        grad_values = jnp.einsum(
            "qk,qd->kd", weights.astype(jnp.bfloat16), grad_rows, preferred_element_type=jnp.float32
        )
        grad_weights = jnp.einsum(
            "qd,kd->qk", grad_rows, value_rows, preferred_element_type=jnp.float32
        )
        centered = jnp.sum(weights * grad_weights, axis=-1, keepdims=True)
        grad_scores = (weights * (grad_weights - centered)).astype(jnp.bfloat16)
        grad_query = jnp.dot(grad_scores, key_rows, preferred_element_type=jnp.float32) * 0.125
        grad_keys = (
            jnp.einsum("qk,qd->kd", grad_scores, query_rows, preferred_element_type=jnp.float32)
            * 0.125
        )
        return (grad_query, grad_keys, grad_values)

    return attend_item


def layer_forward(stream, params, segments, key_docs, allowed, cycle_steps):
    (
        first_gain,
        first_shift,
        merged_weight,
        merged_bias,
        output_weight,
        output_bias,
        second_gain,
        second_shift,
        expand_weight,
        expand_bias,
        reduce_weight,
        reduce_bias,
    ) = params
    fetched = (
        lax.all_gather(first_gain, "dp", axis=0, tiled=True),
        lax.all_gather(first_shift, "dp", axis=0, tiled=True),
        lax.all_gather(merged_weight, "dp", axis=0, tiled=True),
        lax.all_gather(merged_bias, "dp", axis=2, tiled=True),
        lax.all_gather(output_weight, "dp", axis=1, tiled=True),
        lax.all_gather(output_bias, "dp", axis=0, tiled=True),
        lax.all_gather(second_gain, "dp", axis=0, tiled=True),
        lax.all_gather(second_shift, "dp", axis=0, tiled=True),
        lax.all_gather(expand_weight, "dp", axis=0, tiled=True),
        lax.all_gather(expand_bias, "dp", axis=1, tiled=True),
        lax.all_gather(reduce_weight, "dp", axis=1, tiled=True),
        lax.all_gather(reduce_bias, "dp", axis=0, tiled=True),
    )
    (
        first_gain,
        first_shift,
        merged_weight,
        merged_bias,
        output_weight,
        output_bias,
        second_gain,
        second_shift,
        expand_weight,
        expand_bias,
        reduce_weight,
        reduce_bias,
    ) = fetched
    head_count = merged_weight.shape[2] // HD
    normed = layer_norm(
        stream, first_gain.astype(jnp.float32), first_shift.astype(jnp.float32)
    ).astype(jnp.bfloat16)
    first_rows = spread_rows(normed)
    merged_out = jnp.einsum(
        "std,dkf->stkf", first_rows, merged_weight, preferred_element_type=jnp.float32
    )
    bias_pair = merged_bias.astype(jnp.float32).reshape(2, -1)
    query_rows = (merged_out[:, :, 0] + bias_pair[0]).astype(jnp.bfloat16)
    key_rows = merged_out[:, :, 1].astype(jnp.bfloat16)
    value_rows = (merged_out[:, :, 2] + bias_pair[1]).astype(jnp.bfloat16)
    key_list = [key_rows]
    value_list = [value_rows]
    moving = (key_rows, value_rows)
    for offset in range(cycle_steps):
        moving = from_behind((moving[0], moving[1]), "ctx", 1)
        key_list.insert(0, moving[0])
        value_list.insert(0, moving[1])
    query_items = to_items(query_rows, head_count)
    key_items = to_items(jnp.concatenate(key_list, axis=1), head_count)
    value_items = to_items(jnp.concatenate(value_list, axis=1), head_count)
    query_docs = jnp.repeat(segments, head_count, axis=0)
    window_docs = jnp.repeat(key_docs, head_count, axis=0)
    mixed_items, log_total = lax.map(
        attend_forward(allowed), (query_items, key_items, value_items, query_docs, window_docs)
    )
    mixed = from_items(mixed_items, head_count)
    attn_part = jnp.einsum("stf,fd->std", mixed, output_weight, preferred_element_type=jnp.float32)
    middle = stream + gather_sums(attn_part) + output_bias.astype(jnp.float32)
    normed_two = layer_norm(
        middle, second_gain.astype(jnp.float32), second_shift.astype(jnp.float32)
    ).astype(jnp.bfloat16)
    second_rows = spread_rows(normed_two)
    hidden = jnp.einsum(
        "std,df->stf", second_rows, expand_weight, preferred_element_type=jnp.float32
    ) + expand_bias.astype(jnp.float32).reshape(-1)
    activated = gelu_tanh(hidden).astype(jnp.bfloat16)
    mlp_part = jnp.einsum(
        "stf,fd->std", activated, reduce_weight, preferred_element_type=jnp.float32
    )
    result = middle + gather_sums(mlp_part) + reduce_bias.astype(jnp.float32)
    saved_state = (
        fetched,
        stream,
        first_rows,
        query_items,
        key_items,
        value_items,
        query_docs,
        window_docs,
        log_total,
        mixed,
        middle,
        second_rows,
        hidden,
        activated,
    )
    return (result, saved_state)


def reduce_grads(fresh):
    (
        gain_one,
        shift_one,
        merged_weights,
        merged_biases,
        output_weights,
        output_biases,
        gain_two,
        shift_two,
        expand_weights,
        expand_biases,
        reduce_weights,
        reduce_biases,
    ) = fresh
    summed = (
        lax.psum(gain_one.astype(jnp.bfloat16), "ctx").astype(jnp.float32),
        lax.psum(shift_one.astype(jnp.bfloat16), "ctx").astype(jnp.float32),
        lax.psum(merged_weights.astype(jnp.bfloat16), "ctx").astype(jnp.float32),
        lax.psum(merged_biases.astype(jnp.bfloat16), "ctx").astype(jnp.float32),
        lax.psum(output_weights.astype(jnp.bfloat16), "ctx").astype(jnp.float32),
        lax.psum(output_biases.astype(jnp.bfloat16), "ctx").astype(jnp.float32),
        lax.psum(gain_two.astype(jnp.bfloat16), "ctx").astype(jnp.float32),
        lax.psum(shift_two.astype(jnp.bfloat16), "ctx").astype(jnp.float32),
        lax.psum(expand_weights.astype(jnp.bfloat16), "ctx").astype(jnp.float32),
        lax.psum(expand_biases.astype(jnp.bfloat16), "ctx").astype(jnp.float32),
        lax.psum(reduce_weights.astype(jnp.bfloat16), "ctx").astype(jnp.float32),
        lax.psum(reduce_biases.astype(jnp.bfloat16), "ctx").astype(jnp.float32),
    )
    (
        gain_one,
        shift_one,
        merged_weights,
        merged_biases,
        output_weights,
        output_biases,
        gain_two,
        shift_two,
        expand_weights,
        expand_biases,
        reduce_weights,
        reduce_biases,
    ) = summed
    return (
        lax.psum_scatter(
            gain_one.astype(jnp.bfloat16), "dp", scatter_dimension=0, tiled=True
        ).astype(jnp.float32),
        lax.psum_scatter(
            shift_one.astype(jnp.bfloat16), "dp", scatter_dimension=0, tiled=True
        ).astype(jnp.float32),
        lax.psum_scatter(
            merged_weights.astype(jnp.bfloat16), "dp", scatter_dimension=0, tiled=True
        ).astype(jnp.float32),
        lax.psum_scatter(
            merged_biases.astype(jnp.bfloat16), "dp", scatter_dimension=2, tiled=True
        ).astype(jnp.float32),
        lax.psum_scatter(
            output_weights.astype(jnp.bfloat16), "dp", scatter_dimension=1, tiled=True
        ).astype(jnp.float32),
        lax.psum_scatter(
            output_biases.astype(jnp.bfloat16), "dp", scatter_dimension=0, tiled=True
        ).astype(jnp.float32),
        lax.psum_scatter(
            gain_two.astype(jnp.bfloat16), "dp", scatter_dimension=0, tiled=True
        ).astype(jnp.float32),
        lax.psum_scatter(
            shift_two.astype(jnp.bfloat16), "dp", scatter_dimension=0, tiled=True
        ).astype(jnp.float32),
        lax.psum_scatter(
            expand_weights.astype(jnp.bfloat16), "dp", scatter_dimension=0, tiled=True
        ).astype(jnp.float32),
        lax.psum_scatter(
            expand_biases.astype(jnp.bfloat16), "dp", scatter_dimension=1, tiled=True
        ).astype(jnp.float32),
        lax.psum_scatter(
            reduce_weights.astype(jnp.bfloat16), "dp", scatter_dimension=1, tiled=True
        ).astype(jnp.float32),
        lax.psum_scatter(
            reduce_biases.astype(jnp.bfloat16), "dp", scatter_dimension=0, tiled=True
        ).astype(jnp.float32),
    )


def layer_backward(grad_out, saved_state, allowed, cycle_steps, token_count):
    (
        fetched,
        stream,
        first_rows,
        query_items,
        key_items,
        value_items,
        query_docs,
        window_docs,
        log_total,
        mixed,
        middle,
        second_rows,
        hidden,
        activated,
    ) = saved_state
    (
        first_gain,
        first_shift,
        merged_weight,
        merged_bias,
        output_weight,
        output_bias,
        second_gain,
        second_shift,
        expand_weight,
        expand_bias,
        reduce_weight,
        reduce_bias,
    ) = fetched
    head_count = merged_weight.shape[2] // HD
    grad_branch = spread_rows(grad_out.astype(jnp.bfloat16))
    grad_reduce = jnp.einsum(
        "stf,std->fd", activated, grad_branch, preferred_element_type=jnp.float32
    )
    grad_active = jnp.einsum(
        "std,fd->stf", grad_branch, reduce_weight, preferred_element_type=jnp.float32
    )
    _, gelu_pull = jax.vjp(gelu_tanh, hidden)
    grad_hidden = gelu_pull(grad_active)[0].astype(jnp.bfloat16)
    grad_expand_bias = jnp.sum(grad_hidden, axis=(0, 1), dtype=jnp.float32).reshape(
        expand_bias.shape
    )
    grad_expand = jnp.einsum(
        "std,stf->df", second_rows, grad_hidden, preferred_element_type=jnp.float32
    )
    grad_second = gather_sums(
        jnp.einsum("stf,df->std", grad_hidden, expand_weight, preferred_element_type=jnp.float32)
    )
    _, second_pull = jax.vjp(
        layer_norm, middle, second_gain.astype(jnp.float32), second_shift.astype(jnp.float32)
    )
    grad_norm_mid, grad_second_gain, grad_second_shift = second_pull(grad_second)
    grad_middle = grad_out + grad_norm_mid
    grad_reduce_bias = jnp.sum(grad_out, axis=(0, 1))
    grad_attend = spread_rows(grad_middle.astype(jnp.bfloat16))
    grad_output = jnp.einsum("stf,std->fd", mixed, grad_attend, preferred_element_type=jnp.float32)
    grad_mixed = jnp.einsum(
        "std,fd->stf", grad_attend, output_weight, preferred_element_type=jnp.float32
    ).astype(jnp.bfloat16)
    grad_query_items, grad_key_items, grad_value_items = lax.map(
        attend_backward(allowed),
        (
            query_items,
            key_items,
            value_items,
            query_docs,
            window_docs,
            log_total,
            to_items(grad_mixed, head_count),
        ),
    )
    grad_query = from_items(grad_query_items, head_count)
    window_keys = from_items(grad_key_items, head_count)
    window_values = from_items(grad_value_items, head_count)
    local_keys = window_keys[:, cycle_steps * token_count :]
    local_values = window_values[:, cycle_steps * token_count :]
    carried = None
    for offset in range(cycle_steps, 0, -1):
        start_row = (cycle_steps - offset) * token_count
        block_keys = window_keys[:, start_row : start_row + token_count]
        block_values = window_values[:, start_row : start_row + token_count]
        if carried is not None:
            block_keys = block_keys + carried[0]
            block_values = block_values + carried[1]
        carried = (
            from_behind(block_keys.astype(jnp.bfloat16), "ctx", -1).astype(block_keys.dtype),
            from_behind(block_values.astype(jnp.bfloat16), "ctx", -1).astype(block_values.dtype),
        )
    local_keys = local_keys + carried[0]
    local_values = local_values + carried[1]
    grad_merged = jnp.stack([grad_query, local_keys, local_values], axis=2).astype(jnp.bfloat16)
    grad_merged_bias = jnp.stack(
        [
            jnp.sum(grad_merged[:, :, 0], axis=(0, 1), dtype=jnp.float32),
            jnp.sum(grad_merged[:, :, 2], axis=(0, 1), dtype=jnp.float32),
        ]
    ).reshape(merged_bias.shape)
    grad_merged_weight = jnp.einsum(
        "std,stkf->dkf", first_rows, grad_merged, preferred_element_type=jnp.float32
    )
    grad_first = gather_sums(
        jnp.einsum("stkf,dkf->std", grad_merged, merged_weight, preferred_element_type=jnp.float32)
    )
    _, first_pull = jax.vjp(
        layer_norm, stream, first_gain.astype(jnp.float32), first_shift.astype(jnp.float32)
    )
    grad_norm_in, grad_first_gain, grad_first_shift = first_pull(grad_first)
    grad_input = grad_middle + grad_norm_in
    grad_output_bias = jnp.sum(grad_middle, axis=(0, 1))
    vector_grads = lax.psum(
        (
            grad_first_gain,
            grad_first_shift,
            grad_second_gain,
            grad_second_shift,
            grad_output_bias,
            grad_reduce_bias,
        ),
        "tp",
    )
    fresh = (
        vector_grads[0],
        vector_grads[1],
        grad_merged_weight,
        grad_merged_bias,
        grad_output,
        vector_grads[4],
        vector_grads[2],
        vector_grads[3],
        grad_expand,
        grad_expand_bias,
        grad_reduce,
        vector_grads[5],
    )
    return (grad_input, reduce_grads(fresh))


def general_shards(
    inputs,
    segments,
    cotangent,
    student_first_gain,
    student_first_shift,
    student_merged_weight,
    student_merged_bias,
    student_output_weight,
    student_output_bias,
    student_second_gain,
    student_second_shift,
    student_expand_weight,
    student_expand_bias,
    student_reduce_weight,
    student_reduce_bias,
    teacher_first_gain,
    teacher_first_shift,
    teacher_merged_weight,
    teacher_merged_bias,
    teacher_output_weight,
    teacher_output_bias,
    teacher_second_gain,
    teacher_second_shift,
    teacher_expand_weight,
    teacher_expand_bias,
    teacher_reduce_weight,
    teacher_reduce_bias,
):
    student = (
        student_first_gain,
        student_first_shift,
        student_merged_weight,
        student_merged_bias,
        student_output_weight,
        student_output_bias,
        student_second_gain,
        student_second_shift,
        student_expand_weight,
        student_expand_bias,
        student_reduce_weight,
        student_reduce_bias,
    )
    teacher = (
        teacher_first_gain,
        teacher_first_shift,
        teacher_merged_weight,
        teacher_merged_bias,
        teacher_output_weight,
        teacher_output_bias,
        teacher_second_gain,
        teacher_second_shift,
        teacher_expand_weight,
        teacher_expand_bias,
        teacher_reduce_weight,
        teacher_reduce_bias,
    )
    token_count = segments.shape[1]
    context_size = lax.axis_size("ctx")
    context_index = lax.axis_index("ctx")
    doc_long = min(DOC_MAX, token_count * context_size // 2)
    cycle_steps = min((doc_long - 2) // token_count + 1, context_size - 1)
    doc_list = [segments]
    moving = segments
    for offset in range(cycle_steps):
        moving = from_behind(moving, "ctx", 1)
        doc_list.insert(0, moving)
    key_docs = jnp.concatenate(doc_list, axis=1)
    places = jnp.arange((cycle_steps + 1) * token_count, dtype=jnp.int32)
    relative = places - cycle_steps * token_count
    source = cycle_steps - places // token_count
    query_place = jnp.arange(token_count, dtype=jnp.int32)
    allowed = (relative[None, :] <= query_place[:, None]) & (source <= context_index)[None, :]
    stream = inputs.astype(jnp.float32)
    middle_stream, student_saved = layer_forward(
        stream, student, segments, key_docs, allowed, cycle_steps
    )
    final_stream, teacher_saved = layer_forward(
        middle_stream, teacher, segments, key_docs, allowed, cycle_steps
    )
    teacher_in_grad, teacher_grads = layer_backward(
        cotangent.astype(jnp.float32), teacher_saved, allowed, cycle_steps, token_count
    )
    input_grad, student_grads = layer_backward(
        teacher_in_grad, student_saved, allowed, cycle_steps, token_count
    )
    return (
        (final_stream.astype(jnp.bfloat16), input_grad)
        + tuple(student_grads)
        + tuple(teacher_grads)
    )


BF16 = jnp.bfloat16
F32 = jnp.float32
NEG = -1e30
TILE = 256
RELATIVE = (0, 2, 1, 3)


def swap(value, axis, bit):
    route = [(i, i ^ bit) for i in range(lax.axis_size(axis))]
    return lax.ppermute(value, axis, route)


def cross_core(value):
    return swap(value, "tp", 1)


def cross_x(value):
    return swap(value, "tp", 2)


def cross_y(value):
    return swap(value, "ctx", 1)


def shift_z(value, distance):
    count = lax.axis_size("dp")
    return lax.ppermute(value, "dp", [(i, (i + distance) % count) for i in range(count)])


def gather_z(piece):
    return [piece] + [shift_z(piece, k) for k in range(1, lax.axis_size("dp"))]


def scatter_z(pieces):
    total = pieces[0].astype(F32)
    for k in range(1, len(pieces)):
        total = total + shift_z(pieces[k].astype(BF16), -k).astype(F32)
    return total


def y_order(own, other, y_index, axis):
    return jnp.where(
        y_index == 0,
        jnp.concatenate([own, other], axis=axis),
        jnp.concatenate([other, own], axis=axis),
    )


def window_start(block, doc_max):
    return max(0, (block * TILE - doc_max + 1) // TILE) * TILE


def load_rows(source, target, me, columns, scale=None):
    rows = source.shape[0] // 8
    for r in range(4):
        for half in range(2):
            place = pl.multiple_of((half * 4 + (me ^ RELATIVE[r])) * rows, rows)
            value = source[(r * 2 + half) * rows : (r * 2 + half + 1) * rows, columns]
            if scale is not None:
                value = value * scale
            target[pl.ds(place, rows), columns] = value


def store_rows(source, target, me):
    rows = target.shape[0] // 8
    for r in range(4):
        for half in range(2):
            place = pl.multiple_of((half * 4 + (me ^ RELATIVE[r])) * rows, rows)
            target[(r * 2 + half) * rows : (r * 2 + half + 1) * rows, :] = source[
                pl.ds(place, rows), :
            ].astype(target.dtype)


def keep_mask(row_docs, column_docs, block, start):
    size = (block + 1) * TILE - start
    rows = block * TILE + lax.broadcasted_iota(jnp.int32, (TILE, size), 0)
    columns = start + lax.broadcasted_iota(jnp.int32, (TILE, size), 1)
    same = (
        row_docs[block * TILE : (block + 1) * TILE, :] == column_docs[:, start : start + size]
    )
    return same & (columns <= rows)


def attention_forward_kernel(
    heads, doc_max, me_ref, qkv_ref, row_docs, column_docs, mixed_ref, log_ref, qkv, mixed
):
    me = me_ref[0]
    width = heads * HD
    load_rows(qkv_ref, qkv, me, slice(0, width), BF16(0.125))
    load_rows(qkv_ref, qkv, me, slice(width, 3 * width))
    for block in range(qkv.shape[0] // TILE):
        start = window_start(block, doc_max)
        stop = (block + 1) * TILE
        mask = keep_mask(row_docs, column_docs, block, start)
        here = slice(block * TILE, stop)
        for h in range(heads):
            at = slice(h * HD, (h + 1) * HD)
            query = qkv[here, at]
            key = qkv[start:stop, width + h * HD : width + (h + 1) * HD]
            value = qkv[start:stop, 2 * width + h * HD : 2 * width + (h + 1) * HD]
            scores = lax.dot_general(
                query, key, (((1,), (1,)), ((), ())), preferred_element_type=F32
            )
            scores = jnp.where(mask, scores, NEG)
            top = jnp.max(scores, axis=-1, keepdims=True)
            raised = jnp.exp(scores - top)
            total = jnp.sum(raised, axis=-1, keepdims=True)
            weights = (raised * (1.0 / total)).astype(BF16)
            mixed[here, at] = jnp.dot(weights, value, preferred_element_type=F32).astype(BF16)
            log_ref[here, h : h + 1] = top + jnp.log(total)
    store_rows(mixed, mixed_ref, me)


def attention_backward_kernel(
    heads,
    doc_max,
    me_ref,
    qkv_ref,
    row_docs,
    column_docs,
    log_ref,
    mixed_ref,
    grad_ref,
    out_ref,
    qkv,
    grad,
    mixed,
    total,
):
    me = me_ref[0]
    width = heads * HD
    load_rows(qkv_ref, qkv, me, slice(0, width), BF16(0.125))
    load_rows(qkv_ref, qkv, me, slice(width, 3 * width))
    load_rows(grad_ref, grad, me, slice(0, width))
    load_rows(mixed_ref, mixed, me, slice(0, width))
    total[:, width:] = jnp.zeros((total.shape[0], 2 * width), F32)
    for block in range(qkv.shape[0] // TILE):
        start = window_start(block, doc_max)
        stop = (block + 1) * TILE
        mask = keep_mask(row_docs, column_docs, block, start)
        here = slice(block * TILE, stop)
        for h in range(heads):
            at = slice(h * HD, (h + 1) * HD)
            at_key = slice(width + h * HD, width + (h + 1) * HD)
            at_value = slice(2 * width + h * HD, 2 * width + (h + 1) * HD)
            query = qkv[here, at]
            key = qkv[start:stop, at_key]
            value = qkv[start:stop, at_value]
            grad_rows = grad[here, at]
            scores = lax.dot_general(
                query, key, (((1,), (1,)), ((), ())), preferred_element_type=F32
            )
            weights = jnp.where(mask, jnp.exp(scores - log_ref[here, h : h + 1]), 0.0)
            grad_weights = lax.dot_general(
                grad_rows, value, (((1,), (1,)), ((), ())), preferred_element_type=F32
            )
            centered = jnp.sum(
                grad_rows.astype(F32) * mixed[here, at].astype(F32), axis=-1, keepdims=True
            )
            grad_scores = (weights * (grad_weights - centered)).astype(BF16)
            total[here, at] = jnp.dot(grad_scores, key, preferred_element_type=F32) * 0.125
            total[start:stop, at_key] += lax.dot_general(
                grad_scores, query, (((0,), (0,)), ((), ())), preferred_element_type=F32
            )
            total[start:stop, at_value] += lax.dot_general(
                weights.astype(BF16), grad_rows, (((0,), (0,)), ((), ())), preferred_element_type=F32
            )
    store_rows(total, out_ref, me)


def attention_forward(qkv, me, row_docs, column_docs, doc_max):
    length, width = qkv.shape[0], qkv.shape[1] // 3
    heads = width // HD
    area = heads * length * length // 2
    vmem = pl.BlockSpec(memory_space=pltpu.VMEM)

    def body(*refs):
        attention_forward_kernel(heads, doc_max, *refs)

    return pl.pallas_call(
        body,
        out_shape=(
            jax.ShapeDtypeStruct((length, width), BF16),
            jax.ShapeDtypeStruct((length, heads), F32),
        ),
        in_specs=[pl.BlockSpec(memory_space=pltpu.SMEM), vmem, vmem, vmem],
        out_specs=(vmem, vmem),
        scratch_shapes=[pltpu.VMEM((length, 3 * width), BF16), pltpu.VMEM((length, width), BF16)],
        cost_estimate=pl.CostEstimate(
            flops=16 * HD * area, transcendentals=area, bytes_accessed=8 * length * width
        ),
        compiler_params=pltpu.CompilerParams(vmem_limit_bytes=40 << 20),
        name="attention_forward",
    )(me, qkv, row_docs, column_docs)


def attention_backward(qkv, me, row_docs, column_docs, log_total, mixed, grad_mixed, doc_max):
    length, width = qkv.shape[0], qkv.shape[1] // 3
    heads = width // HD
    area = heads * length * length // 2
    vmem = pl.BlockSpec(memory_space=pltpu.VMEM)

    def body(*refs):
        attention_backward_kernel(heads, doc_max, *refs)

    return pl.pallas_call(
        body,
        out_shape=jax.ShapeDtypeStruct((length, 3 * width), BF16),
        in_specs=[pl.BlockSpec(memory_space=pltpu.SMEM)] + [vmem] * 6,
        out_specs=vmem,
        scratch_shapes=[
            pltpu.VMEM((length, 3 * width), BF16),
            pltpu.VMEM((length, width), BF16),
            pltpu.VMEM((length, width), BF16),
            pltpu.VMEM((length, 3 * width), F32),
        ],
        cost_estimate=pl.CostEstimate(
            flops=40 * HD * area, transcendentals=area, bytes_accessed=16 * length * width
        ),
        compiler_params=pltpu.CompilerParams(vmem_limit_bytes=40 << 20),
        name="attention_backward",
    )(me, qkv, row_docs, column_docs, log_total, mixed, grad_mixed)


def normalize(values):
    center = values - jnp.mean(values, axis=-1, keepdims=True)
    spread = jnp.mean(center * center, axis=-1, keepdims=True)
    scale = lax.rsqrt(spread + EPSILON)
    return center * scale, scale


def norm_pullback(grad, unit, scale, gain):
    inner = grad * gain
    return scale * (
        inner
        - jnp.mean(inner, axis=-1, keepdims=True)
        - unit * jnp.mean(inner * unit, axis=-1, keepdims=True)
    )


def gather_rows(rows):
    pair = jnp.concatenate([rows, cross_x(rows)], axis=0)
    return jnp.concatenate([pair, cross_core(pair)], axis=0)


def gather_core(rows):
    return jnp.concatenate([rows, cross_core(rows)], axis=0)


def times(left, right, kind=F32):
    return jnp.dot(left, right, preferred_element_type=F32).astype(kind)


def times_across(left, right, kind=F32):
    return lax.dot_general(
        left, right, (((1,), (1,)), ((), ())), preferred_element_type=F32
    ).astype(kind)


def times_down(left, right, kind=F32):
    return lax.dot_general(
        left, right, (((0,), (0,)), ((), ())), preferred_element_type=F32
    ).astype(kind)


def scatter_rows(left, multiply):
    half = left.shape[0] // 2
    quarter = half // 2
    sent = cross_core(multiply(left[half:], BF16))
    kept = multiply(left[:half], F32) + sent.astype(F32)
    return kept[:quarter] + cross_x(kept[quarter:].astype(BF16)).astype(F32)


def scatter_core(left, multiply):
    half = left.shape[0] // 2
    sent = cross_core(multiply(left[half:], BF16))
    return multiply(left[:half], F32) + sent.astype(F32)


def halves(shard, y_index):
    middle = shard.shape[0] // 2
    own = jnp.where(y_index == 0, shard[:middle], shard[middle:])
    other = jnp.where(y_index == 0, shard[middle:], shard[:middle])
    return own, other


def fetch_matrices(params, y_index):
    merged, output, expand, reduce = params
    rows = merged.shape[0]
    attend_shard = jnp.concatenate([merged.reshape(rows, -1), output.T], axis=1)
    attend_half, _ = halves(attend_shard, y_index)
    attend_part = jnp.concatenate(gather_z(attend_half), axis=0)
    attend = jnp.concatenate([attend_part, cross_y(attend_part)], axis=0)
    expand_half, _ = halves(expand, y_index)
    expand_part = jnp.concatenate(gather_z(expand_half), axis=0)
    expand_part = jnp.concatenate([expand_part, cross_x(expand_part)], axis=1)
    expand_all = jnp.concatenate([expand_part, cross_y(expand_part)], axis=0)
    own, other = halves(reduce.T, y_index)
    pieces = gather_z(jnp.concatenate([own, other], axis=0))
    middle = rows // 2
    reduce_part = jnp.concatenate([p[:middle] for p in pieces] + [p[middle:] for p in pieces], axis=0)
    reduce_all = jnp.concatenate([reduce_part, cross_x(reduce_part)], axis=1)
    width = merged.shape[2] * 3
    return attend[:, :width], attend[:, width:], expand_all, reduce_all


def finish_y(part, y_index):
    part = part.astype(BF16)
    return y_order(part, cross_y(part), y_index, 0).astype(F32)


def return_split(grad, y_index):
    middle = grad.shape[0] // 2
    return grad[:middle].astype(F32) + cross_y(grad[middle:]).astype(F32)


def own_columns(grad):
    middle = grad.shape[1] // 2
    return grad[:, :middle].astype(F32) + cross_x(grad[:, middle:].astype(BF16)).astype(F32)


def blocks_of(grad, count):
    rows = grad.shape[0] // count
    return [grad[k * rows : (k + 1) * rows] for k in range(count)]


def return_attend(grad, y_index):
    count = lax.axis_size("dp")
    part = return_split(grad, y_index)
    return finish_y(scatter_z(blocks_of(part, count)), y_index)


def return_expand(grad, y_index):
    count = lax.axis_size("dp")
    part = own_columns(return_split(grad, y_index))
    return finish_y(scatter_z(blocks_of(part, count)), y_index)


def return_reduce(grad, y_index):
    count = lax.axis_size("dp")
    part = blocks_of(own_columns(grad), 2 * count)
    pieces = [jnp.concatenate([part[k], part[count + k]], axis=0) for k in range(count)]
    mine = scatter_z(pieces).astype(BF16)
    middle = mine.shape[0] // 2
    whole = mine.astype(F32) + cross_y(jnp.concatenate([mine[middle:], mine[:middle]], axis=0)).astype(
        F32
    )
    return jnp.where(y_index == 0, whole, jnp.concatenate([whole[middle:], whole[:middle]], axis=0))


def fetch_vectors(blocks, y_index, z_index):
    count = lax.axis_size("dp")
    rows = []
    for block in blocks:
        gains, merged_bias, expand_bias = block
        local = gains[0].shape[0]
        rows.append(jnp.concatenate([g.reshape(1, local) for g in gains], axis=1))
        rows.append(merged_bias.reshape(1, -1))
        rows.append(expand_bias.reshape(1, -1))
    pack = jnp.concatenate(rows, axis=1)
    pieces = jnp.concatenate(gather_z(pack), axis=0).astype(F32)
    natural = jnp.take(pieces, (z_index - jnp.arange(count)) % count, axis=0)
    result = []
    at = 0
    for block in blocks:
        gains, merged_bias, expand_bias = block
        local = gains[0].shape[0]
        middle = local // 2
        part = pieces[:, at : at + 6 * local].reshape(count, 6, 2, middle)
        part = jnp.where(y_index == 0, part, part[:, :, ::-1])
        vectors = part.transpose(1, 2, 0, 3).reshape(6, 2 * count * middle)
        at = at + 6 * local
        size = merged_bias.size
        part = natural[:, at : at + size].reshape((count,) + merged_bias.shape)
        biases = part.transpose(1, 2, 0, 3).reshape(2, -1)
        at = at + size
        size = expand_bias.size
        part = natural[:, at : at + size].reshape((count,) + expand_bias.shape)
        hidden_bias = part.transpose(1, 0, 2).reshape(1, -1)
        at = at + size
        result.append((vectors, biases, hidden_bias))
    others = cross_x(jnp.concatenate([r[2] for r in result], axis=0).astype(BF16)).astype(F32)
    return [
        (r[0], r[1], jnp.concatenate([r[2], others[i : i + 1]], axis=1))
        for i, r in enumerate(result)
    ]


def fast_forward(stream, weights, vectors, me, row_docs, column_docs, doc_max):
    merged, output, expand, reduce = weights
    gains, biases, hidden_bias = vectors
    width = output.shape[1]
    unit, scale = normalize(stream)
    rows = gather_rows((unit * gains[0] + gains[1]).astype(BF16))
    added = jnp.concatenate([biases[0], jnp.zeros((width,), F32), biases[1]])
    qkv = (times(rows, merged) + added).astype(BF16)
    mixed, log_total = attention_forward(qkv, me, row_docs, column_docs, doc_max)
    middle = stream + gains[2] + scatter_rows(mixed, lambda v, kind: times_across(v, output, kind))
    unit_two, scale_two = normalize(middle)
    rows_two = gather_core((unit_two * gains[3] + gains[4]).astype(BF16))
    hidden = times(rows_two, expand) + hidden_bias
    active = gelu_tanh(hidden).astype(BF16)
    result = (
        middle + gains[5] + scatter_core(active, lambda v, kind: times_across(v, reduce, kind))
    )
    saved = (stream, rows, qkv, mixed, log_total, middle, rows_two, hidden, active)
    return result, saved


def fast_backward(grad_out, saved, weights, vectors, me, row_docs, column_docs, doc_max, y_index):
    stream, rows, qkv, mixed, log_total, middle, rows_two, hidden, active = saved
    merged, output, expand, reduce = weights
    gains, biases, hidden_bias = vectors
    width = output.shape[1]
    branch = gather_core(grad_out.astype(BF16))
    grad_reduce = times_down(branch, active, BF16)
    grad_active = times(branch, reduce)
    _, gelu_pull = jax.vjp(gelu_tanh, hidden)
    grad_hidden = gelu_pull(grad_active)[0].astype(BF16)
    grad_hidden_bias = jnp.sum(grad_hidden.astype(F32), axis=0)
    grad_expand = times_down(rows_two, grad_hidden, BF16)
    grad_second = scatter_core(grad_hidden, lambda v, kind: times_across(v, expand, kind))
    grad_reduce = return_reduce(grad_reduce, y_index)
    grad_expand = return_expand(grad_expand, y_index)
    unit_two, scale_two = normalize(middle)
    grad_middle = grad_out + norm_pullback(grad_second, unit_two, scale_two, gains[3])
    attend = gather_rows(grad_middle.astype(BF16))
    grad_mixed = times(attend, output, BF16)
    grad_qkv = attention_backward(
        qkv, me, row_docs, column_docs, log_total, mixed, grad_mixed, doc_max
    )
    grad_merged = times_down(rows, grad_qkv, BF16)
    grad_output = times_down(attend, mixed, BF16)
    grad_pack = return_attend(jnp.concatenate([grad_merged, grad_output], axis=1), y_index)
    grad_bias = jnp.sum(grad_qkv.astype(F32), axis=0)
    grad_first = scatter_rows(grad_qkv, lambda v, kind: times_across(v, merged, kind))
    unit, scale = normalize(stream)
    grad_in = grad_middle + norm_pullback(grad_first, unit, scale, gains[0])
    sums = jnp.stack(
        [
            jnp.sum(grad_first * unit, axis=0),
            jnp.sum(grad_first, axis=0),
            jnp.sum(grad_middle, axis=0),
            jnp.sum(grad_second * unit_two, axis=0),
            jnp.sum(grad_second, axis=0),
            jnp.sum(grad_out, axis=0),
        ]
    )
    biases = jnp.concatenate([grad_bias[:width], grad_bias[2 * width :]])
    return grad_in, (sums, biases, grad_hidden_bias), (grad_pack, grad_expand, grad_reduce)


def return_vectors(grads, shapes, y_index, z_index):
    count = lax.axis_size("dp")
    sums = jnp.concatenate([g[0] for g in grads], axis=0)
    sums = sums + cross_core(sums)
    sums = sums + cross_x(sums)
    hidden = jnp.stack([g[2] for g in grads])
    middle = hidden.shape[1] // 2
    hidden = hidden[:, :middle] + cross_x(hidden[:, middle:])
    biases = jnp.stack([g[1] for g in grads])
    number = len(grads)
    local = sums.shape[1] // count
    parts = sums.reshape(6 * number, 2, count, local // 2)
    parts = jnp.where(y_index == 0, parts, parts[:, ::-1])
    parts = parts.transpose(2, 0, 1, 3).reshape(count, 1, -1)
    order = (z_index - jnp.arange(count)) % count
    bias_parts = jnp.take(
        biases.reshape(-1, count, biases.shape[1] * number // shapes[0].size * shapes[0].shape[-1])
        if False
        else biases.reshape(-1, count, shapes[0].shape[-1]),
        order,
        axis=1,
    )
    bias_parts = bias_parts.transpose(1, 0, 2).reshape(count, 1, -1)
    hidden_parts = jnp.take(hidden.reshape(-1, count, shapes[1].shape[-1]), order, axis=1)
    hidden_parts = hidden_parts.transpose(1, 0, 2).reshape(count, 1, -1)
    pack = jnp.concatenate([parts, bias_parts, hidden_parts], axis=2)
    pack = pack + cross_y(pack)
    total = pack[0]
    for k in range(1, count):
        total = total + shift_z(pack[k], -k)
    result = []
    first = 6 * number * local
    bias_size = shapes[0].size
    hidden_size = shapes[1].size
    for i in range(number):
        vectors = total[0, i * 6 * local : (i + 1) * 6 * local].reshape(6, local)
        at = first + i * bias_size
        bias = total[0, at : at + bias_size].reshape(shapes[0].shape)
        at = first + number * bias_size + i * hidden_size
        hidden_bias = total[0, at : at + hidden_size].reshape(shapes[1].shape)
        result.append((vectors, bias, hidden_bias))
    return result


def order_matrix(width, y_index, z_index):
    count = lax.axis_size("dp")
    rows = width // (2 * count)
    natural = lax.broadcasted_iota(jnp.int32, (width, width), 0)
    place = lax.broadcasted_iota(jnp.int32, (width, width), 1)
    half, rest = place // (width // 2), place % (width // 2)
    step, inner = rest // rows, rest % rows
    wanted = ((z_index - step) % count) * (2 * rows) + (half ^ y_index) * rows + inner
    return (natural == wanted).astype(BF16)


def my_rows(pair, y_index):
    own = jnp.where(y_index == 0, pair[0], pair[1])
    sent = jnp.where(y_index == 0, pair[1], pair[0])
    return own, cross_y(sent)


def fast_shards(inputs, segments, cotangent, *params):
    y_index = lax.axis_index("ctx")
    z_index = lax.axis_index("dp")
    me = lax.axis_index("tp")
    tokens, features = inputs.shape[1], inputs.shape[2]
    length = segments.shape[1] * 2
    doc_max = min(DOC_MAX, length // 2)
    blocks = (params[:12], params[12:])
    vectors = fetch_vectors(
        [((p[0], p[1], p[5], p[6], p[7], p[11]), p[3], p[9]) for p in blocks], y_index, z_index
    )
    weights = [fetch_matrices((p[2], p[4], p[8], p[10]), y_index) for p in blocks]
    chooser = order_matrix(features, y_index, z_index)
    own, other = my_rows(inputs, y_index)
    stream = times(y_order(own, other, y_index, 0), chooser)
    own, other = my_rows(cotangent, y_index)
    grad_out = times(y_order(own, other, y_index, 0), chooser)
    own, other = my_rows(segments, y_index)
    docs = y_order(own, other, y_index, 0)
    row_docs, column_docs = docs.reshape(length, 1), docs.reshape(1, length)
    me_list = me.astype(jnp.int32).reshape(1)
    context = (me_list, row_docs, column_docs, doc_max)
    middle_stream, student_saved = fast_forward(stream, weights[0], vectors[0], *context)
    final_stream, teacher_saved = fast_forward(middle_stream, weights[1], vectors[1], *context)
    grad_between, teacher_small, teacher_large = fast_backward(
        grad_out, teacher_saved, weights[1], vectors[1], *context, y_index
    )
    grad_in, student_small, student_large = fast_backward(
        grad_between, student_saved, weights[0], vectors[0], *context, y_index
    )
    small = return_vectors(
        [student_small, teacher_small], (params[3], params[9]), y_index, z_index
    )

    def restore(value):
        first, second = value[:tokens], value[tokens:]
        kept = jnp.where(y_index == 0, first, second)
        sent = jnp.where(y_index == 0, second, first)
        received = cross_y(sent)
        return jnp.where(
            y_index == 0, jnp.stack([kept, received]), jnp.stack([received, kept])
        )

    final = times_across(final_stream.astype(BF16), chooser, BF16)
    input_grad = lax.dot_general(
        grad_in,
        chooser.astype(F32),
        (((1,), (1,)), ((), ())),
        precision=lax.Precision.HIGHEST,
        preferred_element_type=F32,
    )
    outputs = [restore(final), restore(input_grad)]
    for (sums, bias, hidden_bias), (pack, expand, reduce), p in zip(
        small, (student_large, teacher_large), blocks
    ):
        wide = p[2].shape[1] * p[2].shape[2]
        outputs += [
            sums[0],
            sums[1],
            pack[:, :wide].reshape(p[2].shape),
            bias,
            pack[:, wide:].T,
            sums[2],
            sums[3],
            sums[4],
            expand,
            hidden_bias,
            reduce.T,
            sums[5],
        ]
    return tuple(outputs)


def solution(mesh):
    quick = mesh.shape["ctx"] == 2 and mesh.shape["tp"] == 4
    placed = (
        P("dp", ("ctx", "tp"), None),
        P("dp", "ctx"),
        P("dp", ("ctx", "tp"), None),
        P("dp"),
        P("dp"),
        P("dp", None, "tp"),
        P(None, "tp", "dp"),
        P("tp", "dp"),
        P("dp"),
        P("dp"),
        P("dp"),
        P("dp", "tp"),
        P("tp", "dp"),
        P("tp", "dp"),
        P("dp"),
        P("dp"),
        P("dp"),
        P("dp", None, "tp"),
        P(None, "tp", "dp"),
        P("tp", "dp"),
        P("dp"),
        P("dp"),
        P("dp"),
        P("dp", "tp"),
        P("tp", "dp"),
        P("tp", "dp"),
        P("dp"),
    )
    return jax.shard_map(
        fast_shards if quick else general_shards,
        mesh=mesh,
        in_specs=placed,
        out_specs=(
            P("dp", ("ctx", "tp"), None),
            P("dp", ("ctx", "tp"), None),
            P("dp"),
            P("dp"),
            P("dp", None, "tp"),
            P(None, "tp", "dp"),
            P("tp", "dp"),
            P("dp"),
            P("dp"),
            P("dp"),
            P("dp", "tp"),
            P("tp", "dp"),
            P("tp", "dp"),
            P("dp"),
            P("dp"),
            P("dp"),
            P("dp", None, "tp"),
            P(None, "tp", "dp"),
            P("tp", "dp"),
            P("dp"),
            P("dp"),
            P("dp"),
            P("dp", "tp"),
            P("tp", "dp"),
            P("tp", "dp"),
            P("dp"),
        ),
        check_vma=False,
    )
```

```python
import jax
import jax.numpy as jnp
from jax import lax
from jax.experimental import pallas as pl
from jax.experimental.layout import Layout, with_layout_constraint
from jax.experimental.pallas import tpu as pltpu
from jax.sharding import PartitionSpec as P

HD = 64
DOC_MAX = 2000


EPSILON = 1e-05
GELU_SCALE = 0.7978845608028654


def from_behind(block, axis, distance):
    devices = range(lax.axis_size(axis))
    route = [(i - distance, i) for i in devices if i - distance in devices]
    return lax.ppermute(block, axis, route)


def layer_norm(values, norm_gain, norm_shift):
    center = values - jnp.mean(values, axis=-1, keepdims=True)
    spread = jnp.mean(center * center, axis=-1, keepdims=True)
    return center * lax.rsqrt(spread + EPSILON) * norm_gain + norm_shift


def gelu_tanh(values):
    return (
        0.5 * values * (1.0 + jnp.tanh(GELU_SCALE * (values + 0.044715 * values * values * values)))
    )


def spread_rows(row_block):
    return lax.all_gather(row_block, "tp", axis=1, tiled=True)


def gather_sums(partial_value):
    return lax.psum_scatter(
        partial_value.astype(jnp.bfloat16), "tp", scatter_dimension=1, tiled=True
    ).astype(jnp.float32)


def to_items(tensor, head_count):
    batches, length, features = tensor.shape
    head_size = features // head_count
    return (
        tensor.reshape(batches, length, head_count, head_size)
        .transpose(0, 2, 1, 3)
        .reshape(batches * head_count, length, head_size)
    )


def from_items(tensor, head_count):
    item_count, length, head_size = tensor.shape
    batches = item_count // head_count
    return (
        tensor.reshape(batches, head_count, length, head_size)
        .transpose(0, 2, 1, 3)
        .reshape(batches, length, head_count * head_size)
    )


def masked_scores(query_rows, key_rows, query_docs, key_docs, allowed):
    raw_scores = (
        jnp.einsum("qd,kd->qk", query_rows, key_rows, preferred_element_type=jnp.float32) * 0.125
    )
    keep_mask = allowed & (key_docs[None, :] == query_docs[:, None])
    return (jnp.where(keep_mask, raw_scores, -1e30), keep_mask)


def attend_forward(allowed):

    def attend_item(packed):
        query_rows, key_rows, value_rows, query_docs, key_docs = packed
        scores, keep_mask = masked_scores(query_rows, key_rows, query_docs, key_docs, allowed)
        row_top = jnp.max(scores, axis=-1, keepdims=True)
        raised = jnp.exp(scores - row_top)
        row_total = jnp.sum(raised, axis=-1, keepdims=True)
        weights = (raised / row_total).astype(jnp.bfloat16)
        mixed_rows = jnp.dot(weights, value_rows, preferred_element_type=jnp.float32).astype(
            jnp.bfloat16
        )
        return (mixed_rows, row_top[:, 0] + jnp.log(row_total[:, 0]))

    return attend_item


def attend_backward(allowed):

    def attend_item(packed):
        query_rows, key_rows, value_rows, query_docs, key_docs, log_total, grad_rows = packed
        scores, keep_mask = masked_scores(query_rows, key_rows, query_docs, key_docs, allowed)
        weights = jnp.where(keep_mask, jnp.exp(scores - log_total[:, None]), 0.0)
        grad_values = jnp.einsum(
            "qk,qd->kd", weights.astype(jnp.bfloat16), grad_rows, preferred_element_type=jnp.float32
        )
        grad_weights = jnp.einsum(
            "qd,kd->qk", grad_rows, value_rows, preferred_element_type=jnp.float32
        )
        centered = jnp.sum(weights * grad_weights, axis=-1, keepdims=True)
        grad_scores = (weights * (grad_weights - centered)).astype(jnp.bfloat16)
        grad_query = jnp.dot(grad_scores, key_rows, preferred_element_type=jnp.float32) * 0.125
        grad_keys = (
            jnp.einsum("qk,qd->kd", grad_scores, query_rows, preferred_element_type=jnp.float32)
            * 0.125
        )
        return (grad_query, grad_keys, grad_values)

    return attend_item


def layer_forward(stream, params, segments, key_docs, allowed, cycle_steps):
    (
        first_gain,
        first_shift,
        merged_weight,
        merged_bias,
        output_weight,
        output_bias,
        second_gain,
        second_shift,
        expand_weight,
        expand_bias,
        reduce_weight,
        reduce_bias,
    ) = params
    fetched = (
        lax.all_gather(first_gain, "dp", axis=0, tiled=True),
        lax.all_gather(first_shift, "dp", axis=0, tiled=True),
        lax.all_gather(merged_weight, "dp", axis=0, tiled=True),
        lax.all_gather(merged_bias, "dp", axis=2, tiled=True),
        lax.all_gather(output_weight, "dp", axis=1, tiled=True),
        lax.all_gather(output_bias, "dp", axis=0, tiled=True),
        lax.all_gather(second_gain, "dp", axis=0, tiled=True),
        lax.all_gather(second_shift, "dp", axis=0, tiled=True),
        lax.all_gather(expand_weight, "dp", axis=0, tiled=True),
        lax.all_gather(expand_bias, "dp", axis=1, tiled=True),
        lax.all_gather(reduce_weight, "dp", axis=1, tiled=True),
        lax.all_gather(reduce_bias, "dp", axis=0, tiled=True),
    )
    (
        first_gain,
        first_shift,
        merged_weight,
        merged_bias,
        output_weight,
        output_bias,
        second_gain,
        second_shift,
        expand_weight,
        expand_bias,
        reduce_weight,
        reduce_bias,
    ) = fetched
    head_count = merged_weight.shape[2] // HD
    normed = layer_norm(
        stream, first_gain.astype(jnp.float32), first_shift.astype(jnp.float32)
    ).astype(jnp.bfloat16)
    first_rows = spread_rows(normed)
    merged_out = jnp.einsum(
        "std,dkf->stkf", first_rows, merged_weight, preferred_element_type=jnp.float32
    )
    bias_pair = merged_bias.astype(jnp.float32).reshape(2, -1)
    query_rows = (merged_out[:, :, 0] + bias_pair[0]).astype(jnp.bfloat16)
    key_rows = merged_out[:, :, 1].astype(jnp.bfloat16)
    value_rows = (merged_out[:, :, 2] + bias_pair[1]).astype(jnp.bfloat16)
    key_list = [key_rows]
    value_list = [value_rows]
    moving = (key_rows, value_rows)
    for offset in range(cycle_steps):
        moving = from_behind((moving[0], moving[1]), "ctx", 1)
        key_list.insert(0, moving[0])
        value_list.insert(0, moving[1])
    query_items = to_items(query_rows, head_count)
    key_items = to_items(jnp.concatenate(key_list, axis=1), head_count)
    value_items = to_items(jnp.concatenate(value_list, axis=1), head_count)
    query_docs = jnp.repeat(segments, head_count, axis=0)
    window_docs = jnp.repeat(key_docs, head_count, axis=0)
    mixed_items, log_total = lax.map(
        attend_forward(allowed), (query_items, key_items, value_items, query_docs, window_docs)
    )
    mixed = from_items(mixed_items, head_count)
    attn_part = jnp.einsum("stf,fd->std", mixed, output_weight, preferred_element_type=jnp.float32)
    middle = stream + gather_sums(attn_part) + output_bias.astype(jnp.float32)
    normed_two = layer_norm(
        middle, second_gain.astype(jnp.float32), second_shift.astype(jnp.float32)
    ).astype(jnp.bfloat16)
    second_rows = spread_rows(normed_two)
    hidden = jnp.einsum(
        "std,df->stf", second_rows, expand_weight, preferred_element_type=jnp.float32
    ) + expand_bias.astype(jnp.float32).reshape(-1)
    activated = gelu_tanh(hidden).astype(jnp.bfloat16)
    mlp_part = jnp.einsum(
        "stf,fd->std", activated, reduce_weight, preferred_element_type=jnp.float32
    )
    result = middle + gather_sums(mlp_part) + reduce_bias.astype(jnp.float32)
    saved_state = (
        fetched,
        stream,
        first_rows,
        query_items,
        key_items,
        value_items,
        query_docs,
        window_docs,
        log_total,
        mixed,
        middle,
        second_rows,
        hidden,
        activated,
    )
    return (result, saved_state)


def reduce_grads(fresh):
    (
        gain_one,
        shift_one,
        merged_weights,
        merged_biases,
        output_weights,
        output_biases,
        gain_two,
        shift_two,
        expand_weights,
        expand_biases,
        reduce_weights,
        reduce_biases,
    ) = fresh
    summed = (
        lax.psum(gain_one.astype(jnp.bfloat16), "ctx").astype(jnp.float32),
        lax.psum(shift_one.astype(jnp.bfloat16), "ctx").astype(jnp.float32),
        lax.psum(merged_weights.astype(jnp.bfloat16), "ctx").astype(jnp.float32),
        lax.psum(merged_biases.astype(jnp.bfloat16), "ctx").astype(jnp.float32),
        lax.psum(output_weights.astype(jnp.bfloat16), "ctx").astype(jnp.float32),
        lax.psum(output_biases.astype(jnp.bfloat16), "ctx").astype(jnp.float32),
        lax.psum(gain_two.astype(jnp.bfloat16), "ctx").astype(jnp.float32),
        lax.psum(shift_two.astype(jnp.bfloat16), "ctx").astype(jnp.float32),
        lax.psum(expand_weights.astype(jnp.bfloat16), "ctx").astype(jnp.float32),
        lax.psum(expand_biases.astype(jnp.bfloat16), "ctx").astype(jnp.float32),
        lax.psum(reduce_weights.astype(jnp.bfloat16), "ctx").astype(jnp.float32),
        lax.psum(reduce_biases.astype(jnp.bfloat16), "ctx").astype(jnp.float32),
    )
    (
        gain_one,
        shift_one,
        merged_weights,
        merged_biases,
        output_weights,
        output_biases,
        gain_two,
        shift_two,
        expand_weights,
        expand_biases,
        reduce_weights,
        reduce_biases,
    ) = summed
    return (
        lax.psum_scatter(
            gain_one.astype(jnp.bfloat16), "dp", scatter_dimension=0, tiled=True
        ).astype(jnp.float32),
        lax.psum_scatter(
            shift_one.astype(jnp.bfloat16), "dp", scatter_dimension=0, tiled=True
        ).astype(jnp.float32),
        lax.psum_scatter(
            merged_weights.astype(jnp.bfloat16), "dp", scatter_dimension=0, tiled=True
        ).astype(jnp.float32),
        lax.psum_scatter(
            merged_biases.astype(jnp.bfloat16), "dp", scatter_dimension=2, tiled=True
        ).astype(jnp.float32),
        lax.psum_scatter(
            output_weights.astype(jnp.bfloat16), "dp", scatter_dimension=1, tiled=True
        ).astype(jnp.float32),
        lax.psum_scatter(
            output_biases.astype(jnp.bfloat16), "dp", scatter_dimension=0, tiled=True
        ).astype(jnp.float32),
        lax.psum_scatter(
            gain_two.astype(jnp.bfloat16), "dp", scatter_dimension=0, tiled=True
        ).astype(jnp.float32),
        lax.psum_scatter(
            shift_two.astype(jnp.bfloat16), "dp", scatter_dimension=0, tiled=True
        ).astype(jnp.float32),
        lax.psum_scatter(
            expand_weights.astype(jnp.bfloat16), "dp", scatter_dimension=0, tiled=True
        ).astype(jnp.float32),
        lax.psum_scatter(
            expand_biases.astype(jnp.bfloat16), "dp", scatter_dimension=1, tiled=True
        ).astype(jnp.float32),
        lax.psum_scatter(
            reduce_weights.astype(jnp.bfloat16), "dp", scatter_dimension=1, tiled=True
        ).astype(jnp.float32),
        lax.psum_scatter(
            reduce_biases.astype(jnp.bfloat16), "dp", scatter_dimension=0, tiled=True
        ).astype(jnp.float32),
    )


def layer_backward(grad_out, saved_state, allowed, cycle_steps, token_count):
    (
        fetched,
        stream,
        first_rows,
        query_items,
        key_items,
        value_items,
        query_docs,
        window_docs,
        log_total,
        mixed,
        middle,
        second_rows,
        hidden,
        activated,
    ) = saved_state
    (
        first_gain,
        first_shift,
        merged_weight,
        merged_bias,
        output_weight,
        output_bias,
        second_gain,
        second_shift,
        expand_weight,
        expand_bias,
        reduce_weight,
        reduce_bias,
    ) = fetched
    head_count = merged_weight.shape[2] // HD
    grad_branch = spread_rows(grad_out.astype(jnp.bfloat16))
    grad_reduce = jnp.einsum(
        "stf,std->fd", activated, grad_branch, preferred_element_type=jnp.float32
    )
    grad_active = jnp.einsum(
        "std,fd->stf", grad_branch, reduce_weight, preferred_element_type=jnp.float32
    )
    _, gelu_pull = jax.vjp(gelu_tanh, hidden)
    grad_hidden = gelu_pull(grad_active)[0].astype(jnp.bfloat16)
    grad_expand_bias = jnp.sum(grad_hidden, axis=(0, 1), dtype=jnp.float32).reshape(
        expand_bias.shape
    )
    grad_expand = jnp.einsum(
        "std,stf->df", second_rows, grad_hidden, preferred_element_type=jnp.float32
    )
    grad_second = gather_sums(
        jnp.einsum("stf,df->std", grad_hidden, expand_weight, preferred_element_type=jnp.float32)
    )
    _, second_pull = jax.vjp(
        layer_norm, middle, second_gain.astype(jnp.float32), second_shift.astype(jnp.float32)
    )
    grad_norm_mid, grad_second_gain, grad_second_shift = second_pull(grad_second)
    grad_middle = grad_out + grad_norm_mid
    grad_reduce_bias = jnp.sum(grad_out, axis=(0, 1))
    grad_attend = spread_rows(grad_middle.astype(jnp.bfloat16))
    grad_output = jnp.einsum("stf,std->fd", mixed, grad_attend, preferred_element_type=jnp.float32)
    grad_mixed = jnp.einsum(
        "std,fd->stf", grad_attend, output_weight, preferred_element_type=jnp.float32
    ).astype(jnp.bfloat16)
    grad_query_items, grad_key_items, grad_value_items = lax.map(
        attend_backward(allowed),
        (
            query_items,
            key_items,
            value_items,
            query_docs,
            window_docs,
            log_total,
            to_items(grad_mixed, head_count),
        ),
    )
    grad_query = from_items(grad_query_items, head_count)
    window_keys = from_items(grad_key_items, head_count)
    window_values = from_items(grad_value_items, head_count)
    local_keys = window_keys[:, cycle_steps * token_count :]
    local_values = window_values[:, cycle_steps * token_count :]
    carried = None
    for offset in range(cycle_steps, 0, -1):
        start_row = (cycle_steps - offset) * token_count
        block_keys = window_keys[:, start_row : start_row + token_count]
        block_values = window_values[:, start_row : start_row + token_count]
        if carried is not None:
            block_keys = block_keys + carried[0]
            block_values = block_values + carried[1]
        carried = (
            from_behind(block_keys.astype(jnp.bfloat16), "ctx", -1).astype(block_keys.dtype),
            from_behind(block_values.astype(jnp.bfloat16), "ctx", -1).astype(block_values.dtype),
        )
    local_keys = local_keys + carried[0]
    local_values = local_values + carried[1]
    grad_merged = jnp.stack([grad_query, local_keys, local_values], axis=2).astype(jnp.bfloat16)
    grad_merged_bias = jnp.stack(
        [
            jnp.sum(grad_merged[:, :, 0], axis=(0, 1), dtype=jnp.float32),
            jnp.sum(grad_merged[:, :, 2], axis=(0, 1), dtype=jnp.float32),
        ]
    ).reshape(merged_bias.shape)
    grad_merged_weight = jnp.einsum(
        "std,stkf->dkf", first_rows, grad_merged, preferred_element_type=jnp.float32
    )
    grad_first = gather_sums(
        jnp.einsum("stkf,dkf->std", grad_merged, merged_weight, preferred_element_type=jnp.float32)
    )
    _, first_pull = jax.vjp(
        layer_norm, stream, first_gain.astype(jnp.float32), first_shift.astype(jnp.float32)
    )
    grad_norm_in, grad_first_gain, grad_first_shift = first_pull(grad_first)
    grad_input = grad_middle + grad_norm_in
    grad_output_bias = jnp.sum(grad_middle, axis=(0, 1))
    vector_grads = lax.psum(
        (
            grad_first_gain,
            grad_first_shift,
            grad_second_gain,
            grad_second_shift,
            grad_output_bias,
            grad_reduce_bias,
        ),
        "tp",
    )
    fresh = (
        vector_grads[0],
        vector_grads[1],
        grad_merged_weight,
        grad_merged_bias,
        grad_output,
        vector_grads[4],
        vector_grads[2],
        vector_grads[3],
        grad_expand,
        grad_expand_bias,
        grad_reduce,
        vector_grads[5],
    )
    return (grad_input, reduce_grads(fresh))


def general_shards(
    inputs,
    segments,
    cotangent,
    student_first_gain,
    student_first_shift,
    student_merged_weight,
    student_merged_bias,
    student_output_weight,
    student_output_bias,
    student_second_gain,
    student_second_shift,
    student_expand_weight,
    student_expand_bias,
    student_reduce_weight,
    student_reduce_bias,
    teacher_first_gain,
    teacher_first_shift,
    teacher_merged_weight,
    teacher_merged_bias,
    teacher_output_weight,
    teacher_output_bias,
    teacher_second_gain,
    teacher_second_shift,
    teacher_expand_weight,
    teacher_expand_bias,
    teacher_reduce_weight,
    teacher_reduce_bias,
):
    student = (
        student_first_gain,
        student_first_shift,
        student_merged_weight,
        student_merged_bias,
        student_output_weight,
        student_output_bias,
        student_second_gain,
        student_second_shift,
        student_expand_weight,
        student_expand_bias,
        student_reduce_weight,
        student_reduce_bias,
    )
    teacher = (
        teacher_first_gain,
        teacher_first_shift,
        teacher_merged_weight,
        teacher_merged_bias,
        teacher_output_weight,
        teacher_output_bias,
        teacher_second_gain,
        teacher_second_shift,
        teacher_expand_weight,
        teacher_expand_bias,
        teacher_reduce_weight,
        teacher_reduce_bias,
    )
    token_count = segments.shape[1]
    context_size = lax.axis_size("ctx")
    context_index = lax.axis_index("ctx")
    doc_long = min(DOC_MAX, token_count * context_size // 2)
    cycle_steps = min((doc_long - 2) // token_count + 1, context_size - 1)
    doc_list = [segments]
    moving = segments
    for offset in range(cycle_steps):
        moving = from_behind(moving, "ctx", 1)
        doc_list.insert(0, moving)
    key_docs = jnp.concatenate(doc_list, axis=1)
    places = jnp.arange((cycle_steps + 1) * token_count, dtype=jnp.int32)
    relative = places - cycle_steps * token_count
    source = cycle_steps - places // token_count
    query_place = jnp.arange(token_count, dtype=jnp.int32)
    allowed = (relative[None, :] <= query_place[:, None]) & (source <= context_index)[None, :]
    stream = inputs.astype(jnp.float32)
    middle_stream, student_saved = layer_forward(
        stream, student, segments, key_docs, allowed, cycle_steps
    )
    final_stream, teacher_saved = layer_forward(
        middle_stream, teacher, segments, key_docs, allowed, cycle_steps
    )
    teacher_in_grad, teacher_grads = layer_backward(
        cotangent.astype(jnp.float32), teacher_saved, allowed, cycle_steps, token_count
    )
    input_grad, student_grads = layer_backward(
        teacher_in_grad, student_saved, allowed, cycle_steps, token_count
    )
    return (
        (final_stream.astype(jnp.bfloat16), input_grad)
        + tuple(student_grads)
        + tuple(teacher_grads)
    )


BF16 = jnp.bfloat16
F32 = jnp.float32
NEG = -1e30
TILE = 256
RELATIVE = (0, 2, 1, 3)


def row_major(value):
    return with_layout_constraint(value, Layout(major_to_minor=tuple(range(value.ndim))))


def swap(value, axis, bit):
    route = [(i, i ^ bit) for i in range(lax.axis_size(axis))]
    if value.ndim == 2:
        return row_major(lax.ppermute(row_major(value), axis, route))
    return lax.ppermute(value, axis, route)


def cross_core(value):
    return swap(value, "tp", 1)


def cross_x(value):
    return swap(value, "tp", 2)


def cross_y(value):
    return swap(value, "ctx", 1)


def cross_near(value):
    return swap(value, "dp", 1)


def cross_far(value):
    return swap(value, "dp", 2)


def cross_both(value):
    return swap(value, "dp", 3)


def stacked(*values):
    return jnp.concatenate(values, axis=0)


def beside(*values):
    return jnp.concatenate(values, axis=1)


def y_order(own, other, y_index, axis):
    return jnp.where(
        y_index == 0,
        jnp.concatenate([own, other], axis=axis),
        jnp.concatenate([other, own], axis=axis),
    )


def pin(*values):
    return lax.optimization_barrier(values)


def window_start(block, doc_max):
    return max(0, (block * TILE - doc_max + 1) // TILE) * TILE


def token_place(me, member, half, rows):
    return pl.multiple_of((half * 4 + (me ^ RELATIVE[member])) * rows, rows)


def to_tokens(value, target, me, first):
    rows = value.shape[0] // 4
    for r in range(2):
        for half in range(2):
            place = token_place(me, first + r, half, rows)
            target[pl.ds(place, rows), :] = value[(r * 2 + half) * rows : (r * 2 + half + 1) * rows]


def from_tokens(source, me, first):
    rows = source.shape[0] // 8
    return jnp.concatenate(
        [
            source[pl.ds(token_place(me, first + r, half, rows), rows), :]
            for r in range(2)
            for half in range(2)
        ],
        axis=0,
    )


def keep_mask(row_docs, column_docs, block, start):
    size = (block + 1) * TILE - start
    rows = block * TILE + lax.broadcasted_iota(jnp.int32, (TILE, size), 0)
    columns = start + lax.broadcasted_iota(jnp.int32, (TILE, size), 1)
    same = (
        row_docs[block * TILE : (block + 1) * TILE, :] == column_docs[:, start : start + size]
    )
    return same & (columns <= rows)


def dot_across(left, right):
    return lax.dot_general(left, right, (((1,), (1,)), ((), ())), preferred_element_type=F32)


def dot_down(left, right):
    return lax.dot_general(left, right, (((0,), (0,)), ((), ())), preferred_element_type=F32)


def attention_forward_kernel(
    heads,
    doc_max,
    me_ref,
    near_ref,
    far_ref,
    attend_ref,
    bias_ref,
    row_docs,
    column_docs,
    sent_ref,
    kept_ref,
    qkv_ref,
    mixed_ref,
    log_ref,
    mixed,
):
    me = me_ref[0]
    width = heads * HD
    weight = attend_ref[:, : 3 * width]
    for piece, first in ((near_ref, 0), (far_ref, 2)):
        rows = jnp.dot(piece[...], weight, preferred_element_type=F32) + bias_ref[...]
        to_tokens(rows.astype(BF16), qkv_ref, me, first)
    for block in range(qkv_ref.shape[0] // TILE):
        start = window_start(block, doc_max)
        stop = (block + 1) * TILE
        mask = keep_mask(row_docs, column_docs, block, start)
        here = slice(block * TILE, stop)
        for h in range(heads):
            at = slice(h * HD, (h + 1) * HD)
            query = qkv_ref[here, at] * BF16(0.125)
            key = qkv_ref[start:stop, width + h * HD : width + (h + 1) * HD]
            value = qkv_ref[start:stop, 2 * width + h * HD : 2 * width + (h + 1) * HD]
            scores = jnp.where(mask, dot_across(query, key), NEG)
            top = jnp.max(scores, axis=-1, keepdims=True)
            raised = jnp.exp(scores - top)
            total = jnp.sum(raised, axis=-1, keepdims=True)
            weights = (raised * (1.0 / total)).astype(BF16)
            mixed[here, at] = jnp.dot(weights, value, preferred_element_type=F32).astype(BF16)
            log_ref[here, h : h + 1] = top + jnp.log(total)
    weight = attend_ref[:, 3 * width :]
    half = qkv_ref.shape[0] // 2
    rows = from_tokens(mixed, me, 2)
    mixed_ref[half:, :] = rows
    sent_ref[...] = dot_across(rows, weight).astype(BF16)
    rows = from_tokens(mixed, me, 0)
    mixed_ref[:half, :] = rows
    kept_ref[...] = dot_across(rows, weight)


def attention_backward_kernel(
    heads,
    doc_max,
    me_ref,
    near_ref,
    far_ref,
    attend_ref,
    row_docs,
    column_docs,
    qkv_ref,
    mixed_ref,
    log_ref,
    sent_ref,
    kept_ref,
    out_ref,
    sum_ref,
    grad,
    mixed,
    total,
):
    me = me_ref[0]
    width = heads * HD
    half = qkv_ref.shape[0] // 2
    weight = attend_ref[:, 3 * width :]
    for piece, first in ((near_ref, 0), (far_ref, 2)):
        rows = jnp.dot(piece[...], weight, preferred_element_type=F32).astype(BF16)
        to_tokens(rows, grad, me, first)
        to_tokens(mixed_ref[first // 2 * half : (first // 2 + 1) * half, :], mixed, me, first)
    total[:, width:] = jnp.zeros((total.shape[0], 2 * width), F32)
    for block in range(qkv_ref.shape[0] // TILE):
        start = window_start(block, doc_max)
        stop = (block + 1) * TILE
        mask = keep_mask(row_docs, column_docs, block, start)
        here = slice(block * TILE, stop)
        for h in range(heads):
            at = slice(h * HD, (h + 1) * HD)
            at_key = slice(width + h * HD, width + (h + 1) * HD)
            at_value = slice(2 * width + h * HD, 2 * width + (h + 1) * HD)
            query = qkv_ref[here, at] * BF16(0.125)
            key = qkv_ref[start:stop, at_key]
            value = qkv_ref[start:stop, at_value]
            grad_rows = grad[here, at]
            weights = jnp.where(
                mask, jnp.exp(dot_across(query, key) - log_ref[here, h : h + 1]), 0.0
            )
            grad_weights = dot_across(grad_rows, value)
            centered = jnp.sum(
                grad_rows.astype(F32) * mixed[here, at].astype(F32), axis=-1, keepdims=True
            )
            grad_scores = (weights * (grad_weights - centered)).astype(BF16)
            total[here, at] = jnp.dot(grad_scores, key, preferred_element_type=F32) * 0.125
            total[start:stop, at_key] += dot_down(grad_scores, query)
            total[start:stop, at_value] += dot_down(weights.astype(BF16), grad_rows)
    weight = attend_ref[:, : 3 * width]
    rows = from_tokens(total, me, 2).astype(BF16)
    out_ref[half:, :] = rows
    sent_ref[...] = dot_across(rows, weight).astype(BF16)
    sums = jnp.sum(rows.astype(F32), axis=0, keepdims=True)
    rows = from_tokens(total, me, 0).astype(BF16)
    out_ref[:half, :] = rows
    kept_ref[...] = dot_across(rows, weight)
    sum_ref[...] = sums + jnp.sum(rows.astype(F32), axis=0, keepdims=True)


VMEM = pl.BlockSpec(memory_space=pltpu.VMEM)
SMEM = pl.BlockSpec(memory_space=pltpu.SMEM)


def call(body, name, inputs, outputs, scratch, flops, transcendentals, limit=24):
    size = sum(v.size * v.dtype.itemsize for v in list(inputs) + list(outputs))
    return pl.pallas_call(
        body,
        out_shape=tuple(outputs),
        in_specs=[SMEM if v.ndim == 1 else VMEM for v in inputs],
        out_specs=tuple(VMEM for _ in outputs),
        scratch_shapes=scratch,
        cost_estimate=pl.CostEstimate(
            flops=flops, transcendentals=transcendentals, bytes_accessed=size
        ),
        compiler_params=pltpu.CompilerParams(vmem_limit_bytes=limit << 20),
        name=name,
    )(*inputs)


def shaped(rows, columns, kind):
    return jax.ShapeDtypeStruct((rows, columns), kind)


def attention_forward(near, far, attend, bias, context, doc_max):
    me, row_docs, column_docs = context
    half, features = near.shape
    width = attend.shape[1] // 4
    heads = width // HD
    area = heads * 2 * half * half

    def body(*refs):
        attention_forward_kernel(heads, doc_max, *refs)

    return call(
        body,
        "attention_forward",
        (me, near, far, attend, bias, row_docs, column_docs),
        (
            shaped(half, features, BF16),
            shaped(half, features, F32),
            shaped(2 * half, 3 * width, BF16),
            shaped(2 * half, width, BF16),
            shaped(2 * half, heads, F32),
        ),
        [pltpu.VMEM((2 * half, width), BF16)],
        16 * HD * area,
        area,
    )


def attention_backward(near, far, attend, context, saved, doc_max):
    me, row_docs, column_docs = context
    qkv, mixed, log_total = saved
    half, features = near.shape
    width = attend.shape[1] // 4
    heads = width // HD
    area = heads * 2 * half * half

    def body(*refs):
        attention_backward_kernel(heads, doc_max, *refs)

    return call(
        body,
        "attention_backward",
        (me, near, far, attend, row_docs, column_docs, qkv, mixed, log_total),
        (
            shaped(half, features, BF16),
            shaped(half, features, F32),
            shaped(2 * half, 3 * width, BF16),
            shaped(1, 3 * width, F32),
        ),
        [
            pltpu.VMEM((2 * half, width), BF16),
            pltpu.VMEM((2 * half, width), BF16),
            pltpu.VMEM((2 * half, 3 * width), F32),
        ],
        40 * HD * area,
        area,
    )


CHUNK = 256


def gelu_both(values):
    inner = GELU_SCALE * (values + 0.044715 * values * values * values)
    bent = jnp.tanh(inner)
    value = 0.5 * values * (1.0 + bent)
    slope = 0.5 * (1.0 + bent) + 0.5 * values * (1.0 - bent * bent) * GELU_SCALE * (
        1.0 + 3.0 * 0.044715 * values * values
    )
    return value, slope


def feed_forward_kernel(near_ref, far_ref, first_ref, second_ref, reduce_ref, bias_ref, sent_ref, kept_ref):
    part = first_ref.shape[1]
    for piece, out in ((far_ref, sent_ref), (near_ref, kept_ref)):

        def step(i, carry):
            at = pl.ds(pl.multiple_of(i * CHUNK, CHUNK), CHUNK)
            rows = piece[at, :]
            total = None
            for k, weight in enumerate((first_ref, second_ref)):
                columns = slice(k * part, (k + 1) * part)
                hidden = jnp.dot(rows, weight[...], preferred_element_type=F32)
                active = gelu_tanh(hidden + bias_ref[:, columns]).astype(BF16)
                product = dot_across(active, reduce_ref[:, columns])
                total = product if total is None else total + product
            out[at, :] = total.astype(out.dtype)
            return carry

        lax.fori_loop(0, piece.shape[0] // CHUNK, step, 0)


def feed_forward(near, far, first, second, reduce, bias):
    half, features = near.shape
    hidden = 2 * first.shape[1]
    return call(
        feed_forward_kernel,
        "feed_forward",
        (near, far, first, second, reduce, bias),
        (shaped(half, features, BF16), shaped(half, features, F32)),
        [],
        8 * half * features * hidden,
        2 * half * hidden,
    )


def feed_backward_kernel(
    near_ref,
    far_ref,
    near_grad,
    far_grad,
    first_ref,
    second_ref,
    reduce_ref,
    bias_ref,
    sent_ref,
    kept_ref,
    active_ref,
    hidden_ref,
    sum_ref,
):
    part = first_ref.shape[1]
    half = near_ref.shape[0]
    sum_ref[...] = jnp.zeros_like(sum_ref)
    for piece, grads, out, base in (
        (far_ref, far_grad, sent_ref, half),
        (near_ref, near_grad, kept_ref, 0),
    ):

        def step(i, carry):
            place = pl.multiple_of(i * CHUNK, CHUNK)
            at = pl.ds(place, CHUNK)
            whole = pl.ds(pl.multiple_of(base + place, CHUNK), CHUNK)
            rows = piece[at, :]
            grad_rows = grads[at, :]
            total = None
            for k, weight in enumerate((first_ref, second_ref)):
                columns = slice(k * part, (k + 1) * part)
                hidden = jnp.dot(rows, weight[...], preferred_element_type=F32)
                value, slope = gelu_both(hidden + bias_ref[:, columns])
                active_ref[whole, columns] = value.astype(BF16)
                grad_active = jnp.dot(
                    grad_rows, reduce_ref[:, columns], preferred_element_type=F32
                )
                grad_hidden = (grad_active * slope).astype(BF16)
                hidden_ref[whole, columns] = grad_hidden
                sum_ref[:, columns] += jnp.sum(grad_hidden.astype(F32), axis=0, keepdims=True)
                product = dot_across(grad_hidden, weight[...])
                total = product if total is None else total + product
            out[at, :] = total.astype(out.dtype)
            return carry

        lax.fori_loop(0, half // CHUNK, step, 0)


def feed_backward(near, far, near_grad, far_grad, first, second, reduce, bias):
    half, features = near.shape
    hidden = 2 * first.shape[1]
    return call(
        feed_backward_kernel,
        "feed_backward",
        (near, far, near_grad, far_grad, first, second, reduce, bias),
        (
            shaped(half, features, BF16),
            shaped(half, features, F32),
            shaped(2 * half, hidden, BF16),
            shaped(2 * half, hidden, BF16),
            shaped(1, hidden, F32),
        ),
        [],
        12 * half * features * hidden,
        2 * half * hidden,
    )


def row_block(rows, columns):
    return pl.BlockSpec((rows, columns), lambda i: (0, 0))


def row_call(body, name, inputs, rows, outputs):
    specs = [row_block(v.shape[0] if v.shape[0] < 16 else rows, v.shape[1]) for v in inputs]
    size = sum(rows * v.shape[1] * v.dtype.itemsize for v in inputs)
    return pl.pallas_call(
        body,
        grid=(1,),
        out_shape=tuple(outputs),
        in_specs=specs,
        out_specs=tuple(row_block(*v.shape) for v in outputs),
        cost_estimate=pl.CostEstimate(
            flops=20 * rows * inputs[0].shape[1], transcendentals=rows, bytes_accessed=2 * size
        ),
        compiler_params=pltpu.CompilerParams(vmem_limit_bytes=10 << 20),
        name=name,
    )(*inputs)


def add_norm(base, addends, vectors, bias_at, norm_vectors, norm_at):
    rows, columns = base.shape

    def body(*refs):
        base_ref, bias_ref, vector_ref = refs[:3]
        parts, (sum_ref, norm_ref) = refs[3:-2], refs[-2:]
        total = base_ref[...]
        if parts:
            total = total + bias_ref[bias_at : bias_at + 1, :]
        for part in parts:
            total = total + part[...].astype(F32)
        sum_ref[...] = total
        gain, shift = vector_ref[norm_at : norm_at + 1, :], vector_ref[norm_at + 1 : norm_at + 2, :]
        norm_ref[...] = (normalize(total)[0] * gain + shift).astype(BF16)

    return row_call(
        body,
        "add_norm",
        [base, vectors, norm_vectors] + list(addends),
        rows,
        (shaped(rows, columns, F32), shaped(rows, columns, BF16)),
    )


def norm_back(skip, addends, value, vectors, norm_at):
    rows, columns = skip.shape

    def body(*refs):
        skip_ref, value_ref, vector_ref = refs[:3]
        parts, (grad_ref, low_ref, sum_ref) = refs[3:-3], refs[-3:]
        grad = parts[0][...].astype(F32)
        for part in parts[1:]:
            grad = grad + part[...].astype(F32)
        unit, scale = normalize(value_ref[...])
        skipped = skip_ref[...]
        sum_ref[...] = jnp.concatenate(
            [jnp.sum(v, axis=0, keepdims=True) for v in (grad * unit, grad, skipped)]
            + [jnp.zeros((5, columns), F32)],
            axis=0,
        )
        total = skipped + norm_pullback(grad, unit, scale, vector_ref[norm_at : norm_at + 1, :])
        grad_ref[...] = total
        low_ref[...] = total.astype(BF16)

    return row_call(
        body,
        "norm_back",
        [skip, value, vectors] + list(addends),
        rows,
        (shaped(rows, columns, F32), shaped(rows, columns, BF16), shaped(8, columns, F32)),
    )


ROWS = 64


def pack_vectors(blocks):
    flat = []
    for gains, merged_bias, expand_bias in blocks:
        flat += list(gains) + [merged_bias, expand_bias]

    def body(*refs):
        out = refs[-1]
        out[...] = jnp.zeros_like(out)
        for b in range(2):
            part = refs[8 * b : 8 * b + 8]
            for i in range(6):
                local = part[i].shape[0]
                out[6 * b + i : 6 * b + i + 1, :local] = part[i][...].astype(F32).reshape(1, local)
            for i in range(2):
                value = part[6][i].astype(F32)
                out[16 + 8 * b + 3 * i : 19 + 8 * b + 3 * i, : value.shape[1]] = value
            value = part[7][...].astype(F32)
            out[32 + 16 * b : 32 + 16 * b + value.shape[0], : value.shape[1]] = value

    return pl.pallas_call(
        body,
        out_shape=shaped(ROWS, 256, F32),
        in_specs=[VMEM] * 16,
        out_specs=VMEM,
        compiler_params=pltpu.CompilerParams(vmem_limit_bytes=4 << 20),
        name="pack_vectors",
    )(*flat)


def unpack_vectors(pieces, place, local, merged_shape, expand_shape):
    heads, few = merged_shape[1], merged_shape[2]
    groups = expand_shape[0]
    width = heads * 4 * few

    def body(place_ref, pieces_ref, *outs):
        y, z = place_ref[0], place_ref[1]
        for b in range(2):
            gains, bias, hidden = outs[3 * b : 3 * b + 3]
            for k in range(4):
                gains[0:6, k * local : (k + 1) * local] = pieces_ref[
                    k * ROWS + 6 * b : k * ROWS + 6 * b + 6, :local
                ]
            bias[...] = jnp.zeros_like(bias)
            for natural in range(4):
                distance = z ^ natural
                base = (2 * (distance & 1) + (distance >> 1)) * ROWS
                part = pieces_ref[pl.ds(pl.multiple_of(base, ROWS), ROWS), :128]
                for i in range(2):
                    for h in range(heads):
                        line = 16 + 8 * b + 3 * i + h
                        at = 2 * i * width + h * 4 * few + natural * few
                        bias[:, at : at + few] = part[line : line + 1, :few]
                lines = part[32 + 16 * b : 32 + 16 * b + groups]
                half = groups // 2
                lines = jnp.where(
                    y == 0, lines, jnp.concatenate([lines[half:], lines[:half]], axis=0)
                )
                for p in range(groups):
                    at = p * 4 * few + natural * few
                    hidden[:, at : at + few] = lines[p : p + 1, :few]

    one = (
        shaped(8, 4 * local, F32),
        shaped(1, 3 * width, F32),
        shaped(1, groups * 4 * few, F32),
    )
    return pl.pallas_call(
        body,
        out_shape=one + one,
        in_specs=[SMEM, VMEM],
        out_specs=(VMEM,) * 6,
        compiler_params=pltpu.CompilerParams(vmem_limit_bytes=4 << 20),
        name="unpack_vectors",
    )(place, pieces)


def prepare(place, merged, output, expand, reduce, split):
    local = output.shape[1]
    half = expand.shape[1] // 2

    def body(place_ref, merged_ref, output_ref, expand_ref, reduce_ref, attend, feed):
        y = place_ref[0]
        eye = (
            lax.broadcasted_iota(jnp.int32, (local, local), 0)
            == lax.broadcasted_iota(jnp.int32, (local, local), 1)
        ).astype(BF16)
        pieces = [merged_ref[k] for k in range(3)] + [dot_across(eye, output_ref[...]).astype(BF16)]
        whole = jnp.concatenate(pieces, axis=1)
        if split:
            whole = jnp.where(y == 0, whole[:, :half], whole[:, half:])
        attend[...] = whole
        turned = dot_across(eye, reduce_ref[...]).astype(BF16)
        first, second = turned[:, :half], turned[:, half:]
        feed[:, :half] = jnp.where(y == 0, expand_ref[:, :half], expand_ref[:, half:])
        feed[:, half : 2 * half] = jnp.where(y == 0, first, second)
        feed[:, 2 * half :] = jnp.where(y == 0, second, first)

    return pl.pallas_call(
        body,
        out_shape=(shaped(local, (2 if split else 4) * local, BF16), shaped(local, 3 * half, BF16)),
        in_specs=[SMEM, VMEM, VMEM, VMEM, VMEM],
        out_specs=(VMEM, VMEM),
        compiler_params=pltpu.CompilerParams(vmem_limit_bytes=12 << 20),
        name="prepare",
    )(place, merged.transpose(1, 0, 2), output, expand, reduce)


def normalize(values):
    center = values - jnp.mean(values, axis=-1, keepdims=True)
    spread = jnp.mean(center * center, axis=-1, keepdims=True)
    scale = lax.rsqrt(spread + EPSILON)
    return center * scale, scale


def norm_rows(values, gain, shift):
    return (normalize(values)[0] * gain + shift).astype(BF16)


def norm_pullback(grad, unit, scale, gain):
    inner = grad * gain
    return scale * (
        inner
        - jnp.mean(inner, axis=-1, keepdims=True)
        - unit * jnp.mean(inner * unit, axis=-1, keepdims=True)
    )


def times(left, right, kind=F32):
    return jnp.dot(left, right, preferred_element_type=F32).astype(kind)


def times_across(left, right, kind=F32):
    return dot_across(left, right).astype(kind)


def times_down(left, right, kind=F32):
    return row_major(dot_down(left, right).astype(kind))


def gather_rows(rows):
    near = stacked(rows, cross_x(rows))
    return near, cross_core(near)


def add_half(value, cross):
    middle = value.shape[0] // 2
    return value[:middle].astype(F32) + cross(value[middle:].astype(BF16)).astype(F32)


def add_columns(value, cross):
    middle = value.shape[1] // 2
    return value[:, :middle].astype(F32) + cross(value[:, middle:].astype(BF16)).astype(F32)


def column_halves(shard, y_index):
    middle = shard.shape[1] // 2
    own = jnp.where(y_index == 0, shard[:, :middle], shard[:, middle:])
    other = jnp.where(y_index == 0, shard[:, middle:], shard[:, :middle])
    return own, other


def natural_columns(own, other, y_index):
    return jnp.where(y_index == 0, beside(own, other), beside(other, own))


def finish_split(part, y_index):
    part = part.astype(BF16)
    return natural_columns(part, cross_y(part), y_index).astype(F32)


def finish_whole(part, y_index):
    part = part.astype(BF16)
    middle = part.shape[1] // 2
    arrived = cross_y(beside(part[:, middle:], part[:, :middle]))
    total = part.astype(F32) + arrived.astype(F32)
    return natural_columns(total[:, :middle], total[:, middle:], y_index)


def vector_pack(blocks):
    rows = []
    for gains, merged_bias, expand_bias in blocks:
        rows += list(gains) + [merged_bias.reshape(-1), expand_bias.reshape(-1)]
    return jnp.concatenate(rows)


def split_vectors(pieces, blocks, z_index):
    pieces = pieces.reshape(4, -1).astype(F32)
    place = z_index ^ jnp.arange(4)
    natural = jnp.take(pieces, 2 * (place & 1) + (place >> 1), axis=0)
    result = []
    at = 0
    for gains, merged_bias, expand_bias in blocks:
        local = gains[0].shape[0]
        part = pieces[:, at : at + 6 * local].reshape(4, 6, local)
        vectors = part.transpose(1, 0, 2).reshape(6, 4 * local)
        at = at + 6 * local
        size = merged_bias.size
        part = natural[:, at : at + size].reshape((4,) + merged_bias.shape)
        biases = part.transpose(1, 2, 0, 3).reshape(2, -1)
        bias = jnp.concatenate([biases[:1], jnp.zeros_like(biases[:1]), biases[1:]], axis=1)
        at = at + size
        size = expand_bias.size
        part = natural[:, at : at + size].reshape((4,) + expand_bias.shape)
        hidden_bias = part.transpose(1, 0, 2).reshape(1, -1)
        at = at + size
        result.append((vectors, bias, hidden_bias))
    return result


def return_vectors(grads, shapes, y_index, z_index):
    sums = jnp.concatenate([g[0] for g in grads], axis=0)
    sums = sums + cross_core(sums)
    sums = sums + cross_x(sums)
    number = len(grads)
    local = sums.shape[1] // 4
    parts = sums.reshape(6 * number, 4, local).transpose(1, 0, 2).reshape(4, -1)
    place = jnp.arange(4)
    order = z_index ^ (2 * (place & 1) + (place >> 1))
    biases = jnp.concatenate([g[1] for g in grads], axis=0)
    bias_parts = jnp.take(biases.reshape(-1, 4, shapes[0].shape[-1]), order, axis=1)
    bias_parts = bias_parts.transpose(1, 0, 2).reshape(4, -1)
    hidden = jnp.concatenate([g[2] for g in grads], axis=0)
    hidden_parts = jnp.take(hidden.reshape(-1, 4, shapes[1].shape[-1]), order, axis=1)
    hidden_parts = hidden_parts.transpose(1, 0, 2).reshape(4, -1)
    pack = jnp.concatenate([parts, bias_parts, hidden_parts], axis=1)
    pack = pack + cross_y(pack)
    pack = pack[:2] + cross_near(pack[2:])
    total = (pack[:1] + cross_far(pack[1:]))[0]
    result = []
    first = 6 * number * local
    bias_size = shapes[0].size
    hidden_size = shapes[1].size
    for i in range(number):
        vectors = total[i * 6 * local : (i + 1) * 6 * local].reshape(6, local)
        at = first + i * bias_size
        bias = total[at : at + bias_size].reshape(shapes[0].shape)
        at = first + number * bias_size + i * hidden_size
        hidden_bias = total[at : at + hidden_size].reshape(shapes[1].shape)
        result.append((vectors, bias, hidden_bias))
    return result


def order_matrix(width, z_index):
    rows = width // 4
    natural = lax.broadcasted_iota(jnp.int32, (width, width), 0)
    place = lax.broadcasted_iota(jnp.int32, (width, width), 1)
    step, inner = place // rows, place % rows
    distance = 2 * (step & 1) + (step >> 1)
    return (natural == (z_index ^ distance) * rows + inner).astype(BF16)


def my_rows(pair, y_index):
    own = jnp.where(y_index == 0, pair[0], pair[1])
    sent = jnp.where(y_index == 0, pair[1], pair[0])
    return y_order(own, cross_y(sent), y_index, 0)


def halves_added(kept, arrived):
    middle = kept.shape[0] // 2
    return (kept[middle:] + arrived[middle:].astype(F32)).astype(BF16)


def send_columns(value, cross):
    middle = value.shape[1] // 2
    return cross(value[:, middle:].astype(BF16))


def keep_columns(value, arrived):
    return value[:, : value.shape[1] // 2].astype(F32) + arrived.astype(F32)


def send_rows(value, cross):
    middle = value.shape[0] // 2
    return cross(value[middle:].astype(BF16))


def keep_rows(value, arrived):
    return value[: value.shape[0] // 2].astype(F32) + arrived.astype(F32)


def fast_shards(inputs, segments, cotangent, *params):
    y_index = lax.axis_index("ctx")
    z_index = lax.axis_index("dp")
    me = lax.axis_index("tp")
    tokens, features = inputs.shape[1], inputs.shape[2]
    length = segments.shape[1] * 2
    doc_max = min(DOC_MAX, length // 2)
    blocks = (params[:12], params[12:])
    local = features // 4
    quarter = local * 2

    small = [((p[0], p[1], p[5], p[6], p[7], p[11]), p[3], p[9]) for p in blocks]
    place = jnp.stack([y_index, z_index]).astype(jnp.int32)
    p = blocks[0]
    attend, feed = prepare(place, p[2], p[4], p[8], p[10], False)
    pack = pack_vectors(small)
    pack_far = cross_far(pack)
    sent_rows = jnp.where(y_index == 0, inputs[1], inputs[0])
    sent_docs = jnp.where(y_index == 0, segments[1:2], segments[0:1]).astype(BF16)
    sent_docs = jnp.pad(sent_docs, ((0, 15), (0, features - sent_docs.shape[1])))
    moved = cross_y(stacked(sent_rows, sent_docs))
    attend, pack_far = pin(attend, pack_far)
    pack = stacked(pack, pack_far)
    pack_near = cross_near(pack)
    far, near = cross_far(attend), cross_near(attend)
    kept_rows = jnp.where(y_index == 0, inputs[0], inputs[1])
    kept_docs = jnp.where(y_index == 0, segments[0:1], segments[1:2])
    chooser = order_matrix(features, z_index)
    stream = times(y_order(kept_rows, moved[:tokens], y_index, 0), chooser)
    column_docs = y_order(
        kept_docs, moved[tokens : tokens + 1, : kept_docs.shape[1]].astype(jnp.int32), y_index, 1
    )
    row_docs = column_docs.reshape(length, 1)
    context = (me.astype(jnp.int32).reshape(1), row_docs, column_docs)
    gains_s, bias_s, hidden_s, gains_t, bias_t, hidden_t = unpack_vectors(
        stacked(pack, pack_near), place, local, blocks[0][3].shape, blocks[0][9].shape
    )
    p = blocks[1]
    place, far = pin(place, far)
    own_a, feed_t = prepare(place, p[2], p[4], p[8], p[10], True)
    x_first = cross_x(feed_t)
    both = cross_near(far)
    own_e_s, own_r_s = feed[:, :quarter], feed[:, quarter:]

    stream, rows = add_norm(stream, (), gains_s, 0, gains_s, 0)
    near_s = stacked(rows, cross_x(rows))
    far_s = cross_core(near_s)
    far_s, far, near, both, x_first, own_e_s, own_r_s = pin(
        far_s, far, near, both, x_first, own_e_s, own_r_s
    )
    attend_s = stacked(attend, far, near, both)
    own_e = beside(feed_t[:, :quarter], x_first[:, :quarter])
    own_r = beside(
        feed_t[:, quarter : 2 * quarter],
        x_first[:, quarter : 2 * quarter],
        feed_t[:, 2 * quarter :],
        x_first[:, 2 * quarter :],
    )
    e_far, r_far = cross_far(own_e_s), cross_far(own_r_s)
    sent, kept, *saved_s = attention_forward(near_s, far_s, attend_s, bias_s, context, doc_max)
    sent, e_far = pin(sent, e_far)
    e_s = stacked(own_e_s, e_far)
    e_near = cross_near(e_s)
    arrived = cross_core(sent)
    across = cross_x(halves_added(kept, arrived))
    across, e_near, r_far, own_a, own_e = pin(across, e_near, r_far, own_a, own_e)
    e_s = stacked(e_s, e_near)
    other_e_s = cross_y(e_s)
    r_s = stacked(own_r_s, r_far)
    r_near = cross_near(r_s)
    a_far, e_far = cross_far(own_a), cross_far(own_e)
    middle_s, rows = add_norm(stream, (kept, arrived, across), gains_s, 2, gains_s, 3)
    near_two_s = stacked(rows, cross_x(rows))
    far_two_s = cross_core(near_two_s)
    far_two_s, r_near, other_e_s, a_far, own_r = pin(far_two_s, r_near, other_e_s, a_far, own_r)
    r_s = stacked(r_s, r_near)
    a_t = stacked(own_a, a_far)
    a_near = cross_near(a_t)
    r_far = cross_far(own_r)
    feed_s = (near_two_s, far_two_s), (e_s, other_e_s, r_s, hidden_s)
    sent, kept = feed_forward(*feed_s[0], *feed_s[1])
    sent, a_near, e_far = pin(sent, a_near, e_far)
    a_t = stacked(a_t, a_near)
    a_other = cross_y(a_t)
    e_t = stacked(own_e, e_far)
    e_near = cross_near(e_t)
    arrived = cross_core(sent)
    across = cross_x(halves_added(kept, arrived))
    between, rows = add_norm(middle_s, (kept, arrived, across), gains_s, 5, gains_t, 0)

    near_t = stacked(rows, cross_x(rows))
    far_t = cross_core(near_t)
    far_t, a_other, r_far, e_near = pin(far_t, a_other, r_far, e_near)
    attend_t = natural_columns(a_t, a_other, y_index)
    r_t = stacked(own_r, r_far)
    r_near = cross_near(r_t)
    e_t = stacked(e_t, e_near)
    other_e_t = cross_y(e_t)
    hidden_x = cross_x(hidden_t)
    hidden_t = beside(
        hidden_t[:, :quarter], hidden_x[:, :quarter], hidden_t[:, quarter:], hidden_x[:, quarter:]
    )
    sent, kept, *saved_t = attention_forward(near_t, far_t, attend_t, bias_t, context, doc_max)
    arrived = cross_core(sent)
    across = cross_x(halves_added(kept, arrived))
    middle_t, near_two_t = add_norm(between, (kept, arrived, across), gains_t, 2, gains_t, 3)
    far_two_t = cross_core(near_two_t)
    far_two_t, r_near, other_e_t = pin(far_two_t, r_near, other_e_t)
    r_t = stacked(r_t, r_near)
    feed_t = (near_two_t, far_two_t), (e_t, other_e_t, r_t, hidden_t)
    final_sent, final_kept = feed_forward(*feed_t[0], *feed_t[1])

    grad_out = times(my_rows(cotangent, y_index), chooser)
    branch = grad_out.astype(BF16)
    branch_far = cross_core(branch)
    sent, kept, active, grad_hidden, hidden_sum_t = feed_backward(
        *feed_t[0], branch, branch_far, *feed_t[1]
    )
    arrived = cross_core(sent)
    grad_middle, rows, sums_t2 = norm_back(grad_out, (kept, arrived), middle_t, gains_t, 3)
    part_r = times_down(stacked(branch, branch_far), active, BF16)
    part_e = times_down(stacked(near_two_t, far_two_t), grad_hidden, BF16)
    r_moved = send_rows(part_r, cross_near)
    e_moved = send_columns(part_e, cross_y)
    near_grad = stacked(rows, cross_x(rows))
    far_grad = cross_core(near_grad)
    sent, kept, grad_qkv, qkv_sum_t = attention_backward(
        near_grad, far_grad, attend_t, context, saved_t, doc_max
    )
    arrived = cross_core(sent)
    across = cross_x(halves_added(kept, arrived))
    part_a = beside(
        times_down(stacked(near_t, far_t), grad_qkv, BF16),
        times_down(stacked(near_grad, far_grad), saved_t[1], BF16),
    )
    part_a, a_moved = column_halves(part_a, y_index)
    a_moved = cross_y(a_moved)
    across, r_moved, e_moved = pin(across, r_moved, e_moved)
    part_r, part_e = keep_rows(part_r, r_moved), keep_columns(part_e, e_moved)
    r_moved, e_moved = send_rows(part_r, cross_far), send_rows(part_e, cross_near)
    grad_between, rows, sums_t1 = norm_back(
        grad_middle, (kept, arrived, across), between, gains_t, 0
    )

    branch = stacked(rows, cross_x(rows))
    branch_far = cross_core(branch)
    branch_far, e_moved, a_moved = pin(branch_far, e_moved, a_moved)
    part_e = keep_rows(part_e, e_moved)
    part_a = part_a.astype(F32) + a_moved.astype(F32)
    e_moved, a_moved = send_rows(part_e, cross_far), send_rows(part_a, cross_near)
    sent, kept, active, grad_hidden, hidden_sum_s = feed_backward(
        *feed_s[0], branch, branch_far, *feed_s[1]
    )
    arrived = cross_core(sent)
    across = cross_x(halves_added(kept, arrived))
    feed_r = times_down(stacked(branch, branch_far), active, BF16)
    feed_e = times_down(stacked(near_two_s, far_two_s), grad_hidden, BF16)
    fe_moved, fr_moved = send_columns(feed_e, cross_y), send_rows(feed_r, cross_near)
    across, r_moved, e_moved, a_moved = pin(across, r_moved, e_moved, a_moved)
    part_r, part_e = keep_rows(part_r, r_moved), keep_rows(part_e, e_moved)
    part_a = keep_rows(part_a, a_moved)
    a_moved = send_rows(part_a, cross_far)
    half = quarter
    x_moved = cross_x(
        beside(
            part_e[:, half:], part_r[:, half : 2 * half], part_r[:, 3 * half :]
        ).astype(BF16)
    )
    grad_middle, rows, sums_s2 = norm_back(
        grad_between, (kept, arrived, across), middle_s, gains_s, 3
    )
    near_grad = stacked(rows, cross_x(rows))
    far_grad = cross_core(near_grad)
    far_grad, fe_moved, fr_moved, x_moved, a_moved = pin(
        far_grad, fe_moved, fr_moved, x_moved, a_moved
    )
    feed_e, feed_r = keep_columns(feed_e, fe_moved), keep_rows(feed_r, fr_moved)
    fe_moved, fr_moved = send_rows(feed_e, cross_near), send_rows(feed_r, cross_far)
    mine_t = (
        beside(
            part_e[:, :half], part_r[:, :half], part_r[:, 2 * half : 3 * half], keep_rows(part_a, a_moved)
        )
        + jnp.pad(x_moved.astype(F32), ((0, 0), (0, half)))
    ).astype(BF16)
    theirs_t = cross_y(
        beside(
            mine_t[:, :half], mine_t[:, 2 * half : 3 * half], mine_t[:, half : 2 * half], mine_t[:, 3 * half :]
        )
    )
    sent, kept, grad_qkv, qkv_sum_s = attention_backward(
        near_grad, far_grad, attend_s, context, saved_s, doc_max
    )
    sent, fe_moved, fr_moved = pin(sent, fe_moved, fr_moved)
    feed_e, feed_r = keep_rows(feed_e, fe_moved), keep_rows(feed_r, fr_moved)
    fe_moved = send_rows(feed_e, cross_far)
    arrived = cross_core(sent)
    across = cross_x(halves_added(kept, arrived))
    part_a = beside(
        times_down(stacked(near_s, far_s), grad_qkv, BF16),
        times_down(stacked(near_grad, far_grad), saved_s[1], BF16),
    )
    part_a, a_moved = column_halves(part_a, y_index)
    a_moved = cross_y(a_moved)
    across, fe_moved, a_moved, theirs_t = pin(across, fe_moved, a_moved, theirs_t)
    part_a = part_a.astype(F32) + a_moved.astype(F32)
    a_moved = send_rows(part_a, cross_near)
    grad_in, _, sums_s1 = norm_back(grad_middle, (kept, arrived, across), stream, gains_s, 0)
    mine_s = beside(keep_rows(feed_e, fe_moved), feed_r).astype(BF16)
    theirs_s = cross_y(
        beside(mine_s[:, :half], mine_s[:, 2 * half :], mine_s[:, half : 2 * half])
    )
    part_a = keep_rows(part_a, a_moved)
    part_a = keep_rows(part_a, send_rows(part_a, cross_far))
    attend_grad_s = finish_split(part_a, y_index)

    def finish(mine, theirs):
        mine, theirs = mine.astype(F32), theirs.astype(F32)
        expand = natural_columns(mine[:, :half], theirs[:, :half], y_index)
        total = mine[:, half : 3 * half] + theirs[:, half : 3 * half]
        reduce = natural_columns(total[:, :half], total[:, half:], y_index)
        return expand, reduce

    expand_grad_s, reduce_grad_s = finish(mine_s, theirs_s)
    expand_grad_t, reduce_grad_t = finish(mine_t, theirs_t)
    attend_grad_t = natural_columns(
        mine_t[:, 3 * half :], theirs_t[:, 3 * half :], y_index
    ).astype(F32)

    hidden_sum_s = natural_columns(hidden_sum_s[:, :half], hidden_sum_s[:, half:], y_index)
    own_half = beside(hidden_sum_t[:, :half], hidden_sum_t[:, 2 * half : 3 * half])
    x_half = beside(hidden_sum_t[:, half : 2 * half], hidden_sum_t[:, 3 * half :])
    hidden_sum_t = own_half + cross_x(x_half)
    hidden_sum_t = natural_columns(hidden_sum_t[:, :half], hidden_sum_t[:, half:], y_index)

    def both_biases(total):
        return stacked(total[:, :local], total[:, 2 * local :])

    vector_grads = return_vectors(
        [
            (
                stacked(sums_s1[:3], sums_s2[:3]),
                both_biases(qkv_sum_s),
                hidden_sum_s,
            ),
            (
                stacked(sums_t1[:3], sums_t2[:3]),
                both_biases(qkv_sum_t),
                hidden_sum_t,
            ),
        ],
        (params[3], params[9]),
        y_index,
        z_index,
    )

    def restore(value):
        first, second = value[:tokens], value[tokens:]
        kept = jnp.where(y_index == 0, first, second)
        received = cross_y(jnp.where(y_index == 0, second, first))
        return jnp.where(y_index == 0, jnp.stack([kept, received]), jnp.stack([received, kept]))

    final_sent, final_kept, grad_between = pin(final_sent, final_kept, grad_between)
    final = middle_t + gains_t[5:6] + final_kept + cross_core(final_sent).astype(F32)
    output = restore(times_across(final.astype(BF16), chooser, BF16))
    input_grad = lax.dot_general(
        grad_in,
        chooser.astype(F32),
        (((1,), (1,)), ((), ())),
        precision=lax.Precision.HIGHEST,
        preferred_element_type=F32,
    )
    outputs = [output, restore(input_grad)]
    large = (
        (attend_grad_s, expand_grad_s, reduce_grad_s),
        (attend_grad_t, expand_grad_t, reduce_grad_t),
    )
    for (sums, bias, hidden_bias), (pack, expand, reduce), p in zip(vector_grads, large, blocks):
        outputs += [
            sums[0],
            sums[1],
            pack[:, : 3 * local].reshape(p[2].shape),
            bias,
            pack[:, 3 * local :].T,
            sums[2],
            sums[3],
            sums[4],
            expand,
            hidden_bias,
            reduce.T,
            sums[5],
        ]
    return tuple(outputs)


def solution(mesh):
    quick = (mesh.shape["dp"], mesh.shape["ctx"], mesh.shape["tp"]) == (4, 2, 4)
    placed = (
        P("dp", ("ctx", "tp"), None),
        P("dp", "ctx"),
        P("dp", ("ctx", "tp"), None),
        P("dp"),
        P("dp"),
        P("dp", None, "tp"),
        P(None, "tp", "dp"),
        P("tp", "dp"),
        P("dp"),
        P("dp"),
        P("dp"),
        P("dp", "tp"),
        P("tp", "dp"),
        P("tp", "dp"),
        P("dp"),
        P("dp"),
        P("dp"),
        P("dp", None, "tp"),
        P(None, "tp", "dp"),
        P("tp", "dp"),
        P("dp"),
        P("dp"),
        P("dp"),
        P("dp", "tp"),
        P("tp", "dp"),
        P("tp", "dp"),
        P("dp"),
    )
    return jax.shard_map(
        fast_shards if quick else general_shards,
        mesh=mesh,
        in_specs=placed,
        out_specs=(
            P("dp", ("ctx", "tp"), None),
            P("dp", ("ctx", "tp"), None),
            P("dp"),
            P("dp"),
            P("dp", None, "tp"),
            P(None, "tp", "dp"),
            P("tp", "dp"),
            P("dp"),
            P("dp"),
            P("dp"),
            P("dp", "tp"),
            P("tp", "dp"),
            P("tp", "dp"),
            P("dp"),
            P("dp"),
            P("dp"),
            P("dp", None, "tp"),
            P(None, "tp", "dp"),
            P("tp", "dp"),
            P("dp"),
            P("dp"),
            P("dp"),
            P("dp", "tp"),
            P("tp", "dp"),
            P("tp", "dp"),
            P("dp"),
        ),
        check_vma=False,
    )
```

```python
import jax
import jax.numpy as jnp
from jax import lax
from jax.experimental import pallas as pl
from jax.experimental.layout import Layout, with_layout_constraint
from jax.experimental.pallas import tpu as pltpu
from jax.sharding import PartitionSpec as P

HD = 64
DOC_MAX = 2000


EPSILON = 1e-05
GELU_SCALE = 0.7978845608028654


def from_behind(block, axis, distance):
    devices = range(lax.axis_size(axis))
    route = [(i - distance, i) for i in devices if i - distance in devices]
    return lax.ppermute(block, axis, route)


def layer_norm(values, norm_gain, norm_shift):
    center = values - jnp.mean(values, axis=-1, keepdims=True)
    spread = jnp.mean(center * center, axis=-1, keepdims=True)
    return center * lax.rsqrt(spread + EPSILON) * norm_gain + norm_shift


def gelu_tanh(values):
    return (
        0.5 * values * (1.0 + jnp.tanh(GELU_SCALE * (values + 0.044715 * values * values * values)))
    )


def spread_rows(row_block):
    return lax.all_gather(row_block, "tp", axis=1, tiled=True)


def gather_sums(partial_value):
    return lax.psum_scatter(
        partial_value.astype(jnp.bfloat16), "tp", scatter_dimension=1, tiled=True
    ).astype(jnp.float32)


def to_items(tensor, head_count):
    batches, length, features = tensor.shape
    head_size = features // head_count
    return (
        tensor.reshape(batches, length, head_count, head_size)
        .transpose(0, 2, 1, 3)
        .reshape(batches * head_count, length, head_size)
    )


def from_items(tensor, head_count):
    item_count, length, head_size = tensor.shape
    batches = item_count // head_count
    return (
        tensor.reshape(batches, head_count, length, head_size)
        .transpose(0, 2, 1, 3)
        .reshape(batches, length, head_count * head_size)
    )


def masked_scores(query_rows, key_rows, query_docs, key_docs, allowed):
    raw_scores = (
        jnp.einsum("qd,kd->qk", query_rows, key_rows, preferred_element_type=jnp.float32) * 0.125
    )
    keep_mask = allowed & (key_docs[None, :] == query_docs[:, None])
    return (jnp.where(keep_mask, raw_scores, -1e30), keep_mask)


def attend_forward(allowed):

    def attend_item(packed):
        query_rows, key_rows, value_rows, query_docs, key_docs = packed
        scores, keep_mask = masked_scores(query_rows, key_rows, query_docs, key_docs, allowed)
        row_top = jnp.max(scores, axis=-1, keepdims=True)
        raised = jnp.exp(scores - row_top)
        row_total = jnp.sum(raised, axis=-1, keepdims=True)
        weights = (raised / row_total).astype(jnp.bfloat16)
        mixed_rows = jnp.dot(weights, value_rows, preferred_element_type=jnp.float32).astype(
            jnp.bfloat16
        )
        return (mixed_rows, row_top[:, 0] + jnp.log(row_total[:, 0]))

    return attend_item


def attend_backward(allowed):

    def attend_item(packed):
        query_rows, key_rows, value_rows, query_docs, key_docs, log_total, grad_rows = packed
        scores, keep_mask = masked_scores(query_rows, key_rows, query_docs, key_docs, allowed)
        weights = jnp.where(keep_mask, jnp.exp(scores - log_total[:, None]), 0.0)
        grad_values = jnp.einsum(
            "qk,qd->kd", weights.astype(jnp.bfloat16), grad_rows, preferred_element_type=jnp.float32
        )
        grad_weights = jnp.einsum(
            "qd,kd->qk", grad_rows, value_rows, preferred_element_type=jnp.float32
        )
        centered = jnp.sum(weights * grad_weights, axis=-1, keepdims=True)
        grad_scores = (weights * (grad_weights - centered)).astype(jnp.bfloat16)
        grad_query = jnp.dot(grad_scores, key_rows, preferred_element_type=jnp.float32) * 0.125
        grad_keys = (
            jnp.einsum("qk,qd->kd", grad_scores, query_rows, preferred_element_type=jnp.float32)
            * 0.125
        )
        return (grad_query, grad_keys, grad_values)

    return attend_item


def layer_forward(stream, params, segments, key_docs, allowed, cycle_steps):
    (
        first_gain,
        first_shift,
        merged_weight,
        merged_bias,
        output_weight,
        output_bias,
        second_gain,
        second_shift,
        expand_weight,
        expand_bias,
        reduce_weight,
        reduce_bias,
    ) = params
    fetched = (
        lax.all_gather(first_gain, "dp", axis=0, tiled=True),
        lax.all_gather(first_shift, "dp", axis=0, tiled=True),
        lax.all_gather(merged_weight, "dp", axis=0, tiled=True),
        lax.all_gather(merged_bias, "dp", axis=2, tiled=True),
        lax.all_gather(output_weight, "dp", axis=1, tiled=True),
        lax.all_gather(output_bias, "dp", axis=0, tiled=True),
        lax.all_gather(second_gain, "dp", axis=0, tiled=True),
        lax.all_gather(second_shift, "dp", axis=0, tiled=True),
        lax.all_gather(expand_weight, "dp", axis=0, tiled=True),
        lax.all_gather(expand_bias, "dp", axis=1, tiled=True),
        lax.all_gather(reduce_weight, "dp", axis=1, tiled=True),
        lax.all_gather(reduce_bias, "dp", axis=0, tiled=True),
    )
    (
        first_gain,
        first_shift,
        merged_weight,
        merged_bias,
        output_weight,
        output_bias,
        second_gain,
        second_shift,
        expand_weight,
        expand_bias,
        reduce_weight,
        reduce_bias,
    ) = fetched
    head_count = merged_weight.shape[2] // HD
    normed = layer_norm(
        stream, first_gain.astype(jnp.float32), first_shift.astype(jnp.float32)
    ).astype(jnp.bfloat16)
    first_rows = spread_rows(normed)
    merged_out = jnp.einsum(
        "std,dkf->stkf", first_rows, merged_weight, preferred_element_type=jnp.float32
    )
    bias_pair = merged_bias.astype(jnp.float32).reshape(2, -1)
    query_rows = (merged_out[:, :, 0] + bias_pair[0]).astype(jnp.bfloat16)
    key_rows = merged_out[:, :, 1].astype(jnp.bfloat16)
    value_rows = (merged_out[:, :, 2] + bias_pair[1]).astype(jnp.bfloat16)
    key_list = [key_rows]
    value_list = [value_rows]
    moving = (key_rows, value_rows)
    for offset in range(cycle_steps):
        moving = from_behind((moving[0], moving[1]), "ctx", 1)
        key_list.insert(0, moving[0])
        value_list.insert(0, moving[1])
    query_items = to_items(query_rows, head_count)
    key_items = to_items(jnp.concatenate(key_list, axis=1), head_count)
    value_items = to_items(jnp.concatenate(value_list, axis=1), head_count)
    query_docs = jnp.repeat(segments, head_count, axis=0)
    window_docs = jnp.repeat(key_docs, head_count, axis=0)
    mixed_items, log_total = lax.map(
        attend_forward(allowed), (query_items, key_items, value_items, query_docs, window_docs)
    )
    mixed = from_items(mixed_items, head_count)
    attn_part = jnp.einsum("stf,fd->std", mixed, output_weight, preferred_element_type=jnp.float32)
    middle = stream + gather_sums(attn_part) + output_bias.astype(jnp.float32)
    normed_two = layer_norm(
        middle, second_gain.astype(jnp.float32), second_shift.astype(jnp.float32)
    ).astype(jnp.bfloat16)
    second_rows = spread_rows(normed_two)
    hidden = jnp.einsum(
        "std,df->stf", second_rows, expand_weight, preferred_element_type=jnp.float32
    ) + expand_bias.astype(jnp.float32).reshape(-1)
    activated = gelu_tanh(hidden).astype(jnp.bfloat16)
    mlp_part = jnp.einsum(
        "stf,fd->std", activated, reduce_weight, preferred_element_type=jnp.float32
    )
    result = middle + gather_sums(mlp_part) + reduce_bias.astype(jnp.float32)
    saved_state = (
        fetched,
        stream,
        first_rows,
        query_items,
        key_items,
        value_items,
        query_docs,
        window_docs,
        log_total,
        mixed,
        middle,
        second_rows,
        hidden,
        activated,
    )
    return (result, saved_state)


def reduce_grads(fresh):
    (
        gain_one,
        shift_one,
        merged_weights,
        merged_biases,
        output_weights,
        output_biases,
        gain_two,
        shift_two,
        expand_weights,
        expand_biases,
        reduce_weights,
        reduce_biases,
    ) = fresh
    summed = (
        lax.psum(gain_one.astype(jnp.bfloat16), "ctx").astype(jnp.float32),
        lax.psum(shift_one.astype(jnp.bfloat16), "ctx").astype(jnp.float32),
        lax.psum(merged_weights.astype(jnp.bfloat16), "ctx").astype(jnp.float32),
        lax.psum(merged_biases.astype(jnp.bfloat16), "ctx").astype(jnp.float32),
        lax.psum(output_weights.astype(jnp.bfloat16), "ctx").astype(jnp.float32),
        lax.psum(output_biases.astype(jnp.bfloat16), "ctx").astype(jnp.float32),
        lax.psum(gain_two.astype(jnp.bfloat16), "ctx").astype(jnp.float32),
        lax.psum(shift_two.astype(jnp.bfloat16), "ctx").astype(jnp.float32),
        lax.psum(expand_weights.astype(jnp.bfloat16), "ctx").astype(jnp.float32),
        lax.psum(expand_biases.astype(jnp.bfloat16), "ctx").astype(jnp.float32),
        lax.psum(reduce_weights.astype(jnp.bfloat16), "ctx").astype(jnp.float32),
        lax.psum(reduce_biases.astype(jnp.bfloat16), "ctx").astype(jnp.float32),
    )
    (
        gain_one,
        shift_one,
        merged_weights,
        merged_biases,
        output_weights,
        output_biases,
        gain_two,
        shift_two,
        expand_weights,
        expand_biases,
        reduce_weights,
        reduce_biases,
    ) = summed
    return (
        lax.psum_scatter(
            gain_one.astype(jnp.bfloat16), "dp", scatter_dimension=0, tiled=True
        ).astype(jnp.float32),
        lax.psum_scatter(
            shift_one.astype(jnp.bfloat16), "dp", scatter_dimension=0, tiled=True
        ).astype(jnp.float32),
        lax.psum_scatter(
            merged_weights.astype(jnp.bfloat16), "dp", scatter_dimension=0, tiled=True
        ).astype(jnp.float32),
        lax.psum_scatter(
            merged_biases.astype(jnp.bfloat16), "dp", scatter_dimension=2, tiled=True
        ).astype(jnp.float32),
        lax.psum_scatter(
            output_weights.astype(jnp.bfloat16), "dp", scatter_dimension=1, tiled=True
        ).astype(jnp.float32),
        lax.psum_scatter(
            output_biases.astype(jnp.bfloat16), "dp", scatter_dimension=0, tiled=True
        ).astype(jnp.float32),
        lax.psum_scatter(
            gain_two.astype(jnp.bfloat16), "dp", scatter_dimension=0, tiled=True
        ).astype(jnp.float32),
        lax.psum_scatter(
            shift_two.astype(jnp.bfloat16), "dp", scatter_dimension=0, tiled=True
        ).astype(jnp.float32),
        lax.psum_scatter(
            expand_weights.astype(jnp.bfloat16), "dp", scatter_dimension=0, tiled=True
        ).astype(jnp.float32),
        lax.psum_scatter(
            expand_biases.astype(jnp.bfloat16), "dp", scatter_dimension=1, tiled=True
        ).astype(jnp.float32),
        lax.psum_scatter(
            reduce_weights.astype(jnp.bfloat16), "dp", scatter_dimension=1, tiled=True
        ).astype(jnp.float32),
        lax.psum_scatter(
            reduce_biases.astype(jnp.bfloat16), "dp", scatter_dimension=0, tiled=True
        ).astype(jnp.float32),
    )


def layer_backward(grad_out, saved_state, allowed, cycle_steps, token_count):
    (
        fetched,
        stream,
        first_rows,
        query_items,
        key_items,
        value_items,
        query_docs,
        window_docs,
        log_total,
        mixed,
        middle,
        second_rows,
        hidden,
        activated,
    ) = saved_state
    (
        first_gain,
        first_shift,
        merged_weight,
        merged_bias,
        output_weight,
        output_bias,
        second_gain,
        second_shift,
        expand_weight,
        expand_bias,
        reduce_weight,
        reduce_bias,
    ) = fetched
    head_count = merged_weight.shape[2] // HD
    grad_branch = spread_rows(grad_out.astype(jnp.bfloat16))
    grad_reduce = jnp.einsum(
        "stf,std->fd", activated, grad_branch, preferred_element_type=jnp.float32
    )
    grad_active = jnp.einsum(
        "std,fd->stf", grad_branch, reduce_weight, preferred_element_type=jnp.float32
    )
    _, gelu_pull = jax.vjp(gelu_tanh, hidden)
    grad_hidden = gelu_pull(grad_active)[0].astype(jnp.bfloat16)
    grad_expand_bias = jnp.sum(grad_hidden, axis=(0, 1), dtype=jnp.float32).reshape(
        expand_bias.shape
    )
    grad_expand = jnp.einsum(
        "std,stf->df", second_rows, grad_hidden, preferred_element_type=jnp.float32
    )
    grad_second = gather_sums(
        jnp.einsum("stf,df->std", grad_hidden, expand_weight, preferred_element_type=jnp.float32)
    )
    _, second_pull = jax.vjp(
        layer_norm, middle, second_gain.astype(jnp.float32), second_shift.astype(jnp.float32)
    )
    grad_norm_mid, grad_second_gain, grad_second_shift = second_pull(grad_second)
    grad_middle = grad_out + grad_norm_mid
    grad_reduce_bias = jnp.sum(grad_out, axis=(0, 1))
    grad_attend = spread_rows(grad_middle.astype(jnp.bfloat16))
    grad_output = jnp.einsum("stf,std->fd", mixed, grad_attend, preferred_element_type=jnp.float32)
    grad_mixed = jnp.einsum(
        "std,fd->stf", grad_attend, output_weight, preferred_element_type=jnp.float32
    ).astype(jnp.bfloat16)
    grad_query_items, grad_key_items, grad_value_items = lax.map(
        attend_backward(allowed),
        (
            query_items,
            key_items,
            value_items,
            query_docs,
            window_docs,
            log_total,
            to_items(grad_mixed, head_count),
        ),
    )
    grad_query = from_items(grad_query_items, head_count)
    window_keys = from_items(grad_key_items, head_count)
    window_values = from_items(grad_value_items, head_count)
    local_keys = window_keys[:, cycle_steps * token_count :]
    local_values = window_values[:, cycle_steps * token_count :]
    carried = None
    for offset in range(cycle_steps, 0, -1):
        start_row = (cycle_steps - offset) * token_count
        block_keys = window_keys[:, start_row : start_row + token_count]
        block_values = window_values[:, start_row : start_row + token_count]
        if carried is not None:
            block_keys = block_keys + carried[0]
            block_values = block_values + carried[1]
        carried = (
            from_behind(block_keys.astype(jnp.bfloat16), "ctx", -1).astype(block_keys.dtype),
            from_behind(block_values.astype(jnp.bfloat16), "ctx", -1).astype(block_values.dtype),
        )
    local_keys = local_keys + carried[0]
    local_values = local_values + carried[1]
    grad_merged = jnp.stack([grad_query, local_keys, local_values], axis=2).astype(jnp.bfloat16)
    grad_merged_bias = jnp.stack(
        [
            jnp.sum(grad_merged[:, :, 0], axis=(0, 1), dtype=jnp.float32),
            jnp.sum(grad_merged[:, :, 2], axis=(0, 1), dtype=jnp.float32),
        ]
    ).reshape(merged_bias.shape)
    grad_merged_weight = jnp.einsum(
        "std,stkf->dkf", first_rows, grad_merged, preferred_element_type=jnp.float32
    )
    grad_first = gather_sums(
        jnp.einsum("stkf,dkf->std", grad_merged, merged_weight, preferred_element_type=jnp.float32)
    )
    _, first_pull = jax.vjp(
        layer_norm, stream, first_gain.astype(jnp.float32), first_shift.astype(jnp.float32)
    )
    grad_norm_in, grad_first_gain, grad_first_shift = first_pull(grad_first)
    grad_input = grad_middle + grad_norm_in
    grad_output_bias = jnp.sum(grad_middle, axis=(0, 1))
    vector_grads = lax.psum(
        (
            grad_first_gain,
            grad_first_shift,
            grad_second_gain,
            grad_second_shift,
            grad_output_bias,
            grad_reduce_bias,
        ),
        "tp",
    )
    fresh = (
        vector_grads[0],
        vector_grads[1],
        grad_merged_weight,
        grad_merged_bias,
        grad_output,
        vector_grads[4],
        vector_grads[2],
        vector_grads[3],
        grad_expand,
        grad_expand_bias,
        grad_reduce,
        vector_grads[5],
    )
    return (grad_input, reduce_grads(fresh))


def general_shards(
    inputs,
    segments,
    cotangent,
    student_first_gain,
    student_first_shift,
    student_merged_weight,
    student_merged_bias,
    student_output_weight,
    student_output_bias,
    student_second_gain,
    student_second_shift,
    student_expand_weight,
    student_expand_bias,
    student_reduce_weight,
    student_reduce_bias,
    teacher_first_gain,
    teacher_first_shift,
    teacher_merged_weight,
    teacher_merged_bias,
    teacher_output_weight,
    teacher_output_bias,
    teacher_second_gain,
    teacher_second_shift,
    teacher_expand_weight,
    teacher_expand_bias,
    teacher_reduce_weight,
    teacher_reduce_bias,
):
    student = (
        student_first_gain,
        student_first_shift,
        student_merged_weight,
        student_merged_bias,
        student_output_weight,
        student_output_bias,
        student_second_gain,
        student_second_shift,
        student_expand_weight,
        student_expand_bias,
        student_reduce_weight,
        student_reduce_bias,
    )
    teacher = (
        teacher_first_gain,
        teacher_first_shift,
        teacher_merged_weight,
        teacher_merged_bias,
        teacher_output_weight,
        teacher_output_bias,
        teacher_second_gain,
        teacher_second_shift,
        teacher_expand_weight,
        teacher_expand_bias,
        teacher_reduce_weight,
        teacher_reduce_bias,
    )
    token_count = segments.shape[1]
    context_size = lax.axis_size("ctx")
    context_index = lax.axis_index("ctx")
    doc_long = min(DOC_MAX, token_count * context_size // 2)
    cycle_steps = min((doc_long - 2) // token_count + 1, context_size - 1)
    doc_list = [segments]
    moving = segments
    for offset in range(cycle_steps):
        moving = from_behind(moving, "ctx", 1)
        doc_list.insert(0, moving)
    key_docs = jnp.concatenate(doc_list, axis=1)
    places = jnp.arange((cycle_steps + 1) * token_count, dtype=jnp.int32)
    relative = places - cycle_steps * token_count
    source = cycle_steps - places // token_count
    query_place = jnp.arange(token_count, dtype=jnp.int32)
    allowed = (relative[None, :] <= query_place[:, None]) & (source <= context_index)[None, :]
    stream = inputs.astype(jnp.float32)
    middle_stream, student_saved = layer_forward(
        stream, student, segments, key_docs, allowed, cycle_steps
    )
    final_stream, teacher_saved = layer_forward(
        middle_stream, teacher, segments, key_docs, allowed, cycle_steps
    )
    teacher_in_grad, teacher_grads = layer_backward(
        cotangent.astype(jnp.float32), teacher_saved, allowed, cycle_steps, token_count
    )
    input_grad, student_grads = layer_backward(
        teacher_in_grad, student_saved, allowed, cycle_steps, token_count
    )
    return (
        (final_stream.astype(jnp.bfloat16), input_grad)
        + tuple(student_grads)
        + tuple(teacher_grads)
    )


BF16 = jnp.bfloat16
F32 = jnp.float32
NEG = -1e30
TILE = 256
RELATIVE = (0, 2, 1, 3)


def row_major(value):
    return with_layout_constraint(value, Layout(major_to_minor=tuple(range(value.ndim))))


def swap(value, axis, bit):
    route = [(i, i ^ bit) for i in range(lax.axis_size(axis))]
    if value.ndim == 2:
        return row_major(lax.ppermute(row_major(value), axis, route))
    return lax.ppermute(value, axis, route)


def cross_core(value):
    return swap(value, "tp", 1)


def cross_x(value):
    return swap(value, "tp", 2)


def cross_y(value):
    return swap(value, "ctx", 1)


def cross_near(value):
    return swap(value, "dp", 1)


def cross_far(value):
    return swap(value, "dp", 2)


def cross_both(value):
    return swap(value, "dp", 3)


def stacked(*values):
    return jnp.concatenate(values, axis=0)


def beside(*values):
    return jnp.concatenate(values, axis=1)


def y_order(own, other, y_index, axis):
    return jnp.where(
        y_index == 0,
        jnp.concatenate([own, other], axis=axis),
        jnp.concatenate([other, own], axis=axis),
    )


def pin(*values):
    return lax.optimization_barrier(values)


def window_start(block, doc_max):
    return max(0, (block * TILE - doc_max + 1) // TILE) * TILE


def token_place(me, member, half, rows):
    return pl.multiple_of((half * 4 + (me ^ RELATIVE[member])) * rows, rows)


def to_tokens(value, target, me, first):
    rows = value.shape[0] // 4
    for r in range(2):
        for half in range(2):
            place = token_place(me, first + r, half, rows)
            target[pl.ds(place, rows), :] = value[(r * 2 + half) * rows : (r * 2 + half + 1) * rows]


def from_tokens(source, me, first):
    rows = source.shape[0] // 8
    return jnp.concatenate(
        [
            source[pl.ds(token_place(me, first + r, half, rows), rows), :]
            for r in range(2)
            for half in range(2)
        ],
        axis=0,
    )


def upright(line):
    size = line.shape[1]
    rows = lax.broadcasted_iota(jnp.int32, (size, size), 0)
    columns = lax.broadcasted_iota(jnp.int32, (size, size), 1)
    return jnp.sum(jnp.where(rows == columns, line, 0.0), axis=1, keepdims=True)


def keep_mask(docs, block, start):
    size = (block + 1) * TILE - start
    rows = block * TILE + lax.broadcasted_iota(jnp.int32, (TILE, size), 0)
    columns = start + lax.broadcasted_iota(jnp.int32, (TILE, size), 1)
    same = upright(docs[:, block * TILE : (block + 1) * TILE]) == docs[:, start : start + size]
    return same & (columns <= rows)


def join(pieces, whole):
    row, column = 0, 0
    most = whole.shape[0] * whole.shape[1] // sum(piece.shape[1] for piece in pieces)
    for piece in pieces:
        rows = min(piece.shape[0], most) if len(pieces) == 4 else piece.shape[0]
        whole[row : row + rows, column : column + piece.shape[1]] = piece[:rows, :]
        row += rows
        if row == whole.shape[0]:
            row, column = 0, column + piece.shape[1]


def dot_across(left, right):
    return lax.dot_general(left, right, (((1,), (1,)), ((), ())), preferred_element_type=F32)


def dot_down(left, right):
    return lax.dot_general(left, right, (((0,), (0,)), ((), ())), preferred_element_type=F32)


def attention_forward_kernel(
    heads,
    doc_max,
    count,
    scaled,
    me_ref,
    near_ref,
    far_ref,
    bias_ref,
    docs,
    *refs,
):
    mixed, attend_ref = refs[-2:]
    refs = refs[:-2]
    sources = (near_ref, far_ref)
    if scaled:
        gains, refs, normed = refs[0], refs[1:-2], refs[-2:]
        for source, target in zip(sources, normed):
            target[...] = (source[...].astype(F32) * gains[0:1, :] + gains[1:2, :]).astype(BF16)
        sources = normed
    pieces, (sent_ref, kept_ref, qkv_ref, mixed_ref, log_ref) = refs[:count], refs[count:]
    join(pieces, attend_ref)
    me = me_ref[0]
    width = heads * HD
    weight = attend_ref[:, : 3 * width]
    for piece, first in zip(sources, (0, 2)):
        rows = jnp.dot(piece[...], weight, preferred_element_type=F32) + bias_ref[...]
        to_tokens(rows.astype(BF16), qkv_ref, me, first)
    for block in range(qkv_ref.shape[0] // TILE):
        start = window_start(block, doc_max)
        stop = (block + 1) * TILE
        mask = keep_mask(docs, block, start)
        here = slice(block * TILE, stop)
        for h in range(heads):
            at = slice(h * HD, (h + 1) * HD)
            query = qkv_ref[here, at] * BF16(0.125)
            key = qkv_ref[start:stop, width + h * HD : width + (h + 1) * HD]
            value = qkv_ref[start:stop, 2 * width + h * HD : 2 * width + (h + 1) * HD]
            scores = jnp.where(mask, dot_across(query, key), NEG)
            top = jnp.max(scores, axis=-1, keepdims=True)
            raised = jnp.exp(scores - top)
            total = jnp.sum(raised, axis=-1, keepdims=True)
            weights = (raised * (1.0 / total)).astype(BF16)
            mixed[here, at] = jnp.dot(weights, value, preferred_element_type=F32).astype(BF16)
            log_ref[here, h : h + 1] = top + jnp.log(total)
    weight = attend_ref[:, 3 * width :]
    half = qkv_ref.shape[0] // 2
    rows = from_tokens(mixed, me, 2)
    mixed_ref[half:, :] = rows
    sent_ref[...] = dot_across(rows, weight).astype(BF16)
    rows = from_tokens(mixed, me, 0)
    mixed_ref[:half, :] = rows
    kept_ref[...] = dot_across(rows, weight)


def attention_backward_kernel(
    heads,
    doc_max,
    count,
    me_ref,
    near_ref,
    far_ref,
    docs,
    qkv_ref,
    mixed_ref,
    log_ref,
    *refs,
):
    pieces, (sent_ref, kept_ref, out_ref, sum_ref) = refs[:count], refs[count:-4]
    grad, mixed, total, attend_ref = refs[-4:]
    join(pieces, attend_ref)
    me = me_ref[0]
    width = heads * HD
    half = qkv_ref.shape[0] // 2
    weight = attend_ref[:, 3 * width :]
    for piece, first in ((near_ref, 0), (far_ref, 2)):
        rows = jnp.dot(piece[...], weight, preferred_element_type=F32).astype(BF16)
        to_tokens(rows, grad, me, first)
        to_tokens(mixed_ref[first // 2 * half : (first // 2 + 1) * half, :], mixed, me, first)
    total[:, width:] = jnp.zeros((total.shape[0], 2 * width), F32)
    for block in range(qkv_ref.shape[0] // TILE):
        start = window_start(block, doc_max)
        stop = (block + 1) * TILE
        mask = keep_mask(docs, block, start)
        here = slice(block * TILE, stop)
        for h in range(heads):
            at = slice(h * HD, (h + 1) * HD)
            at_key = slice(width + h * HD, width + (h + 1) * HD)
            at_value = slice(2 * width + h * HD, 2 * width + (h + 1) * HD)
            query = qkv_ref[here, at] * BF16(0.125)
            key = qkv_ref[start:stop, at_key]
            value = qkv_ref[start:stop, at_value]
            grad_rows = grad[here, at]
            weights = jnp.where(
                mask, jnp.exp(dot_across(query, key) - log_ref[here, h : h + 1]), 0.0
            )
            grad_weights = dot_across(grad_rows, value)
            centered = jnp.sum(
                grad_rows.astype(F32) * mixed[here, at].astype(F32), axis=-1, keepdims=True
            )
            grad_scores = (weights * (grad_weights - centered)).astype(BF16)
            total[here, at] = jnp.dot(grad_scores, key, preferred_element_type=F32) * 0.125
            total[start:stop, at_key] += dot_down(grad_scores, query)
            total[start:stop, at_value] += dot_down(weights.astype(BF16), grad_rows)
    weight = attend_ref[:, : 3 * width]
    rows = from_tokens(total, me, 2).astype(BF16)
    out_ref[half:, :] = rows
    sent_ref[...] = dot_across(rows, weight).astype(BF16)
    sums = jnp.sum(rows.astype(F32), axis=0, keepdims=True)
    rows = from_tokens(total, me, 0).astype(BF16)
    out_ref[:half, :] = rows
    kept_ref[...] = dot_across(rows, weight)
    sum_ref[...] = sums + jnp.sum(rows.astype(F32), axis=0, keepdims=True)


VMEM = pl.BlockSpec(memory_space=pltpu.VMEM)
SMEM = pl.BlockSpec(memory_space=pltpu.SMEM)


def call(body, name, inputs, outputs, scratch, flops, transcendentals, limit=24):
    size = sum(v.size * v.dtype.itemsize for v in list(inputs) + list(outputs))
    return pl.pallas_call(
        body,
        out_shape=tuple(outputs),
        in_specs=[SMEM if v.ndim == 1 else VMEM for v in inputs],
        out_specs=tuple(VMEM for _ in outputs),
        scratch_shapes=scratch,
        cost_estimate=pl.CostEstimate(
            flops=flops, transcendentals=transcendentals, bytes_accessed=size
        ),
        compiler_params=pltpu.CompilerParams(vmem_limit_bytes=limit << 20),
        name=name,
    )(*inputs)


def shaped(rows, columns, kind):
    return jax.ShapeDtypeStruct((rows, columns), kind)


def attention_forward(near, far, attend, bias, context, doc_max, gains=()):
    me, docs = context
    half, features = near.shape
    width = bias.shape[1] // 3
    heads = width // HD
    area = heads * 2 * half * half

    def body(*refs):
        attention_forward_kernel(heads, doc_max, len(attend), len(gains) > 0, *refs)

    return call(
        body,
        "attention_forward",
        (me, near, far, bias, docs) + tuple(gains) + tuple(attend),
        (
            shaped(half, features, BF16),
            shaped(half, features, F32),
            shaped(2 * half, 3 * width, BF16),
            shaped(2 * half, width, BF16),
            shaped(2 * half, heads, F32),
        )
        + (shaped(half, features, BF16),) * (2 * len(gains)),
        [pltpu.VMEM((2 * half, width), BF16), pltpu.VMEM((features, 4 * width), BF16)],
        16 * HD * area,
        area,
    )


def attention_backward(near, far, attend, context, saved, doc_max):
    me, docs = context
    qkv, mixed, log_total = saved
    half, features = near.shape
    width = qkv.shape[1] // 3
    heads = width // HD
    area = heads * 2 * half * half

    def body(*refs):
        attention_backward_kernel(heads, doc_max, len(attend), *refs)

    return call(
        body,
        "attention_backward",
        (me, near, far, docs, qkv, mixed, log_total) + tuple(attend),
        (
            shaped(half, features, BF16),
            shaped(half, features, F32),
            shaped(2 * half, 3 * width, BF16),
            shaped(1, 3 * width, F32),
        ),
        [
            pltpu.VMEM((2 * half, width), BF16),
            pltpu.VMEM((2 * half, width), BF16),
            pltpu.VMEM((2 * half, 3 * width), F32),
            pltpu.VMEM((features, 4 * width), BF16),
        ],
        40 * HD * area,
        area,
    )


CHUNK = 256


def gelu_both(values):
    inner = GELU_SCALE * (values + 0.044715 * values * values * values)
    bent = jnp.tanh(inner)
    value = 0.5 * values * (1.0 + bent)
    slope = 0.5 * (1.0 + bent) + 0.5 * values * (1.0 - bent * bent) * GELU_SCALE * (
        1.0 + 3.0 * 0.044715 * values * values
    )
    return value, slope


def split_parts(weight):
    size = min(weight.shape[1], 768)
    return [slice(at, at + size) for at in range(0, weight.shape[1], size)]


def feed_forward_kernel(
    count, near_ref, far_ref, bias_ref, *refs
):
    sent_ref, kept_ref, expand_ref, reduce_ref = refs[-4:]
    join(refs[:count], expand_ref)
    join(refs[count:-4], reduce_ref)
    parts = split_parts(expand_ref)
    for piece, out in ((far_ref, sent_ref), (near_ref, kept_ref)):

        def step(i, carry):
            at = pl.ds(pl.multiple_of(i * CHUNK, CHUNK), CHUNK)
            rows = piece[at, :]
            total = None
            for columns in parts:
                hidden = jnp.dot(rows, expand_ref[:, columns], preferred_element_type=F32)
                active = gelu_tanh(hidden + bias_ref[:, columns]).astype(BF16)
                product = dot_across(active, reduce_ref[:, columns])
                total = product if total is None else total + product
            out[at, :] = total.astype(out.dtype)
            return carry

        lax.fori_loop(0, piece.shape[0] // CHUNK, step, 0)


def feed_forward(near, far, expand, reduce, bias):
    half, features = near.shape
    hidden = bias.shape[1]

    def body(*refs):
        feed_forward_kernel(len(expand), *refs)

    return call(
        body,
        "feed_forward",
        (near, far, bias) + tuple(expand) + tuple(reduce),
        (shaped(half, features, BF16), shaped(half, features, F32)),
        [pltpu.VMEM((features, hidden), BF16), pltpu.VMEM((features, hidden), BF16)],
        8 * half * features * hidden,
        2 * half * hidden,
    )


def feed_backward_kernel(
    count,
    near_ref,
    far_ref,
    near_grad,
    far_grad,
    bias_ref,
    *refs,
):
    sent_ref, kept_ref, active_ref, hidden_ref, sum_ref, expand_ref, reduce_ref = refs[-7:]
    join(refs[:count], expand_ref)
    join(refs[count:-7], reduce_ref)
    parts = split_parts(expand_ref)
    half = near_ref.shape[0]
    sum_ref[...] = jnp.zeros_like(sum_ref)
    for piece, grads, out, base in (
        (far_ref, far_grad, sent_ref, half),
        (near_ref, near_grad, kept_ref, 0),
    ):

        def step(i, carry):
            place = pl.multiple_of(i * CHUNK, CHUNK)
            at = pl.ds(place, CHUNK)
            whole = pl.ds(pl.multiple_of(base + place, CHUNK), CHUNK)
            rows = piece[at, :]
            grad_rows = grads[at, :]
            total = None
            for columns in parts:
                hidden = jnp.dot(rows, expand_ref[:, columns], preferred_element_type=F32)
                value, slope = gelu_both(hidden + bias_ref[:, columns])
                active_ref[whole, columns] = value.astype(BF16)
                grad_active = jnp.dot(
                    grad_rows, reduce_ref[:, columns], preferred_element_type=F32
                )
                grad_hidden = (grad_active * slope).astype(BF16)
                hidden_ref[whole, columns] = grad_hidden
                sum_ref[:, columns] += jnp.sum(grad_hidden.astype(F32), axis=0, keepdims=True)
                product = dot_across(grad_hidden, expand_ref[:, columns])
                total = product if total is None else total + product
            out[at, :] = total.astype(out.dtype)
            return carry

        lax.fori_loop(0, half // CHUNK, step, 0)


def feed_backward(near, far, near_grad, far_grad, expand, reduce, bias):
    half, features = near.shape
    hidden = bias.shape[1]

    def body(*refs):
        feed_backward_kernel(len(expand), *refs)

    return call(
        body,
        "feed_backward",
        (near, far, near_grad, far_grad, bias) + tuple(expand) + tuple(reduce),
        (
            shaped(half, features, BF16),
            shaped(half, features, F32),
            shaped(2 * half, hidden, BF16),
            shaped(2 * half, hidden, BF16),
            shaped(1, hidden, F32),
        ),
        [pltpu.VMEM((features, hidden), BF16), pltpu.VMEM((features, hidden), BF16)],
        12 * half * features * hidden,
        2 * half * hidden,
    )


def row_block(rows, columns):
    return pl.BlockSpec((rows, columns), lambda i: (0, 0))


def row_call(body, name, inputs, rows, outputs):
    specs = [row_block(v.shape[0] if v.shape[0] <= 16 else rows, v.shape[1]) for v in inputs]
    size = sum(rows * v.shape[1] * v.dtype.itemsize for v in inputs)
    return pl.pallas_call(
        body,
        grid=(1,),
        out_shape=tuple(outputs),
        in_specs=specs,
        out_specs=tuple(row_block(*v.shape) for v in outputs),
        cost_estimate=pl.CostEstimate(
            flops=20 * rows * inputs[0].shape[1], transcendentals=rows, bytes_accessed=2 * size
        ),
        compiler_params=pltpu.CompilerParams(vmem_limit_bytes=10 << 20),
        name=name,
    )(*inputs)


def add_norm(base, addends, vectors, bias_at, norm_vectors, norm_at):
    rows, columns = base.shape

    def body(*refs):
        base_ref, bias_ref, vector_ref = refs[:3]
        parts, (sum_ref, norm_ref) = refs[3:-2], refs[-2:]
        total = base_ref[...]
        if parts:
            total = total + bias_ref[bias_at : bias_at + 1, :]
        for part in parts:
            total = total + part[...].astype(F32)
        sum_ref[...] = total
        gain, shift = vector_ref[norm_at : norm_at + 1, :], vector_ref[norm_at + 1 : norm_at + 2, :]
        norm_ref[...] = (normalize(total)[0] * gain + shift).astype(BF16)

    return row_call(
        body,
        "add_norm",
        [base, vectors, norm_vectors] + list(addends),
        rows,
        (shaped(rows, columns, F32), shaped(rows, columns, BF16)),
    )


def norm_only(values):
    rows, columns = values.shape

    def body(value_ref, unit_ref):
        unit_ref[...] = normalize(value_ref[...])[0].astype(BF16)

    return row_call(body, "norm_only", [values], rows, (shaped(rows, columns, BF16),))[0]


def norm_back(skip, addends, value, vectors, norm_at, sums, sums_at):
    rows, columns = skip.shape

    def body(*refs):
        skip_ref, value_ref, vector_ref, old_ref = refs[:4]
        parts, (grad_ref, low_ref, sum_ref) = refs[4:-3], refs[-3:]
        grad = parts[0][...].astype(F32)
        for part in parts[1:]:
            grad = grad + part[...].astype(F32)
        unit, scale = normalize(value_ref[...])
        skipped = skip_ref[...]
        sum_ref[...] = old_ref[...]
        for i, each in enumerate((grad * unit, grad, skipped)):
            sum_ref[sums_at + i : sums_at + i + 1, :] = jnp.sum(each, axis=0, keepdims=True)
        total = skipped + norm_pullback(grad, unit, scale, vector_ref[norm_at : norm_at + 1, :])
        grad_ref[...] = total
        low_ref[...] = total.astype(BF16)

    return row_call(
        body,
        "norm_back",
        [skip, value, vectors, sums] + list(addends),
        rows,
        (shaped(rows, columns, F32), shaped(rows, columns, BF16), shaped(16, columns, F32)),
    )


def normalize(values):
    center = values - jnp.mean(values, axis=-1, keepdims=True)
    spread = jnp.mean(center * center, axis=-1, keepdims=True)
    scale = lax.rsqrt(spread + EPSILON)
    return center * scale, scale


def norm_rows(values, gain, shift):
    return (normalize(values)[0] * gain + shift).astype(BF16)


def norm_pullback(grad, unit, scale, gain):
    inner = grad * gain
    return scale * (
        inner
        - jnp.mean(inner, axis=-1, keepdims=True)
        - unit * jnp.mean(inner * unit, axis=-1, keepdims=True)
    )


def times(left, right, kind=F32):
    return jnp.dot(left, right, preferred_element_type=F32).astype(kind)


def times_across(left, right, kind=F32):
    return dot_across(left, right).astype(kind)


def times_down(left, right, kind=F32):
    return row_major(dot_down(left, right).astype(kind))


def gather_rows(rows):
    near = stacked(rows, cross_x(rows))
    return near, cross_core(near)


def add_half(value, cross):
    middle = value.shape[0] // 2
    return value[:middle].astype(F32) + cross(value[middle:].astype(BF16)).astype(F32)


def add_columns(value, cross):
    middle = value.shape[1] // 2
    return value[:, :middle].astype(F32) + cross(value[:, middle:].astype(BF16)).astype(F32)


def column_halves(shard, y_index):
    middle = shard.shape[1] // 2
    own = jnp.where(y_index == 0, shard[:, :middle], shard[:, middle:])
    other = jnp.where(y_index == 0, shard[:, middle:], shard[:, :middle])
    return own, other


def natural_columns(own, other, y_index):
    return jnp.where(y_index == 0, beside(own, other), beside(other, own))


def order_matrix(width, z_index):
    rows = width // 4
    natural = lax.broadcasted_iota(jnp.int32, (width, width), 0)
    place = lax.broadcasted_iota(jnp.int32, (width, width), 1)
    step, inner = place // rows, place % rows
    distance = 2 * (step & 1) + (step >> 1)
    return (natural == (z_index ^ distance) * rows + inner).astype(BF16)


def my_rows(pair, y_index):
    own = jnp.where(y_index == 0, pair[0], pair[1])
    sent = jnp.where(y_index == 0, pair[1], pair[0])
    return y_order(own, cross_y(sent), y_index, 0)


ROWS = 64
SPARE = ROWS // 2


def turn(value):
    size = value.shape[0]
    eye = (
        lax.broadcasted_iota(jnp.int32, (size, size), 0)
        == lax.broadcasted_iota(jnp.int32, (size, size), 1)
    ).astype(BF16)
    return dot_down(value, eye)


def pack_vectors(blocks, place):
    flat = []
    for gains, merged_bias, expand_bias in blocks:
        flat += list(gains) + [merged_bias.transpose(1, 0, 2), expand_bias]

    number = len(flat)

    def body(*refs):
        refs = refs[1:]
        out, part, sem = refs[number], refs[number + 1 : -1], refs[-1]
        copies = [
            pltpu.make_async_copy(refs[i], part[i], sem.at[i]) for i in range(number)
        ]
        for copy in copies:
            copy.start()
        out[...] = jnp.zeros_like(out)
        for copy in copies:
            copy.wait()
        for b in range(2):
            vectors, merged_bias, expand_bias = part[8 * b : 8 * b + 6], part[8 * b + 6], part[8 * b + 7]
            for i in range(6):
                local = vectors[i].shape[0]
                out[6 * b + i : 6 * b + i + 1, :local] = vectors[i][...].astype(F32).reshape(1, local)
            for h in range(merged_bias.shape[0]):
                value = merged_bias[h].astype(F32)
                out[16 + 8 * b + 2 * h : 18 + 8 * b + 2 * h, : value.shape[1]] = value
            value = expand_bias[...].astype(F32)
            out[32 + 16 * b : 32 + 16 * b + value.shape[0], : value.shape[1]] = value

    return pl.pallas_call(
        body,
        out_shape=shaped(ROWS, 256, F32),
        in_specs=[SMEM] + [pl.BlockSpec(memory_space=pltpu.HBM)] * number,
        out_specs=VMEM,
        scratch_shapes=[pltpu.VMEM(v.shape, v.dtype) for v in flat]
        + [pltpu.SemaphoreType.DMA((number,))],
        compiler_params=pltpu.CompilerParams(vmem_limit_bytes=60 << 20),
        name="pack_vectors",
    )(place, *flat)


def prepare_first(place, merged, output, blocks):
    flat = []
    for gains, merged_bias, expand_bias in blocks:
        flat += list(gains) + [merged_bias.transpose(1, 0, 2), expand_bias]
    flat += [merged.transpose(1, 0, 2), output]
    number = len(flat)
    local = output.shape[1]

    def body(*refs):
        out, part, small, sem = refs[number], refs[number + 1 : -2], refs[-2], refs[-1]
        copies = [pltpu.make_async_copy(refs[i], part[i], sem.at[i]) for i in range(number)]
        for copy in copies:
            copy.start()
        small[...] = jnp.zeros_like(small)
        for copy in copies:
            copy.wait()
        for b in range(2):
            vectors, merged_bias, expand_bias = part[8 * b : 8 * b + 6], part[8 * b + 6], part[8 * b + 7]
            for i in range(6):
                small[6 * b + i : 6 * b + i + 1, :local] = (
                    vectors[i][...].astype(F32).reshape(1, local)
                )
            for h in range(merged_bias.shape[0]):
                value = merged_bias[h].astype(F32)
                small[16 + 8 * b + 2 * h : 18 + 8 * b + 2 * h, : value.shape[1]] = value
            value = expand_bias[...].astype(F32)
            small[32 + 16 * b : 32 + 16 * b + value.shape[0], : value.shape[1]] = value
        merged_ref, output_ref = part[-2:]
        pieces = [merged_ref[k] for k in range(3)] + [turn(output_ref[...]).astype(BF16)]
        out[:local, :] = jnp.concatenate(pieces, axis=1)
        out[local:, :256] = small[:SPARE, :].astype(BF16)
        out[local:, 256:512] = small[SPARE:, :].astype(BF16)
        out[local:, 512:] = jnp.zeros((SPARE, 4 * local - 512), BF16)

    return pl.pallas_call(
        body,
        out_shape=shaped(local + SPARE, 4 * local, BF16),
        in_specs=[pl.BlockSpec(memory_space=pltpu.HBM)] * number,
        out_specs=VMEM,
        scratch_shapes=[pltpu.VMEM(v.shape, v.dtype) for v in flat]
        + [pltpu.VMEM((ROWS, 256), F32), pltpu.SemaphoreType.DMA((number,))],
        compiler_params=pltpu.CompilerParams(vmem_limit_bytes=60 << 20),
        name="prepare_first",
    )(*flat)


def unpack_vectors(pieces, place, local, merged_shape, expand_shape):
    heads, few = merged_shape[1], merged_shape[2]
    groups = expand_shape[0]
    width = heads * 4 * few

    def body(place_ref, *refs):
        pieces, outs, pieces_ref = refs[:4], refs[4:-1], refs[-1]
        for k in range(4):
            for i in range(2):
                pieces_ref[k * ROWS + i * SPARE : k * ROWS + (i + 1) * SPARE, :] = pieces[k][
                    local:, 256 * i : 256 * (i + 1)
                ].astype(F32)
        y, z = place_ref[0], place_ref[1]
        for b in range(2):
            gains, bias, hidden = outs[3 * b : 3 * b + 3]
            for k in range(4):
                gains[0:6, k * local : (k + 1) * local] = pieces_ref[
                    k * ROWS + 6 * b : k * ROWS + 6 * b + 6, :local
                ]
            bias[...] = jnp.zeros_like(bias)
            for natural in range(4):
                distance = z ^ natural
                base = (2 * (distance & 1) + (distance >> 1)) * ROWS
                part = pieces_ref[pl.ds(pl.multiple_of(base, ROWS), ROWS), :128]
                for i in range(2):
                    for h in range(heads):
                        line = 16 + 8 * b + 2 * h + i
                        at = 2 * i * width + h * 4 * few + natural * few
                        bias[:, at : at + few] = part[line : line + 1, :few]
                lines = part[32 + 16 * b : 32 + 16 * b + groups]
                half = groups // 2
                lines = jnp.where(
                    y == 0, lines, jnp.concatenate([lines[half:], lines[:half]], axis=0)
                )
                for p in range(groups):
                    at = p * 4 * few + natural * few
                    hidden[:, at : at + few] = lines[p : p + 1, :few]

    one = (
        shaped(8, 4 * local, F32),
        shaped(1, 3 * width, F32),
        shaped(1, groups * 4 * few, F32),
    )
    return pl.pallas_call(
        body,
        out_shape=one + one,
        in_specs=[SMEM] + [VMEM] * 4,
        out_specs=(VMEM,) * 6,
        scratch_shapes=[pltpu.VMEM((4 * ROWS, 256), F32)],
        compiler_params=pltpu.CompilerParams(vmem_limit_bytes=8 << 20),
        name="unpack_vectors",
    )(place, *pieces)


def prepare_attend(place, merged, output):
    local = output.shape[1]
    half = 2 * local

    def body(place_ref, merged_ref, output_ref, attend):
        y = place_ref[0]
        pieces = [merged_ref[k] for k in range(3)] + [turn(output_ref[...]).astype(BF16)]
        whole = jnp.concatenate(pieces, axis=1)
        attend[...] = jnp.where(y == 0, whole[:, :half], whole[:, half:])

    return pl.pallas_call(
        body,
        out_shape=shaped(local, half, BF16),
        in_specs=[SMEM, VMEM, VMEM],
        out_specs=VMEM,
        compiler_params=pltpu.CompilerParams(vmem_limit_bytes=12 << 20),
        name="prepare_attend",
    )(place, merged.transpose(1, 0, 2), output)


def prepare_feed(place, expand, reduce):
    local, half = expand.shape[0], expand.shape[1] // 2

    def body(place_ref, expand_ref, reduce_ref, feed):
        y = place_ref[0]
        first, second = reduce_ref[:, :half], reduce_ref[:, half:]
        feed[:, :half] = jnp.where(y == 0, expand_ref[:, :half], expand_ref[:, half:])
        feed[:, half : 2 * half] = jnp.where(y == 0, first, second)
        feed[:, 2 * half :] = jnp.where(y == 0, second, first)

    return pl.pallas_call(
        body,
        out_shape=shaped(local, 3 * half, BF16),
        in_specs=[SMEM, VMEM, VMEM],
        out_specs=VMEM,
        compiler_params=pltpu.CompilerParams(vmem_limit_bytes=12 << 20),
        name="prepare_feed",
    )(place, expand, reduce.T)


def pack_grads(sums, biases, hiddens, place, local, merged_shape, expand_shape):
    heads, few = merged_shape[1], merged_shape[2]
    groups = expand_shape[0]
    width = heads * 4 * few

    def body(place_ref, sum_ref, bias_s, bias_t, hidden_s, hidden_t, out):
        y, z = place_ref[0], place_ref[1]
        out[...] = jnp.zeros_like(out)
        for k in range(4):
            out[k * ROWS : k * ROWS + 12, :local] = sum_ref[0:12, k * local : (k + 1) * local]
        for natural in range(4):
            distance = z ^ natural
            base = pl.multiple_of((2 * (distance & 1) + (distance >> 1)) * ROWS, ROWS)
            lines = []
            for bias in (bias_s, bias_t):
                for h in range(heads):
                    for i in range(2):
                        at = 2 * i * width + h * 4 * few + natural * few
                        lines.append(bias[:, at : at + few])
                lines.append(jnp.zeros((2, few), F32))
            for hidden in (hidden_s, hidden_t):
                rows = [
                    hidden[:, p * 4 * few + natural * few : p * 4 * few + natural * few + few]
                    for p in range(groups)
                ]
                first, second = rows[: groups // 2], rows[groups // 2 :]
                first, second = jnp.concatenate(first, axis=0), jnp.concatenate(second, axis=0)
                lines.append(jnp.where(y == 0, first, second))
                lines.append(jnp.where(y == 0, second, first))
                lines.append(jnp.zeros((16 - groups, few), F32))
            out[pl.ds(pl.multiple_of(base + 16, 16), ROWS - 16), :few] = jnp.concatenate(lines, axis=0)

    return pl.pallas_call(
        body,
        out_shape=shaped(4 * ROWS, 256, F32),
        in_specs=[SMEM] + [VMEM] * 5,
        out_specs=VMEM,
        compiler_params=pltpu.CompilerParams(vmem_limit_bytes=4 << 20),
        name="pack_grads",
    )(place, sums, *biases, *hiddens)


def unpack_grads(mine, arrived, local, merged_shape, expand_shape):
    heads, few = merged_shape[1], merged_shape[2]
    groups = expand_shape[0]

    def body(mine_ref, arrived_ref, *outs):
        total = mine_ref[0:ROWS, :] + arrived_ref[...]
        for b in range(2):
            vectors, merged_bias, expand_bias = outs[8 * b : 8 * b + 6], outs[8 * b + 6], outs[8 * b + 7]
            for i in range(6):
                vectors[i][...] = total[6 * b + i : 6 * b + i + 1, :local].reshape(local)
            for h in range(heads):
                merged_bias[h] = total[16 + 8 * b + 2 * h : 18 + 8 * b + 2 * h, :few]
            expand_bias[...] = total[32 + 16 * b : 32 + 16 * b + groups, :few]

    one = [jax.ShapeDtypeStruct((local,), F32)] * 6 + [
        jax.ShapeDtypeStruct((heads, 2, few), F32),
        jax.ShapeDtypeStruct(expand_shape, F32),
    ]
    values = pl.pallas_call(
        body,
        out_shape=tuple(one + one),
        in_specs=[VMEM] * 2,
        out_specs=(VMEM,) * 16,
        compiler_params=pltpu.CompilerParams(vmem_limit_bytes=4 << 20),
        name="unpack_grads",
    )(mine, arrived)
    return [v.transpose(1, 0, 2) if v.ndim == 3 else v for v in values]


def finish_feed(mine, theirs, place, half):
    local = mine.shape[0]
    whole = mine.shape[1] == 3 * half

    def body(place_ref, mine_ref, theirs_ref, expand, reduce):
        y = place_ref[0]
        own, other = mine_ref[:, :half].astype(F32), theirs_ref[:, :half].astype(F32)
        expand[:, :half] = jnp.where(y == 0, own, other)
        expand[:, half:] = jnp.where(y == 0, other, own)
        if whole:
            total = mine_ref[:, half:].astype(F32) + theirs_ref[:, half:].astype(F32)
            own, other = total[:, :half], total[:, half:]
        else:
            own, other = mine_ref[:, half:].astype(F32), theirs_ref[:, half:].astype(F32)
        reduce[:, :half] = jnp.where(y == 0, own, other)
        reduce[:, half:] = jnp.where(y == 0, other, own)

    expand, reduce = pl.pallas_call(
        body,
        out_shape=(shaped(local, 2 * half, F32), shaped(local, 2 * half, F32)),
        in_specs=[SMEM, VMEM, VMEM],
        out_specs=(VMEM, VMEM),
        compiler_params=pltpu.CompilerParams(vmem_limit_bytes=12 << 20),
        name="finish_feed",
    )(place, mine, theirs)
    return expand, reduce.T


def finish_attend(added, mine, theirs, place):
    local = mine.shape[0]

    def body(place_ref, *refs):
        mine_ref, theirs_ref, merged, output = refs[-4:]
        y = place_ref[0]
        own, other = mine_ref[...], theirs_ref[...]
        split = jnp.concatenate(
            [jnp.where(y == 0, own, other), jnp.where(y == 0, other, own)], axis=1
        )
        output[...] = turn(split[:, -local:])
        whole = split.astype(F32)
        if added:
            total = refs[0][...].astype(F32) + refs[1][...].astype(F32)
            whole = jnp.concatenate([total, whole], axis=1)
        for k in range(3):
            merged[k] = whole[:, k * local : (k + 1) * local]

    merged, output = pl.pallas_call(
        body,
        out_shape=(jax.ShapeDtypeStruct((3, local, local), F32), shaped(local, local, F32)),
        in_specs=[SMEM] + [VMEM] * (2 + len(added)),
        out_specs=(VMEM, VMEM),
        compiler_params=pltpu.CompilerParams(vmem_limit_bytes=12 << 20),
        name="finish_attend",
    )(place, *added, mine, theirs)
    return merged.transpose(1, 0, 2), output


def halves_added(kept, arrived):
    middle = kept.shape[0] // 2
    return (kept[middle:] + arrived[middle:].astype(F32)).astype(BF16)


def send_columns(value, cross):
    middle = value.shape[1] // 2
    return cross(value[:, middle:].astype(BF16))


def keep_columns(value, arrived):
    return value[:, : value.shape[1] // 2].astype(F32) + arrived.astype(F32)


def send_rows(value, cross):
    middle = value.shape[0] // 2
    return cross(value[middle:].astype(BF16))


def keep_rows(value, arrived):
    return value[: value.shape[0] // 2].astype(F32) + arrived.astype(F32)


def fast_shards(inputs, segments, cotangent, *params):
    y_index = lax.axis_index("ctx")
    z_index = lax.axis_index("dp")
    me = lax.axis_index("tp")
    tokens, features = inputs.shape[1], inputs.shape[2]
    length = segments.shape[1] * 2
    doc_max = min(DOC_MAX, length // 2)
    blocks = (params[:12], params[12:])
    local = features // 4
    half = local * 2

    small = [((p[0], p[1], p[5], p[6], p[7], p[11]), p[3], p[9]) for p in blocks]
    place = jnp.stack([y_index, z_index]).astype(jnp.int32)
    p = blocks[0]
    attend = prepare_first(place, p[2], p[4], small)
    inputs, attend = pin(inputs, attend)
    far, near = cross_far(attend), cross_near(attend)
    sent_rows = jnp.where(y_index == 0, inputs[1], inputs[0])
    sent_docs = jnp.where(y_index == 0, segments[1:2], segments[0:1]).astype(BF16)
    sent_docs = jnp.pad(sent_docs, ((0, 15), (0, features - sent_docs.shape[1])))
    moved = cross_y(stacked(sent_rows, sent_docs))
    kept_rows = jnp.where(y_index == 0, inputs[0], inputs[1])
    kept_docs = jnp.where(y_index == 0, segments[0:1], segments[1:2]).astype(F32)
    chooser = order_matrix(features, z_index)
    stream = times(y_order(kept_rows, moved[:tokens], y_index, 0), chooser)
    docs = y_order(
        kept_docs, moved[tokens : tokens + 1, : kept_docs.shape[1]].astype(F32), y_index, 1
    )
    context = (me.astype(jnp.int32).reshape(1), docs)
    rows = norm_only(stream)
    both = cross_near(far)
    feed = prepare_feed(place, blocks[0][8], blocks[0][10])
    feed, far = pin(feed, far)
    first = feed[:, : 2 * half]
    p_far = cross_far(first)
    moved_grad = cross_y(jnp.where(y_index == 0, cotangent[1], cotangent[0]))
    rows, place_t = pin(rows, place)
    p = blocks[1]
    own_a = prepare_attend(place_t, p[2], p[4])
    feed_t = prepare_feed(place_t, p[8], p[10])

    near_s = stacked(rows, cross_x(rows))
    near_s, near, both, p_far, feed_t, moved_grad = pin(
        near_s, near, both, p_far, feed_t, moved_grad
    )
    gains_s, bias_s, hidden_s, gains_t, bias_t, hidden_t = unpack_vectors(
        (attend, far, near, both), place, local, blocks[0][3].shape, blocks[0][9].shape
    )
    far_s = cross_core(near_s)
    attend_s = (attend, far, near, both)
    p_two = stacked(first, p_far)
    e_near = cross_near(p_two[:, :half])
    x_first = cross_x(feed_t)
    sent, kept, *saved_s, near_s, far_s = attention_forward(
        near_s, far_s, attend_s, bias_s, context, doc_max, (gains_s,)
    )
    sent, e_near, x_first, p_two = pin(sent, e_near, x_first, p_two)
    own_e = beside(feed_t[:, :half], x_first[:, :half])
    own_r = (
        beside(feed_t[:, half : 2 * half], x_first[:, half : 2 * half]),
        beside(feed_t[:, 2 * half :], x_first[:, 2 * half :]),
    )
    e_s = stacked(p_two[:, :half], e_near)
    e_other = cross_y(e_s)
    r_near = cross_near(p_two[:, half:])
    te_far = cross_far(own_e)
    arrived = cross_core(sent)
    across = cross_x(halves_added(kept, arrived))
    middle_s, rows = add_norm(stream, (kept, arrived, across), gains_s, 2, gains_s, 3)
    rows, e_other, r_near, te_far, own_a = pin(rows, e_other, r_near, te_far, own_a)
    r_s = stacked(p_two[:, half:], r_near)
    r_other = cross_y(r_s)
    te_two = stacked(own_e, te_far)
    te_near = cross_near(te_two)
    ta_far = cross_far(own_a)
    near_two_s = stacked(rows, cross_x(rows))
    near_two_s, r_other, te_near, ta_far, own_r = pin(near_two_s, r_other, te_near, ta_far, own_r)
    far_two_s = cross_core(near_two_s)
    feed_s = (near_two_s, far_two_s), ((e_s, e_other), (r_s, r_other), hidden_s)
    te = stacked(te_two, te_near)
    te_other_one = cross_y(te[:half])
    ta_two = stacked(own_a, ta_far)
    ta_near = cross_near(ta_two)
    ra_far = cross_far(own_r[0])
    sent, kept = feed_forward(*feed_s[0], *feed_s[1])
    arrived = cross_core(sent)
    across = cross_x(halves_added(kept, arrived))
    between, rows = add_norm(middle_s, (kept, arrived, across), gains_s, 5, gains_t, 0)
    rows, te_other_one, ta_near, ra_far, own_r = pin(rows, te_other_one, ta_near, ra_far, own_r)
    ta = stacked(ta_two, ta_near)
    ta_other = cross_y(ta)
    ra_two = stacked(own_r[0], ra_far)
    ra_near_one = cross_near(ra_two[:, :half])
    rb_far = cross_far(own_r[1])

    near_t = stacked(rows, cross_x(rows))
    near_t, ta_other, ra_near_one, rb_far, ra_two = pin(
        near_t, ta_other, ra_near_one, rb_far, ra_two
    )
    far_t = cross_core(near_t)
    attend_t = (
        jnp.where(y_index == 0, ta, ta_other),
        jnp.where(y_index == 0, ta_other, ta),
    )
    rb_two = stacked(own_r[1], rb_far)
    ra_near_two = cross_near(ra_two[:, half:])
    hidden_x = cross_x(hidden_t)
    hidden_t = beside(
        hidden_t[:, :half], hidden_x[:, :half], hidden_t[:, half:], hidden_x[:, half:]
    )
    sent, kept, *saved_t = attention_forward(near_t, far_t, attend_t, bias_t, context, doc_max)
    sent, ra_near_two, rb_two, te = pin(sent, ra_near_two, rb_two, te)
    te_other_two = cross_y(te[half:])
    rb_near = cross_near(rb_two)
    arrived = cross_core(sent)
    across = cross_x(halves_added(kept, arrived))
    middle_t, near_two_t = add_norm(between, (kept, arrived, across), gains_t, 2, gains_t, 3)
    near_two_t, te_other_two, rb_near = pin(near_two_t, te_other_two, rb_near)
    far_two_t = cross_core(near_two_t)
    expand_t = (te, te_other_one, te_other_two)
    reduce_t = (
        ra_two[:, :half],
        ra_near_one,
        ra_two[:, half:],
        ra_near_two,
        rb_two,
        rb_near,
    )
    feed_t = (near_two_t, far_two_t), (expand_t, reduce_t, hidden_t)
    final_sent, final_kept = feed_forward(*feed_t[0], *feed_t[1])
    grad_out = y_order(jnp.where(y_index == 0, cotangent[0], cotangent[1]), moved_grad, y_index, 0)

    grad_out = times(grad_out, chooser)
    sums = jnp.zeros((16, features), F32)
    branch = grad_out.astype(BF16)
    branch_far = cross_core(branch)
    sent, kept, active, grad_hidden, hidden_sum_t = feed_backward(
        *feed_t[0], branch, branch_far, *feed_t[1]
    )
    arrived = cross_core(sent)
    grad_middle, rows, sums = norm_back(
        grad_out, (kept, arrived), middle_t, gains_t, 3, sums, 9
    )
    moved = cross_x(rows)
    part_r = times_down(stacked(branch, branch_far), active, BF16)
    part_e = times_down(stacked(near_two_t, far_two_t), grad_hidden, BF16)
    near_grad = stacked(rows, moved)
    near_grad, part_r, part_e = pin(near_grad, part_r, part_e)
    ea_moved = cross_y(part_e[:half, 2 * half :])
    ra_moved = cross_near(part_r[half:, : 2 * half])
    far_grad = cross_core(near_grad)
    sent, kept, grad_qkv, qkv_sum_t = attention_backward(
        near_grad, far_grad, attend_t, context, saved_t, doc_max
    )
    sent, ea_moved, ra_moved, part_e, part_r = pin(sent, ea_moved, ra_moved, part_e, part_r)
    eb_moved = cross_y(part_e[half:, 2 * half :])
    rb_moved = cross_near(part_r[half:, 2 * half :])
    arrived = cross_core(sent)
    across = cross_x(halves_added(kept, arrived))
    part_a = beside(
        times_down(stacked(near_t, far_t), grad_qkv, BF16),
        times_down(stacked(near_grad, far_grad), saved_t[1], BF16),
    )
    part_a = beside(*column_halves(part_a, y_index))
    grad_between, rows, sums = norm_back(
        grad_middle, (kept, arrived, across), between, gains_t, 0, sums, 6
    )
    rows, eb_moved, rb_moved, part_a = pin(rows, eb_moved, rb_moved, part_a)
    part_e = keep_columns(part_e, stacked(ea_moved, eb_moved))
    part_r = keep_rows(part_r, beside(ra_moved, rb_moved))
    e_moved = send_rows(part_e, cross_near)
    a_moved = send_columns(part_a, cross_y)

    branch = stacked(rows, cross_x(rows))
    branch, e_moved, a_moved = pin(branch, e_moved, a_moved)
    branch_far = cross_core(branch)
    part_e = keep_rows(part_e, e_moved)
    ex_moved = send_columns(part_e, cross_x)
    part_a = keep_columns(part_a, a_moved)
    sent, kept, active, grad_hidden, hidden_sum_s = feed_backward(
        *feed_s[0], branch, branch_far, *feed_s[1]
    )
    sent, ex_moved, part_r, part_a = pin(sent, ex_moved, part_r, part_a)
    part_e = keep_columns(part_e, ex_moved)
    a_moved = send_rows(part_a, cross_near)
    ra_moved = cross_far(part_r[local:, : 2 * half].astype(BF16))
    arrived = cross_core(sent)
    across = cross_x(halves_added(kept, arrived))
    feed_r = times_down(stacked(branch, branch_far), active, BF16)
    feed_e = times_down(stacked(near_two_s, far_two_s), grad_hidden, BF16)
    grad_middle, rows, sums = norm_back(
        grad_between, (kept, arrived, across), middle_s, gains_s, 3, sums, 3
    )
    rows, a_moved, ra_moved, feed_e, feed_r, part_r, part_e = pin(
        rows, a_moved, ra_moved, feed_e, feed_r, part_r, part_e
    )
    fe_moved = send_columns(feed_e, cross_y)
    part_a = keep_rows(part_a, a_moved)
    rb_moved = cross_far(part_r[local:, 2 * half :].astype(BF16))
    near_grad = stacked(rows, cross_x(rows))
    near_grad, fe_moved, rb_moved, feed_r, part_e, part_a = pin(
        near_grad, fe_moved, rb_moved, feed_r, part_e, part_a
    )
    far_grad = cross_core(near_grad)
    part_r = part_r[:local] + beside(ra_moved, rb_moved).astype(F32)
    e_moved = send_rows(part_e, cross_far)
    fr_moved = send_rows(feed_r, cross_near)
    rx_moved = cross_x(
        beside(part_r[:, half : 2 * half], part_r[:, 3 * half :]).astype(BF16)
    )
    feed_e = keep_columns(feed_e, fe_moved)
    sent, kept, grad_qkv, qkv_sum_s = attention_backward(
        near_grad, far_grad, attend_s, context, saved_s, doc_max
    )
    sent, e_moved, part_a, fr_moved, rx_moved = pin(sent, e_moved, part_a, fr_moved, rx_moved)
    part_r = beside(part_r[:, :half], part_r[:, 2 * half : 3 * half]) + rx_moved.astype(F32)
    mine_t = beside(keep_rows(part_e, e_moved), part_r).astype(BF16)
    theirs_t = cross_y(
        beside(mine_t[:, :half], mine_t[:, 2 * half :], mine_t[:, half : 2 * half])
    )
    at_moved = send_rows(part_a, cross_far)
    feed_r = keep_rows(feed_r, fr_moved)
    fe_moved, fr_moved = send_rows(feed_e, cross_near), send_rows(feed_r, cross_far)
    arrived = cross_core(sent)
    across = cross_x(halves_added(kept, arrived))
    grad_a = beside(
        times_down(stacked(near_s, far_s), grad_qkv, BF16),
        times_down(stacked(near_grad, far_grad), saved_s[1], BF16),
    )
    whole = features - 256
    grad_z, grad_a = grad_a[:, :whole], grad_a[:, whole:]
    grad_a, y_moved = column_halves(grad_a, y_index)
    y_moved, z_moved = cross_y(y_moved), send_rows(grad_z, cross_near)
    grad_in, _, sums = norm_back(
        grad_middle, (kept, arrived, across), stream, gains_s, 0, sums, 0
    )
    sums_moved = cross_core(sums)
    input_grad = lax.dot_general(
        grad_in,
        chooser.astype(F32),
        (((1,), (1,)), ((), ())),
        precision=lax.Precision.HIGHEST,
        preferred_element_type=F32,
    )

    def swapped(value):
        first, second = value[:tokens], value[tokens:]
        return cross_y(jnp.where(y_index == 0, second, first))

    def restore(value, received):
        kept = jnp.where(y_index == 0, value[:tokens], value[tokens:])
        return jnp.where(y_index == 0, jnp.stack([kept, received]), jnp.stack([received, kept]))

    y_moved, z_moved, sums_moved, input_grad = pin(y_moved, z_moved, sums_moved, input_grad)
    grad_a = grad_a.astype(F32) + y_moved.astype(F32)
    grad_z = keep_rows(grad_z, z_moved)
    y_moved, z_moved = send_rows(grad_a, cross_near), send_rows(grad_z, cross_far)
    sums = sums + sums_moved
    sums_moved = cross_x(sums)
    grad_moved = swapped(input_grad.astype(BF16)).astype(F32)
    own_half = beside(hidden_sum_t[:, :half], hidden_sum_t[:, 2 * half : 3 * half])
    x_half = beside(hidden_sum_t[:, half : 2 * half], hidden_sum_t[:, 3 * half :])
    hidden_sum_t = own_half + cross_x(x_half)
    y_moved, z_moved, sums_moved, fe_moved, fr_moved = pin(
        y_moved, z_moved, sums_moved, fe_moved, fr_moved
    )
    feed_e, feed_r = keep_rows(feed_e, fe_moved), keep_rows(feed_r, fr_moved)
    fe_moved = send_rows(feed_e, cross_far)
    grad_a = keep_rows(grad_a, y_moved)
    grad_z = keep_rows(grad_z, z_moved).astype(BF16)
    y_moved, z_moved = send_rows(grad_a, cross_far), cross_y(grad_z)
    pack = pack_grads(
        sums + sums_moved,
        (qkv_sum_s, qkv_sum_t),
        (hidden_sum_s, hidden_sum_t),
        place,
        local,
        params[3].shape,
        params[9].shape,
    )
    pack_moved = cross_y(pack)
    y_moved, z_moved, pack_moved, fe_moved, at_moved, theirs_t = pin(
        y_moved, z_moved, pack_moved, fe_moved, at_moved, theirs_t
    )
    mine_a = keep_rows(grad_a, y_moved).astype(BF16)
    mine_b = keep_rows(part_a, at_moved).astype(BF16)
    theirs_a = cross_y(beside(mine_a, mine_b))
    pack = pack + pack_moved
    pack_near = cross_near(pack[2 * ROWS :])
    mine_s = beside(keep_rows(feed_e, fe_moved), feed_r).astype(BF16)
    theirs_s = cross_y(
        beside(mine_s[:, :half], mine_s[:, 2 * half :], mine_s[:, half : 2 * half])
    )
    expand_grad_t, reduce_grad_t = finish_feed(mine_t, theirs_t, place, half)
    pack_near, theirs_a, expand_grad_t, reduce_grad_t = pin(
        pack_near, theirs_a, expand_grad_t, reduce_grad_t
    )
    pack = pack[: 2 * ROWS] + pack_near
    pack_far = cross_far(pack[ROWS:])
    merged_grad_s, output_grad_s = finish_attend(
        (grad_z, z_moved), mine_a, theirs_a[:, : mine_a.shape[1]], place
    )
    merged_grad_t, output_grad_t = finish_attend(
        (), mine_b, theirs_a[:, mine_a.shape[1] :], place
    )
    expand_grad_s, reduce_grad_s = finish_feed(mine_s, theirs_s, place, half)
    vectors = unpack_grads(pack, pack_far, local, params[3].shape, params[9].shape)
    final_sent, final_kept, grad_between = pin(final_sent, final_kept, grad_between)
    final = middle_t + gains_t[5:6] + final_kept + cross_core(final_sent).astype(F32)
    final = times_across(final.astype(BF16), chooser, BF16)
    outputs = [restore(final, swapped(final)), restore(input_grad, grad_moved)]
    for vector, merged, output, expand, reduce in (
        (vectors[:8], merged_grad_s, output_grad_s, expand_grad_s, reduce_grad_s),
        (vectors[8:], merged_grad_t, output_grad_t, expand_grad_t, reduce_grad_t),
    ):
        outputs += [
            vector[0],
            vector[1],
            merged,
            vector[6],
            output,
            vector[2],
            vector[3],
            vector[4],
            expand,
            vector[7],
            reduce,
            vector[5],
        ]
    return tuple(outputs)


def solution(mesh):
    quick = (mesh.shape["dp"], mesh.shape["ctx"], mesh.shape["tp"]) == (4, 2, 4)
    placed = (
        P("dp", ("ctx", "tp"), None),
        P("dp", "ctx"),
        P("dp", ("ctx", "tp"), None),
        P("dp"),
        P("dp"),
        P("dp", None, "tp"),
        P(None, "tp", "dp"),
        P("tp", "dp"),
        P("dp"),
        P("dp"),
        P("dp"),
        P("dp", "tp"),
        P("tp", "dp"),
        P("tp", "dp"),
        P("dp"),
        P("dp"),
        P("dp"),
        P("dp", None, "tp"),
        P(None, "tp", "dp"),
        P("tp", "dp"),
        P("dp"),
        P("dp"),
        P("dp"),
        P("dp", "tp"),
        P("tp", "dp"),
        P("tp", "dp"),
        P("dp"),
    )
    return jax.shard_map(
        fast_shards if quick else general_shards,
        mesh=mesh,
        in_specs=placed,
        out_specs=(
            P("dp", ("ctx", "tp"), None),
            P("dp", ("ctx", "tp"), None),
            P("dp"),
            P("dp"),
            P("dp", None, "tp"),
            P(None, "tp", "dp"),
            P("tp", "dp"),
            P("dp"),
            P("dp"),
            P("dp"),
            P("dp", "tp"),
            P("tp", "dp"),
            P("tp", "dp"),
            P("dp"),
            P("dp"),
            P("dp"),
            P("dp", None, "tp"),
            P(None, "tp", "dp"),
            P("tp", "dp"),
            P("dp"),
            P("dp"),
            P("dp"),
            P("dp", "tp"),
            P("tp", "dp"),
            P("tp", "dp"),
            P("dp"),
        ),
        check_vma=False,
    )
```

```python
import jax
import jax.numpy as jnp
from jax import lax
from jax.experimental import pallas as pl
from jax.experimental.layout import Layout, with_layout_constraint
from jax.experimental.pallas import tpu as pltpu
from jax.sharding import PartitionSpec as P

HD = 64
DOC_MAX = 2000


EPSILON = 1e-05
GELU_SCALE = 0.7978845608028654


def from_behind(block, axis, distance):
    devices = range(lax.axis_size(axis))
    route = [(i - distance, i) for i in devices if i - distance in devices]
    return lax.ppermute(block, axis, route)


def layer_norm(values, norm_gain, norm_shift):
    center = values - jnp.mean(values, axis=-1, keepdims=True)
    spread = jnp.mean(center * center, axis=-1, keepdims=True)
    return center * lax.rsqrt(spread + EPSILON) * norm_gain + norm_shift


def gelu_tanh(values):
    return (
        0.5 * values * (1.0 + jnp.tanh(GELU_SCALE * (values + 0.044715 * values * values * values)))
    )


def spread_rows(row_block):
    return lax.all_gather(row_block, "tp", axis=1, tiled=True)


def gather_sums(partial_value):
    return lax.psum_scatter(
        partial_value.astype(jnp.bfloat16), "tp", scatter_dimension=1, tiled=True
    ).astype(jnp.float32)


def to_items(tensor, head_count):
    batches, length, features = tensor.shape
    head_size = features // head_count
    return (
        tensor.reshape(batches, length, head_count, head_size)
        .transpose(0, 2, 1, 3)
        .reshape(batches * head_count, length, head_size)
    )


def from_items(tensor, head_count):
    item_count, length, head_size = tensor.shape
    batches = item_count // head_count
    return (
        tensor.reshape(batches, head_count, length, head_size)
        .transpose(0, 2, 1, 3)
        .reshape(batches, length, head_count * head_size)
    )


def masked_scores(query_rows, key_rows, query_docs, key_docs, allowed):
    raw_scores = (
        jnp.einsum("qd,kd->qk", query_rows, key_rows, preferred_element_type=jnp.float32) * 0.125
    )
    keep_mask = allowed & (key_docs[None, :] == query_docs[:, None])
    return (jnp.where(keep_mask, raw_scores, -1e30), keep_mask)


def attend_forward(allowed):

    def attend_item(packed):
        query_rows, key_rows, value_rows, query_docs, key_docs = packed
        scores, keep_mask = masked_scores(query_rows, key_rows, query_docs, key_docs, allowed)
        row_top = jnp.max(scores, axis=-1, keepdims=True)
        raised = jnp.exp(scores - row_top)
        row_total = jnp.sum(raised, axis=-1, keepdims=True)
        weights = (raised / row_total).astype(jnp.bfloat16)
        mixed_rows = jnp.dot(weights, value_rows, preferred_element_type=jnp.float32).astype(
            jnp.bfloat16
        )
        return (mixed_rows, row_top[:, 0] + jnp.log(row_total[:, 0]))

    return attend_item


def attend_backward(allowed):

    def attend_item(packed):
        query_rows, key_rows, value_rows, query_docs, key_docs, log_total, grad_rows = packed
        scores, keep_mask = masked_scores(query_rows, key_rows, query_docs, key_docs, allowed)
        weights = jnp.where(keep_mask, jnp.exp(scores - log_total[:, None]), 0.0)
        grad_values = jnp.einsum(
            "qk,qd->kd", weights.astype(jnp.bfloat16), grad_rows, preferred_element_type=jnp.float32
        )
        grad_weights = jnp.einsum(
            "qd,kd->qk", grad_rows, value_rows, preferred_element_type=jnp.float32
        )
        centered = jnp.sum(weights * grad_weights, axis=-1, keepdims=True)
        grad_scores = (weights * (grad_weights - centered)).astype(jnp.bfloat16)
        grad_query = jnp.dot(grad_scores, key_rows, preferred_element_type=jnp.float32) * 0.125
        grad_keys = (
            jnp.einsum("qk,qd->kd", grad_scores, query_rows, preferred_element_type=jnp.float32)
            * 0.125
        )
        return (grad_query, grad_keys, grad_values)

    return attend_item


def layer_forward(stream, params, segments, key_docs, allowed, cycle_steps):
    (
        first_gain,
        first_shift,
        merged_weight,
        merged_bias,
        output_weight,
        output_bias,
        second_gain,
        second_shift,
        expand_weight,
        expand_bias,
        reduce_weight,
        reduce_bias,
    ) = params
    fetched = (
        lax.all_gather(first_gain, "dp", axis=0, tiled=True),
        lax.all_gather(first_shift, "dp", axis=0, tiled=True),
        lax.all_gather(merged_weight, "dp", axis=0, tiled=True),
        lax.all_gather(merged_bias, "dp", axis=2, tiled=True),
        lax.all_gather(output_weight, "dp", axis=1, tiled=True),
        lax.all_gather(output_bias, "dp", axis=0, tiled=True),
        lax.all_gather(second_gain, "dp", axis=0, tiled=True),
        lax.all_gather(second_shift, "dp", axis=0, tiled=True),
        lax.all_gather(expand_weight, "dp", axis=0, tiled=True),
        lax.all_gather(expand_bias, "dp", axis=1, tiled=True),
        lax.all_gather(reduce_weight, "dp", axis=1, tiled=True),
        lax.all_gather(reduce_bias, "dp", axis=0, tiled=True),
    )
    (
        first_gain,
        first_shift,
        merged_weight,
        merged_bias,
        output_weight,
        output_bias,
        second_gain,
        second_shift,
        expand_weight,
        expand_bias,
        reduce_weight,
        reduce_bias,
    ) = fetched
    head_count = merged_weight.shape[2] // HD
    normed = layer_norm(
        stream, first_gain.astype(jnp.float32), first_shift.astype(jnp.float32)
    ).astype(jnp.bfloat16)
    first_rows = spread_rows(normed)
    merged_out = jnp.einsum(
        "std,dkf->stkf", first_rows, merged_weight, preferred_element_type=jnp.float32
    )
    bias_pair = merged_bias.astype(jnp.float32).reshape(2, -1)
    query_rows = (merged_out[:, :, 0] + bias_pair[0]).astype(jnp.bfloat16)
    key_rows = merged_out[:, :, 1].astype(jnp.bfloat16)
    value_rows = (merged_out[:, :, 2] + bias_pair[1]).astype(jnp.bfloat16)
    key_list = [key_rows]
    value_list = [value_rows]
    moving = (key_rows, value_rows)
    for offset in range(cycle_steps):
        moving = from_behind((moving[0], moving[1]), "ctx", 1)
        key_list.insert(0, moving[0])
        value_list.insert(0, moving[1])
    query_items = to_items(query_rows, head_count)
    key_items = to_items(jnp.concatenate(key_list, axis=1), head_count)
    value_items = to_items(jnp.concatenate(value_list, axis=1), head_count)
    query_docs = jnp.repeat(segments, head_count, axis=0)
    window_docs = jnp.repeat(key_docs, head_count, axis=0)
    mixed_items, log_total = lax.map(
        attend_forward(allowed), (query_items, key_items, value_items, query_docs, window_docs)
    )
    mixed = from_items(mixed_items, head_count)
    attn_part = jnp.einsum("stf,fd->std", mixed, output_weight, preferred_element_type=jnp.float32)
    middle = stream + gather_sums(attn_part) + output_bias.astype(jnp.float32)
    normed_two = layer_norm(
        middle, second_gain.astype(jnp.float32), second_shift.astype(jnp.float32)
    ).astype(jnp.bfloat16)
    second_rows = spread_rows(normed_two)
    hidden = jnp.einsum(
        "std,df->stf", second_rows, expand_weight, preferred_element_type=jnp.float32
    ) + expand_bias.astype(jnp.float32).reshape(-1)
    activated = gelu_tanh(hidden).astype(jnp.bfloat16)
    mlp_part = jnp.einsum(
        "stf,fd->std", activated, reduce_weight, preferred_element_type=jnp.float32
    )
    result = middle + gather_sums(mlp_part) + reduce_bias.astype(jnp.float32)
    saved_state = (
        fetched,
        stream,
        first_rows,
        query_items,
        key_items,
        value_items,
        query_docs,
        window_docs,
        log_total,
        mixed,
        middle,
        second_rows,
        hidden,
        activated,
    )
    return (result, saved_state)


def reduce_grads(fresh):
    (
        gain_one,
        shift_one,
        merged_weights,
        merged_biases,
        output_weights,
        output_biases,
        gain_two,
        shift_two,
        expand_weights,
        expand_biases,
        reduce_weights,
        reduce_biases,
    ) = fresh
    summed = (
        lax.psum(gain_one.astype(jnp.bfloat16), "ctx").astype(jnp.float32),
        lax.psum(shift_one.astype(jnp.bfloat16), "ctx").astype(jnp.float32),
        lax.psum(merged_weights.astype(jnp.bfloat16), "ctx").astype(jnp.float32),
        lax.psum(merged_biases.astype(jnp.bfloat16), "ctx").astype(jnp.float32),
        lax.psum(output_weights.astype(jnp.bfloat16), "ctx").astype(jnp.float32),
        lax.psum(output_biases.astype(jnp.bfloat16), "ctx").astype(jnp.float32),
        lax.psum(gain_two.astype(jnp.bfloat16), "ctx").astype(jnp.float32),
        lax.psum(shift_two.astype(jnp.bfloat16), "ctx").astype(jnp.float32),
        lax.psum(expand_weights.astype(jnp.bfloat16), "ctx").astype(jnp.float32),
        lax.psum(expand_biases.astype(jnp.bfloat16), "ctx").astype(jnp.float32),
        lax.psum(reduce_weights.astype(jnp.bfloat16), "ctx").astype(jnp.float32),
        lax.psum(reduce_biases.astype(jnp.bfloat16), "ctx").astype(jnp.float32),
    )
    (
        gain_one,
        shift_one,
        merged_weights,
        merged_biases,
        output_weights,
        output_biases,
        gain_two,
        shift_two,
        expand_weights,
        expand_biases,
        reduce_weights,
        reduce_biases,
    ) = summed
    return (
        lax.psum_scatter(
            gain_one.astype(jnp.bfloat16), "dp", scatter_dimension=0, tiled=True
        ).astype(jnp.float32),
        lax.psum_scatter(
            shift_one.astype(jnp.bfloat16), "dp", scatter_dimension=0, tiled=True
        ).astype(jnp.float32),
        lax.psum_scatter(
            merged_weights.astype(jnp.bfloat16), "dp", scatter_dimension=0, tiled=True
        ).astype(jnp.float32),
        lax.psum_scatter(
            merged_biases.astype(jnp.bfloat16), "dp", scatter_dimension=2, tiled=True
        ).astype(jnp.float32),
        lax.psum_scatter(
            output_weights.astype(jnp.bfloat16), "dp", scatter_dimension=1, tiled=True
        ).astype(jnp.float32),
        lax.psum_scatter(
            output_biases.astype(jnp.bfloat16), "dp", scatter_dimension=0, tiled=True
        ).astype(jnp.float32),
        lax.psum_scatter(
            gain_two.astype(jnp.bfloat16), "dp", scatter_dimension=0, tiled=True
        ).astype(jnp.float32),
        lax.psum_scatter(
            shift_two.astype(jnp.bfloat16), "dp", scatter_dimension=0, tiled=True
        ).astype(jnp.float32),
        lax.psum_scatter(
            expand_weights.astype(jnp.bfloat16), "dp", scatter_dimension=0, tiled=True
        ).astype(jnp.float32),
        lax.psum_scatter(
            expand_biases.astype(jnp.bfloat16), "dp", scatter_dimension=1, tiled=True
        ).astype(jnp.float32),
        lax.psum_scatter(
            reduce_weights.astype(jnp.bfloat16), "dp", scatter_dimension=1, tiled=True
        ).astype(jnp.float32),
        lax.psum_scatter(
            reduce_biases.astype(jnp.bfloat16), "dp", scatter_dimension=0, tiled=True
        ).astype(jnp.float32),
    )


def layer_backward(grad_out, saved_state, allowed, cycle_steps, token_count):
    (
        fetched,
        stream,
        first_rows,
        query_items,
        key_items,
        value_items,
        query_docs,
        window_docs,
        log_total,
        mixed,
        middle,
        second_rows,
        hidden,
        activated,
    ) = saved_state
    (
        first_gain,
        first_shift,
        merged_weight,
        merged_bias,
        output_weight,
        output_bias,
        second_gain,
        second_shift,
        expand_weight,
        expand_bias,
        reduce_weight,
        reduce_bias,
    ) = fetched
    head_count = merged_weight.shape[2] // HD
    grad_branch = spread_rows(grad_out.astype(jnp.bfloat16))
    grad_reduce = jnp.einsum(
        "stf,std->fd", activated, grad_branch, preferred_element_type=jnp.float32
    )
    grad_active = jnp.einsum(
        "std,fd->stf", grad_branch, reduce_weight, preferred_element_type=jnp.float32
    )
    _, gelu_pull = jax.vjp(gelu_tanh, hidden)
    grad_hidden = gelu_pull(grad_active)[0].astype(jnp.bfloat16)
    grad_expand_bias = jnp.sum(grad_hidden, axis=(0, 1), dtype=jnp.float32).reshape(
        expand_bias.shape
    )
    grad_expand = jnp.einsum(
        "std,stf->df", second_rows, grad_hidden, preferred_element_type=jnp.float32
    )
    grad_second = gather_sums(
        jnp.einsum("stf,df->std", grad_hidden, expand_weight, preferred_element_type=jnp.float32)
    )
    _, second_pull = jax.vjp(
        layer_norm, middle, second_gain.astype(jnp.float32), second_shift.astype(jnp.float32)
    )
    grad_norm_mid, grad_second_gain, grad_second_shift = second_pull(grad_second)
    grad_middle = grad_out + grad_norm_mid
    grad_reduce_bias = jnp.sum(grad_out, axis=(0, 1))
    grad_attend = spread_rows(grad_middle.astype(jnp.bfloat16))
    grad_output = jnp.einsum("stf,std->fd", mixed, grad_attend, preferred_element_type=jnp.float32)
    grad_mixed = jnp.einsum(
        "std,fd->stf", grad_attend, output_weight, preferred_element_type=jnp.float32
    ).astype(jnp.bfloat16)
    grad_query_items, grad_key_items, grad_value_items = lax.map(
        attend_backward(allowed),
        (
            query_items,
            key_items,
            value_items,
            query_docs,
            window_docs,
            log_total,
            to_items(grad_mixed, head_count),
        ),
    )
    grad_query = from_items(grad_query_items, head_count)
    window_keys = from_items(grad_key_items, head_count)
    window_values = from_items(grad_value_items, head_count)
    local_keys = window_keys[:, cycle_steps * token_count :]
    local_values = window_values[:, cycle_steps * token_count :]
    carried = None
    for offset in range(cycle_steps, 0, -1):
        start_row = (cycle_steps - offset) * token_count
        block_keys = window_keys[:, start_row : start_row + token_count]
        block_values = window_values[:, start_row : start_row + token_count]
        if carried is not None:
            block_keys = block_keys + carried[0]
            block_values = block_values + carried[1]
        carried = (
            from_behind(block_keys.astype(jnp.bfloat16), "ctx", -1).astype(block_keys.dtype),
            from_behind(block_values.astype(jnp.bfloat16), "ctx", -1).astype(block_values.dtype),
        )
    local_keys = local_keys + carried[0]
    local_values = local_values + carried[1]
    grad_merged = jnp.stack([grad_query, local_keys, local_values], axis=2).astype(jnp.bfloat16)
    grad_merged_bias = jnp.stack(
        [
            jnp.sum(grad_merged[:, :, 0], axis=(0, 1), dtype=jnp.float32),
            jnp.sum(grad_merged[:, :, 2], axis=(0, 1), dtype=jnp.float32),
        ]
    ).reshape(merged_bias.shape)
    grad_merged_weight = jnp.einsum(
        "std,stkf->dkf", first_rows, grad_merged, preferred_element_type=jnp.float32
    )
    grad_first = gather_sums(
        jnp.einsum("stkf,dkf->std", grad_merged, merged_weight, preferred_element_type=jnp.float32)
    )
    _, first_pull = jax.vjp(
        layer_norm, stream, first_gain.astype(jnp.float32), first_shift.astype(jnp.float32)
    )
    grad_norm_in, grad_first_gain, grad_first_shift = first_pull(grad_first)
    grad_input = grad_middle + grad_norm_in
    grad_output_bias = jnp.sum(grad_middle, axis=(0, 1))
    vector_grads = lax.psum(
        (
            grad_first_gain,
            grad_first_shift,
            grad_second_gain,
            grad_second_shift,
            grad_output_bias,
            grad_reduce_bias,
        ),
        "tp",
    )
    fresh = (
        vector_grads[0],
        vector_grads[1],
        grad_merged_weight,
        grad_merged_bias,
        grad_output,
        vector_grads[4],
        vector_grads[2],
        vector_grads[3],
        grad_expand,
        grad_expand_bias,
        grad_reduce,
        vector_grads[5],
    )
    return (grad_input, reduce_grads(fresh))


def general_shards(
    inputs,
    segments,
    cotangent,
    student_first_gain,
    student_first_shift,
    student_merged_weight,
    student_merged_bias,
    student_output_weight,
    student_output_bias,
    student_second_gain,
    student_second_shift,
    student_expand_weight,
    student_expand_bias,
    student_reduce_weight,
    student_reduce_bias,
    teacher_first_gain,
    teacher_first_shift,
    teacher_merged_weight,
    teacher_merged_bias,
    teacher_output_weight,
    teacher_output_bias,
    teacher_second_gain,
    teacher_second_shift,
    teacher_expand_weight,
    teacher_expand_bias,
    teacher_reduce_weight,
    teacher_reduce_bias,
):
    student = (
        student_first_gain,
        student_first_shift,
        student_merged_weight,
        student_merged_bias,
        student_output_weight,
        student_output_bias,
        student_second_gain,
        student_second_shift,
        student_expand_weight,
        student_expand_bias,
        student_reduce_weight,
        student_reduce_bias,
    )
    teacher = (
        teacher_first_gain,
        teacher_first_shift,
        teacher_merged_weight,
        teacher_merged_bias,
        teacher_output_weight,
        teacher_output_bias,
        teacher_second_gain,
        teacher_second_shift,
        teacher_expand_weight,
        teacher_expand_bias,
        teacher_reduce_weight,
        teacher_reduce_bias,
    )
    token_count = segments.shape[1]
    context_size = lax.axis_size("ctx")
    context_index = lax.axis_index("ctx")
    doc_long = min(DOC_MAX, token_count * context_size // 2)
    cycle_steps = min((doc_long - 2) // token_count + 1, context_size - 1)
    doc_list = [segments]
    moving = segments
    for offset in range(cycle_steps):
        moving = from_behind(moving, "ctx", 1)
        doc_list.insert(0, moving)
    key_docs = jnp.concatenate(doc_list, axis=1)
    places = jnp.arange((cycle_steps + 1) * token_count, dtype=jnp.int32)
    relative = places - cycle_steps * token_count
    source = cycle_steps - places // token_count
    query_place = jnp.arange(token_count, dtype=jnp.int32)
    allowed = (relative[None, :] <= query_place[:, None]) & (source <= context_index)[None, :]
    stream = inputs.astype(jnp.float32)
    middle_stream, student_saved = layer_forward(
        stream, student, segments, key_docs, allowed, cycle_steps
    )
    final_stream, teacher_saved = layer_forward(
        middle_stream, teacher, segments, key_docs, allowed, cycle_steps
    )
    teacher_in_grad, teacher_grads = layer_backward(
        cotangent.astype(jnp.float32), teacher_saved, allowed, cycle_steps, token_count
    )
    input_grad, student_grads = layer_backward(
        teacher_in_grad, student_saved, allowed, cycle_steps, token_count
    )
    return (
        (final_stream.astype(jnp.bfloat16), input_grad)
        + tuple(student_grads)
        + tuple(teacher_grads)
    )


BF16 = jnp.bfloat16
F32 = jnp.float32
NEG = -1e30
TILE = 256
RELATIVE = (0, 2, 1, 3)


def row_major(value):
    return with_layout_constraint(value, Layout(major_to_minor=tuple(range(value.ndim))))


def swap(value, axis, bit):
    route = [(i, i ^ bit) for i in range(lax.axis_size(axis))]
    if value.ndim == 2:
        return row_major(lax.ppermute(row_major(value), axis, route))
    return lax.ppermute(value, axis, route)


def cross_core(value):
    return swap(value, "tp", 1)


def cross_x(value):
    return swap(value, "tp", 2)


def cross_y(value):
    return swap(value, "ctx", 1)


def cross_near(value):
    return swap(value, "dp", 1)


def cross_far(value):
    return swap(value, "dp", 2)


def cross_both(value):
    return swap(value, "dp", 3)


def stacked(*values):
    return jnp.concatenate(values, axis=0)


def beside(*values):
    return jnp.concatenate(values, axis=1)


def y_order(own, other, y_index, axis):
    return jnp.where(
        y_index == 0,
        jnp.concatenate([own, other], axis=axis),
        jnp.concatenate([other, own], axis=axis),
    )


def pin(*values):
    return lax.optimization_barrier(values)


def window_start(block, doc_max):
    return max(0, (block * TILE - doc_max + 1) // TILE) * TILE


def upright(line):
    size = line.shape[1]
    rows = lax.broadcasted_iota(jnp.int32, (size, size), 0)
    columns = lax.broadcasted_iota(jnp.int32, (size, size), 1)
    return jnp.sum(jnp.where(rows == columns, line, 0.0), axis=1, keepdims=True)


def join(pieces, whole):
    row, column = 0, 0
    most = whole.shape[0] * whole.shape[1] // sum(piece.shape[1] for piece in pieces)
    for piece in pieces:
        rows = min(piece.shape[0], most) if len(pieces) == 4 else piece.shape[0]
        whole[row : row + rows, column : column + piece.shape[1]] = piece[:rows, :]
        row += rows
        if row == whole.shape[0]:
            row, column = 0, column + piece.shape[1]


def dot_across(left, right):
    return lax.dot_general(left, right, (((1,), (1,)), ((), ())), preferred_element_type=F32)


def dot_down(left, right):
    return lax.dot_general(left, right, (((0,), (0,)), ((), ())), preferred_element_type=F32)


def token_place(me, member, half, rows):
    return pl.multiple_of((half * 4 + (me ^ (2 * (member & 1) + (member >> 1)))) * rows, rows)


def flat(column):
    size = column.shape[0]
    rows = lax.broadcasted_iota(jnp.int32, (size, size), 0)
    columns = lax.broadcasted_iota(jnp.int32, (size, size), 1)
    return jnp.sum(jnp.where(rows == columns, column, 0.0), axis=0, keepdims=True)


def fill_masks_across(docs, masks, doc_max):
    for block in range(docs.shape[1] // TILE):
        start, stop = window_start(block, doc_max), (block + 1) * TILE
        here = slice(block * TILE, stop)
        rows = block * TILE + lax.broadcasted_iota(jnp.int32, (TILE, stop - start), 0)
        columns = start + lax.broadcasted_iota(jnp.int32, (TILE, stop - start), 1)
        same = upright(docs[:, here]) == docs[:, start:stop]
        masks[here, : stop - start] = jnp.where(same & (columns <= rows), 0.0, NEG)


def mask_columns(length, doc_max):
    return max((block + 1) * TILE - window_start(block, doc_max) for block in range(length // TILE))


def fill_masks(docs, masks, doc_max):
    at = 0
    for block in range(docs.shape[1] // TILE):
        start = window_start(block, doc_max)
        size = (block + 1) * TILE - start
        for first in range(0, size, TILE):
            keys = slice(start + first, start + first + TILE)
            same = upright(docs[:, keys]) == docs[:, block * TILE : (block + 1) * TILE]
            if start + first == block * TILE:
                rows = lax.broadcasted_iota(jnp.int32, (TILE, TILE), 0)
                columns = lax.broadcasted_iota(jnp.int32, (TILE, TILE), 1)
                same = same & (rows <= columns)
            masks[at : at + TILE, :] = jnp.where(same, 0.0, NEG)
            at += TILE


def mask_rows(length, doc_max):
    return sum(
        (block + 1) * TILE - window_start(block, doc_max) for block in range(length // TILE)
    )


def split_heads(value, target, first, me, member):
    rows = value.shape[0] // 2
    for half in range(2):
        place = pl.ds(token_place(me, member, half, rows), rows)
        for j in range(value.shape[1] // HD):
            target[first + j, place, :] = value[half * rows : (half + 1) * rows, j * HD : (j + 1) * HD]


def merge_heads(source, me, member, rows):
    return jnp.concatenate(
        [
            jnp.concatenate(
                [
                    source[j, pl.ds(token_place(me, member, half, rows), rows), :]
                    for j in range(source.shape[0])
                ],
                axis=1,
            )
            for half in range(2)
        ],
        axis=0,
    )


def by_member(count, step):
    for i in range(count):
        step(i)


def attention_forward_kernel(
    heads,
    doc_max,
    count,
    scaled,
    me_ref,
    near_ref,
    far_ref,
    bias_ref,
    docs,
    *refs,
):
    mixed, attend_ref, masks = refs[-3:]
    refs = refs[:-3]
    sources = (near_ref, far_ref)
    if scaled:
        gains, refs, normed = refs[0], refs[1:-2], refs[-2:]
        for source, target in zip(sources, normed):
            target[...] = (source[...].astype(F32) * gains[0:1, :] + gains[1:2, :]).astype(BF16)
        sources = normed
    pieces, (sent_ref, kept_ref, split_ref, mixed_ref, log_ref) = refs[:count], refs[count:]
    join(pieces, attend_ref)
    fill_masks_across(docs, masks, doc_max)
    me = me_ref[0]
    width = heads * HD
    size = near_ref.shape[0] // 2
    length = 4 * size
    for source, first in zip(sources, (0, 2)):

        def project(i, source=source, first=first):
            at = pl.ds(pl.multiple_of(i * size, size), size)
            value = jnp.dot(source[at, :], attend_ref[:, : 3 * width], preferred_element_type=F32)
            value = (value + bias_ref[...]).astype(BF16)
            split_heads(value[:, :width] * BF16(0.125), split_ref, 0, me, first + i)
            split_heads(value[:, width:], split_ref, heads, me, first + i)

        by_member(2, project)

    def attend(h):
        for block in range(length // TILE):
            start, stop = window_start(block, doc_max), (block + 1) * TILE
            here = slice(block * TILE, stop)
            key, value = split_ref[heads + h, start:stop, :], split_ref[2 * heads + h, start:stop, :]
            scores = dot_across(split_ref[h, here, :], key) + masks[here, : stop - start]
            top = jnp.max(scores, axis=1, keepdims=True)
            raised = jnp.exp(scores - top)
            total = jnp.sum(raised, axis=1, keepdims=True)
            product = jnp.dot(raised.astype(BF16), value, preferred_element_type=F32)
            mixed[h, here, :] = (product * (1.0 / total)).astype(BF16)
            log_ref[h, :, here] = flat(top + jnp.log(total))

    lax.fori_loop(0, heads, lambda h, carry: (attend(h), carry)[1], 0)
    for out, first in ((sent_ref, 2), (kept_ref, 0)):

        def finish(i, out=out, first=first):
            rows = merge_heads(mixed, me, first + i, size // 2)
            mixed_ref[pl.ds(pl.multiple_of((first + i) * size, size), size), :] = rows
            at = pl.ds(pl.multiple_of(i * size, size), size)
            out[at, :] = dot_across(rows, attend_ref[:, 3 * width :]).astype(out.dtype)

        by_member(2, finish)


def attention_backward_kernel(
    heads,
    doc_max,
    count,
    me_ref,
    near_ref,
    far_ref,
    docs,
    split_ref,
    log_ref,
    *refs,
):
    pieces, (sent_ref, kept_ref, out_ref, sum_ref) = refs[:count], refs[count:-4]
    grad, total, attend_ref, masks = refs[-4:]
    join(pieces, attend_ref)
    fill_masks(docs, masks, doc_max)
    me = me_ref[0]
    width = heads * HD
    size = near_ref.shape[0] // 2
    length = 4 * size
    for source, first in ((near_ref, 0), (far_ref, 2)):

        def project(i, source=source, first=first):
            at = pl.ds(pl.multiple_of(i * size, size), size)
            value = jnp.dot(source[at, :], attend_ref[:, 3 * width :], preferred_element_type=F32)
            split_heads(value.astype(BF16), grad, 0, me, first + i)

        by_member(2, project)

    def attend(h):
        total[heads + h] = jnp.zeros((length, HD), F32)
        total[2 * heads + h] = jnp.zeros((length, HD), F32)
        at = 0
        for block in range(length // TILE):
            start, stop = window_start(block, doc_max), (block + 1) * TILE
            here, window = slice(block * TILE, stop), slice(start, stop)
            query, key, value = (
                split_ref[h, here, :],
                split_ref[heads + h, window, :],
                split_ref[2 * heads + h, window, :],
            )
            grad_rows = grad[h, here, :]
            scores = dot_across(key, query) + masks[at : at + stop - start, :]
            at += stop - start
            weights = jnp.exp(scores - log_ref[h, :, here])
            weighted = weights * dot_across(value, grad_rows)
            centered = jnp.sum(weighted, axis=0, keepdims=True)
            grad_scores = (weighted - weights * centered).astype(BF16)
            total[2 * heads + h, window, :] += jnp.dot(
                weights.astype(BF16), grad_rows, preferred_element_type=F32
            )
            total[heads + h, window, :] += jnp.dot(
                grad_scores, query, preferred_element_type=F32
            )
            total[h, here, :] = dot_down(key, grad_scores).T * 0.125

    lax.fori_loop(0, heads, lambda h, carry: (attend(h), carry)[1], 0)
    sum_ref[...] = jnp.zeros_like(sum_ref)
    for out, first in ((sent_ref, 2), (kept_ref, 0)):

        def finish(i, out=out, first=first):
            rows = merge_heads(total, me, first + i, size // 2).astype(BF16)
            out_ref[pl.ds(pl.multiple_of((first + i) * size, size), size), :] = rows
            sum_ref[...] += jnp.sum(rows.astype(F32), axis=0, keepdims=True)
            at = pl.ds(pl.multiple_of(i * size, size), size)
            out[at, :] = dot_across(rows, attend_ref[:, : 3 * width]).astype(out.dtype)

        by_member(2, finish)


VMEM = pl.BlockSpec(memory_space=pltpu.VMEM)
SMEM = pl.BlockSpec(memory_space=pltpu.SMEM)


def call(body, name, inputs, outputs, scratch, flops, transcendentals, limit=24):
    size = sum(v.size * v.dtype.itemsize for v in list(inputs) + list(outputs))
    return pl.pallas_call(
        body,
        out_shape=tuple(outputs),
        in_specs=[SMEM if v.ndim == 1 else VMEM for v in inputs],
        out_specs=tuple(VMEM for _ in outputs),
        scratch_shapes=scratch,
        cost_estimate=pl.CostEstimate(
            flops=flops, transcendentals=transcendentals, bytes_accessed=size
        ),
        compiler_params=pltpu.CompilerParams(vmem_limit_bytes=limit << 20),
        name=name,
    )(*inputs)


def shaped(rows, columns, kind):
    return jax.ShapeDtypeStruct((rows, columns), kind)


def attention_forward(near, far, attend, bias, context, doc_max, gains=()):
    me, docs = context
    half, features = near.shape
    width = bias.shape[1] // 3
    heads = width // HD
    area = heads * 2 * half * half

    def body(*refs):
        attention_forward_kernel(heads, doc_max, len(attend), len(gains) > 0, *refs)

    return call(
        body,
        "attention_forward",
        (me, near, far, bias, docs) + tuple(gains) + tuple(attend),
        (
            shaped(half, features, BF16),
            shaped(half, features, F32),
            jax.ShapeDtypeStruct((3 * heads, 2 * half, HD), BF16),
            shaped(2 * half, width, BF16),
            jax.ShapeDtypeStruct((heads, 1, 2 * half), F32),
        )
        + (shaped(half, features, BF16),) * (2 * len(gains)),
        [
            pltpu.VMEM((heads, 2 * half, HD), BF16),
            pltpu.VMEM((features, 4 * width), BF16),
            pltpu.VMEM((2 * half, mask_columns(2 * half, doc_max)), F32),
        ],
        16 * HD * area,
        area,
    )


def attention_backward(near, far, attend, context, saved, doc_max):
    me, docs = context
    split, _, log_total = saved
    half, features = near.shape
    heads = split.shape[0] // 3
    width = heads * HD
    area = heads * 2 * half * half

    def body(*refs):
        attention_backward_kernel(heads, doc_max, len(attend), *refs)

    return call(
        body,
        "attention_backward",
        (me, near, far, docs, split, log_total) + tuple(attend),
        (
            shaped(half, features, BF16),
            shaped(half, features, F32),
            shaped(2 * half, 3 * width, BF16),
            shaped(1, 3 * width, F32),
        ),
        [
            pltpu.VMEM((heads, 2 * half, HD), BF16),
            pltpu.VMEM((3 * heads, 2 * half, HD), F32),
            pltpu.VMEM((features, 4 * width), BF16),
            pltpu.VMEM((mask_rows(2 * half, doc_max), TILE), F32),
        ],
        40 * HD * area,
        area,
    )


CHUNK = 256


def gelu_both(values):
    inner = GELU_SCALE * (values + 0.044715 * values * values * values)
    bent = jnp.tanh(inner)
    value = 0.5 * values * (1.0 + bent)
    slope = 0.5 * (1.0 + bent) + 0.5 * values * (1.0 - bent * bent) * GELU_SCALE * (
        1.0 + 3.0 * 0.044715 * values * values
    )
    return value, slope


def split_parts(weight):
    size = min(weight.shape[1], 768)
    return [slice(at, at + size) for at in range(0, weight.shape[1], size)]


def feed_forward_kernel(
    count, near_ref, far_ref, bias_ref, *refs
):
    sent_ref, kept_ref, expand_ref, reduce_ref = refs[-4:]
    join(refs[:count], expand_ref)
    join(refs[count:-4], reduce_ref)
    parts = split_parts(expand_ref)
    for piece, out in ((far_ref, sent_ref), (near_ref, kept_ref)):

        def step(i, carry):
            at = pl.ds(pl.multiple_of(i * CHUNK, CHUNK), CHUNK)
            rows = piece[at, :]
            total = None
            for columns in parts:
                hidden = jnp.dot(rows, expand_ref[:, columns], preferred_element_type=F32)
                active = gelu_tanh(hidden + bias_ref[:, columns]).astype(BF16)
                product = dot_across(active, reduce_ref[:, columns])
                total = product if total is None else total + product
            out[at, :] = total.astype(out.dtype)
            return carry

        lax.fori_loop(0, piece.shape[0] // CHUNK, step, 0)


def feed_forward(near, far, expand, reduce, bias):
    half, features = near.shape
    hidden = bias.shape[1]

    def body(*refs):
        feed_forward_kernel(len(expand), *refs)

    return call(
        body,
        "feed_forward",
        (near, far, bias) + tuple(expand) + tuple(reduce),
        (shaped(half, features, BF16), shaped(half, features, F32)),
        [pltpu.VMEM((features, hidden), BF16), pltpu.VMEM((features, hidden), BF16)],
        8 * half * features * hidden,
        2 * half * hidden,
    )


def feed_backward_kernel(
    count,
    near_ref,
    far_ref,
    near_grad,
    far_grad,
    bias_ref,
    *refs,
):
    sent_ref, kept_ref, active_ref, hidden_ref, sum_ref, expand_ref, reduce_ref = refs[-7:]
    join(refs[:count], expand_ref)
    join(refs[count:-7], reduce_ref)
    parts = split_parts(expand_ref)
    half = near_ref.shape[0]
    sum_ref[...] = jnp.zeros_like(sum_ref)
    for piece, grads, out, base in (
        (far_ref, far_grad, sent_ref, half),
        (near_ref, near_grad, kept_ref, 0),
    ):

        def step(i, carry):
            place = pl.multiple_of(i * CHUNK, CHUNK)
            at = pl.ds(place, CHUNK)
            whole = pl.ds(pl.multiple_of(base + place, CHUNK), CHUNK)
            rows = piece[at, :]
            grad_rows = grads[at, :]
            total = None
            for columns in parts:
                hidden = jnp.dot(rows, expand_ref[:, columns], preferred_element_type=F32)
                value, slope = gelu_both(hidden + bias_ref[:, columns])
                active_ref[whole, columns] = value.astype(BF16)
                grad_active = jnp.dot(
                    grad_rows, reduce_ref[:, columns], preferred_element_type=F32
                )
                grad_hidden = (grad_active * slope).astype(BF16)
                hidden_ref[whole, columns] = grad_hidden
                sum_ref[:, columns] += jnp.sum(grad_hidden.astype(F32), axis=0, keepdims=True)
                product = dot_across(grad_hidden, expand_ref[:, columns])
                total = product if total is None else total + product
            out[at, :] = total.astype(out.dtype)
            return carry

        lax.fori_loop(0, half // CHUNK, step, 0)


def feed_backward(near, far, near_grad, far_grad, expand, reduce, bias):
    half, features = near.shape
    hidden = bias.shape[1]

    def body(*refs):
        feed_backward_kernel(len(expand), *refs)

    return call(
        body,
        "feed_backward",
        (near, far, near_grad, far_grad, bias) + tuple(expand) + tuple(reduce),
        (
            shaped(half, features, BF16),
            shaped(half, features, F32),
            shaped(2 * half, hidden, BF16),
            shaped(2 * half, hidden, BF16),
            shaped(1, hidden, F32),
        ),
        [pltpu.VMEM((features, hidden), BF16), pltpu.VMEM((features, hidden), BF16)],
        12 * half * features * hidden,
        2 * half * hidden,
    )


def row_block(rows, columns):
    return pl.BlockSpec((rows, columns), lambda i: (0, 0))


def row_call(body, name, inputs, rows, outputs):
    specs = [row_block(v.shape[0] if v.shape[0] <= 16 else rows, v.shape[1]) for v in inputs]
    size = sum(rows * v.shape[1] * v.dtype.itemsize for v in inputs)
    return pl.pallas_call(
        body,
        grid=(1,),
        out_shape=tuple(outputs),
        in_specs=specs,
        out_specs=tuple(row_block(*v.shape) for v in outputs),
        cost_estimate=pl.CostEstimate(
            flops=20 * rows * inputs[0].shape[1], transcendentals=rows, bytes_accessed=2 * size
        ),
        compiler_params=pltpu.CompilerParams(vmem_limit_bytes=18 << 20),
        name=name,
    )(*inputs)


STEP = 128


def add_norm(base, partial, across, vectors, bias_at, norm_vectors, norm_at):
    rows, columns = base.shape

    def body(base_ref, bias_ref, vector_ref, partial_ref, across_ref, sum_ref, norm_ref):
        bias = bias_ref[bias_at : bias_at + 1, :]
        gain, shift = vector_ref[norm_at : norm_at + 1, :], vector_ref[norm_at + 1 : norm_at + 2, :]

        def step(i, carry):
            here = pl.ds(pl.multiple_of(i * STEP, STEP), STEP)
            there = pl.ds(pl.multiple_of((i * STEP + rows // 2) % rows, STEP), STEP)
            total = partial_ref[here, :].astype(F32) + across_ref[there, :].astype(F32)
            total = base_ref[here, :].astype(F32) + bias + total
            sum_ref[here, :] = total
            norm_ref[here, :] = (normalize(total)[0] * gain + shift).astype(BF16)
            return carry

        lax.fori_loop(0, rows // STEP, step, 0)

    return row_call(
        body,
        "add_norm",
        [base, vectors, norm_vectors, partial, across],
        rows,
        (shaped(rows, columns, F32), shaped(rows, columns, BF16)),
    )


def norm_back_near(skip, partial, across, value, vectors, norm_at, sums, sums_at):
    rows, columns = skip.shape

    def body(skip_ref, value_ref, vector_ref, old_ref, partial_ref, across_ref, *outs):
        grad_ref, low_ref, sum_ref = outs
        gain = vector_ref[norm_at : norm_at + 1, :]
        sum_ref[...] = old_ref[...]

        def step(i, own):
            here = pl.ds(pl.multiple_of(i * STEP, STEP), STEP)
            there = pl.ds(pl.multiple_of((i * STEP + rows // 2) % rows, STEP), STEP)
            grad = partial_ref[here, :].astype(F32) + across_ref[there, :].astype(F32)
            unit, scale = normalize(value_ref[here, :].astype(F32))
            skipped = skip_ref[here, :].astype(F32)
            if own:
                for j, each in enumerate((grad * unit, grad, skipped)):
                    sum_ref[sums_at + j : sums_at + j + 1, :] += jnp.sum(each, axis=0, keepdims=True)
            total = skipped + norm_pullback(grad, unit, scale, gain)
            grad_ref[here, :] = total
            low_ref[here, :] = total.astype(BF16)

        count = rows // STEP // 2
        lax.fori_loop(0, count, lambda i, carry: (step(i, True), carry)[1], 0)
        lax.fori_loop(count, 2 * count, lambda i, carry: (step(i, False), carry)[1], 0)

    return row_call(
        body,
        "norm_back_near",
        [skip, value, vectors, sums, partial, across],
        rows,
        (shaped(rows, columns, F32), shaped(rows, columns, BF16), shaped(16, columns, F32)),
    )


def norm_only(values):
    rows, columns = values.shape

    def body(value_ref, unit_ref):
        unit_ref[...] = normalize(value_ref[...].astype(F32))[0].astype(BF16)

    return row_call(body, "norm_only", [values], rows, (shaped(rows, columns, BF16),))[0]


def norm_back(skip, addends, value, vectors, norm_at, sums, sums_at):
    rows, columns = addends[-1].shape

    def body(*refs):
        skip_ref, value_ref, vector_ref, old_ref = refs[:4]
        parts, (grad_ref, low_ref, sum_ref) = refs[4:-3], refs[-3:]
        grad = parts[0][...].astype(F32)
        for part in parts[1:]:
            grad = grad + part[...].astype(F32)
        unit, scale = normalize(value_ref[...].astype(F32))
        skipped = skip_ref[...]
        sum_ref[...] = old_ref[...]
        for i, each in enumerate((grad * unit, grad, skipped)):
            sum_ref[sums_at + i : sums_at + i + 1, :] = jnp.sum(each, axis=0, keepdims=True)
        total = skipped + norm_pullback(grad, unit, scale, vector_ref[norm_at : norm_at + 1, :])
        grad_ref[...] = total
        low_ref[...] = total.astype(BF16)

    return row_call(
        body,
        "norm_back",
        [skip, value, vectors, sums] + list(addends),
        rows,
        (shaped(rows, columns, F32), shaped(rows, columns, BF16), shaped(16, columns, F32)),
    )


def normalize(values):
    center = values - jnp.mean(values, axis=-1, keepdims=True)
    spread = jnp.mean(center * center, axis=-1, keepdims=True)
    scale = lax.rsqrt(spread + EPSILON)
    return center * scale, scale


def norm_rows(values, gain, shift):
    return (normalize(values)[0] * gain + shift).astype(BF16)


def norm_pullback(grad, unit, scale, gain):
    inner = grad * gain
    return scale * (
        inner
        - jnp.mean(inner, axis=-1, keepdims=True)
        - unit * jnp.mean(inner * unit, axis=-1, keepdims=True)
    )


def times(left, right, kind=F32):
    return jnp.dot(left, right, preferred_element_type=F32).astype(kind)


def times_across(left, right, kind=F32):
    return dot_across(left, right).astype(kind)


def times_down(left, right, kind=F32):
    return row_major(dot_down(left, right).astype(kind))


def gather_rows(rows):
    near = stacked(rows, cross_x(rows))
    return near, cross_core(near)


def add_half(value, cross):
    middle = value.shape[0] // 2
    return value[:middle].astype(F32) + cross(value[middle:].astype(BF16)).astype(F32)


def add_columns(value, cross):
    middle = value.shape[1] // 2
    return value[:, :middle].astype(F32) + cross(value[:, middle:].astype(BF16)).astype(F32)


def column_halves(shard, y_index):
    middle = shard.shape[1] // 2
    own = jnp.where(y_index == 0, shard[:, :middle], shard[:, middle:])
    other = jnp.where(y_index == 0, shard[:, middle:], shard[:, :middle])
    return own, other


def natural_columns(own, other, y_index):
    return jnp.where(y_index == 0, beside(own, other), beside(other, own))


def order_matrix(width, z_index):
    rows = width // 4
    natural = lax.broadcasted_iota(jnp.int32, (width, width), 0)
    place = lax.broadcasted_iota(jnp.int32, (width, width), 1)
    step, inner = place // rows, place % rows
    distance = 2 * (step & 1) + (step >> 1)
    return (natural == (z_index ^ distance) * rows + inner).astype(BF16)


def my_rows(pair, y_index):
    own = jnp.where(y_index == 0, pair[0], pair[1])
    sent = jnp.where(y_index == 0, pair[1], pair[0])
    return y_order(own, cross_y(sent), y_index, 0)


ROWS = 64
SPARE = ROWS // 2


def turn(value):
    size = value.shape[0]
    eye = (
        lax.broadcasted_iota(jnp.int32, (size, size), 0)
        == lax.broadcasted_iota(jnp.int32, (size, size), 1)
    ).astype(BF16)
    return dot_down(value, eye)


def pack_vectors(blocks, place):
    flat = []
    for gains, merged_bias, expand_bias in blocks:
        flat += list(gains) + [merged_bias.transpose(1, 0, 2), expand_bias]

    number = len(flat)

    def body(*refs):
        refs = refs[1:]
        out, part, sem = refs[number], refs[number + 1 : -1], refs[-1]
        copies = [
            pltpu.make_async_copy(refs[i], part[i], sem.at[i]) for i in range(number)
        ]
        for copy in copies:
            copy.start()
        out[...] = jnp.zeros_like(out)
        for copy in copies:
            copy.wait()
        for b in range(2):
            vectors, merged_bias, expand_bias = part[8 * b : 8 * b + 6], part[8 * b + 6], part[8 * b + 7]
            for i in range(6):
                local = vectors[i].shape[0]
                out[6 * b + i : 6 * b + i + 1, :local] = vectors[i][...].astype(F32).reshape(1, local)
            for h in range(merged_bias.shape[0]):
                value = merged_bias[h].astype(F32)
                out[16 + 8 * b + 2 * h : 18 + 8 * b + 2 * h, : value.shape[1]] = value
            value = expand_bias[...].astype(F32)
            out[32 + 16 * b : 32 + 16 * b + value.shape[0], : value.shape[1]] = value

    return pl.pallas_call(
        body,
        out_shape=shaped(ROWS, 256, F32),
        in_specs=[SMEM] + [pl.BlockSpec(memory_space=pltpu.HBM)] * number,
        out_specs=VMEM,
        scratch_shapes=[pltpu.VMEM(v.shape, v.dtype) for v in flat]
        + [pltpu.SemaphoreType.DMA((number,))],
        compiler_params=pltpu.CompilerParams(vmem_limit_bytes=60 << 20),
        name="pack_vectors",
    )(place, *flat)


def prepare_first(place, merged, output, blocks):
    flat = []
    for gains, merged_bias, expand_bias in blocks:
        flat += list(gains) + [merged_bias.transpose(1, 0, 2), expand_bias]
    flat += [merged.transpose(1, 0, 2), output]
    number = len(flat)
    local = output.shape[1]

    def body(*refs):
        out, part, small, sem = refs[number], refs[number + 1 : -2], refs[-2], refs[-1]
        copies = [pltpu.make_async_copy(refs[i], part[i], sem.at[i]) for i in range(number)]
        for copy in copies:
            copy.start()
        small[...] = jnp.zeros_like(small)
        for copy in copies:
            copy.wait()
        for b in range(2):
            vectors, merged_bias, expand_bias = part[8 * b : 8 * b + 6], part[8 * b + 6], part[8 * b + 7]
            for i in range(6):
                small[6 * b + i : 6 * b + i + 1, :local] = (
                    vectors[i][...].astype(F32).reshape(1, local)
                )
            for h in range(merged_bias.shape[0]):
                value = merged_bias[h].astype(F32)
                small[16 + 8 * b + 2 * h : 18 + 8 * b + 2 * h, : value.shape[1]] = value
            value = expand_bias[...].astype(F32)
            small[32 + 16 * b : 32 + 16 * b + value.shape[0], : value.shape[1]] = value
        merged_ref, output_ref = part[-2:]
        pieces = [merged_ref[k] for k in range(3)] + [turn(output_ref[...]).astype(BF16)]
        out[:local, :] = jnp.concatenate(pieces, axis=1)
        out[local:, :256] = small[:SPARE, :].astype(BF16)
        out[local:, 256:512] = small[SPARE:, :].astype(BF16)
        out[local:, 512:] = jnp.zeros((SPARE, 4 * local - 512), BF16)

    return pl.pallas_call(
        body,
        out_shape=shaped(local + SPARE, 4 * local, BF16),
        in_specs=[pl.BlockSpec(memory_space=pltpu.HBM)] * number,
        out_specs=VMEM,
        scratch_shapes=[pltpu.VMEM(v.shape, v.dtype) for v in flat]
        + [pltpu.VMEM((ROWS, 256), F32), pltpu.SemaphoreType.DMA((number,))],
        compiler_params=pltpu.CompilerParams(vmem_limit_bytes=60 << 20),
        name="prepare_first",
    )(*flat)


def unpack_vectors(pieces, place, local, merged_shape, expand_shape):
    heads, few = merged_shape[1], merged_shape[2]
    groups = expand_shape[0]
    width = heads * 4 * few

    def body(place_ref, *refs):
        pieces, outs, pieces_ref = refs[:4], refs[4:-1], refs[-1]
        for k in range(4):
            for i in range(2):
                pieces_ref[k * ROWS + i * SPARE : k * ROWS + (i + 1) * SPARE, :] = pieces[k][
                    local:, 256 * i : 256 * (i + 1)
                ].astype(F32)
        y, z = place_ref[0], place_ref[1]
        for b in range(2):
            gains, bias, hidden = outs[3 * b : 3 * b + 3]
            for k in range(4):
                gains[0:6, k * local : (k + 1) * local] = pieces_ref[
                    k * ROWS + 6 * b : k * ROWS + 6 * b + 6, :local
                ]
            bias[...] = jnp.zeros_like(bias)
            for natural in range(4):
                distance = z ^ natural
                base = (2 * (distance & 1) + (distance >> 1)) * ROWS
                part = pieces_ref[pl.ds(pl.multiple_of(base, ROWS), ROWS), :128]
                for i in range(2):
                    for h in range(heads):
                        line = 16 + 8 * b + 2 * h + i
                        at = 2 * i * width + h * 4 * few + natural * few
                        bias[:, at : at + few] = part[line : line + 1, :few]
                lines = part[32 + 16 * b : 32 + 16 * b + groups]
                half = groups // 2
                lines = jnp.where(
                    y == 0, lines, jnp.concatenate([lines[half:], lines[:half]], axis=0)
                )
                for p in range(groups):
                    at = p * 4 * few + natural * few
                    hidden[:, at : at + few] = lines[p : p + 1, :few]

    one = (
        shaped(8, 4 * local, F32),
        shaped(1, 3 * width, F32),
        shaped(1, groups * 4 * few, F32),
    )
    return pl.pallas_call(
        body,
        out_shape=one + one,
        in_specs=[SMEM] + [VMEM] * 4,
        out_specs=(VMEM,) * 6,
        scratch_shapes=[pltpu.VMEM((4 * ROWS, 256), F32)],
        compiler_params=pltpu.CompilerParams(vmem_limit_bytes=8 << 20),
        name="unpack_vectors",
    )(place, *pieces)


def prepare_attend(merged, output):
    local = output.shape[1]

    def body(merged_ref, output_ref, attend):
        pieces = [merged_ref[k] for k in range(3)] + [turn(output_ref[...]).astype(BF16)]
        attend[...] = jnp.concatenate(pieces, axis=1)

    return pl.pallas_call(
        body,
        out_shape=shaped(local, 4 * local, BF16),
        in_specs=[VMEM, VMEM],
        out_specs=VMEM,
        compiler_params=pltpu.CompilerParams(vmem_limit_bytes=12 << 20),
        name="prepare_attend",
    )(merged.transpose(1, 0, 2), output)


def prepare_feed(place, expand, reduce):
    local, half = expand.shape[0], expand.shape[1] // 2

    def body(place_ref, expand_ref, reduce_ref, feed):
        y = place_ref[0]
        first, second = reduce_ref[:, :half], reduce_ref[:, half:]
        feed[:, :half] = jnp.where(y == 0, expand_ref[:, :half], expand_ref[:, half:])
        feed[:, half : 2 * half] = jnp.where(y == 0, first, second)
        feed[:, 2 * half :] = jnp.where(y == 0, second, first)

    return pl.pallas_call(
        body,
        out_shape=shaped(local, 3 * half, BF16),
        in_specs=[SMEM, VMEM, VMEM],
        out_specs=VMEM,
        compiler_params=pltpu.CompilerParams(vmem_limit_bytes=12 << 20),
        name="prepare_feed",
    )(place, expand, reduce.T)


def pack_grads(sums, biases, hiddens, place, local, merged_shape, expand_shape):
    heads, few = merged_shape[1], merged_shape[2]
    groups = expand_shape[0]
    width = heads * 4 * few

    def body(place_ref, sum_ref, bias_s, bias_t, hidden_s, hidden_t, out):
        y, z = place_ref[0], place_ref[1]
        out[...] = jnp.zeros_like(out)
        for k in range(4):
            out[k * ROWS : k * ROWS + 12, :local] = sum_ref[0:12, k * local : (k + 1) * local]
        for natural in range(4):
            distance = z ^ natural
            base = pl.multiple_of((2 * (distance & 1) + (distance >> 1)) * ROWS, ROWS)
            lines = []
            for bias in (bias_s, bias_t):
                for h in range(heads):
                    for i in range(2):
                        at = 2 * i * width + h * 4 * few + natural * few
                        lines.append(bias[:, at : at + few])
                lines.append(jnp.zeros((2, few), F32))
            for hidden in (hidden_s, hidden_t):
                rows = [
                    hidden[:, p * 4 * few + natural * few : p * 4 * few + natural * few + few]
                    for p in range(groups)
                ]
                first, second = rows[: groups // 2], rows[groups // 2 :]
                first, second = jnp.concatenate(first, axis=0), jnp.concatenate(second, axis=0)
                lines.append(jnp.where(y == 0, first, second))
                lines.append(jnp.where(y == 0, second, first))
                lines.append(jnp.zeros((16 - groups, few), F32))
            out[pl.ds(pl.multiple_of(base + 16, 16), ROWS - 16), :few] = jnp.concatenate(lines, axis=0)

    return pl.pallas_call(
        body,
        out_shape=shaped(4 * ROWS, 256, F32),
        in_specs=[SMEM] + [VMEM] * 5,
        out_specs=VMEM,
        compiler_params=pltpu.CompilerParams(vmem_limit_bytes=4 << 20),
        name="pack_grads",
    )(place, sums, *biases, *hiddens)


def unpack_grads(mine, arrived, local, merged_shape, expand_shape):
    heads, few = merged_shape[1], merged_shape[2]
    groups = expand_shape[0]

    def body(mine_ref, arrived_ref, *outs):
        total = mine_ref[0:ROWS, :] + arrived_ref[...]
        for b in range(2):
            vectors, merged_bias, expand_bias = outs[8 * b : 8 * b + 6], outs[8 * b + 6], outs[8 * b + 7]
            for i in range(6):
                vectors[i][...] = total[6 * b + i : 6 * b + i + 1, :local].reshape(local)
            for h in range(heads):
                merged_bias[h] = total[16 + 8 * b + 2 * h : 18 + 8 * b + 2 * h, :few]
            expand_bias[...] = total[32 + 16 * b : 32 + 16 * b + groups, :few]

    one = [jax.ShapeDtypeStruct((local,), F32)] * 6 + [
        jax.ShapeDtypeStruct((heads, 2, few), F32),
        jax.ShapeDtypeStruct(expand_shape, F32),
    ]
    values = pl.pallas_call(
        body,
        out_shape=tuple(one + one),
        in_specs=[VMEM] * 2,
        out_specs=(VMEM,) * 16,
        compiler_params=pltpu.CompilerParams(vmem_limit_bytes=4 << 20),
        name="unpack_grads",
    )(mine, arrived)
    return [v.transpose(1, 0, 2) if v.ndim == 3 else v for v in values]


def finish_feed(mine, theirs, place, half):
    local = mine.shape[0]
    whole = mine.shape[1] == 3 * half

    def body(place_ref, mine_ref, theirs_ref, expand, reduce):
        y = place_ref[0]
        own, other = mine_ref[:, :half].astype(F32), theirs_ref[:, :half].astype(F32)
        expand[:, :half] = jnp.where(y == 0, own, other)
        expand[:, half:] = jnp.where(y == 0, other, own)
        if whole:
            total = mine_ref[:, half:].astype(F32) + theirs_ref[:, half:].astype(F32)
            own, other = total[:, :half], total[:, half:]
        else:
            own, other = mine_ref[:, half:].astype(F32), theirs_ref[:, half:].astype(F32)
        reduce[:, :half] = jnp.where(y == 0, own, other)
        reduce[:, half:] = jnp.where(y == 0, other, own)

    expand, reduce = pl.pallas_call(
        body,
        out_shape=(shaped(local, 2 * half, F32), shaped(local, 2 * half, F32)),
        in_specs=[SMEM, VMEM, VMEM],
        out_specs=(VMEM, VMEM),
        compiler_params=pltpu.CompilerParams(vmem_limit_bytes=12 << 20),
        name="finish_feed",
    )(place, mine, theirs)
    return expand, reduce.T


def finish_attend(added, mine, theirs, place):
    local = mine.shape[0]

    def body(place_ref, *refs):
        mine_ref, theirs_ref, merged, output = refs[-4:]
        y = place_ref[0]
        own, other = mine_ref[...], theirs_ref[...]
        split = jnp.concatenate(
            [jnp.where(y == 0, own, other), jnp.where(y == 0, other, own)], axis=1
        )
        output[...] = turn(split[:, -local:])
        whole = split.astype(F32)
        if added:
            total = refs[0][...].astype(F32) + refs[1][...].astype(F32)
            whole = jnp.concatenate([total, whole], axis=1)
        for k in range(3):
            merged[k] = whole[:, k * local : (k + 1) * local]

    merged, output = pl.pallas_call(
        body,
        out_shape=(jax.ShapeDtypeStruct((3, local, local), F32), shaped(local, local, F32)),
        in_specs=[SMEM] + [VMEM] * (2 + len(added)),
        out_specs=(VMEM, VMEM),
        compiler_params=pltpu.CompilerParams(vmem_limit_bytes=12 << 20),
        name="finish_attend",
    )(place, *added, mine, theirs)
    return merged.transpose(1, 0, 2), output


def halves_added(kept, arrived):
    middle = kept.shape[0] // 2
    return (kept[middle:] + arrived[middle:].astype(F32)).astype(BF16)


def core_sum(kept, arrived):
    return (kept + arrived.astype(F32)).astype(BF16)


def send_columns(value, cross):
    middle = value.shape[1] // 2
    return cross(value[:, middle:].astype(BF16))


def keep_columns(value, arrived):
    return value[:, : value.shape[1] // 2].astype(F32) + arrived.astype(F32)


def send_rows(value, cross):
    middle = value.shape[0] // 2
    return cross(value[middle:].astype(BF16))


def keep_rows(value, arrived):
    return value[: value.shape[0] // 2].astype(F32) + arrived.astype(F32)


def fast_shards(inputs, segments, cotangent, *params):
    y_index = lax.axis_index("ctx")
    z_index = lax.axis_index("dp")
    me = lax.axis_index("tp")
    tokens, features = inputs.shape[1], inputs.shape[2]
    length = segments.shape[1] * 2
    doc_max = min(DOC_MAX, length // 2)
    blocks = (params[:12], params[12:])
    local = features // 4
    half = local * 2

    small = [((p[0], p[1], p[5], p[6], p[7], p[11]), p[3], p[9]) for p in blocks]
    place = jnp.stack([y_index, z_index]).astype(jnp.int32)
    p = blocks[0]
    attend = prepare_first(place, p[2], p[4], small)
    inputs, attend = pin(inputs, attend)
    far, near = cross_far(attend), cross_near(attend)
    sent_rows = jnp.where(y_index == 0, inputs[1], inputs[0])
    sent_docs = jnp.where(y_index == 0, segments[1:2], segments[0:1]).astype(BF16)
    sent_docs = jnp.pad(sent_docs, ((0, 15), (0, features - sent_docs.shape[1])))
    moved = cross_y(stacked(sent_rows, sent_docs))
    kept_rows = jnp.where(y_index == 0, inputs[0], inputs[1])
    kept_docs = jnp.where(y_index == 0, segments[0:1], segments[1:2]).astype(F32)
    chooser = order_matrix(features, z_index)
    raw = times(y_order(kept_rows, moved[:tokens], y_index, 0), chooser, BF16)
    docs = y_order(
        kept_docs, moved[tokens : tokens + 1, : kept_docs.shape[1]].astype(F32), y_index, 1
    )
    context = (me.astype(jnp.int32).reshape(1), docs)
    both = cross_near(far)
    feed = prepare_feed(place, blocks[0][8], blocks[0][10])
    feed, far = pin(feed, far)
    p_far = cross_far(feed[:, : 2 * half])
    moved_grad = cross_y(jnp.where(y_index == 0, cotangent[1], cotangent[0]))
    raw, place_t, output_t = pin(raw, place, blocks[1][4])
    own_a = prepare_attend(blocks[1][2], output_t)
    feed_t = prepare_feed(place_t, blocks[1][8], blocks[1][10])

    stream = stacked(raw, cross_x(raw))
    stream, near, both, p_far, own_a, feed_t, moved_grad = pin(
        stream, near, both, p_far, own_a, feed_t, moved_grad
    )
    near_s = norm_only(stream)
    gains_s, bias_s, hidden_s, gains_t, bias_t, hidden_t = unpack_vectors(
        (attend, far, near, both), place, local, blocks[0][3].shape, blocks[0][9].shape
    )
    far_s = cross_core(near_s)
    attend_s = (attend, far, near, both)
    e_two = stacked(feed[:, :half], p_far[:, :half])
    e_near = cross_near(e_two)
    r_far = cross_far(feed[:, 2 * half :])
    grad_out = times(
        y_order(jnp.where(y_index == 0, cotangent[0], cotangent[1]), moved_grad, y_index, 0),
        chooser,
        BF16,
    )
    moved_grad = cross_x(grad_out)
    sent, kept, *saved_s, near_s, far_s = attention_forward(
        near_s, far_s, attend_s, bias_s, context, doc_max, (gains_s,)
    )
    sent, e_near, r_far, moved_grad = pin(sent, e_near, r_far, moved_grad)
    e_s = stacked(e_two, e_near)
    e_other = cross_y(e_s)
    r_two = stacked(feed[:, half:], beside(p_far[:, half:], r_far))
    r_near = cross_near(r_two)
    a_far = cross_far(own_a)
    partial = core_sum(kept, cross_core(sent))
    middle_s, near_two_s = add_norm(stream, partial, cross_x(partial), gains_s, 2, gains_s, 3)
    near_two_s, e_other, r_near, a_far, feed_t = pin(near_two_s, e_other, r_near, a_far, feed_t)
    a_two = stacked(own_a, a_far)
    a_near = cross_near(a_two)
    te_far, tr_far = cross_far(feed_t[:, :half]), cross_far(feed_t[:, 2 * half :])
    far_two_s = cross_core(near_two_s)
    feed_s = (near_two_s, far_two_s), ((e_s, e_other), (r_two, r_near), hidden_s)
    sent, kept = feed_forward(*feed_s[0], *feed_s[1])
    partial = core_sum(kept, cross_core(sent))
    between, near_t = add_norm(middle_s, partial, cross_x(partial), gains_s, 5, gains_t, 0)

    near_t, a_near, te_far, tr_far, feed_t = pin(near_t, a_near, te_far, tr_far, feed_t)
    attend_t = (a_two, a_near)
    te_two = stacked(feed_t[:, :half], te_far)
    te_near = cross_near(te_two)
    tr_far_one = cross_far(feed_t[:, half : 2 * half])
    far_t = cross_core(near_t)
    sent, kept, *saved_t = attention_forward(near_t, far_t, attend_t, bias_t, context, doc_max)
    sent, te_near, tr_far_one = pin(sent, te_near, tr_far_one)
    te = stacked(te_two, te_near)
    te_other = cross_y(te)
    tr_two = stacked(feed_t[:, half:], beside(tr_far_one, tr_far))
    tr_near = cross_near(tr_two)
    branch = stacked(grad_out, moved_grad)
    branch_far = cross_core(branch)
    partial = core_sum(kept, cross_core(sent))
    middle_t, near_two_t = add_norm(between, partial, cross_x(partial), gains_t, 2, gains_t, 3)
    near_two_t, te_other, tr_near, branch_far = pin(near_two_t, te_other, tr_near, branch_far)
    far_two_t = cross_core(near_two_t)
    feed_t = (near_two_t, far_two_t), ((te, te_other), (tr_two, tr_near), hidden_t)

    sums = jnp.zeros((16, features), F32)
    sent, kept, active, grad_hidden, hidden_sum_t = feed_backward(
        *feed_t[0], branch, branch_far, *feed_t[1]
    )
    partial = core_sum(kept, cross_core(sent))
    final_sent, final_kept = feed_forward(*feed_t[0], *feed_t[1])
    part_r = times_down(stacked(branch, branch_far), active, BF16)
    part_e = times_down(stacked(near_two_t, far_two_t), grad_hidden, BF16)
    grad_middle, near_grad, sums = norm_back_near(
        branch, partial, cross_x(partial), middle_t, gains_t, 3, sums, 9
    )
    near_grad, part_r, part_e, final_sent, final_kept = pin(
        near_grad, part_r, part_e, final_sent, final_kept
    )
    r_moved, e_moved = send_rows(part_r, cross_near), send_columns(part_e, cross_y)
    far_grad = cross_core(near_grad)
    final_arrived = cross_core(final_sent)
    final_across = cross_x(halves_added(final_kept, final_arrived))
    sent, kept, grad_qkv, qkv_sum_t = attention_backward(
        near_grad, far_grad, attend_t, context, saved_t, doc_max
    )
    sent, final_across = pin(sent, final_across)
    partial = core_sum(kept, cross_core(sent))
    part_a = beside(
        times_down(stacked(near_t, far_t), grad_qkv, BF16),
        times_down(stacked(near_grad, far_grad), saved_t[1], BF16),
    )
    part_a = beside(*column_halves(part_a, y_index))
    grad_between, branch, sums = norm_back_near(
        grad_middle, partial, cross_x(partial), between, gains_t, 0, sums, 6
    )

    branch, r_moved, e_moved, part_a = pin(branch, r_moved, e_moved, part_a)
    part_e, part_r = keep_columns(part_e, e_moved), keep_rows(part_r, r_moved)
    e_moved, r_moved = send_rows(part_e, cross_near), send_rows(part_r, cross_far)
    a_moved = send_columns(part_a, cross_y)
    branch_far = cross_core(branch)
    sent, kept, active, grad_hidden, hidden_sum_s = feed_backward(
        *feed_s[0], branch, branch_far, *feed_s[1]
    )
    partial = core_sum(kept, cross_core(sent))
    feed_r = times_down(stacked(branch, branch_far), active, BF16)
    feed_e = times_down(stacked(near_two_s, far_two_s), grad_hidden, BF16)
    grad_middle, near_grad, sums = norm_back_near(
        grad_between, partial, cross_x(partial), middle_s, gains_s, 3, sums, 3
    )
    near_grad, e_moved, r_moved, a_moved, feed_e, feed_r = pin(
        near_grad, e_moved, r_moved, a_moved, feed_e, feed_r
    )
    part_e, part_r = keep_rows(part_e, e_moved), keep_rows(part_r, r_moved)
    part_a = keep_columns(part_a, a_moved)
    e_moved, a_moved = send_rows(part_e, cross_far), send_rows(part_a, cross_near)
    fe_moved = cross_y(feed_e[:half, half:])
    far_grad = cross_core(near_grad)
    sent, kept, grad_qkv, qkv_sum_s = attention_backward(
        near_grad, far_grad, attend_s, context, saved_s, doc_max
    )
    sent, e_moved, a_moved, fe_moved, feed_r = pin(sent, e_moved, a_moved, fe_moved, feed_r)
    part_e, part_a = keep_rows(part_e, e_moved), keep_rows(part_a, a_moved)
    fe_moved_two = cross_y(feed_e[half:, half:])
    fr_moved, at_moved = send_rows(feed_r, cross_near), send_rows(part_a, cross_far)
    arrived = cross_core(sent)
    across = cross_x(halves_added(kept, arrived))
    grad_a = beside(
        times_down(stacked(near_s, far_s), grad_qkv, BF16),
        times_down(stacked(near_grad, far_grad), saved_s[1], BF16),
    )
    whole = features - 256
    grad_z, grad_a = grad_a[:, :whole], grad_a[:, whole:]
    grad_a, y_moved = column_halves(grad_a, y_index)
    y_moved, z_moved = cross_y(y_moved), send_rows(grad_z, cross_near)
    grad_in, _, sums = norm_back(
        grad_middle, (kept, arrived, across), stream, gains_s, 0, sums, 0
    )
    sums_moved = cross_core(sums)
    input_grad = lax.dot_general(
        grad_in,
        chooser.astype(F32),
        (((1,), (1,)), ((), ())),
        precision=lax.Precision.HIGHEST,
        preferred_element_type=F32,
    )

    def swapped(value):
        first, second = value[:tokens], value[tokens:]
        return cross_y(jnp.where(y_index == 0, second, first))

    def restore(value, received):
        kept = jnp.where(y_index == 0, value[:tokens], value[tokens:])
        return jnp.where(y_index == 0, jnp.stack([kept, received]), jnp.stack([received, kept]))

    y_moved, z_moved, sums_moved, input_grad, fe_moved_two, fr_moved, at_moved = pin(
        y_moved, z_moved, sums_moved, input_grad, fe_moved_two, fr_moved, at_moved
    )
    grad_a = grad_a.astype(F32) + y_moved.astype(F32)
    grad_z = keep_rows(grad_z, z_moved)
    y_moved, z_moved = send_rows(grad_a, cross_near), send_rows(grad_z, cross_far)
    sums = sums + sums_moved
    sums_moved = cross_x(sums)
    feed_e, feed_r = keep_columns(feed_e, stacked(fe_moved, fe_moved_two)), keep_rows(feed_r, fr_moved)
    fe_moved, fr_moved = send_rows(feed_e, cross_near), send_rows(feed_r, cross_far)
    mine_t = beside(part_e, part_r, keep_rows(part_a, at_moved)).astype(BF16)
    theirs_t = cross_y(
        beside(
            mine_t[:, :half], mine_t[:, 2 * half : 3 * half], mine_t[:, half : 2 * half], mine_t[:, 3 * half :]
        )
    )
    grad_moved = swapped(input_grad.astype(BF16)).astype(F32)
    y_moved, z_moved, sums_moved, fe_moved, fr_moved = pin(
        y_moved, z_moved, sums_moved, fe_moved, fr_moved
    )
    grad_a = keep_rows(grad_a, y_moved)
    grad_z = keep_rows(grad_z, z_moved).astype(BF16)
    y_moved, z_moved = send_rows(grad_a, cross_far), cross_y(grad_z)
    feed_e, feed_r = keep_rows(feed_e, fe_moved), keep_rows(feed_r, fr_moved)
    fe_moved = send_rows(feed_e, cross_far)
    pack = pack_grads(
        sums + sums_moved,
        (qkv_sum_s, qkv_sum_t),
        (hidden_sum_s, hidden_sum_t),
        place,
        local,
        params[3].shape,
        params[9].shape,
    )
    pack_moved = cross_y(pack)
    y_moved, fe_moved = pin(y_moved, fe_moved)
    mine_a = keep_rows(grad_a, y_moved).astype(BF16)
    theirs_a = cross_y(mine_a)
    mine_s = beside(keep_rows(feed_e, fe_moved), feed_r).astype(BF16)
    theirs_s = cross_y(
        beside(mine_s[:, :half], mine_s[:, 2 * half :], mine_s[:, half : 2 * half])
    )
    z_moved, pack_moved, theirs_t = pin(z_moved, pack_moved, theirs_t)
    pack = pack + pack_moved
    pack_near = cross_near(pack[2 * ROWS :])
    expand_grad_t, reduce_grad_t = finish_feed(
        mine_t[:, : 3 * half], theirs_t[:, : 3 * half], place, half
    )
    pack_near, theirs_a, expand_grad_t, reduce_grad_t = pin(
        pack_near, theirs_a, expand_grad_t, reduce_grad_t
    )
    pack = pack[: 2 * ROWS] + pack_near
    pack_far = cross_far(pack[ROWS:])
    merged_grad_s, output_grad_s = finish_attend(
        (grad_z, z_moved), mine_a, theirs_a, place
    )
    merged_grad_t, output_grad_t = finish_attend(
        (), mine_t[:, 3 * half :], theirs_t[:, 3 * half :], place
    )
    expand_grad_s, reduce_grad_s = finish_feed(mine_s, theirs_s, place, half)
    vectors = unpack_grads(pack, pack_far, local, params[3].shape, params[9].shape)
    middle_t, final_across, grad_between = pin(middle_t, final_across, grad_between)
    rows = 2 * tokens
    final = middle_t[:rows] + gains_t[5:6] + final_kept[:rows] + final_across.astype(F32)
    final = final + final_arrived[:rows].astype(F32)
    final = times_across(final.astype(BF16), chooser, BF16)
    outputs = [restore(final, swapped(final)), restore(input_grad, grad_moved)]
    for vector, merged, output, expand, reduce in (
        (vectors[:8], merged_grad_s, output_grad_s, expand_grad_s, reduce_grad_s),
        (vectors[8:], merged_grad_t, output_grad_t, expand_grad_t, reduce_grad_t),
    ):
        outputs += [
            vector[0],
            vector[1],
            merged,
            vector[6],
            output,
            vector[2],
            vector[3],
            vector[4],
            expand,
            vector[7],
            reduce,
            vector[5],
        ]
    return tuple(outputs)


def solution(mesh):
    quick = (mesh.shape["dp"], mesh.shape["ctx"], mesh.shape["tp"]) == (4, 2, 4)
    placed = (
        P("dp", ("ctx", "tp"), None),
        P("dp", "ctx"),
        P("dp", ("ctx", "tp"), None),
        P("dp"),
        P("dp"),
        P("dp", None, "tp"),
        P(None, "tp", "dp"),
        P("tp", "dp"),
        P("dp"),
        P("dp"),
        P("dp"),
        P("dp", "tp"),
        P("tp", "dp"),
        P("tp", "dp"),
        P("dp"),
        P("dp"),
        P("dp"),
        P("dp", None, "tp"),
        P(None, "tp", "dp"),
        P("tp", "dp"),
        P("dp"),
        P("dp"),
        P("dp"),
        P("dp", "tp"),
        P("tp", "dp"),
        P("tp", "dp"),
        P("dp"),
    )
    return jax.shard_map(
        fast_shards if quick else general_shards,
        mesh=mesh,
        in_specs=placed,
        out_specs=(
            P("dp", ("ctx", "tp"), None),
            P("dp", ("ctx", "tp"), None),
            P("dp"),
            P("dp"),
            P("dp", None, "tp"),
            P(None, "tp", "dp"),
            P("tp", "dp"),
            P("dp"),
            P("dp"),
            P("dp"),
            P("dp", "tp"),
            P("tp", "dp"),
            P("tp", "dp"),
            P("dp"),
            P("dp"),
            P("dp"),
            P("dp", None, "tp"),
            P(None, "tp", "dp"),
            P("tp", "dp"),
            P("dp"),
            P("dp"),
            P("dp"),
            P("dp", "tp"),
            P("tp", "dp"),
            P("tp", "dp"),
            P("dp"),
        ),
        check_vma=False,
    )
```

```python
import jax
import jax.numpy as jnp
from jax import lax
from jax.experimental import pallas as pl
from jax.experimental.layout import Layout, with_layout_constraint
from jax.experimental.pallas import tpu as pltpu
from jax.sharding import PartitionSpec as P

HD = 64
DOC_MAX = 2000


EPSILON = 1e-05
GELU_SCALE = 0.7978845608028654


def from_behind(block, axis, distance):
    devices = range(lax.axis_size(axis))
    route = [(i - distance, i) for i in devices if i - distance in devices]
    return lax.ppermute(block, axis, route)


def layer_norm(values, norm_gain, norm_shift):
    center = values - jnp.mean(values, axis=-1, keepdims=True)
    spread = jnp.mean(center * center, axis=-1, keepdims=True)
    return center * lax.rsqrt(spread + EPSILON) * norm_gain + norm_shift


def gelu_tanh(values):
    return (
        0.5 * values * (1.0 + jnp.tanh(GELU_SCALE * (values + 0.044715 * values * values * values)))
    )


def spread_rows(row_block):
    return lax.all_gather(row_block, "tp", axis=1, tiled=True)


def gather_sums(partial_value):
    return lax.psum_scatter(
        partial_value.astype(jnp.bfloat16), "tp", scatter_dimension=1, tiled=True
    ).astype(jnp.float32)


def to_items(tensor, head_count):
    batches, length, features = tensor.shape
    head_size = features // head_count
    return (
        tensor.reshape(batches, length, head_count, head_size)
        .transpose(0, 2, 1, 3)
        .reshape(batches * head_count, length, head_size)
    )


def from_items(tensor, head_count):
    item_count, length, head_size = tensor.shape
    batches = item_count // head_count
    return (
        tensor.reshape(batches, head_count, length, head_size)
        .transpose(0, 2, 1, 3)
        .reshape(batches, length, head_count * head_size)
    )


def masked_scores(query_rows, key_rows, query_docs, key_docs, allowed):
    raw_scores = (
        jnp.einsum("qd,kd->qk", query_rows, key_rows, preferred_element_type=jnp.float32) * 0.125
    )
    keep_mask = allowed & (key_docs[None, :] == query_docs[:, None])
    return (jnp.where(keep_mask, raw_scores, -1e30), keep_mask)


def attend_forward(allowed):

    def attend_item(packed):
        query_rows, key_rows, value_rows, query_docs, key_docs = packed
        scores, keep_mask = masked_scores(query_rows, key_rows, query_docs, key_docs, allowed)
        row_top = jnp.max(scores, axis=-1, keepdims=True)
        raised = jnp.exp(scores - row_top)
        row_total = jnp.sum(raised, axis=-1, keepdims=True)
        weights = (raised / row_total).astype(jnp.bfloat16)
        mixed_rows = jnp.dot(weights, value_rows, preferred_element_type=jnp.float32).astype(
            jnp.bfloat16
        )
        return (mixed_rows, row_top[:, 0] + jnp.log(row_total[:, 0]))

    return attend_item


def attend_backward(allowed):

    def attend_item(packed):
        query_rows, key_rows, value_rows, query_docs, key_docs, log_total, grad_rows = packed
        scores, keep_mask = masked_scores(query_rows, key_rows, query_docs, key_docs, allowed)
        weights = jnp.where(keep_mask, jnp.exp(scores - log_total[:, None]), 0.0)
        grad_values = jnp.einsum(
            "qk,qd->kd", weights.astype(jnp.bfloat16), grad_rows, preferred_element_type=jnp.float32
        )
        grad_weights = jnp.einsum(
            "qd,kd->qk", grad_rows, value_rows, preferred_element_type=jnp.float32
        )
        centered = jnp.sum(weights * grad_weights, axis=-1, keepdims=True)
        grad_scores = (weights * (grad_weights - centered)).astype(jnp.bfloat16)
        grad_query = jnp.dot(grad_scores, key_rows, preferred_element_type=jnp.float32) * 0.125
        grad_keys = (
            jnp.einsum("qk,qd->kd", grad_scores, query_rows, preferred_element_type=jnp.float32)
            * 0.125
        )
        return (grad_query, grad_keys, grad_values)

    return attend_item


def layer_forward(stream, params, segments, key_docs, allowed, cycle_steps):
    (
        first_gain,
        first_shift,
        merged_weight,
        merged_bias,
        output_weight,
        output_bias,
        second_gain,
        second_shift,
        expand_weight,
        expand_bias,
        reduce_weight,
        reduce_bias,
    ) = params
    fetched = (
        lax.all_gather(first_gain, "dp", axis=0, tiled=True),
        lax.all_gather(first_shift, "dp", axis=0, tiled=True),
        lax.all_gather(merged_weight, "dp", axis=0, tiled=True),
        lax.all_gather(merged_bias, "dp", axis=2, tiled=True),
        lax.all_gather(output_weight, "dp", axis=1, tiled=True),
        lax.all_gather(output_bias, "dp", axis=0, tiled=True),
        lax.all_gather(second_gain, "dp", axis=0, tiled=True),
        lax.all_gather(second_shift, "dp", axis=0, tiled=True),
        lax.all_gather(expand_weight, "dp", axis=0, tiled=True),
        lax.all_gather(expand_bias, "dp", axis=1, tiled=True),
        lax.all_gather(reduce_weight, "dp", axis=1, tiled=True),
        lax.all_gather(reduce_bias, "dp", axis=0, tiled=True),
    )
    (
        first_gain,
        first_shift,
        merged_weight,
        merged_bias,
        output_weight,
        output_bias,
        second_gain,
        second_shift,
        expand_weight,
        expand_bias,
        reduce_weight,
        reduce_bias,
    ) = fetched
    head_count = merged_weight.shape[2] // HD
    normed = layer_norm(
        stream, first_gain.astype(jnp.float32), first_shift.astype(jnp.float32)
    ).astype(jnp.bfloat16)
    first_rows = spread_rows(normed)
    merged_out = jnp.einsum(
        "std,dkf->stkf", first_rows, merged_weight, preferred_element_type=jnp.float32
    )
    bias_pair = merged_bias.astype(jnp.float32).reshape(2, -1)
    query_rows = (merged_out[:, :, 0] + bias_pair[0]).astype(jnp.bfloat16)
    key_rows = merged_out[:, :, 1].astype(jnp.bfloat16)
    value_rows = (merged_out[:, :, 2] + bias_pair[1]).astype(jnp.bfloat16)
    key_list = [key_rows]
    value_list = [value_rows]
    moving = (key_rows, value_rows)
    for offset in range(cycle_steps):
        moving = from_behind((moving[0], moving[1]), "ctx", 1)
        key_list.insert(0, moving[0])
        value_list.insert(0, moving[1])
    query_items = to_items(query_rows, head_count)
    key_items = to_items(jnp.concatenate(key_list, axis=1), head_count)
    value_items = to_items(jnp.concatenate(value_list, axis=1), head_count)
    query_docs = jnp.repeat(segments, head_count, axis=0)
    window_docs = jnp.repeat(key_docs, head_count, axis=0)
    mixed_items, log_total = lax.map(
        attend_forward(allowed), (query_items, key_items, value_items, query_docs, window_docs)
    )
    mixed = from_items(mixed_items, head_count)
    attn_part = jnp.einsum("stf,fd->std", mixed, output_weight, preferred_element_type=jnp.float32)
    middle = stream + gather_sums(attn_part) + output_bias.astype(jnp.float32)
    normed_two = layer_norm(
        middle, second_gain.astype(jnp.float32), second_shift.astype(jnp.float32)
    ).astype(jnp.bfloat16)
    second_rows = spread_rows(normed_two)
    hidden = jnp.einsum(
        "std,df->stf", second_rows, expand_weight, preferred_element_type=jnp.float32
    ) + expand_bias.astype(jnp.float32).reshape(-1)
    activated = gelu_tanh(hidden).astype(jnp.bfloat16)
    mlp_part = jnp.einsum(
        "stf,fd->std", activated, reduce_weight, preferred_element_type=jnp.float32
    )
    result = middle + gather_sums(mlp_part) + reduce_bias.astype(jnp.float32)
    saved_state = (
        fetched,
        stream,
        first_rows,
        query_items,
        key_items,
        value_items,
        query_docs,
        window_docs,
        log_total,
        mixed,
        middle,
        second_rows,
        hidden,
        activated,
    )
    return (result, saved_state)


def reduce_grads(fresh):
    (
        gain_one,
        shift_one,
        merged_weights,
        merged_biases,
        output_weights,
        output_biases,
        gain_two,
        shift_two,
        expand_weights,
        expand_biases,
        reduce_weights,
        reduce_biases,
    ) = fresh
    summed = (
        lax.psum(gain_one.astype(jnp.bfloat16), "ctx").astype(jnp.float32),
        lax.psum(shift_one.astype(jnp.bfloat16), "ctx").astype(jnp.float32),
        lax.psum(merged_weights.astype(jnp.bfloat16), "ctx").astype(jnp.float32),
        lax.psum(merged_biases.astype(jnp.bfloat16), "ctx").astype(jnp.float32),
        lax.psum(output_weights.astype(jnp.bfloat16), "ctx").astype(jnp.float32),
        lax.psum(output_biases.astype(jnp.bfloat16), "ctx").astype(jnp.float32),
        lax.psum(gain_two.astype(jnp.bfloat16), "ctx").astype(jnp.float32),
        lax.psum(shift_two.astype(jnp.bfloat16), "ctx").astype(jnp.float32),
        lax.psum(expand_weights.astype(jnp.bfloat16), "ctx").astype(jnp.float32),
        lax.psum(expand_biases.astype(jnp.bfloat16), "ctx").astype(jnp.float32),
        lax.psum(reduce_weights.astype(jnp.bfloat16), "ctx").astype(jnp.float32),
        lax.psum(reduce_biases.astype(jnp.bfloat16), "ctx").astype(jnp.float32),
    )
    (
        gain_one,
        shift_one,
        merged_weights,
        merged_biases,
        output_weights,
        output_biases,
        gain_two,
        shift_two,
        expand_weights,
        expand_biases,
        reduce_weights,
        reduce_biases,
    ) = summed
    return (
        lax.psum_scatter(
            gain_one.astype(jnp.bfloat16), "dp", scatter_dimension=0, tiled=True
        ).astype(jnp.float32),
        lax.psum_scatter(
            shift_one.astype(jnp.bfloat16), "dp", scatter_dimension=0, tiled=True
        ).astype(jnp.float32),
        lax.psum_scatter(
            merged_weights.astype(jnp.bfloat16), "dp", scatter_dimension=0, tiled=True
        ).astype(jnp.float32),
        lax.psum_scatter(
            merged_biases.astype(jnp.bfloat16), "dp", scatter_dimension=2, tiled=True
        ).astype(jnp.float32),
        lax.psum_scatter(
            output_weights.astype(jnp.bfloat16), "dp", scatter_dimension=1, tiled=True
        ).astype(jnp.float32),
        lax.psum_scatter(
            output_biases.astype(jnp.bfloat16), "dp", scatter_dimension=0, tiled=True
        ).astype(jnp.float32),
        lax.psum_scatter(
            gain_two.astype(jnp.bfloat16), "dp", scatter_dimension=0, tiled=True
        ).astype(jnp.float32),
        lax.psum_scatter(
            shift_two.astype(jnp.bfloat16), "dp", scatter_dimension=0, tiled=True
        ).astype(jnp.float32),
        lax.psum_scatter(
            expand_weights.astype(jnp.bfloat16), "dp", scatter_dimension=0, tiled=True
        ).astype(jnp.float32),
        lax.psum_scatter(
            expand_biases.astype(jnp.bfloat16), "dp", scatter_dimension=1, tiled=True
        ).astype(jnp.float32),
        lax.psum_scatter(
            reduce_weights.astype(jnp.bfloat16), "dp", scatter_dimension=1, tiled=True
        ).astype(jnp.float32),
        lax.psum_scatter(
            reduce_biases.astype(jnp.bfloat16), "dp", scatter_dimension=0, tiled=True
        ).astype(jnp.float32),
    )


def layer_backward(grad_out, saved_state, allowed, cycle_steps, token_count):
    (
        fetched,
        stream,
        first_rows,
        query_items,
        key_items,
        value_items,
        query_docs,
        window_docs,
        log_total,
        mixed,
        middle,
        second_rows,
        hidden,
        activated,
    ) = saved_state
    (
        first_gain,
        first_shift,
        merged_weight,
        merged_bias,
        output_weight,
        output_bias,
        second_gain,
        second_shift,
        expand_weight,
        expand_bias,
        reduce_weight,
        reduce_bias,
    ) = fetched
    head_count = merged_weight.shape[2] // HD
    grad_branch = spread_rows(grad_out.astype(jnp.bfloat16))
    grad_reduce = jnp.einsum(
        "stf,std->fd", activated, grad_branch, preferred_element_type=jnp.float32
    )
    grad_active = jnp.einsum(
        "std,fd->stf", grad_branch, reduce_weight, preferred_element_type=jnp.float32
    )
    _, gelu_pull = jax.vjp(gelu_tanh, hidden)
    grad_hidden = gelu_pull(grad_active)[0].astype(jnp.bfloat16)
    grad_expand_bias = jnp.sum(grad_hidden, axis=(0, 1), dtype=jnp.float32).reshape(
        expand_bias.shape
    )
    grad_expand = jnp.einsum(
        "std,stf->df", second_rows, grad_hidden, preferred_element_type=jnp.float32
    )
    grad_second = gather_sums(
        jnp.einsum("stf,df->std", grad_hidden, expand_weight, preferred_element_type=jnp.float32)
    )
    _, second_pull = jax.vjp(
        layer_norm, middle, second_gain.astype(jnp.float32), second_shift.astype(jnp.float32)
    )
    grad_norm_mid, grad_second_gain, grad_second_shift = second_pull(grad_second)
    grad_middle = grad_out + grad_norm_mid
    grad_reduce_bias = jnp.sum(grad_out, axis=(0, 1))
    grad_attend = spread_rows(grad_middle.astype(jnp.bfloat16))
    grad_output = jnp.einsum("stf,std->fd", mixed, grad_attend, preferred_element_type=jnp.float32)
    grad_mixed = jnp.einsum(
        "std,fd->stf", grad_attend, output_weight, preferred_element_type=jnp.float32
    ).astype(jnp.bfloat16)
    grad_query_items, grad_key_items, grad_value_items = lax.map(
        attend_backward(allowed),
        (
            query_items,
            key_items,
            value_items,
            query_docs,
            window_docs,
            log_total,
            to_items(grad_mixed, head_count),
        ),
    )
    grad_query = from_items(grad_query_items, head_count)
    window_keys = from_items(grad_key_items, head_count)
    window_values = from_items(grad_value_items, head_count)
    local_keys = window_keys[:, cycle_steps * token_count :]
    local_values = window_values[:, cycle_steps * token_count :]
    carried = None
    for offset in range(cycle_steps, 0, -1):
        start_row = (cycle_steps - offset) * token_count
        block_keys = window_keys[:, start_row : start_row + token_count]
        block_values = window_values[:, start_row : start_row + token_count]
        if carried is not None:
            block_keys = block_keys + carried[0]
            block_values = block_values + carried[1]
        carried = (
            from_behind(block_keys.astype(jnp.bfloat16), "ctx", -1).astype(block_keys.dtype),
            from_behind(block_values.astype(jnp.bfloat16), "ctx", -1).astype(block_values.dtype),
        )
    local_keys = local_keys + carried[0]
    local_values = local_values + carried[1]
    grad_merged = jnp.stack([grad_query, local_keys, local_values], axis=2).astype(jnp.bfloat16)
    grad_merged_bias = jnp.stack(
        [
            jnp.sum(grad_merged[:, :, 0], axis=(0, 1), dtype=jnp.float32),
            jnp.sum(grad_merged[:, :, 2], axis=(0, 1), dtype=jnp.float32),
        ]
    ).reshape(merged_bias.shape)
    grad_merged_weight = jnp.einsum(
        "std,stkf->dkf", first_rows, grad_merged, preferred_element_type=jnp.float32
    )
    grad_first = gather_sums(
        jnp.einsum("stkf,dkf->std", grad_merged, merged_weight, preferred_element_type=jnp.float32)
    )
    _, first_pull = jax.vjp(
        layer_norm, stream, first_gain.astype(jnp.float32), first_shift.astype(jnp.float32)
    )
    grad_norm_in, grad_first_gain, grad_first_shift = first_pull(grad_first)
    grad_input = grad_middle + grad_norm_in
    grad_output_bias = jnp.sum(grad_middle, axis=(0, 1))
    vector_grads = lax.psum(
        (
            grad_first_gain,
            grad_first_shift,
            grad_second_gain,
            grad_second_shift,
            grad_output_bias,
            grad_reduce_bias,
        ),
        "tp",
    )
    fresh = (
        vector_grads[0],
        vector_grads[1],
        grad_merged_weight,
        grad_merged_bias,
        grad_output,
        vector_grads[4],
        vector_grads[2],
        vector_grads[3],
        grad_expand,
        grad_expand_bias,
        grad_reduce,
        vector_grads[5],
    )
    return (grad_input, reduce_grads(fresh))


def general_shards(
    inputs,
    segments,
    cotangent,
    student_first_gain,
    student_first_shift,
    student_merged_weight,
    student_merged_bias,
    student_output_weight,
    student_output_bias,
    student_second_gain,
    student_second_shift,
    student_expand_weight,
    student_expand_bias,
    student_reduce_weight,
    student_reduce_bias,
    teacher_first_gain,
    teacher_first_shift,
    teacher_merged_weight,
    teacher_merged_bias,
    teacher_output_weight,
    teacher_output_bias,
    teacher_second_gain,
    teacher_second_shift,
    teacher_expand_weight,
    teacher_expand_bias,
    teacher_reduce_weight,
    teacher_reduce_bias,
):
    student = (
        student_first_gain,
        student_first_shift,
        student_merged_weight,
        student_merged_bias,
        student_output_weight,
        student_output_bias,
        student_second_gain,
        student_second_shift,
        student_expand_weight,
        student_expand_bias,
        student_reduce_weight,
        student_reduce_bias,
    )
    teacher = (
        teacher_first_gain,
        teacher_first_shift,
        teacher_merged_weight,
        teacher_merged_bias,
        teacher_output_weight,
        teacher_output_bias,
        teacher_second_gain,
        teacher_second_shift,
        teacher_expand_weight,
        teacher_expand_bias,
        teacher_reduce_weight,
        teacher_reduce_bias,
    )
    token_count = segments.shape[1]
    context_size = lax.axis_size("ctx")
    context_index = lax.axis_index("ctx")
    doc_long = min(DOC_MAX, token_count * context_size // 2)
    cycle_steps = min((doc_long - 2) // token_count + 1, context_size - 1)
    doc_list = [segments]
    moving = segments
    for offset in range(cycle_steps):
        moving = from_behind(moving, "ctx", 1)
        doc_list.insert(0, moving)
    key_docs = jnp.concatenate(doc_list, axis=1)
    places = jnp.arange((cycle_steps + 1) * token_count, dtype=jnp.int32)
    relative = places - cycle_steps * token_count
    source = cycle_steps - places // token_count
    query_place = jnp.arange(token_count, dtype=jnp.int32)
    allowed = (relative[None, :] <= query_place[:, None]) & (source <= context_index)[None, :]
    stream = inputs.astype(jnp.float32)
    middle_stream, student_saved = layer_forward(
        stream, student, segments, key_docs, allowed, cycle_steps
    )
    final_stream, teacher_saved = layer_forward(
        middle_stream, teacher, segments, key_docs, allowed, cycle_steps
    )
    teacher_in_grad, teacher_grads = layer_backward(
        cotangent.astype(jnp.float32), teacher_saved, allowed, cycle_steps, token_count
    )
    input_grad, student_grads = layer_backward(
        teacher_in_grad, student_saved, allowed, cycle_steps, token_count
    )
    return (
        (final_stream.astype(jnp.bfloat16), input_grad)
        + tuple(student_grads)
        + tuple(teacher_grads)
    )


BF16 = jnp.bfloat16
F32 = jnp.float32
NEG = -1e30
TILE = 256
RELATIVE = (0, 2, 1, 3)


def row_major(value):
    return with_layout_constraint(value, Layout(major_to_minor=tuple(range(value.ndim))))


def swap(value, axis, bit):
    route = [(i, i ^ bit) for i in range(lax.axis_size(axis))]
    if value.ndim == 2:
        return row_major(lax.ppermute(row_major(value), axis, route))
    return lax.ppermute(value, axis, route)


def cross_core(value):
    return swap(value, "tp", 1)


def cross_x(value):
    return swap(value, "tp", 2)


def cross_y(value):
    return swap(value, "ctx", 1)


def cross_near(value):
    return swap(value, "dp", 1)


def cross_far(value):
    return swap(value, "dp", 2)


def cross_both(value):
    return swap(value, "dp", 3)


def stacked(*values):
    return jnp.concatenate(values, axis=0)


def beside(*values):
    return jnp.concatenate(values, axis=1)


def y_order(own, other, y_index, axis):
    return jnp.where(
        y_index == 0,
        jnp.concatenate([own, other], axis=axis),
        jnp.concatenate([other, own], axis=axis),
    )


def pin(*values):
    return lax.optimization_barrier(values)


def window_start(block, doc_max):
    return max(0, (block * TILE - doc_max + 1) // TILE) * TILE


def upright(line):
    size = line.shape[1]
    rows = lax.broadcasted_iota(jnp.int32, (size, size), 0)
    columns = lax.broadcasted_iota(jnp.int32, (size, size), 1)
    return jnp.sum(jnp.where(rows == columns, line, 0.0), axis=1, keepdims=True)


def join(pieces, whole):
    row, column = 0, 0
    most = whole.shape[0] * whole.shape[1] // sum(piece.shape[1] for piece in pieces)
    for piece in pieces:
        rows = min(piece.shape[0], most) if len(pieces) == 4 else piece.shape[0]
        whole[row : row + rows, column : column + piece.shape[1]] = piece[:rows, :]
        row += rows
        if row == whole.shape[0]:
            row, column = 0, column + piece.shape[1]


def dot_across(left, right):
    return lax.dot_general(left, right, (((1,), (1,)), ((), ())), preferred_element_type=F32)


def dot_down(left, right):
    return lax.dot_general(left, right, (((0,), (0,)), ((), ())), preferred_element_type=F32)


def token_place(me, member, half, rows):
    return pl.multiple_of((half * 4 + (me ^ (2 * (member & 1) + (member >> 1)))) * rows, rows)


def flat(column):
    size = column.shape[0]
    rows = lax.broadcasted_iota(jnp.int32, (size, size), 0)
    columns = lax.broadcasted_iota(jnp.int32, (size, size), 1)
    return jnp.sum(jnp.where(rows == columns, column, 0.0), axis=0, keepdims=True)


def fill_masks_across(docs, masks, doc_max):
    for block in range(docs.shape[1] // TILE):
        start, stop = window_start(block, doc_max), (block + 1) * TILE
        here = slice(block * TILE, stop)
        rows = block * TILE + lax.broadcasted_iota(jnp.int32, (TILE, stop - start), 0)
        columns = start + lax.broadcasted_iota(jnp.int32, (TILE, stop - start), 1)
        same = upright(docs[:, here]) == docs[:, start:stop]
        masks[here, : stop - start] = jnp.where(same & (columns <= rows), 0.0, NEG)


def mask_columns(length, doc_max):
    return max((block + 1) * TILE - window_start(block, doc_max) for block in range(length // TILE))


def fill_masks(docs, masks, doc_max):
    at = 0
    for block in range(docs.shape[1] // TILE):
        start = window_start(block, doc_max)
        size = (block + 1) * TILE - start
        for first in range(0, size, TILE):
            keys = slice(start + first, start + first + TILE)
            same = upright(docs[:, keys]) == docs[:, block * TILE : (block + 1) * TILE]
            if start + first == block * TILE:
                rows = lax.broadcasted_iota(jnp.int32, (TILE, TILE), 0)
                columns = lax.broadcasted_iota(jnp.int32, (TILE, TILE), 1)
                same = same & (rows <= columns)
            masks[at : at + TILE, :] = jnp.where(same, 0.0, NEG)
            at += TILE


def mask_rows(length, doc_max):
    return sum(
        (block + 1) * TILE - window_start(block, doc_max) for block in range(length // TILE)
    )


def split_heads(value, target, first, me, member):
    rows = value.shape[0] // 2
    for half in range(2):
        place = pl.ds(token_place(me, member, half, rows), rows)
        for j in range(value.shape[1] // HD):
            target[first + j, place, :] = value[half * rows : (half + 1) * rows, j * HD : (j + 1) * HD]


def merge_heads(source, me, member, rows):
    return jnp.concatenate(
        [
            jnp.concatenate(
                [
                    source[j, pl.ds(token_place(me, member, half, rows), rows), :]
                    for j in range(source.shape[0])
                ],
                axis=1,
            )
            for half in range(2)
        ],
        axis=0,
    )


def by_member(count, step):
    for i in range(count):
        step(i)


def attention_forward_kernel(
    heads,
    doc_max,
    count,
    scaled,
    me_ref,
    near_ref,
    far_ref,
    bias_ref,
    docs,
    *refs,
):
    mixed, attend_ref, masks = refs[-3:]
    refs = refs[:-3]
    sources = (near_ref, far_ref)
    if scaled:
        gains, refs, normed = refs[0], refs[1:-2], refs[-2:]
        for source, target in zip(sources, normed):
            target[...] = (source[...].astype(F32) * gains[0:1, :] + gains[1:2, :]).astype(BF16)
        sources = normed
    pieces, (sent_ref, kept_ref, split_ref, mixed_ref, log_ref) = refs[:count], refs[count:]
    join(pieces, attend_ref)
    fill_masks_across(docs, masks, doc_max)
    me = me_ref[0]
    width = heads * HD
    size = near_ref.shape[0] // 2
    length = 4 * size
    for source, first in zip(sources, (0, 2)):

        def project(i, source=source, first=first):
            at = pl.ds(pl.multiple_of(i * size, size), size)
            value = jnp.dot(source[at, :], attend_ref[:, : 3 * width], preferred_element_type=F32)
            value = (value + bias_ref[...]).astype(BF16)
            split_heads(value[:, :width] * BF16(0.125), split_ref, 0, me, first + i)
            split_heads(value[:, width:], split_ref, heads, me, first + i)

        by_member(2, project)

    def attend(h):
        for block in range(length // TILE):
            start, stop = window_start(block, doc_max), (block + 1) * TILE
            here = slice(block * TILE, stop)
            key, value = split_ref[heads + h, start:stop, :], split_ref[2 * heads + h, start:stop, :]
            scores = dot_across(split_ref[h, here, :], key) + masks[here, : stop - start]
            top = jnp.max(scores, axis=1, keepdims=True)
            raised = jnp.exp(scores - top)
            total = jnp.sum(raised, axis=1, keepdims=True)
            product = jnp.dot(raised.astype(BF16), value, preferred_element_type=F32)
            mixed[h, here, :] = (product * (1.0 / total)).astype(BF16)
            log_ref[h, :, here] = flat(top + jnp.log(total))

    lax.fori_loop(0, heads, lambda h, carry: (attend(h), carry)[1], 0)
    for out, first in ((sent_ref, 2), (kept_ref, 0)):

        def finish(i, out=out, first=first):
            rows = merge_heads(mixed, me, first + i, size // 2)
            mixed_ref[pl.ds(pl.multiple_of((first + i) * size, size), size), :] = rows
            at = pl.ds(pl.multiple_of(i * size, size), size)
            out[at, :] = dot_across(rows, attend_ref[:, 3 * width :]).astype(out.dtype)

        by_member(2, finish)


def attention_backward_kernel(
    heads,
    doc_max,
    count,
    me_ref,
    near_ref,
    far_ref,
    docs,
    split_ref,
    log_ref,
    *refs,
):
    pieces, (sent_ref, kept_ref, out_ref, sum_ref) = refs[:count], refs[count:-4]
    grad, total, attend_ref, masks = refs[-4:]
    join(pieces, attend_ref)
    fill_masks(docs, masks, doc_max)
    me = me_ref[0]
    width = heads * HD
    size = near_ref.shape[0] // 2
    length = 4 * size
    for source, first in ((near_ref, 0), (far_ref, 2)):

        def project(i, source=source, first=first):
            at = pl.ds(pl.multiple_of(i * size, size), size)
            value = jnp.dot(source[at, :], attend_ref[:, 3 * width :], preferred_element_type=F32)
            split_heads(value.astype(BF16), grad, 0, me, first + i)

        by_member(2, project)

    def attend(h):
        total[heads + h] = jnp.zeros((length, HD), F32)
        total[2 * heads + h] = jnp.zeros((length, HD), F32)
        at = 0
        for block in range(length // TILE):
            start, stop = window_start(block, doc_max), (block + 1) * TILE
            here, window = slice(block * TILE, stop), slice(start, stop)
            query, key, value = (
                split_ref[h, here, :],
                split_ref[heads + h, window, :],
                split_ref[2 * heads + h, window, :],
            )
            grad_rows = grad[h, here, :]
            scores = dot_across(key, query) + masks[at : at + stop - start, :]
            at += stop - start
            weights = jnp.exp(scores - log_ref[h, :, here])
            weighted = weights * dot_across(value, grad_rows)
            centered = jnp.sum(weighted, axis=0, keepdims=True)
            grad_scores = (weighted - weights * centered).astype(BF16)
            total[2 * heads + h, window, :] += jnp.dot(
                weights.astype(BF16), grad_rows, preferred_element_type=F32
            )
            total[heads + h, window, :] += jnp.dot(
                grad_scores, query, preferred_element_type=F32
            )
            total[h, here, :] = dot_down(key, grad_scores).T * 0.125

    lax.fori_loop(0, heads, lambda h, carry: (attend(h), carry)[1], 0)
    sum_ref[...] = jnp.zeros_like(sum_ref)
    for out, first in ((sent_ref, 2), (kept_ref, 0)):

        def finish(i, out=out, first=first):
            rows = merge_heads(total, me, first + i, size // 2).astype(BF16)
            out_ref[pl.ds(pl.multiple_of((first + i) * size, size), size), :] = rows
            sum_ref[...] += jnp.sum(rows.astype(F32), axis=0, keepdims=True)
            at = pl.ds(pl.multiple_of(i * size, size), size)
            out[at, :] = dot_across(rows, attend_ref[:, : 3 * width]).astype(out.dtype)

        by_member(2, finish)


VMEM = pl.BlockSpec(memory_space=pltpu.VMEM)
SMEM = pl.BlockSpec(memory_space=pltpu.SMEM)


def call(body, name, inputs, outputs, scratch, flops, transcendentals, limit=24):
    size = sum(v.size * v.dtype.itemsize for v in list(inputs) + list(outputs))
    return pl.pallas_call(
        body,
        out_shape=tuple(outputs),
        in_specs=[SMEM if v.ndim == 1 else VMEM for v in inputs],
        out_specs=tuple(VMEM for _ in outputs),
        scratch_shapes=scratch,
        cost_estimate=pl.CostEstimate(
            flops=flops, transcendentals=transcendentals, bytes_accessed=size
        ),
        compiler_params=pltpu.CompilerParams(vmem_limit_bytes=limit << 20),
        name=name,
    )(*inputs)


def shaped(rows, columns, kind):
    return jax.ShapeDtypeStruct((rows, columns), kind)


def attention_forward(near, far, attend, bias, context, doc_max, gains=()):
    me, docs = context
    half, features = near.shape
    width = bias.shape[1] // 3
    heads = width // HD
    area = heads * 2 * half * half

    def body(*refs):
        attention_forward_kernel(heads, doc_max, len(attend), len(gains) > 0, *refs)

    return call(
        body,
        "attention_forward",
        (me, near, far, bias, docs) + tuple(gains) + tuple(attend),
        (
            shaped(half, features, BF16),
            shaped(half, features, F32),
            jax.ShapeDtypeStruct((3 * heads, 2 * half, HD), BF16),
            shaped(2 * half, width, BF16),
            jax.ShapeDtypeStruct((heads, 1, 2 * half), F32),
        )
        + (shaped(half, features, BF16),) * (2 * len(gains)),
        [
            pltpu.VMEM((heads, 2 * half, HD), BF16),
            pltpu.VMEM((features, 4 * width), BF16),
            pltpu.VMEM((2 * half, mask_columns(2 * half, doc_max)), F32),
        ],
        16 * HD * area,
        area,
    )


def attention_backward(near, far, attend, context, saved, doc_max):
    me, docs = context
    split, _, log_total = saved
    half, features = near.shape
    heads = split.shape[0] // 3
    width = heads * HD
    area = heads * 2 * half * half

    def body(*refs):
        attention_backward_kernel(heads, doc_max, len(attend), *refs)

    return call(
        body,
        "attention_backward",
        (me, near, far, docs, split, log_total) + tuple(attend),
        (
            shaped(half, features, BF16),
            shaped(half, features, F32),
            shaped(2 * half, 3 * width, BF16),
            shaped(1, 3 * width, F32),
        ),
        [
            pltpu.VMEM((heads, 2 * half, HD), BF16),
            pltpu.VMEM((3 * heads, 2 * half, HD), F32),
            pltpu.VMEM((features, 4 * width), BF16),
            pltpu.VMEM((mask_rows(2 * half, doc_max), TILE), F32),
        ],
        40 * HD * area,
        area,
    )


CHUNK = 256


def gelu_both(values):
    inner = GELU_SCALE * (values + 0.044715 * values * values * values)
    bent = jnp.tanh(inner)
    value = 0.5 * values * (1.0 + bent)
    slope = 0.5 * (1.0 + bent) + 0.5 * values * (1.0 - bent * bent) * GELU_SCALE * (
        1.0 + 3.0 * 0.044715 * values * values
    )
    return value, slope


def split_parts(weight):
    size = min(weight.shape[1], 768)
    return [slice(at, at + size) for at in range(0, weight.shape[1], size)]


def feed_forward_kernel(
    count, near_ref, far_ref, bias_ref, *refs
):
    sent_ref, kept_ref, expand_ref, reduce_ref = refs[-4:]
    join(refs[:count], expand_ref)
    join(refs[count:-4], reduce_ref)
    parts = split_parts(expand_ref)
    for piece, out in ((far_ref, sent_ref), (near_ref, kept_ref)):

        def step(i, carry):
            at = pl.ds(pl.multiple_of(i * CHUNK, CHUNK), CHUNK)
            rows = piece[at, :]
            total = None
            for columns in parts:
                hidden = jnp.dot(rows, expand_ref[:, columns], preferred_element_type=F32)
                active = gelu_tanh(hidden + bias_ref[:, columns]).astype(BF16)
                product = dot_across(active, reduce_ref[:, columns])
                total = product if total is None else total + product
            out[at, :] = total.astype(out.dtype)
            return carry

        lax.fori_loop(0, piece.shape[0] // CHUNK, step, 0)


def feed_forward(near, far, expand, reduce, bias):
    half, features = near.shape
    hidden = bias.shape[1]

    def body(*refs):
        feed_forward_kernel(len(expand), *refs)

    return call(
        body,
        "feed_forward",
        (near, far, bias) + tuple(expand) + tuple(reduce),
        (shaped(half, features, BF16), shaped(half, features, F32)),
        [pltpu.VMEM((features, hidden), BF16), pltpu.VMEM((features, hidden), BF16)],
        8 * half * features * hidden,
        2 * half * hidden,
    )


def feed_backward_kernel(
    count,
    near_ref,
    far_ref,
    near_grad,
    far_grad,
    bias_ref,
    *refs,
):
    sent_ref, kept_ref, active_ref, hidden_ref, sum_ref, expand_ref, reduce_ref = refs[-7:]
    join(refs[:count], expand_ref)
    join(refs[count:-7], reduce_ref)
    parts = split_parts(expand_ref)
    half = near_ref.shape[0]
    sum_ref[...] = jnp.zeros_like(sum_ref)
    for piece, grads, out, base in (
        (far_ref, far_grad, sent_ref, half),
        (near_ref, near_grad, kept_ref, 0),
    ):

        def step(i, carry):
            place = pl.multiple_of(i * CHUNK, CHUNK)
            at = pl.ds(place, CHUNK)
            whole = pl.ds(pl.multiple_of(base + place, CHUNK), CHUNK)
            rows = piece[at, :]
            grad_rows = grads[at, :]
            total = None
            for columns in parts:
                hidden = jnp.dot(rows, expand_ref[:, columns], preferred_element_type=F32)
                value, slope = gelu_both(hidden + bias_ref[:, columns])
                active_ref[whole, columns] = value.astype(BF16)
                grad_active = jnp.dot(
                    grad_rows, reduce_ref[:, columns], preferred_element_type=F32
                )
                grad_hidden = (grad_active * slope).astype(BF16)
                hidden_ref[whole, columns] = grad_hidden
                sum_ref[:, columns] += jnp.sum(grad_hidden.astype(F32), axis=0, keepdims=True)
                product = dot_across(grad_hidden, expand_ref[:, columns])
                total = product if total is None else total + product
            out[at, :] = total.astype(out.dtype)
            return carry

        lax.fori_loop(0, half // CHUNK, step, 0)


def feed_backward(near, far, near_grad, far_grad, expand, reduce, bias):
    half, features = near.shape
    hidden = bias.shape[1]

    def body(*refs):
        feed_backward_kernel(len(expand), *refs)

    return call(
        body,
        "feed_backward",
        (near, far, near_grad, far_grad, bias) + tuple(expand) + tuple(reduce),
        (
            shaped(half, features, BF16),
            shaped(half, features, F32),
            shaped(2 * half, hidden, BF16),
            shaped(2 * half, hidden, BF16),
            shaped(1, hidden, F32),
        ),
        [pltpu.VMEM((features, hidden), BF16), pltpu.VMEM((features, hidden), BF16)],
        12 * half * features * hidden,
        2 * half * hidden,
    )


def row_block(rows, columns):
    return pl.BlockSpec((rows, columns), lambda i: (0, 0))


def row_call(body, name, inputs, rows, outputs):
    specs = [row_block(v.shape[0] if v.shape[0] <= 16 else rows, v.shape[1]) for v in inputs]
    size = sum(rows * v.shape[1] * v.dtype.itemsize for v in inputs)
    return pl.pallas_call(
        body,
        grid=(1,),
        out_shape=tuple(outputs),
        in_specs=specs,
        out_specs=tuple(row_block(*v.shape) for v in outputs),
        cost_estimate=pl.CostEstimate(
            flops=20 * rows * inputs[0].shape[1], transcendentals=rows, bytes_accessed=2 * size
        ),
        compiler_params=pltpu.CompilerParams(vmem_limit_bytes=18 << 20),
        name=name,
    )(*inputs)


STEP = 128


def add_norm(base, partial, across, vectors, bias_at, norm_vectors, norm_at):
    rows, columns = base.shape

    def body(base_ref, bias_ref, vector_ref, partial_ref, across_ref, sum_ref, norm_ref):
        bias = bias_ref[bias_at : bias_at + 1, :]
        gain, shift = vector_ref[norm_at : norm_at + 1, :], vector_ref[norm_at + 1 : norm_at + 2, :]

        def step(i, carry):
            here = pl.ds(pl.multiple_of(i * STEP, STEP), STEP)
            there = pl.ds(pl.multiple_of((i * STEP + rows // 2) % rows, STEP), STEP)
            total = partial_ref[here, :].astype(F32) + across_ref[there, :].astype(F32)
            total = base_ref[here, :].astype(F32) + bias + total
            sum_ref[here, :] = total
            norm_ref[here, :] = (normalize(total)[0] * gain + shift).astype(BF16)
            return carry

        lax.fori_loop(0, rows // STEP, step, 0)

    return row_call(
        body,
        "add_norm",
        [base, vectors, norm_vectors, partial, across],
        rows,
        (shaped(rows, columns, F32), shaped(rows, columns, BF16)),
    )


def norm_back_near(skip, partial, across, value, vectors, norm_at, sums, sums_at):
    rows, columns = skip.shape

    def body(skip_ref, value_ref, vector_ref, old_ref, partial_ref, across_ref, *outs):
        grad_ref, low_ref, sum_ref = outs
        gain = vector_ref[norm_at : norm_at + 1, :]
        sum_ref[...] = old_ref[...]

        def step(i, own):
            here = pl.ds(pl.multiple_of(i * STEP, STEP), STEP)
            there = pl.ds(pl.multiple_of((i * STEP + rows // 2) % rows, STEP), STEP)
            grad = partial_ref[here, :].astype(F32) + across_ref[there, :].astype(F32)
            unit, scale = normalize(value_ref[here, :].astype(F32))
            skipped = skip_ref[here, :].astype(F32)
            if own:
                for j, each in enumerate((grad * unit, grad, skipped)):
                    sum_ref[sums_at + j : sums_at + j + 1, :] += jnp.sum(each, axis=0, keepdims=True)
            total = skipped + norm_pullback(grad, unit, scale, gain)
            grad_ref[here, :] = total
            low_ref[here, :] = total.astype(BF16)

        count = rows // STEP // 2
        lax.fori_loop(0, count, lambda i, carry: (step(i, True), carry)[1], 0)
        lax.fori_loop(count, 2 * count, lambda i, carry: (step(i, False), carry)[1], 0)

    return row_call(
        body,
        "norm_back_near",
        [skip, value, vectors, sums, partial, across],
        rows,
        (shaped(rows, columns, F32), shaped(rows, columns, BF16), shaped(16, columns, F32)),
    )


def norm_only(values):
    rows, columns = values.shape

    def body(value_ref, unit_ref):
        unit_ref[...] = normalize(value_ref[...].astype(F32))[0].astype(BF16)

    return row_call(body, "norm_only", [values], rows, (shaped(rows, columns, BF16),))[0]


def norm_back(skip, addends, value, vectors, norm_at, sums, sums_at):
    rows, columns = addends[-1].shape

    def body(*refs):
        skip_ref, value_ref, vector_ref, old_ref = refs[:4]
        parts, (grad_ref, low_ref, sum_ref) = refs[4:-3], refs[-3:]
        grad = parts[0][...].astype(F32)
        for part in parts[1:]:
            grad = grad + part[...].astype(F32)
        unit, scale = normalize(value_ref[...].astype(F32))
        skipped = skip_ref[...]
        sum_ref[...] = old_ref[...]
        for i, each in enumerate((grad * unit, grad, skipped)):
            sum_ref[sums_at + i : sums_at + i + 1, :] = jnp.sum(each, axis=0, keepdims=True)
        total = skipped + norm_pullback(grad, unit, scale, vector_ref[norm_at : norm_at + 1, :])
        grad_ref[...] = total
        low_ref[...] = total.astype(BF16)

    return row_call(
        body,
        "norm_back",
        [skip, value, vectors, sums] + list(addends),
        rows,
        (shaped(rows, columns, F32), shaped(rows, columns, BF16), shaped(16, columns, F32)),
    )


def normalize(values):
    center = values - jnp.mean(values, axis=-1, keepdims=True)
    spread = jnp.mean(center * center, axis=-1, keepdims=True)
    scale = lax.rsqrt(spread + EPSILON)
    return center * scale, scale


def norm_rows(values, gain, shift):
    return (normalize(values)[0] * gain + shift).astype(BF16)


def norm_pullback(grad, unit, scale, gain):
    inner = grad * gain
    return scale * (
        inner
        - jnp.mean(inner, axis=-1, keepdims=True)
        - unit * jnp.mean(inner * unit, axis=-1, keepdims=True)
    )


def times(left, right, kind=F32):
    return jnp.dot(left, right, preferred_element_type=F32).astype(kind)


def times_across(left, right, kind=F32):
    return dot_across(left, right).astype(kind)


def times_down(left, right, kind=F32):
    return row_major(dot_down(left, right).astype(kind))


def gather_rows(rows):
    near = stacked(rows, cross_x(rows))
    return near, cross_core(near)


def add_half(value, cross):
    middle = value.shape[0] // 2
    return value[:middle].astype(F32) + cross(value[middle:].astype(BF16)).astype(F32)


def add_columns(value, cross):
    middle = value.shape[1] // 2
    return value[:, :middle].astype(F32) + cross(value[:, middle:].astype(BF16)).astype(F32)


def column_halves(shard, y_index):
    middle = shard.shape[1] // 2
    own = jnp.where(y_index == 0, shard[:, :middle], shard[:, middle:])
    other = jnp.where(y_index == 0, shard[:, middle:], shard[:, :middle])
    return own, other


def natural_columns(own, other, y_index):
    return jnp.where(y_index == 0, beside(own, other), beside(other, own))


def order_matrix(width, z_index):
    rows = width // 4
    natural = lax.broadcasted_iota(jnp.int32, (width, width), 0)
    place = lax.broadcasted_iota(jnp.int32, (width, width), 1)
    step, inner = place // rows, place % rows
    distance = 2 * (step & 1) + (step >> 1)
    return (natural == (z_index ^ distance) * rows + inner).astype(BF16)


def my_rows(pair, y_index):
    own = jnp.where(y_index == 0, pair[0], pair[1])
    sent = jnp.where(y_index == 0, pair[1], pair[0])
    return y_order(own, cross_y(sent), y_index, 0)


ROWS = 64
SPARE = ROWS // 2


def turn(value):
    size = value.shape[0]
    eye = (
        lax.broadcasted_iota(jnp.int32, (size, size), 0)
        == lax.broadcasted_iota(jnp.int32, (size, size), 1)
    ).astype(BF16)
    return dot_down(value, eye)


def pack_vectors(blocks, place):
    flat = []
    for gains, merged_bias, expand_bias in blocks:
        flat += list(gains) + [merged_bias.transpose(1, 0, 2), expand_bias]

    number = len(flat)

    def body(*refs):
        refs = refs[1:]
        out, part, sem = refs[number], refs[number + 1 : -1], refs[-1]
        copies = [
            pltpu.make_async_copy(refs[i], part[i], sem.at[i]) for i in range(number)
        ]
        for copy in copies:
            copy.start()
        out[...] = jnp.zeros_like(out)
        for copy in copies:
            copy.wait()
        for b in range(2):
            vectors, merged_bias, expand_bias = part[8 * b : 8 * b + 6], part[8 * b + 6], part[8 * b + 7]
            for i in range(6):
                local = vectors[i].shape[0]
                out[6 * b + i : 6 * b + i + 1, :local] = vectors[i][...].astype(F32).reshape(1, local)
            for h in range(merged_bias.shape[0]):
                value = merged_bias[h].astype(F32)
                out[16 + 8 * b + 2 * h : 18 + 8 * b + 2 * h, : value.shape[1]] = value
            value = expand_bias[...].astype(F32)
            out[32 + 16 * b : 32 + 16 * b + value.shape[0], : value.shape[1]] = value

    return pl.pallas_call(
        body,
        out_shape=shaped(ROWS, 256, F32),
        in_specs=[SMEM] + [pl.BlockSpec(memory_space=pltpu.HBM)] * number,
        out_specs=VMEM,
        scratch_shapes=[pltpu.VMEM(v.shape, v.dtype) for v in flat]
        + [pltpu.SemaphoreType.DMA((number,))],
        compiler_params=pltpu.CompilerParams(vmem_limit_bytes=60 << 20),
        name="pack_vectors",
    )(place, *flat)


def prepare_first(place, merged, output, blocks):
    flat = []
    for gains, merged_bias, expand_bias in blocks:
        flat += list(gains) + [merged_bias.transpose(1, 0, 2), expand_bias]
    flat += [merged.transpose(1, 0, 2), output]
    number = len(flat)
    local = output.shape[1]

    def body(*refs):
        out, part, small, sem = refs[number], refs[number + 1 : -2], refs[-2], refs[-1]
        copies = [pltpu.make_async_copy(refs[i], part[i], sem.at[i]) for i in range(number)]
        for copy in copies:
            copy.start()
        small[...] = jnp.zeros_like(small)
        for copy in copies:
            copy.wait()
        for b in range(2):
            vectors, merged_bias, expand_bias = part[8 * b : 8 * b + 6], part[8 * b + 6], part[8 * b + 7]
            for i in range(6):
                small[6 * b + i : 6 * b + i + 1, :local] = (
                    vectors[i][...].astype(F32).reshape(1, local)
                )
            for h in range(merged_bias.shape[0]):
                value = merged_bias[h].astype(F32)
                small[16 + 8 * b + 2 * h : 18 + 8 * b + 2 * h, : value.shape[1]] = value
            value = expand_bias[...].astype(F32)
            small[32 + 16 * b : 32 + 16 * b + value.shape[0], : value.shape[1]] = value
        merged_ref, output_ref = part[-2:]
        pieces = [merged_ref[k] for k in range(3)] + [turn(output_ref[...]).astype(BF16)]
        out[:local, :] = jnp.concatenate(pieces, axis=1)
        out[local:, :256] = small[:SPARE, :].astype(BF16)
        out[local:, 256:512] = small[SPARE:, :].astype(BF16)
        out[local:, 512:] = jnp.zeros((SPARE, 4 * local - 512), BF16)

    return pl.pallas_call(
        body,
        out_shape=shaped(local + SPARE, 4 * local, BF16),
        in_specs=[pl.BlockSpec(memory_space=pltpu.HBM)] * number,
        out_specs=VMEM,
        scratch_shapes=[pltpu.VMEM(v.shape, v.dtype) for v in flat]
        + [pltpu.VMEM((ROWS, 256), F32), pltpu.SemaphoreType.DMA((number,))],
        compiler_params=pltpu.CompilerParams(vmem_limit_bytes=60 << 20),
        name="prepare_first",
    )(*flat)


def unpack_vectors(pieces, place, local, merged_shape, expand_shape):
    heads, few = merged_shape[1], merged_shape[2]
    groups = expand_shape[0]
    width = heads * 4 * few

    def body(place_ref, *refs):
        pieces, outs, pieces_ref = refs[:4], refs[4:-1], refs[-1]
        for k in range(4):
            for i in range(2):
                pieces_ref[k * ROWS + i * SPARE : k * ROWS + (i + 1) * SPARE, :] = pieces[k][
                    local:, 256 * i : 256 * (i + 1)
                ].astype(F32)
        y, z = place_ref[0], place_ref[1]
        for b in range(2):
            gains, bias, hidden = outs[3 * b : 3 * b + 3]
            for k in range(4):
                gains[0:6, k * local : (k + 1) * local] = pieces_ref[
                    k * ROWS + 6 * b : k * ROWS + 6 * b + 6, :local
                ]
            bias[...] = jnp.zeros_like(bias)
            for natural in range(4):
                distance = z ^ natural
                base = (2 * (distance & 1) + (distance >> 1)) * ROWS
                part = pieces_ref[pl.ds(pl.multiple_of(base, ROWS), ROWS), :128]
                for i in range(2):
                    for h in range(heads):
                        line = 16 + 8 * b + 2 * h + i
                        at = 2 * i * width + h * 4 * few + natural * few
                        bias[:, at : at + few] = part[line : line + 1, :few]
                lines = part[32 + 16 * b : 32 + 16 * b + groups]
                half = groups // 2
                lines = jnp.where(
                    y == 0, lines, jnp.concatenate([lines[half:], lines[:half]], axis=0)
                )
                for p in range(groups):
                    at = p * 4 * few + natural * few
                    hidden[:, at : at + few] = lines[p : p + 1, :few]

    one = (
        shaped(8, 4 * local, F32),
        shaped(1, 3 * width, F32),
        shaped(1, groups * 4 * few, F32),
    )
    return pl.pallas_call(
        body,
        out_shape=one + one,
        in_specs=[SMEM] + [VMEM] * 4,
        out_specs=(VMEM,) * 6,
        scratch_shapes=[pltpu.VMEM((4 * ROWS, 256), F32)],
        compiler_params=pltpu.CompilerParams(vmem_limit_bytes=8 << 20),
        name="unpack_vectors",
    )(place, *pieces)


def prepare_attend(merged, output):
    local = output.shape[1]

    def body(merged_ref, output_ref, attend):
        pieces = [merged_ref[k] for k in range(3)] + [turn(output_ref[...]).astype(BF16)]
        attend[...] = jnp.concatenate(pieces, axis=1)

    return pl.pallas_call(
        body,
        out_shape=shaped(local, 4 * local, BF16),
        in_specs=[VMEM, VMEM],
        out_specs=VMEM,
        compiler_params=pltpu.CompilerParams(vmem_limit_bytes=12 << 20),
        name="prepare_attend",
    )(merged.transpose(1, 0, 2), output)


def prepare_feed(place, expand, reduce):
    local, half = expand.shape[0], expand.shape[1] // 2

    def body(place_ref, expand_ref, reduce_ref, feed):
        y = place_ref[0]
        first, second = reduce_ref[:, :half], reduce_ref[:, half:]
        feed[:, :half] = jnp.where(y == 0, expand_ref[:, :half], expand_ref[:, half:])
        feed[:, half : 2 * half] = jnp.where(y == 0, first, second)
        feed[:, 2 * half :] = jnp.where(y == 0, second, first)

    return pl.pallas_call(
        body,
        out_shape=shaped(local, 3 * half, BF16),
        in_specs=[SMEM, VMEM, VMEM],
        out_specs=VMEM,
        compiler_params=pltpu.CompilerParams(vmem_limit_bytes=12 << 20),
        name="prepare_feed",
    )(place, expand, reduce.T)


def pack_grads(sums, biases, hiddens, place, local, merged_shape, expand_shape):
    heads, few = merged_shape[1], merged_shape[2]
    groups = expand_shape[0]
    width = heads * 4 * few

    def body(place_ref, sum_ref, bias_s, bias_t, hidden_s, hidden_t, out):
        y, z = place_ref[0], place_ref[1]
        out[...] = jnp.zeros_like(out)
        for k in range(4):
            out[k * ROWS : k * ROWS + 12, :local] = sum_ref[0:12, k * local : (k + 1) * local]
        for natural in range(4):
            distance = z ^ natural
            base = pl.multiple_of((2 * (distance & 1) + (distance >> 1)) * ROWS, ROWS)
            lines = []
            for bias in (bias_s, bias_t):
                for h in range(heads):
                    for i in range(2):
                        at = 2 * i * width + h * 4 * few + natural * few
                        lines.append(bias[:, at : at + few])
                lines.append(jnp.zeros((2, few), F32))
            for hidden in (hidden_s, hidden_t):
                rows = [
                    hidden[:, p * 4 * few + natural * few : p * 4 * few + natural * few + few]
                    for p in range(groups)
                ]
                first, second = rows[: groups // 2], rows[groups // 2 :]
                first, second = jnp.concatenate(first, axis=0), jnp.concatenate(second, axis=0)
                lines.append(jnp.where(y == 0, first, second))
                lines.append(jnp.where(y == 0, second, first))
                lines.append(jnp.zeros((16 - groups, few), F32))
            out[pl.ds(pl.multiple_of(base + 16, 16), ROWS - 16), :few] = jnp.concatenate(lines, axis=0)

    return pl.pallas_call(
        body,
        out_shape=shaped(4 * ROWS, 256, F32),
        in_specs=[SMEM] + [VMEM] * 5,
        out_specs=VMEM,
        compiler_params=pltpu.CompilerParams(vmem_limit_bytes=4 << 20),
        name="pack_grads",
    )(place, sums, *biases, *hiddens)


def unpack_grads(mine, arrived, local, merged_shape, expand_shape):
    heads, few = merged_shape[1], merged_shape[2]
    groups = expand_shape[0]

    def body(mine_ref, arrived_ref, *outs):
        total = mine_ref[0:ROWS, :] + arrived_ref[...]
        for b in range(2):
            vectors, merged_bias, expand_bias = outs[8 * b : 8 * b + 6], outs[8 * b + 6], outs[8 * b + 7]
            for i in range(6):
                vectors[i][...] = total[6 * b + i : 6 * b + i + 1, :local].reshape(local)
            for h in range(heads):
                merged_bias[h] = total[16 + 8 * b + 2 * h : 18 + 8 * b + 2 * h, :few]
            expand_bias[...] = total[32 + 16 * b : 32 + 16 * b + groups, :few]

    one = [jax.ShapeDtypeStruct((local,), F32)] * 6 + [
        jax.ShapeDtypeStruct((heads, 2, few), F32),
        jax.ShapeDtypeStruct(expand_shape, F32),
    ]
    values = pl.pallas_call(
        body,
        out_shape=tuple(one + one),
        in_specs=[VMEM] * 2,
        out_specs=(VMEM,) * 16,
        compiler_params=pltpu.CompilerParams(vmem_limit_bytes=4 << 20),
        name="unpack_grads",
    )(mine, arrived)
    return [v.transpose(1, 0, 2) if v.ndim == 3 else v for v in values]


def finish_feed(mine, theirs, place, half):
    local = mine.shape[0]
    whole = mine.shape[1] == 3 * half

    def body(place_ref, mine_ref, theirs_ref, expand, reduce):
        y = place_ref[0]
        own, other = mine_ref[:, :half].astype(F32), theirs_ref[:, :half].astype(F32)
        expand[:, :half] = jnp.where(y == 0, own, other)
        expand[:, half:] = jnp.where(y == 0, other, own)
        if whole:
            total = mine_ref[:, half:].astype(F32) + theirs_ref[:, half:].astype(F32)
            own, other = total[:, :half], total[:, half:]
        else:
            own, other = mine_ref[:, half:].astype(F32), theirs_ref[:, half:].astype(F32)
        reduce[:, :half] = jnp.where(y == 0, own, other)
        reduce[:, half:] = jnp.where(y == 0, other, own)

    expand, reduce = pl.pallas_call(
        body,
        out_shape=(shaped(local, 2 * half, F32), shaped(local, 2 * half, F32)),
        in_specs=[SMEM, VMEM, VMEM],
        out_specs=(VMEM, VMEM),
        compiler_params=pltpu.CompilerParams(vmem_limit_bytes=12 << 20),
        name="finish_feed",
    )(place, mine, theirs)
    return expand, reduce.T


def finish_attend(added, mine, theirs, place):
    local = mine.shape[0]

    def body(place_ref, *refs):
        mine_ref, theirs_ref, merged, output = refs[-4:]
        y = place_ref[0]
        own, other = mine_ref[...], theirs_ref[...]
        split = jnp.concatenate(
            [jnp.where(y == 0, own, other), jnp.where(y == 0, other, own)], axis=1
        )
        output[...] = turn(split[:, -local:])
        whole = split.astype(F32)
        if added:
            total = refs[0][...].astype(F32) + refs[1][...].astype(F32)
            whole = jnp.concatenate([total, whole], axis=1)
        for k in range(3):
            merged[k] = whole[:, k * local : (k + 1) * local]

    merged, output = pl.pallas_call(
        body,
        out_shape=(jax.ShapeDtypeStruct((3, local, local), F32), shaped(local, local, F32)),
        in_specs=[SMEM] + [VMEM] * (2 + len(added)),
        out_specs=(VMEM, VMEM),
        compiler_params=pltpu.CompilerParams(vmem_limit_bytes=12 << 20),
        name="finish_attend",
    )(place, *added, mine, theirs)
    return merged.transpose(1, 0, 2), output


def halves_added(kept, arrived):
    middle = kept.shape[0] // 2
    return (kept[middle:] + arrived[middle:].astype(F32)).astype(BF16)


def core_sum(kept, arrived):
    return (kept + arrived.astype(F32)).astype(BF16)


def added(first, second):
    return (first.astype(F32) + second.astype(F32)).astype(BF16)


def send_columns(value, cross):
    middle = value.shape[1] // 2
    return cross(value[:, middle:].astype(BF16))


def keep_columns(value, arrived):
    return value[:, : value.shape[1] // 2].astype(F32) + arrived.astype(F32)


def send_rows(value, cross):
    middle = value.shape[0] // 2
    return cross(value[middle:].astype(BF16))


def keep_rows(value, arrived):
    return value[: value.shape[0] // 2].astype(F32) + arrived.astype(F32)


def fast_shards(inputs, segments, cotangent, *params):
    y_index = lax.axis_index("ctx")
    z_index = lax.axis_index("dp")
    me = lax.axis_index("tp")
    tokens, features = inputs.shape[1], inputs.shape[2]
    length = segments.shape[1] * 2
    doc_max = min(DOC_MAX, length // 2)
    blocks = (params[:12], params[12:])
    local = features // 4
    half = local * 2

    small = [((p[0], p[1], p[5], p[6], p[7], p[11]), p[3], p[9]) for p in blocks]
    place = jnp.stack([y_index, z_index]).astype(jnp.int32)
    p = blocks[0]
    attend = prepare_first(place, p[2], p[4], small)
    inputs, attend = pin(inputs, attend)
    far, near = cross_far(attend), cross_near(attend)
    sent_rows = jnp.where(y_index == 0, inputs[1], inputs[0])
    sent_docs = jnp.where(y_index == 0, segments[1:2], segments[0:1]).astype(BF16)
    sent_docs = jnp.pad(sent_docs, ((0, 15), (0, features - sent_docs.shape[1])))
    moved = cross_y(stacked(sent_rows, sent_docs))
    kept_rows = jnp.where(y_index == 0, inputs[0], inputs[1])
    kept_docs = jnp.where(y_index == 0, segments[0:1], segments[1:2]).astype(F32)
    chooser = order_matrix(features, z_index)
    raw = times(y_order(kept_rows, moved[:tokens], y_index, 0), chooser, BF16)
    docs = y_order(
        kept_docs, moved[tokens : tokens + 1, : kept_docs.shape[1]].astype(F32), y_index, 1
    )
    context = (me.astype(jnp.int32).reshape(1), docs)
    both = cross_near(far)
    feed = prepare_feed(place, blocks[0][8], blocks[0][10])
    feed, far = pin(feed, far)
    p_far = cross_far(feed[:, : 2 * half])
    moved_grad = cross_y(jnp.where(y_index == 0, cotangent[1], cotangent[0]))
    raw, place_t, output_t = pin(raw, place, blocks[1][4])
    own_a = prepare_attend(blocks[1][2], output_t)
    feed_t = prepare_feed(place_t, blocks[1][8], blocks[1][10])

    stream = stacked(raw, cross_x(raw))
    stream, near, both, p_far, own_a, feed_t, moved_grad = pin(
        stream, near, both, p_far, own_a, feed_t, moved_grad
    )
    near_s = norm_only(stream)
    gains_s, bias_s, hidden_s, gains_t, bias_t, hidden_t = unpack_vectors(
        (attend, far, near, both), place, local, blocks[0][3].shape, blocks[0][9].shape
    )
    far_s = cross_core(near_s)
    attend_s = (attend, far, near, both)
    e_two = stacked(feed[:, :half], p_far[:, :half])
    e_near = cross_near(e_two)
    r_far = cross_far(feed[:, 2 * half :])
    grad_out = times(
        y_order(jnp.where(y_index == 0, cotangent[0], cotangent[1]), moved_grad, y_index, 0),
        chooser,
        BF16,
    )
    moved_grad = cross_x(grad_out)
    sent, kept, *saved_s, near_s, far_s = attention_forward(
        near_s, far_s, attend_s, bias_s, context, doc_max, (gains_s,)
    )
    sent, e_near, r_far, moved_grad = pin(sent, e_near, r_far, moved_grad)
    e_s = stacked(e_two, e_near)
    e_other = cross_y(e_s)
    r_two = stacked(feed[:, half:], beside(p_far[:, half:], r_far))
    r_near = cross_near(r_two)
    a_far = cross_far(own_a)
    partial = core_sum(kept, cross_core(sent))
    middle_s, near_two_s = add_norm(stream, partial, cross_x(partial), gains_s, 2, gains_s, 3)
    near_two_s, e_other, r_near, a_far, feed_t = pin(near_two_s, e_other, r_near, a_far, feed_t)
    a_two = stacked(own_a, a_far)
    a_near = cross_near(a_two)
    te_far, tr_far = cross_far(feed_t[:, :half]), cross_far(feed_t[:, 2 * half :])
    far_two_s = cross_core(near_two_s)
    feed_s = (near_two_s, far_two_s), ((e_s, e_other), (r_two, r_near), hidden_s)
    sent, kept = feed_forward(*feed_s[0], *feed_s[1])
    partial = core_sum(kept, cross_core(sent))
    between, near_t = add_norm(middle_s, partial, cross_x(partial), gains_s, 5, gains_t, 0)

    near_t, a_near, te_far, tr_far, feed_t = pin(near_t, a_near, te_far, tr_far, feed_t)
    attend_t = (a_two, a_near)
    te_two = stacked(feed_t[:, :half], te_far)
    te_near = cross_near(te_two)
    tr_far_one = cross_far(feed_t[:, half : 2 * half])
    far_t = cross_core(near_t)
    sent, kept, *saved_t = attention_forward(near_t, far_t, attend_t, bias_t, context, doc_max)
    sent, te_near, tr_far_one = pin(sent, te_near, tr_far_one)
    te = stacked(te_two, te_near)
    te_other = cross_y(te)
    tr_two = stacked(feed_t[:, half:], beside(tr_far_one, tr_far))
    tr_near = cross_near(tr_two)
    branch = stacked(grad_out, moved_grad)
    branch_far = cross_core(branch)
    partial = core_sum(kept, cross_core(sent))
    middle_t, near_two_t = add_norm(between, partial, cross_x(partial), gains_t, 2, gains_t, 3)
    near_two_t, te_other, tr_near, branch_far = pin(near_two_t, te_other, tr_near, branch_far)
    far_two_t = cross_core(near_two_t)
    feed_t = (near_two_t, far_two_t), ((te, te_other), (tr_two, tr_near), hidden_t)

    sums = jnp.zeros((16, features), F32)
    sent, kept, active, grad_hidden, hidden_sum_t = feed_backward(
        *feed_t[0], branch, branch_far, *feed_t[1]
    )
    partial = core_sum(kept, cross_core(sent))
    part_r = times_down(stacked(branch, branch_far), active, BF16)
    part_r, partial = pin(part_r, partial)
    r_moved = send_rows(part_r, cross_near)
    part_e = times_down(stacked(near_two_t, far_two_t), grad_hidden, BF16)
    e_moved = send_columns(part_e, cross_y)
    late_t, _ = pin(near_two_t, part_e)
    final_sent, final_kept = feed_forward(late_t, far_two_t, *feed_t[1])
    grad_middle, near_grad, sums = norm_back_near(
        branch, partial, cross_x(partial), middle_t, gains_t, 3, sums, 9
    )
    near_grad, r_moved, e_moved, final_sent, final_kept = pin(
        near_grad, r_moved, e_moved, final_sent, final_kept
    )
    part_e, part_r = keep_columns(part_e, e_moved), keep_rows(part_r, r_moved)
    e_moved = send_rows(part_e, cross_near)
    far_grad = cross_core(near_grad)
    sent, kept, grad_qkv, qkv_sum_t = attention_backward(
        near_grad, far_grad, attend_t, context, saved_t, doc_max
    )
    sent, e_moved, part_r = pin(sent, e_moved, part_r)
    part_e = keep_rows(part_e, e_moved)
    e_moved, r_moved = send_rows(part_e, cross_far), send_rows(part_r, cross_far)
    partial = core_sum(kept, cross_core(sent))
    part_a = beside(
        times_down(stacked(near_t, far_t), grad_qkv, BF16),
        times_down(stacked(near_grad, far_grad), saved_t[1], BF16),
    )
    part_a, a_moved = column_halves(part_a, y_index)
    a_moved = cross_y(a_moved)
    grad_between, branch, sums = norm_back_near(
        grad_middle, partial, cross_x(partial), between, gains_t, 0, sums, 6
    )

    branch, e_moved, r_moved, a_moved = pin(branch, e_moved, r_moved, a_moved)
    part_e, part_r = keep_rows(part_e, e_moved), keep_rows(part_r, r_moved)
    part_a = part_a.astype(F32) + a_moved.astype(F32)
    branch_far = cross_core(branch)
    sent, kept, active, grad_hidden, hidden_sum_s = feed_backward(
        *feed_s[0], branch, branch_far, *feed_s[1]
    )
    partial = core_sum(kept, cross_core(sent))
    feed_r = times_down(stacked(branch, branch_far), active, BF16)
    feed_r, part_a, partial = pin(feed_r, part_a, partial)
    fr_moved, a_moved = send_rows(feed_r, cross_near), send_rows(part_a, cross_near)
    feed_e = times_down(stacked(near_two_s, far_two_s), grad_hidden, BF16)
    fe_moved = send_columns(feed_e, cross_y)
    grad_middle, near_grad, sums = norm_back_near(
        grad_between, partial, cross_x(partial), middle_s, gains_s, 3, sums, 3
    )
    near_grad, a_moved, fr_moved, fe_moved, part_e, part_r = pin(
        near_grad, a_moved, fr_moved, fe_moved, part_e, part_r
    )
    part_a, feed_r, feed_e = (
        keep_rows(part_a, a_moved),
        keep_rows(feed_r, fr_moved),
        keep_columns(feed_e, fe_moved),
    )
    a_moved, fe_moved = send_rows(part_a, cross_far), send_rows(feed_e, cross_near)
    mine_t = beside(part_e, part_r).astype(BF16)
    theirs_t = cross_y(
        beside(mine_t[:, :half], mine_t[:, 2 * half :], mine_t[:, half : 2 * half])
    )
    far_grad = cross_core(near_grad)
    sent, kept, grad_qkv, qkv_sum_s = attention_backward(
        near_grad, far_grad, attend_s, context, saved_s, doc_max
    )
    sent, a_moved, fe_moved, theirs_t, feed_r = pin(sent, a_moved, fe_moved, theirs_t, feed_r)
    mine_at, feed_e = keep_rows(part_a, a_moved), keep_rows(feed_e, fe_moved)
    fr_moved, fe_moved = send_rows(feed_r, cross_far), send_rows(feed_e, cross_far)
    arrived = cross_core(sent)
    across = cross_x(halves_added(kept, arrived))
    grad_a = beside(
        times_down(stacked(near_s, far_s), grad_qkv, BF16),
        times_down(stacked(near_grad, far_grad), saved_s[1], BF16),
    )
    grad_a, y_moved = column_halves(grad_a, y_index)
    y_moved = cross_y(y_moved)
    grad_in, _, sums = norm_back(
        grad_middle, (kept, arrived, across), stream, gains_s, 0, sums, 0
    )
    sums_moved = cross_core(sums)
    input_grad = lax.dot_general(
        grad_in,
        chooser.astype(F32),
        (((1,), (1,)), ((), ())),
        precision=lax.Precision.HIGHEST,
        preferred_element_type=F32,
    )

    def swapped(value):
        first, second = value[:tokens], value[tokens:]
        return cross_y(jnp.where(y_index == 0, second, first))

    def restore(value, received):
        kept = jnp.where(y_index == 0, value[:tokens], value[tokens:])
        return jnp.where(y_index == 0, jnp.stack([kept, received]), jnp.stack([received, kept]))

    grad_moved = swapped(input_grad.astype(BF16))
    y_moved, sums_moved = pin(y_moved, sums_moved)
    grad_a = grad_a.astype(F32) + y_moved.astype(F32)
    y_moved = send_rows(grad_a, cross_near)
    sums = sums + sums_moved
    sums_moved = cross_x(sums)
    final_arrived = cross_core(final_sent)
    fe_moved, fr_moved, mine_at, sums_moved, final_arrived, grad_moved = pin(
        fe_moved, fr_moved, mine_at, sums_moved, final_arrived, grad_moved
    )
    final_across = cross_x(halves_added(final_kept, final_arrived))
    pack = pack_grads(
        sums + sums_moved,
        (qkv_sum_s, qkv_sum_t),
        (hidden_sum_s, hidden_sum_t),
        place,
        local,
        params[3].shape,
        params[9].shape,
    )
    mine_s = beside(keep_rows(feed_e, fe_moved), keep_rows(feed_r, fr_moved), mine_at).astype(BF16)
    pack, mine_s = pin(pack, mine_s)
    pack_moved = cross_y(pack)
    theirs_s = cross_y(
        beside(
            mine_s[:, :half], mine_s[:, 2 * half : 3 * half], mine_s[:, half : 2 * half], mine_s[:, 3 * half :]
        )
    )
    expand_grad_t, reduce_grad_t = finish_feed(mine_t, theirs_t, place, half)
    y_moved, final_across, expand_grad_t = pin(y_moved, final_across, expand_grad_t)
    grad_a = keep_rows(grad_a, y_moved)
    y_moved = send_rows(grad_a, cross_far)
    rows = 2 * tokens
    final = middle_t[:rows] + gains_t[5:6] + final_kept[:rows] + final_across.astype(F32)
    final = final + final_arrived[:rows].astype(F32)
    final = times_across(final.astype(BF16), chooser, BF16)
    y_moved, pack_moved, final = pin(y_moved, pack_moved, final)
    pack = pack + pack_moved
    pack_near = cross_near(pack[2 * ROWS :])
    mine_a = keep_rows(grad_a, y_moved).astype(BF16)
    theirs_a = cross_y(mine_a)
    final_moved = swapped(final)
    merged_grad_t, output_grad_t = finish_attend(
        (), mine_s[:, 3 * half :], theirs_s[:, 3 * half :], place
    )
    pack_near, output_grad_t = pin(pack_near, output_grad_t)
    pack = pack[: 2 * ROWS] + pack_near
    pack_far = cross_far(pack[ROWS:])
    theirs_a, final_moved = pin(theirs_a, final_moved)
    grad_moved = grad_moved.astype(F32)
    merged_grad_s, output_grad_s = finish_attend((), mine_a, theirs_a, place)
    expand_grad_s, reduce_grad_s = finish_feed(
        mine_s[:, : 3 * half], theirs_s[:, : 3 * half], place, half
    )
    vectors = unpack_grads(pack, pack_far, local, params[3].shape, params[9].shape)
    outputs = [restore(final, final_moved), restore(input_grad, grad_moved)]
    for vector, merged, output, expand, reduce in (
        (vectors[:8], merged_grad_s, output_grad_s, expand_grad_s, reduce_grad_s),
        (vectors[8:], merged_grad_t, output_grad_t, expand_grad_t, reduce_grad_t),
    ):
        outputs += [
            vector[0],
            vector[1],
            merged,
            vector[6],
            output,
            vector[2],
            vector[3],
            vector[4],
            expand,
            vector[7],
            reduce,
            vector[5],
        ]
    return tuple(outputs)


def solution(mesh):
    quick = (mesh.shape["dp"], mesh.shape["ctx"], mesh.shape["tp"]) == (4, 2, 4)
    placed = (
        P("dp", ("ctx", "tp"), None),
        P("dp", "ctx"),
        P("dp", ("ctx", "tp"), None),
        P("dp"),
        P("dp"),
        P("dp", None, "tp"),
        P(None, "tp", "dp"),
        P("tp", "dp"),
        P("dp"),
        P("dp"),
        P("dp"),
        P("dp", "tp"),
        P("tp", "dp"),
        P("tp", "dp"),
        P("dp"),
        P("dp"),
        P("dp"),
        P("dp", None, "tp"),
        P(None, "tp", "dp"),
        P("tp", "dp"),
        P("dp"),
        P("dp"),
        P("dp"),
        P("dp", "tp"),
        P("tp", "dp"),
        P("tp", "dp"),
        P("dp"),
    )
    return jax.shard_map(
        fast_shards if quick else general_shards,
        mesh=mesh,
        in_specs=placed,
        out_specs=(
            P("dp", ("ctx", "tp"), None),
            P("dp", ("ctx", "tp"), None),
            P("dp"),
            P("dp"),
            P("dp", None, "tp"),
            P(None, "tp", "dp"),
            P("tp", "dp"),
            P("dp"),
            P("dp"),
            P("dp"),
            P("dp", "tp"),
            P("tp", "dp"),
            P("tp", "dp"),
            P("dp"),
            P("dp"),
            P("dp"),
            P("dp", None, "tp"),
            P(None, "tp", "dp"),
            P("tp", "dp"),
            P("dp"),
            P("dp"),
            P("dp"),
            P("dp", "tp"),
            P("tp", "dp"),
            P("tp", "dp"),
            P("dp"),
        ),
        check_vma=False,
    )
```

```python
import jax
import jax.numpy as jnp
from jax import lax
from jax.experimental import pallas as pl
from jax.experimental.layout import Layout, with_layout_constraint
from jax.experimental.pallas import tpu as pltpu
from jax.sharding import PartitionSpec as P

HD = 64
DOC_MAX = 2000


EPSILON = 1e-05
GELU_SCALE = 0.7978845608028654


def from_behind(block, axis, distance):
    devices = range(lax.axis_size(axis))
    route = [(i - distance, i) for i in devices if i - distance in devices]
    return lax.ppermute(block, axis, route)


def layer_norm(values, norm_gain, norm_shift):
    center = values - jnp.mean(values, axis=-1, keepdims=True)
    spread = jnp.mean(center * center, axis=-1, keepdims=True)
    return center * lax.rsqrt(spread + EPSILON) * norm_gain + norm_shift


def gelu_tanh(values):
    return (
        0.5 * values * (1.0 + jnp.tanh(GELU_SCALE * (values + 0.044715 * values * values * values)))
    )


def spread_rows(row_block):
    return lax.all_gather(row_block, "tp", axis=1, tiled=True)


def gather_sums(partial_value):
    return lax.psum_scatter(
        partial_value.astype(jnp.bfloat16), "tp", scatter_dimension=1, tiled=True
    ).astype(jnp.float32)


def to_items(tensor, head_count):
    batches, length, features = tensor.shape
    head_size = features // head_count
    return (
        tensor.reshape(batches, length, head_count, head_size)
        .transpose(0, 2, 1, 3)
        .reshape(batches * head_count, length, head_size)
    )


def from_items(tensor, head_count):
    item_count, length, head_size = tensor.shape
    batches = item_count // head_count
    return (
        tensor.reshape(batches, head_count, length, head_size)
        .transpose(0, 2, 1, 3)
        .reshape(batches, length, head_count * head_size)
    )


def masked_scores(query_rows, key_rows, query_docs, key_docs, allowed):
    raw_scores = (
        jnp.einsum("qd,kd->qk", query_rows, key_rows, preferred_element_type=jnp.float32) * 0.125
    )
    keep_mask = allowed & (key_docs[None, :] == query_docs[:, None])
    return (jnp.where(keep_mask, raw_scores, -1e30), keep_mask)


def attend_forward(allowed):

    def attend_item(packed):
        query_rows, key_rows, value_rows, query_docs, key_docs = packed
        scores, keep_mask = masked_scores(query_rows, key_rows, query_docs, key_docs, allowed)
        row_top = jnp.max(scores, axis=-1, keepdims=True)
        raised = jnp.exp(scores - row_top)
        row_total = jnp.sum(raised, axis=-1, keepdims=True)
        weights = (raised / row_total).astype(jnp.bfloat16)
        mixed_rows = jnp.dot(weights, value_rows, preferred_element_type=jnp.float32).astype(
            jnp.bfloat16
        )
        return (mixed_rows, row_top[:, 0] + jnp.log(row_total[:, 0]))

    return attend_item


def attend_backward(allowed):

    def attend_item(packed):
        query_rows, key_rows, value_rows, query_docs, key_docs, log_total, grad_rows = packed
        scores, keep_mask = masked_scores(query_rows, key_rows, query_docs, key_docs, allowed)
        weights = jnp.where(keep_mask, jnp.exp(scores - log_total[:, None]), 0.0)
        grad_values = jnp.einsum(
            "qk,qd->kd", weights.astype(jnp.bfloat16), grad_rows, preferred_element_type=jnp.float32
        )
        grad_weights = jnp.einsum(
            "qd,kd->qk", grad_rows, value_rows, preferred_element_type=jnp.float32
        )
        centered = jnp.sum(weights * grad_weights, axis=-1, keepdims=True)
        grad_scores = (weights * (grad_weights - centered)).astype(jnp.bfloat16)
        grad_query = jnp.dot(grad_scores, key_rows, preferred_element_type=jnp.float32) * 0.125
        grad_keys = (
            jnp.einsum("qk,qd->kd", grad_scores, query_rows, preferred_element_type=jnp.float32)
            * 0.125
        )
        return (grad_query, grad_keys, grad_values)

    return attend_item


def layer_forward(stream, params, segments, key_docs, allowed, cycle_steps):
    (
        first_gain,
        first_shift,
        merged_weight,
        merged_bias,
        output_weight,
        output_bias,
        second_gain,
        second_shift,
        expand_weight,
        expand_bias,
        reduce_weight,
        reduce_bias,
    ) = params
    fetched = (
        lax.all_gather(first_gain, "dp", axis=0, tiled=True),
        lax.all_gather(first_shift, "dp", axis=0, tiled=True),
        lax.all_gather(merged_weight, "dp", axis=0, tiled=True),
        lax.all_gather(merged_bias, "dp", axis=2, tiled=True),
        lax.all_gather(output_weight, "dp", axis=1, tiled=True),
        lax.all_gather(output_bias, "dp", axis=0, tiled=True),
        lax.all_gather(second_gain, "dp", axis=0, tiled=True),
        lax.all_gather(second_shift, "dp", axis=0, tiled=True),
        lax.all_gather(expand_weight, "dp", axis=0, tiled=True),
        lax.all_gather(expand_bias, "dp", axis=1, tiled=True),
        lax.all_gather(reduce_weight, "dp", axis=1, tiled=True),
        lax.all_gather(reduce_bias, "dp", axis=0, tiled=True),
    )
    (
        first_gain,
        first_shift,
        merged_weight,
        merged_bias,
        output_weight,
        output_bias,
        second_gain,
        second_shift,
        expand_weight,
        expand_bias,
        reduce_weight,
        reduce_bias,
    ) = fetched
    head_count = merged_weight.shape[2] // HD
    normed = layer_norm(
        stream, first_gain.astype(jnp.float32), first_shift.astype(jnp.float32)
    ).astype(jnp.bfloat16)
    first_rows = spread_rows(normed)
    merged_out = jnp.einsum(
        "std,dkf->stkf", first_rows, merged_weight, preferred_element_type=jnp.float32
    )
    bias_pair = merged_bias.astype(jnp.float32).reshape(2, -1)
    query_rows = (merged_out[:, :, 0] + bias_pair[0]).astype(jnp.bfloat16)
    key_rows = merged_out[:, :, 1].astype(jnp.bfloat16)
    value_rows = (merged_out[:, :, 2] + bias_pair[1]).astype(jnp.bfloat16)
    key_list = [key_rows]
    value_list = [value_rows]
    moving = (key_rows, value_rows)
    for offset in range(cycle_steps):
        moving = from_behind((moving[0], moving[1]), "ctx", 1)
        key_list.insert(0, moving[0])
        value_list.insert(0, moving[1])
    query_items = to_items(query_rows, head_count)
    key_items = to_items(jnp.concatenate(key_list, axis=1), head_count)
    value_items = to_items(jnp.concatenate(value_list, axis=1), head_count)
    query_docs = jnp.repeat(segments, head_count, axis=0)
    window_docs = jnp.repeat(key_docs, head_count, axis=0)
    mixed_items, log_total = lax.map(
        attend_forward(allowed), (query_items, key_items, value_items, query_docs, window_docs)
    )
    mixed = from_items(mixed_items, head_count)
    attn_part = jnp.einsum("stf,fd->std", mixed, output_weight, preferred_element_type=jnp.float32)
    middle = stream + gather_sums(attn_part) + output_bias.astype(jnp.float32)
    normed_two = layer_norm(
        middle, second_gain.astype(jnp.float32), second_shift.astype(jnp.float32)
    ).astype(jnp.bfloat16)
    second_rows = spread_rows(normed_two)
    hidden = jnp.einsum(
        "std,df->stf", second_rows, expand_weight, preferred_element_type=jnp.float32
    ) + expand_bias.astype(jnp.float32).reshape(-1)
    activated = gelu_tanh(hidden).astype(jnp.bfloat16)
    mlp_part = jnp.einsum(
        "stf,fd->std", activated, reduce_weight, preferred_element_type=jnp.float32
    )
    result = middle + gather_sums(mlp_part) + reduce_bias.astype(jnp.float32)
    saved_state = (
        fetched,
        stream,
        first_rows,
        query_items,
        key_items,
        value_items,
        query_docs,
        window_docs,
        log_total,
        mixed,
        middle,
        second_rows,
        hidden,
        activated,
    )
    return (result, saved_state)


def reduce_grads(fresh):
    (
        gain_one,
        shift_one,
        merged_weights,
        merged_biases,
        output_weights,
        output_biases,
        gain_two,
        shift_two,
        expand_weights,
        expand_biases,
        reduce_weights,
        reduce_biases,
    ) = fresh
    summed = (
        lax.psum(gain_one.astype(jnp.bfloat16), "ctx").astype(jnp.float32),
        lax.psum(shift_one.astype(jnp.bfloat16), "ctx").astype(jnp.float32),
        lax.psum(merged_weights.astype(jnp.bfloat16), "ctx").astype(jnp.float32),
        lax.psum(merged_biases.astype(jnp.bfloat16), "ctx").astype(jnp.float32),
        lax.psum(output_weights.astype(jnp.bfloat16), "ctx").astype(jnp.float32),
        lax.psum(output_biases.astype(jnp.bfloat16), "ctx").astype(jnp.float32),
        lax.psum(gain_two.astype(jnp.bfloat16), "ctx").astype(jnp.float32),
        lax.psum(shift_two.astype(jnp.bfloat16), "ctx").astype(jnp.float32),
        lax.psum(expand_weights.astype(jnp.bfloat16), "ctx").astype(jnp.float32),
        lax.psum(expand_biases.astype(jnp.bfloat16), "ctx").astype(jnp.float32),
        lax.psum(reduce_weights.astype(jnp.bfloat16), "ctx").astype(jnp.float32),
        lax.psum(reduce_biases.astype(jnp.bfloat16), "ctx").astype(jnp.float32),
    )
    (
        gain_one,
        shift_one,
        merged_weights,
        merged_biases,
        output_weights,
        output_biases,
        gain_two,
        shift_two,
        expand_weights,
        expand_biases,
        reduce_weights,
        reduce_biases,
    ) = summed
    return (
        lax.psum_scatter(
            gain_one.astype(jnp.bfloat16), "dp", scatter_dimension=0, tiled=True
        ).astype(jnp.float32),
        lax.psum_scatter(
            shift_one.astype(jnp.bfloat16), "dp", scatter_dimension=0, tiled=True
        ).astype(jnp.float32),
        lax.psum_scatter(
            merged_weights.astype(jnp.bfloat16), "dp", scatter_dimension=0, tiled=True
        ).astype(jnp.float32),
        lax.psum_scatter(
            merged_biases.astype(jnp.bfloat16), "dp", scatter_dimension=2, tiled=True
        ).astype(jnp.float32),
        lax.psum_scatter(
            output_weights.astype(jnp.bfloat16), "dp", scatter_dimension=1, tiled=True
        ).astype(jnp.float32),
        lax.psum_scatter(
            output_biases.astype(jnp.bfloat16), "dp", scatter_dimension=0, tiled=True
        ).astype(jnp.float32),
        lax.psum_scatter(
            gain_two.astype(jnp.bfloat16), "dp", scatter_dimension=0, tiled=True
        ).astype(jnp.float32),
        lax.psum_scatter(
            shift_two.astype(jnp.bfloat16), "dp", scatter_dimension=0, tiled=True
        ).astype(jnp.float32),
        lax.psum_scatter(
            expand_weights.astype(jnp.bfloat16), "dp", scatter_dimension=0, tiled=True
        ).astype(jnp.float32),
        lax.psum_scatter(
            expand_biases.astype(jnp.bfloat16), "dp", scatter_dimension=1, tiled=True
        ).astype(jnp.float32),
        lax.psum_scatter(
            reduce_weights.astype(jnp.bfloat16), "dp", scatter_dimension=1, tiled=True
        ).astype(jnp.float32),
        lax.psum_scatter(
            reduce_biases.astype(jnp.bfloat16), "dp", scatter_dimension=0, tiled=True
        ).astype(jnp.float32),
    )


def layer_backward(grad_out, saved_state, allowed, cycle_steps, token_count):
    (
        fetched,
        stream,
        first_rows,
        query_items,
        key_items,
        value_items,
        query_docs,
        window_docs,
        log_total,
        mixed,
        middle,
        second_rows,
        hidden,
        activated,
    ) = saved_state
    (
        first_gain,
        first_shift,
        merged_weight,
        merged_bias,
        output_weight,
        output_bias,
        second_gain,
        second_shift,
        expand_weight,
        expand_bias,
        reduce_weight,
        reduce_bias,
    ) = fetched
    head_count = merged_weight.shape[2] // HD
    grad_branch = spread_rows(grad_out.astype(jnp.bfloat16))
    grad_reduce = jnp.einsum(
        "stf,std->fd", activated, grad_branch, preferred_element_type=jnp.float32
    )
    grad_active = jnp.einsum(
        "std,fd->stf", grad_branch, reduce_weight, preferred_element_type=jnp.float32
    )
    _, gelu_pull = jax.vjp(gelu_tanh, hidden)
    grad_hidden = gelu_pull(grad_active)[0].astype(jnp.bfloat16)
    grad_expand_bias = jnp.sum(grad_hidden, axis=(0, 1), dtype=jnp.float32).reshape(
        expand_bias.shape
    )
    grad_expand = jnp.einsum(
        "std,stf->df", second_rows, grad_hidden, preferred_element_type=jnp.float32
    )
    grad_second = gather_sums(
        jnp.einsum("stf,df->std", grad_hidden, expand_weight, preferred_element_type=jnp.float32)
    )
    _, second_pull = jax.vjp(
        layer_norm, middle, second_gain.astype(jnp.float32), second_shift.astype(jnp.float32)
    )
    grad_norm_mid, grad_second_gain, grad_second_shift = second_pull(grad_second)
    grad_middle = grad_out + grad_norm_mid
    grad_reduce_bias = jnp.sum(grad_out, axis=(0, 1))
    grad_attend = spread_rows(grad_middle.astype(jnp.bfloat16))
    grad_output = jnp.einsum("stf,std->fd", mixed, grad_attend, preferred_element_type=jnp.float32)
    grad_mixed = jnp.einsum(
        "std,fd->stf", grad_attend, output_weight, preferred_element_type=jnp.float32
    ).astype(jnp.bfloat16)
    grad_query_items, grad_key_items, grad_value_items = lax.map(
        attend_backward(allowed),
        (
            query_items,
            key_items,
            value_items,
            query_docs,
            window_docs,
            log_total,
            to_items(grad_mixed, head_count),
        ),
    )
    grad_query = from_items(grad_query_items, head_count)
    window_keys = from_items(grad_key_items, head_count)
    window_values = from_items(grad_value_items, head_count)
    local_keys = window_keys[:, cycle_steps * token_count :]
    local_values = window_values[:, cycle_steps * token_count :]
    carried = None
    for offset in range(cycle_steps, 0, -1):
        start_row = (cycle_steps - offset) * token_count
        block_keys = window_keys[:, start_row : start_row + token_count]
        block_values = window_values[:, start_row : start_row + token_count]
        if carried is not None:
            block_keys = block_keys + carried[0]
            block_values = block_values + carried[1]
        carried = (
            from_behind(block_keys.astype(jnp.bfloat16), "ctx", -1).astype(block_keys.dtype),
            from_behind(block_values.astype(jnp.bfloat16), "ctx", -1).astype(block_values.dtype),
        )
    local_keys = local_keys + carried[0]
    local_values = local_values + carried[1]
    grad_merged = jnp.stack([grad_query, local_keys, local_values], axis=2).astype(jnp.bfloat16)
    grad_merged_bias = jnp.stack(
        [
            jnp.sum(grad_merged[:, :, 0], axis=(0, 1), dtype=jnp.float32),
            jnp.sum(grad_merged[:, :, 2], axis=(0, 1), dtype=jnp.float32),
        ]
    ).reshape(merged_bias.shape)
    grad_merged_weight = jnp.einsum(
        "std,stkf->dkf", first_rows, grad_merged, preferred_element_type=jnp.float32
    )
    grad_first = gather_sums(
        jnp.einsum("stkf,dkf->std", grad_merged, merged_weight, preferred_element_type=jnp.float32)
    )
    _, first_pull = jax.vjp(
        layer_norm, stream, first_gain.astype(jnp.float32), first_shift.astype(jnp.float32)
    )
    grad_norm_in, grad_first_gain, grad_first_shift = first_pull(grad_first)
    grad_input = grad_middle + grad_norm_in
    grad_output_bias = jnp.sum(grad_middle, axis=(0, 1))
    vector_grads = lax.psum(
        (
            grad_first_gain,
            grad_first_shift,
            grad_second_gain,
            grad_second_shift,
            grad_output_bias,
            grad_reduce_bias,
        ),
        "tp",
    )
    fresh = (
        vector_grads[0],
        vector_grads[1],
        grad_merged_weight,
        grad_merged_bias,
        grad_output,
        vector_grads[4],
        vector_grads[2],
        vector_grads[3],
        grad_expand,
        grad_expand_bias,
        grad_reduce,
        vector_grads[5],
    )
    return (grad_input, reduce_grads(fresh))


def general_shards(
    inputs,
    segments,
    cotangent,
    student_first_gain,
    student_first_shift,
    student_merged_weight,
    student_merged_bias,
    student_output_weight,
    student_output_bias,
    student_second_gain,
    student_second_shift,
    student_expand_weight,
    student_expand_bias,
    student_reduce_weight,
    student_reduce_bias,
    teacher_first_gain,
    teacher_first_shift,
    teacher_merged_weight,
    teacher_merged_bias,
    teacher_output_weight,
    teacher_output_bias,
    teacher_second_gain,
    teacher_second_shift,
    teacher_expand_weight,
    teacher_expand_bias,
    teacher_reduce_weight,
    teacher_reduce_bias,
):
    student = (
        student_first_gain,
        student_first_shift,
        student_merged_weight,
        student_merged_bias,
        student_output_weight,
        student_output_bias,
        student_second_gain,
        student_second_shift,
        student_expand_weight,
        student_expand_bias,
        student_reduce_weight,
        student_reduce_bias,
    )
    teacher = (
        teacher_first_gain,
        teacher_first_shift,
        teacher_merged_weight,
        teacher_merged_bias,
        teacher_output_weight,
        teacher_output_bias,
        teacher_second_gain,
        teacher_second_shift,
        teacher_expand_weight,
        teacher_expand_bias,
        teacher_reduce_weight,
        teacher_reduce_bias,
    )
    token_count = segments.shape[1]
    context_size = lax.axis_size("ctx")
    context_index = lax.axis_index("ctx")
    doc_long = min(DOC_MAX, token_count * context_size // 2)
    cycle_steps = min((doc_long - 2) // token_count + 1, context_size - 1)
    doc_list = [segments]
    moving = segments
    for offset in range(cycle_steps):
        moving = from_behind(moving, "ctx", 1)
        doc_list.insert(0, moving)
    key_docs = jnp.concatenate(doc_list, axis=1)
    places = jnp.arange((cycle_steps + 1) * token_count, dtype=jnp.int32)
    relative = places - cycle_steps * token_count
    source = cycle_steps - places // token_count
    query_place = jnp.arange(token_count, dtype=jnp.int32)
    allowed = (relative[None, :] <= query_place[:, None]) & (source <= context_index)[None, :]
    stream = inputs.astype(jnp.float32)
    middle_stream, student_saved = layer_forward(
        stream, student, segments, key_docs, allowed, cycle_steps
    )
    final_stream, teacher_saved = layer_forward(
        middle_stream, teacher, segments, key_docs, allowed, cycle_steps
    )
    teacher_in_grad, teacher_grads = layer_backward(
        cotangent.astype(jnp.float32), teacher_saved, allowed, cycle_steps, token_count
    )
    input_grad, student_grads = layer_backward(
        teacher_in_grad, student_saved, allowed, cycle_steps, token_count
    )
    return (
        (final_stream.astype(jnp.bfloat16), input_grad)
        + tuple(student_grads)
        + tuple(teacher_grads)
    )


BF16 = jnp.bfloat16
F32 = jnp.float32
NEG = -1e30
TILE = 256
RELATIVE = (0, 2, 1, 3)


def row_major(value):
    return with_layout_constraint(value, Layout(major_to_minor=tuple(range(value.ndim))))


def swap(value, axis, bit):
    route = [(i, i ^ bit) for i in range(lax.axis_size(axis))]
    if value.ndim == 2:
        return row_major(lax.ppermute(row_major(value), axis, route))
    return lax.ppermute(value, axis, route)


def cross_core(value):
    return swap(value, "tp", 1)


def cross_x(value):
    return swap(value, "tp", 2)


def cross_y(value):
    return swap(value, "ctx", 1)


def cross_near(value):
    return swap(value, "dp", 1)


def cross_far(value):
    return swap(value, "dp", 2)


def cross_both(value):
    return swap(value, "dp", 3)


def stacked(*values):
    return jnp.concatenate(values, axis=0)


def beside(*values):
    return jnp.concatenate(values, axis=1)


def y_order(own, other, y_index, axis):
    return jnp.where(
        y_index == 0,
        jnp.concatenate([own, other], axis=axis),
        jnp.concatenate([other, own], axis=axis),
    )


def pin(*values):
    return lax.optimization_barrier(values)


def window_start(block, doc_max):
    return max(0, (block * TILE - doc_max + 1) // TILE) * TILE


def upright(line):
    size = line.shape[1]
    rows = lax.broadcasted_iota(jnp.int32, (size, size), 0)
    columns = lax.broadcasted_iota(jnp.int32, (size, size), 1)
    return jnp.sum(jnp.where(rows == columns, line, 0.0), axis=1, keepdims=True)


def join(pieces, whole):
    row, column = 0, 0
    most = whole.shape[0] * whole.shape[1] // sum(piece.shape[1] for piece in pieces)
    for piece in pieces:
        rows = min(piece.shape[0], most) if len(pieces) == 4 else piece.shape[0]
        whole[row : row + rows, column : column + piece.shape[1]] = piece[:rows, :]
        row += rows
        if row == whole.shape[0]:
            row, column = 0, column + piece.shape[1]


def dot_across(left, right):
    return lax.dot_general(left, right, (((1,), (1,)), ((), ())), preferred_element_type=F32)


def dot_down(left, right):
    return lax.dot_general(left, right, (((0,), (0,)), ((), ())), preferred_element_type=F32)


def token_place(me, member, half, rows):
    return pl.multiple_of((half * 4 + (me ^ (2 * (member & 1) + (member >> 1)))) * rows, rows)


def flat(column):
    size = column.shape[0]
    rows = lax.broadcasted_iota(jnp.int32, (size, size), 0)
    columns = lax.broadcasted_iota(jnp.int32, (size, size), 1)
    return jnp.sum(jnp.where(rows == columns, column, 0.0), axis=0, keepdims=True)


def fill_masks_across(docs, masks, doc_max):
    for block in range(docs.shape[1] // TILE):
        start, stop = window_start(block, doc_max), (block + 1) * TILE
        here = slice(block * TILE, stop)
        rows = block * TILE + lax.broadcasted_iota(jnp.int32, (TILE, stop - start), 0)
        columns = start + lax.broadcasted_iota(jnp.int32, (TILE, stop - start), 1)
        same = upright(docs[:, here]) == docs[:, start:stop]
        masks[here, : stop - start] = jnp.where(same & (columns <= rows), 0.0, NEG)


def mask_columns(length, doc_max):
    return max((block + 1) * TILE - window_start(block, doc_max) for block in range(length // TILE))


def fill_masks(docs, masks, doc_max):
    at = 0
    for block in range(docs.shape[1] // TILE):
        start = window_start(block, doc_max)
        size = (block + 1) * TILE - start
        for first in range(0, size, TILE):
            keys = slice(start + first, start + first + TILE)
            same = upright(docs[:, keys]) == docs[:, block * TILE : (block + 1) * TILE]
            if start + first == block * TILE:
                rows = lax.broadcasted_iota(jnp.int32, (TILE, TILE), 0)
                columns = lax.broadcasted_iota(jnp.int32, (TILE, TILE), 1)
                same = same & (rows <= columns)
            masks[at : at + TILE, :] = jnp.where(same, 0.0, NEG)
            at += TILE


def mask_rows(length, doc_max):
    return sum(
        (block + 1) * TILE - window_start(block, doc_max) for block in range(length // TILE)
    )


def split_heads(value, target, first, me, member):
    rows = value.shape[0] // 2
    for half in range(2):
        place = pl.ds(token_place(me, member, half, rows), rows)
        for j in range(value.shape[1] // HD):
            target[first + j, place, :] = value[half * rows : (half + 1) * rows, j * HD : (j + 1) * HD]


def merge_heads(source, me, member, rows):
    return jnp.concatenate(
        [
            jnp.concatenate(
                [
                    source[j, pl.ds(token_place(me, member, half, rows), rows), :]
                    for j in range(source.shape[0])
                ],
                axis=1,
            )
            for half in range(2)
        ],
        axis=0,
    )


def by_member(count, step):
    for i in range(count):
        step(i)


def attention_forward_kernel(
    heads,
    doc_max,
    count,
    scaled,
    me_ref,
    near_ref,
    far_ref,
    bias_ref,
    docs,
    *refs,
):
    mixed, attend_ref, masks = refs[-3:]
    refs = refs[:-3]
    sources = (near_ref, far_ref)
    if scaled:
        gains, refs, normed = refs[0], refs[1:-2], refs[-2:]
        for source, target in zip(sources, normed):
            target[...] = (source[...].astype(F32) * gains[0:1, :] + gains[1:2, :]).astype(BF16)
        sources = normed
    pieces, (sent_ref, kept_ref, split_ref, mixed_ref, log_ref) = refs[:count], refs[count:]
    join(pieces, attend_ref)
    fill_masks_across(docs, masks, doc_max)
    me = me_ref[0]
    width = heads * HD
    size = near_ref.shape[0] // 2
    length = 4 * size
    for source, first in zip(sources, (0, 2)):

        def project(i, source=source, first=first):
            at = pl.ds(pl.multiple_of(i * size, size), size)
            value = jnp.dot(source[at, :], attend_ref[:, : 3 * width], preferred_element_type=F32)
            value = (value + bias_ref[...]).astype(BF16)
            split_heads(value[:, :width] * BF16(0.125), split_ref, 0, me, first + i)
            split_heads(value[:, width:], split_ref, heads, me, first + i)

        by_member(2, project)

    def attend(h):
        for block in range(length // TILE):
            start, stop = window_start(block, doc_max), (block + 1) * TILE
            here = slice(block * TILE, stop)
            key, value = split_ref[heads + h, start:stop, :], split_ref[2 * heads + h, start:stop, :]
            scores = dot_across(split_ref[h, here, :], key) + masks[here, : stop - start]
            top = jnp.max(scores, axis=1, keepdims=True)
            raised = jnp.exp(scores - top)
            total = jnp.sum(raised, axis=1, keepdims=True)
            product = jnp.dot(raised.astype(BF16), value, preferred_element_type=F32)
            mixed[h, here, :] = (product * (1.0 / total)).astype(BF16)
            log_ref[h, :, here] = flat(top + jnp.log(total))

    lax.fori_loop(0, heads, lambda h, carry: (attend(h), carry)[1], 0)
    for out, first in ((sent_ref, 2), (kept_ref, 0)):

        def finish(i, out=out, first=first):
            rows = merge_heads(mixed, me, first + i, size // 2)
            mixed_ref[pl.ds(pl.multiple_of((first + i) * size, size), size), :] = rows
            at = pl.ds(pl.multiple_of(i * size, size), size)
            out[at, :] = dot_across(rows, attend_ref[:, 3 * width :]).astype(out.dtype)

        by_member(2, finish)


def attention_backward_kernel(
    heads,
    doc_max,
    count,
    me_ref,
    near_ref,
    far_ref,
    docs,
    split_ref,
    log_ref,
    *refs,
):
    pieces, (sent_ref, kept_ref, out_ref, sum_ref) = refs[:count], refs[count:-4]
    grad, total, attend_ref, masks = refs[-4:]
    join(pieces, attend_ref)
    fill_masks(docs, masks, doc_max)
    me = me_ref[0]
    width = heads * HD
    size = near_ref.shape[0] // 2
    length = 4 * size
    for source, first in ((near_ref, 0), (far_ref, 2)):

        def project(i, source=source, first=first):
            at = pl.ds(pl.multiple_of(i * size, size), size)
            value = jnp.dot(source[at, :], attend_ref[:, 3 * width :], preferred_element_type=F32)
            split_heads(value.astype(BF16), grad, 0, me, first + i)

        by_member(2, project)

    def attend(h):
        total[heads + h] = jnp.zeros((length, HD), F32)
        total[2 * heads + h] = jnp.zeros((length, HD), F32)
        at = 0
        for block in range(length // TILE):
            start, stop = window_start(block, doc_max), (block + 1) * TILE
            here, window = slice(block * TILE, stop), slice(start, stop)
            query, key, value = (
                split_ref[h, here, :],
                split_ref[heads + h, window, :],
                split_ref[2 * heads + h, window, :],
            )
            grad_rows = grad[h, here, :]
            scores = dot_across(key, query) + masks[at : at + stop - start, :]
            at += stop - start
            weights = jnp.exp(scores - log_ref[h, :, here])
            weighted = weights * dot_across(value, grad_rows)
            centered = jnp.sum(weighted, axis=0, keepdims=True)
            grad_scores = (weighted - weights * centered).astype(BF16)
            total[2 * heads + h, window, :] += jnp.dot(
                weights.astype(BF16), grad_rows, preferred_element_type=F32
            )
            total[heads + h, window, :] += jnp.dot(
                grad_scores, query, preferred_element_type=F32
            )
            total[h, here, :] = dot_down(key, grad_scores).T * 0.125

    lax.fori_loop(0, heads, lambda h, carry: (attend(h), carry)[1], 0)
    sum_ref[...] = jnp.zeros_like(sum_ref)
    for out, first in ((sent_ref, 2), (kept_ref, 0)):

        def finish(i, out=out, first=first):
            rows = merge_heads(total, me, first + i, size // 2).astype(BF16)
            out_ref[pl.ds(pl.multiple_of((first + i) * size, size), size), :] = rows
            sum_ref[...] += jnp.sum(rows.astype(F32), axis=0, keepdims=True)
            at = pl.ds(pl.multiple_of(i * size, size), size)
            out[at, :] = dot_across(rows, attend_ref[:, : 3 * width]).astype(out.dtype)

        by_member(2, finish)


VMEM = pl.BlockSpec(memory_space=pltpu.VMEM)
SMEM = pl.BlockSpec(memory_space=pltpu.SMEM)


def call(body, name, inputs, outputs, scratch, flops, transcendentals, limit=24):
    size = sum(v.size * v.dtype.itemsize for v in list(inputs) + list(outputs))
    return pl.pallas_call(
        body,
        out_shape=tuple(outputs),
        in_specs=[SMEM if v.ndim == 1 else VMEM for v in inputs],
        out_specs=tuple(VMEM for _ in outputs),
        scratch_shapes=scratch,
        cost_estimate=pl.CostEstimate(
            flops=flops, transcendentals=transcendentals, bytes_accessed=size
        ),
        compiler_params=pltpu.CompilerParams(vmem_limit_bytes=limit << 20),
        name=name,
    )(*inputs)


def shaped(rows, columns, kind):
    return jax.ShapeDtypeStruct((rows, columns), kind)


def attention_forward(near, far, attend, bias, context, doc_max, gains=()):
    me, docs = context
    half, features = near.shape
    width = bias.shape[1] // 3
    heads = width // HD
    area = heads * 2 * half * half

    def body(*refs):
        attention_forward_kernel(heads, doc_max, len(attend), len(gains) > 0, *refs)

    return call(
        body,
        "attention_forward",
        (me, near, far, bias, docs) + tuple(gains) + tuple(attend),
        (
            shaped(half, features, BF16),
            shaped(half, features, F32),
            jax.ShapeDtypeStruct((3 * heads, 2 * half, HD), BF16),
            shaped(2 * half, width, BF16),
            jax.ShapeDtypeStruct((heads, 1, 2 * half), F32),
        )
        + (shaped(half, features, BF16),) * (2 * len(gains)),
        [
            pltpu.VMEM((heads, 2 * half, HD), BF16),
            pltpu.VMEM((features, 4 * width), BF16),
            pltpu.VMEM((2 * half, mask_columns(2 * half, doc_max)), F32),
        ],
        16 * HD * area,
        area,
    )


def attention_backward(near, far, attend, context, saved, doc_max):
    me, docs = context
    split, _, log_total = saved
    half, features = near.shape
    heads = split.shape[0] // 3
    width = heads * HD
    area = heads * 2 * half * half

    def body(*refs):
        attention_backward_kernel(heads, doc_max, len(attend), *refs)

    return call(
        body,
        "attention_backward",
        (me, near, far, docs, split, log_total) + tuple(attend),
        (
            shaped(half, features, BF16),
            shaped(half, features, F32),
            shaped(2 * half, 3 * width, BF16),
            shaped(1, 3 * width, F32),
        ),
        [
            pltpu.VMEM((heads, 2 * half, HD), BF16),
            pltpu.VMEM((3 * heads, 2 * half, HD), F32),
            pltpu.VMEM((features, 4 * width), BF16),
            pltpu.VMEM((mask_rows(2 * half, doc_max), TILE), F32),
        ],
        40 * HD * area,
        area,
    )


CHUNK = 256


def gelu_both(values):
    inner = GELU_SCALE * (values + 0.044715 * values * values * values)
    bent = jnp.tanh(inner)
    value = 0.5 * values * (1.0 + bent)
    slope = 0.5 * (1.0 + bent) + 0.5 * values * (1.0 - bent * bent) * GELU_SCALE * (
        1.0 + 3.0 * 0.044715 * values * values
    )
    return value, slope


def feed_forward_kernel(count, piece, bias_ref, *refs):
    out, expand_ref, reduce_ref = refs[-3:]
    join(refs[:count], expand_ref)
    join(refs[count:-3], reduce_ref)

    def step(i, carry):
        at = pl.ds(pl.multiple_of(i * CHUNK, CHUNK), CHUNK)
        hidden = jnp.dot(piece[at, :], expand_ref[...], preferred_element_type=F32)
        active = gelu_tanh(hidden + bias_ref[...]).astype(BF16)
        out[at, :] = dot_across(active, reduce_ref[...]).astype(out.dtype)
        return carry

    lax.fori_loop(0, piece.shape[0] // CHUNK, step, 0)


def feed_rows(piece, weights, kind):
    expand, reduce, bias = weights
    rows, features = piece.shape
    hidden = bias.shape[1]

    def body(*refs):
        feed_forward_kernel(len(expand), *refs)

    return call(
        body,
        "feed_forward",
        (piece, bias) + tuple(expand) + tuple(reduce),
        (shaped(rows, features, kind),),
        [pltpu.VMEM((features, hidden), BF16), pltpu.VMEM((features, hidden), BF16)],
        4 * rows * features * hidden,
        rows * hidden,
    )[0]


def feed_forward(near, far, expand, reduce, bias):
    weights = expand, reduce, bias
    return feed_rows(far, weights, BF16), feed_rows(near, weights, F32)


def feed_backward_kernel(count, piece, grads, bias_ref, *refs):
    out, active_ref, hidden_ref, sum_ref, expand_ref, reduce_ref = refs[-6:]
    join(refs[:count], expand_ref)
    join(refs[count:-6], reduce_ref)
    sum_ref[...] = jnp.zeros_like(sum_ref)

    def step(i, carry):
        at = pl.ds(pl.multiple_of(i * CHUNK, CHUNK), CHUNK)
        hidden = jnp.dot(piece[at, :], expand_ref[...], preferred_element_type=F32)
        value, slope = gelu_both(hidden + bias_ref[...])
        active_ref[at, :] = value.astype(BF16)
        grad_active = jnp.dot(grads[at, :], reduce_ref[...], preferred_element_type=F32)
        grad_hidden = (grad_active * slope).astype(BF16)
        hidden_ref[at, :] = grad_hidden
        sum_ref[...] += jnp.sum(grad_hidden.astype(F32), axis=0, keepdims=True)
        out[at, :] = dot_across(grad_hidden, expand_ref[...]).astype(out.dtype)
        return carry

    lax.fori_loop(0, piece.shape[0] // CHUNK, step, 0)


def feed_back_rows(piece, grads, weights, kind):
    expand, reduce, bias = weights
    rows, features = piece.shape
    hidden = bias.shape[1]

    def body(*refs):
        feed_backward_kernel(len(expand), *refs)

    return call(
        body,
        "feed_backward",
        (piece, grads, bias) + tuple(expand) + tuple(reduce),
        (
            shaped(rows, features, kind),
            shaped(rows, hidden, BF16),
            shaped(rows, hidden, BF16),
            shaped(1, hidden, F32),
        ),
        [pltpu.VMEM((features, hidden), BF16), pltpu.VMEM((features, hidden), BF16)],
        6 * rows * features * hidden,
        rows * hidden,
    )


def feed_backward(near, far, near_grad, far_grad, expand, reduce, bias):
    weights = expand, reduce, bias
    sent, far_active, far_hidden, far_sum = feed_back_rows(far, far_grad, weights, BF16)
    kept, active, hidden, sums = feed_back_rows(near, near_grad, weights, F32)
    return (
        sent,
        kept,
        jnp.concatenate([active, far_active], axis=0),
        jnp.concatenate([hidden, far_hidden], axis=0),
        sums + far_sum,
    )


def row_block(rows, columns):
    return pl.BlockSpec((rows, columns), lambda i: (0, 0))


def row_call(body, name, inputs, rows, outputs):
    specs = [row_block(v.shape[0] if v.shape[0] <= 16 else rows, v.shape[1]) for v in inputs]
    size = sum(rows * v.shape[1] * v.dtype.itemsize for v in inputs)
    return pl.pallas_call(
        body,
        grid=(1,),
        out_shape=tuple(outputs),
        in_specs=specs,
        out_specs=tuple(row_block(*v.shape) for v in outputs),
        cost_estimate=pl.CostEstimate(
            flops=20 * rows * inputs[0].shape[1], transcendentals=rows, bytes_accessed=2 * size
        ),
        compiler_params=pltpu.CompilerParams(vmem_limit_bytes=18 << 20),
        name=name,
    )(*inputs)


STEP = 128


def add_norm(base, partial, across, vectors, bias_at, norm_vectors, norm_at):
    rows, columns = base.shape

    def body(base_ref, bias_ref, vector_ref, partial_ref, across_ref, sum_ref, norm_ref):
        bias = bias_ref[bias_at : bias_at + 1, :]
        gain, shift = vector_ref[norm_at : norm_at + 1, :], vector_ref[norm_at + 1 : norm_at + 2, :]

        def step(i, carry):
            here = pl.ds(pl.multiple_of(i * STEP, STEP), STEP)
            there = pl.ds(pl.multiple_of((i * STEP + rows // 2) % rows, STEP), STEP)
            total = partial_ref[here, :].astype(F32) + across_ref[there, :].astype(F32)
            total = base_ref[here, :].astype(F32) + bias + total
            sum_ref[here, :] = total
            norm_ref[here, :] = (normalize(total)[0] * gain + shift).astype(BF16)
            return carry

        lax.fori_loop(0, rows // STEP, step, 0)

    return row_call(
        body,
        "add_norm",
        [base, vectors, norm_vectors, partial, across],
        rows,
        (shaped(rows, columns, F32), shaped(rows, columns, BF16)),
    )


def norm_back_near(skip, partial, across, value, vectors, norm_at, sums, sums_at):
    rows, columns = skip.shape

    def body(skip_ref, value_ref, vector_ref, old_ref, partial_ref, across_ref, *outs):
        grad_ref, low_ref, sum_ref = outs
        gain = vector_ref[norm_at : norm_at + 1, :]
        sum_ref[...] = old_ref[...]

        def step(i, own):
            here = pl.ds(pl.multiple_of(i * STEP, STEP), STEP)
            there = pl.ds(pl.multiple_of((i * STEP + rows // 2) % rows, STEP), STEP)
            grad = partial_ref[here, :].astype(F32) + across_ref[there, :].astype(F32)
            unit, scale = normalize(value_ref[here, :].astype(F32))
            skipped = skip_ref[here, :].astype(F32)
            if own:
                for j, each in enumerate((grad * unit, grad, skipped)):
                    sum_ref[sums_at + j : sums_at + j + 1, :] += jnp.sum(each, axis=0, keepdims=True)
            total = skipped + norm_pullback(grad, unit, scale, gain)
            grad_ref[here, :] = total
            low_ref[here, :] = total.astype(BF16)

        count = rows // STEP // 2
        lax.fori_loop(0, count, lambda i, carry: (step(i, True), carry)[1], 0)
        lax.fori_loop(count, 2 * count, lambda i, carry: (step(i, False), carry)[1], 0)

    return row_call(
        body,
        "norm_back_near",
        [skip, value, vectors, sums, partial, across],
        rows,
        (shaped(rows, columns, F32), shaped(rows, columns, BF16), shaped(16, columns, F32)),
    )


def norm_only(values):
    rows, columns = values.shape

    def body(value_ref, unit_ref):
        unit_ref[...] = normalize(value_ref[...].astype(F32))[0].astype(BF16)

    return row_call(body, "norm_only", [values], rows, (shaped(rows, columns, BF16),))[0]


def norm_back(skip, addends, value, vectors, norm_at, sums, sums_at):
    rows, columns = addends[-1].shape

    def body(*refs):
        skip_ref, value_ref, vector_ref, old_ref = refs[:4]
        parts, (grad_ref, low_ref, sum_ref) = refs[4:-3], refs[-3:]
        grad = parts[0][...].astype(F32)
        for part in parts[1:]:
            grad = grad + part[...].astype(F32)
        unit, scale = normalize(value_ref[...].astype(F32))
        skipped = skip_ref[...]
        sum_ref[...] = old_ref[...]
        for i, each in enumerate((grad * unit, grad, skipped)):
            sum_ref[sums_at + i : sums_at + i + 1, :] = jnp.sum(each, axis=0, keepdims=True)
        total = skipped + norm_pullback(grad, unit, scale, vector_ref[norm_at : norm_at + 1, :])
        grad_ref[...] = total
        low_ref[...] = total.astype(BF16)

    return row_call(
        body,
        "norm_back",
        [skip, value, vectors, sums] + list(addends),
        rows,
        (shaped(rows, columns, F32), shaped(rows, columns, BF16), shaped(16, columns, F32)),
    )


def normalize(values):
    center = values - jnp.mean(values, axis=-1, keepdims=True)
    spread = jnp.mean(center * center, axis=-1, keepdims=True)
    scale = lax.rsqrt(spread + EPSILON)
    return center * scale, scale


def norm_rows(values, gain, shift):
    return (normalize(values)[0] * gain + shift).astype(BF16)


def norm_pullback(grad, unit, scale, gain):
    inner = grad * gain
    return scale * (
        inner
        - jnp.mean(inner, axis=-1, keepdims=True)
        - unit * jnp.mean(inner * unit, axis=-1, keepdims=True)
    )


def times(left, right, kind=F32):
    return jnp.dot(left, right, preferred_element_type=F32).astype(kind)


def times_across(left, right, kind=F32):
    return dot_across(left, right).astype(kind)


def times_down(left, right, kind=F32):
    return row_major(dot_down(left, right).astype(kind))


def gather_rows(rows):
    near = stacked(rows, cross_x(rows))
    return near, cross_core(near)


def add_half(value, cross):
    middle = value.shape[0] // 2
    return value[:middle].astype(F32) + cross(value[middle:].astype(BF16)).astype(F32)


def add_columns(value, cross):
    middle = value.shape[1] // 2
    return value[:, :middle].astype(F32) + cross(value[:, middle:].astype(BF16)).astype(F32)


def column_halves(shard, y_index):
    middle = shard.shape[1] // 2
    own = jnp.where(y_index == 0, shard[:, :middle], shard[:, middle:])
    other = jnp.where(y_index == 0, shard[:, middle:], shard[:, :middle])
    return own, other


def natural_columns(own, other, y_index):
    return jnp.where(y_index == 0, beside(own, other), beside(other, own))


def order_matrix(width, z_index):
    rows = width // 4
    natural = lax.broadcasted_iota(jnp.int32, (width, width), 0)
    place = lax.broadcasted_iota(jnp.int32, (width, width), 1)
    step, inner = place // rows, place % rows
    distance = 2 * (step & 1) + (step >> 1)
    return (natural == (z_index ^ distance) * rows + inner).astype(BF16)


def my_rows(pair, y_index):
    own = jnp.where(y_index == 0, pair[0], pair[1])
    sent = jnp.where(y_index == 0, pair[1], pair[0])
    return y_order(own, cross_y(sent), y_index, 0)


ROWS = 64
SPARE = ROWS // 4


def turn(value):
    size = value.shape[0]
    eye = (
        lax.broadcasted_iota(jnp.int32, (size, size), 0)
        == lax.broadcasted_iota(jnp.int32, (size, size), 1)
    ).astype(BF16)
    return dot_down(value, eye)


def pack_vectors(blocks, place):
    flat = []
    for gains, merged_bias, expand_bias in blocks:
        flat += list(gains) + [merged_bias.transpose(1, 0, 2), expand_bias]

    number = len(flat)

    def body(*refs):
        refs = refs[1:]
        out, part, sem = refs[number], refs[number + 1 : -1], refs[-1]
        copies = [
            pltpu.make_async_copy(refs[i], part[i], sem.at[i]) for i in range(number)
        ]
        for copy in copies:
            copy.start()
        out[...] = jnp.zeros_like(out)
        for copy in copies:
            copy.wait()
        for b in range(2):
            vectors, merged_bias, expand_bias = part[8 * b : 8 * b + 6], part[8 * b + 6], part[8 * b + 7]
            for i in range(6):
                local = vectors[i].shape[0]
                out[6 * b + i : 6 * b + i + 1, :local] = vectors[i][...].astype(F32).reshape(1, local)
            for h in range(merged_bias.shape[0]):
                value = merged_bias[h].astype(F32)
                out[16 + 8 * b + 2 * h : 18 + 8 * b + 2 * h, : value.shape[1]] = value
            value = expand_bias[...].astype(F32)
            out[32 + 16 * b : 32 + 16 * b + value.shape[0], : value.shape[1]] = value

    return pl.pallas_call(
        body,
        out_shape=shaped(ROWS, 256, F32),
        in_specs=[SMEM] + [pl.BlockSpec(memory_space=pltpu.HBM)] * number,
        out_specs=VMEM,
        scratch_shapes=[pltpu.VMEM(v.shape, v.dtype) for v in flat]
        + [pltpu.SemaphoreType.DMA((number,))],
        compiler_params=pltpu.CompilerParams(vmem_limit_bytes=60 << 20),
        name="pack_vectors",
    )(place, *flat)


def prepare_first(place, merged, output, blocks):
    flat = []
    for gains, merged_bias, expand_bias in blocks:
        flat += list(gains) + [merged_bias.transpose(1, 0, 2), expand_bias]
    flat += [merged.transpose(1, 0, 2), output]
    number = len(flat)
    local = output.shape[1]

    def body(*refs):
        out, part, small, sem = refs[number], refs[number + 1 : -2], refs[-2], refs[-1]
        copies = [pltpu.make_async_copy(refs[i], part[i], sem.at[i]) for i in range(number)]
        for copy in copies:
            copy.start()
        small[...] = jnp.zeros_like(small)
        for copy in copies:
            copy.wait()
        for b in range(2):
            vectors, merged_bias, expand_bias = part[8 * b : 8 * b + 6], part[8 * b + 6], part[8 * b + 7]
            for i in range(6):
                small[6 * b + i : 6 * b + i + 1, :local] = (
                    vectors[i][...].astype(F32).reshape(1, local)
                )
            for h in range(merged_bias.shape[0]):
                value = merged_bias[h].astype(F32)
                small[16 + 8 * b + 2 * h : 18 + 8 * b + 2 * h, : value.shape[1]] = value
            value = expand_bias[...].astype(F32)
            small[32 + 16 * b : 32 + 16 * b + value.shape[0], : value.shape[1]] = value
        merged_ref, output_ref = part[-2:]
        pieces = [merged_ref[k] for k in range(3)] + [turn(output_ref[...]).astype(BF16)]
        out[:local, :] = jnp.concatenate(pieces, axis=1)
        for i in range(4):
            out[local:, local * i : local * (i + 1)] = small[
                SPARE * i : SPARE * (i + 1), :local
            ].astype(BF16)

    return pl.pallas_call(
        body,
        out_shape=shaped(local + SPARE, 4 * local, BF16),
        in_specs=[pl.BlockSpec(memory_space=pltpu.HBM)] * number,
        out_specs=VMEM,
        scratch_shapes=[pltpu.VMEM(v.shape, v.dtype) for v in flat]
        + [pltpu.VMEM((ROWS, 256), F32), pltpu.SemaphoreType.DMA((number,))],
        compiler_params=pltpu.CompilerParams(vmem_limit_bytes=60 << 20),
        name="prepare_first",
    )(*flat)


def unpack_vectors(pieces, place, local, merged_shape, expand_shape):
    heads, few = merged_shape[1], merged_shape[2]
    groups = expand_shape[0]
    width = heads * 4 * few

    def body(place_ref, *refs):
        pieces, outs, pieces_ref = refs[:4], refs[4:-1], refs[-1]
        for k in range(4):
            for i in range(4):
                pieces_ref[k * ROWS + i * SPARE : k * ROWS + (i + 1) * SPARE, :local] = pieces[k][
                    local:, local * i : local * (i + 1)
                ].astype(F32)
        y, z = place_ref[0], place_ref[1]
        for b in range(2):
            gains, bias, hidden = outs[3 * b : 3 * b + 3]
            for k in range(4):
                gains[0:6, k * local : (k + 1) * local] = pieces_ref[
                    k * ROWS + 6 * b : k * ROWS + 6 * b + 6, :local
                ]
            bias[...] = jnp.zeros_like(bias)
            for natural in range(4):
                distance = z ^ natural
                base = (2 * (distance & 1) + (distance >> 1)) * ROWS
                part = pieces_ref[pl.ds(pl.multiple_of(base, ROWS), ROWS), :128]
                for i in range(2):
                    for h in range(heads):
                        line = 16 + 8 * b + 2 * h + i
                        at = 2 * i * width + h * 4 * few + natural * few
                        bias[:, at : at + few] = part[line : line + 1, :few]
                lines = part[32 + 16 * b : 32 + 16 * b + groups]
                half = groups // 2
                lines = jnp.where(
                    y == 0, lines, jnp.concatenate([lines[half:], lines[:half]], axis=0)
                )
                for p in range(groups):
                    at = p * 4 * few + natural * few
                    hidden[:, at : at + few] = lines[p : p + 1, :few]

    one = (
        shaped(8, 4 * local, F32),
        shaped(1, 3 * width, F32),
        shaped(1, groups * 4 * few, F32),
    )
    return pl.pallas_call(
        body,
        out_shape=one + one,
        in_specs=[SMEM] + [VMEM] * 4,
        out_specs=(VMEM,) * 6,
        scratch_shapes=[pltpu.VMEM((4 * ROWS, 256), F32)],
        compiler_params=pltpu.CompilerParams(vmem_limit_bytes=8 << 20),
        name="unpack_vectors",
    )(place, *pieces)


def prepare_attend(merged, output):
    local = output.shape[1]

    def body(merged_ref, output_ref, attend):
        pieces = [merged_ref[k] for k in range(3)] + [turn(output_ref[...]).astype(BF16)]
        attend[...] = jnp.concatenate(pieces, axis=1)

    return pl.pallas_call(
        body,
        out_shape=shaped(local, 4 * local, BF16),
        in_specs=[VMEM, VMEM],
        out_specs=VMEM,
        compiler_params=pltpu.CompilerParams(vmem_limit_bytes=12 << 20),
        name="prepare_attend",
    )(merged.transpose(1, 0, 2), output)


def prepare_feed(place, expand, reduce):
    local, half = expand.shape[0], expand.shape[1] // 2

    def body(place_ref, expand_ref, reduce_ref, feed):
        y = place_ref[0]
        first, second = reduce_ref[:, :half], reduce_ref[:, half:]
        feed[:, :half] = jnp.where(y == 0, expand_ref[:, :half], expand_ref[:, half:])
        feed[:, half : 2 * half] = jnp.where(y == 0, first, second)
        feed[:, 2 * half :] = jnp.where(y == 0, second, first)

    return pl.pallas_call(
        body,
        out_shape=shaped(local, 3 * half, BF16),
        in_specs=[SMEM, VMEM, VMEM],
        out_specs=VMEM,
        compiler_params=pltpu.CompilerParams(vmem_limit_bytes=12 << 20),
        name="prepare_feed",
    )(place, expand, reduce.T)


def pack_grads(sums, biases, hiddens, place, local, merged_shape, expand_shape):
    heads, few = merged_shape[1], merged_shape[2]
    groups = expand_shape[0]
    width = heads * 4 * few

    def body(place_ref, sum_ref, bias_s, bias_t, hidden_s, hidden_t, out):
        y, z = place_ref[0], place_ref[1]
        out[...] = jnp.zeros_like(out)
        for k in range(4):
            out[k * ROWS : k * ROWS + 12, :local] = sum_ref[0:12, k * local : (k + 1) * local]
        for natural in range(4):
            distance = z ^ natural
            base = pl.multiple_of((2 * (distance & 1) + (distance >> 1)) * ROWS, ROWS)
            lines = []
            for bias in (bias_s, bias_t):
                for h in range(heads):
                    for i in range(2):
                        at = 2 * i * width + h * 4 * few + natural * few
                        lines.append(bias[:, at : at + few])
                lines.append(jnp.zeros((2, few), F32))
            for hidden in (hidden_s, hidden_t):
                rows = [
                    hidden[:, p * 4 * few + natural * few : p * 4 * few + natural * few + few]
                    for p in range(groups)
                ]
                first, second = rows[: groups // 2], rows[groups // 2 :]
                first, second = jnp.concatenate(first, axis=0), jnp.concatenate(second, axis=0)
                lines.append(jnp.where(y == 0, first, second))
                lines.append(jnp.where(y == 0, second, first))
                lines.append(jnp.zeros((16 - groups, few), F32))
            out[pl.ds(pl.multiple_of(base + 16, 16), ROWS - 16), :few] = jnp.concatenate(lines, axis=0)

    return pl.pallas_call(
        body,
        out_shape=shaped(4 * ROWS, 256, F32),
        in_specs=[SMEM] + [VMEM] * 5,
        out_specs=VMEM,
        compiler_params=pltpu.CompilerParams(vmem_limit_bytes=4 << 20),
        name="pack_grads",
    )(place, sums, *biases, *hiddens)


def unpack_grads(mine, arrived, local, merged_shape, expand_shape):
    heads, few = merged_shape[1], merged_shape[2]
    groups = expand_shape[0]

    def body(mine_ref, arrived_ref, *outs):
        total = mine_ref[0:ROWS, :] + arrived_ref[...]
        for b in range(2):
            vectors, merged_bias, expand_bias = outs[8 * b : 8 * b + 6], outs[8 * b + 6], outs[8 * b + 7]
            for i in range(6):
                vectors[i][...] = total[6 * b + i : 6 * b + i + 1, :local].reshape(local)
            for h in range(heads):
                merged_bias[h] = total[16 + 8 * b + 2 * h : 18 + 8 * b + 2 * h, :few]
            expand_bias[...] = total[32 + 16 * b : 32 + 16 * b + groups, :few]

    one = [jax.ShapeDtypeStruct((local,), F32)] * 6 + [
        jax.ShapeDtypeStruct((heads, 2, few), F32),
        jax.ShapeDtypeStruct(expand_shape, F32),
    ]
    values = pl.pallas_call(
        body,
        out_shape=tuple(one + one),
        in_specs=[VMEM] * 2,
        out_specs=(VMEM,) * 16,
        compiler_params=pltpu.CompilerParams(vmem_limit_bytes=4 << 20),
        name="unpack_grads",
    )(mine, arrived)
    return [v.transpose(1, 0, 2) if v.ndim == 3 else v for v in values]


def finish_feed(mine, theirs, place, half):
    local = mine.shape[0]
    whole = mine.shape[1] == 3 * half

    def body(place_ref, mine_ref, theirs_ref, expand, reduce):
        y = place_ref[0]
        own, other = mine_ref[:, :half].astype(F32), theirs_ref[:, :half].astype(F32)
        expand[:, :half] = jnp.where(y == 0, own, other)
        expand[:, half:] = jnp.where(y == 0, other, own)
        if whole:
            total = mine_ref[:, half:].astype(F32) + theirs_ref[:, half:].astype(F32)
            own, other = total[:, :half], total[:, half:]
        else:
            own, other = mine_ref[:, half:].astype(F32), theirs_ref[:, half:].astype(F32)
        reduce[:, :half] = jnp.where(y == 0, own, other)
        reduce[:, half:] = jnp.where(y == 0, other, own)

    expand, reduce = pl.pallas_call(
        body,
        out_shape=(shaped(local, 2 * half, F32), shaped(local, 2 * half, F32)),
        in_specs=[SMEM, VMEM, VMEM],
        out_specs=(VMEM, VMEM),
        compiler_params=pltpu.CompilerParams(vmem_limit_bytes=12 << 20),
        name="finish_feed",
    )(place, mine, theirs)
    return expand, reduce.T


def finish_attend(added, mine, theirs, place):
    local = mine.shape[0]

    def body(place_ref, *refs):
        mine_ref, theirs_ref, merged, output = refs[-4:]
        y = place_ref[0]
        own, other = mine_ref[...], theirs_ref[...]
        split = jnp.concatenate(
            [jnp.where(y == 0, own, other), jnp.where(y == 0, other, own)], axis=1
        )
        output[...] = turn(split[:, -local:])
        whole = split.astype(F32)
        if added:
            total = refs[0][...].astype(F32) + refs[1][...].astype(F32)
            whole = jnp.concatenate([total, whole], axis=1)
        for k in range(3):
            merged[k] = whole[:, k * local : (k + 1) * local]

    merged, output = pl.pallas_call(
        body,
        out_shape=(jax.ShapeDtypeStruct((3, local, local), F32), shaped(local, local, F32)),
        in_specs=[SMEM] + [VMEM] * (2 + len(added)),
        out_specs=(VMEM, VMEM),
        compiler_params=pltpu.CompilerParams(vmem_limit_bytes=12 << 20),
        name="finish_attend",
    )(place, *added, mine, theirs)
    return merged.transpose(1, 0, 2), output


def halves_added(kept, arrived):
    middle = kept.shape[0] // 2
    return (kept[middle:] + arrived[middle:].astype(F32)).astype(BF16)


def core_sum(kept, arrived):
    return (kept + arrived.astype(F32)).astype(BF16)


def added(first, second):
    return (first.astype(F32) + second.astype(F32)).astype(BF16)


def send_columns(value, cross):
    middle = value.shape[1] // 2
    return cross(value[:, middle:].astype(BF16))


def keep_columns(value, arrived):
    return value[:, : value.shape[1] // 2].astype(F32) + arrived.astype(F32)


def send_rows(value, cross):
    middle = value.shape[0] // 2
    return cross(value[middle:].astype(BF16))


def keep_rows(value, arrived):
    return value[: value.shape[0] // 2].astype(F32) + arrived.astype(F32)


def fast_shards(inputs, segments, cotangent, *params):
    y_index = lax.axis_index("ctx")
    z_index = lax.axis_index("dp")
    me = lax.axis_index("tp")
    tokens, features = inputs.shape[1], inputs.shape[2]
    length = segments.shape[1] * 2
    doc_max = min(DOC_MAX, length // 2)
    blocks = (params[:12], params[12:])
    local = features // 4
    half = local * 2

    small = [((p[0], p[1], p[5], p[6], p[7], p[11]), p[3], p[9]) for p in blocks]
    place = jnp.stack([y_index, z_index]).astype(jnp.int32)
    p = blocks[0]
    attend = prepare_first(place, p[2], p[4], small)
    inputs, attend = pin(inputs, attend)
    far = cross_far(attend)
    sent_rows = jnp.where(y_index == 0, inputs[1], inputs[0])
    sent_rows, late = pin(sent_rows, attend)
    near = cross_near(late)
    sent_docs = jnp.where(y_index == 0, segments[1:2], segments[0:1]).astype(BF16)
    sent_docs = jnp.pad(sent_docs, ((0, 15), (0, features - sent_docs.shape[1])))
    moved = cross_y(stacked(sent_rows, sent_docs))
    kept_rows = jnp.where(y_index == 0, inputs[0], inputs[1])
    kept_docs = jnp.where(y_index == 0, segments[0:1], segments[1:2]).astype(F32)
    chooser = order_matrix(features, z_index)
    raw = times(y_order(kept_rows, moved[:tokens], y_index, 0), chooser, BF16)
    docs = y_order(
        kept_docs, moved[tokens : tokens + 1, : kept_docs.shape[1]].astype(F32), y_index, 1
    )
    context = (me.astype(jnp.int32).reshape(1), docs)
    both = cross_near(far)
    feed = prepare_feed(place, blocks[0][8], blocks[0][10])
    feed, far = pin(feed, far)
    p_far = cross_far(feed[:, : 2 * half])
    moved_grad = cross_y(jnp.where(y_index == 0, cotangent[1], cotangent[0]))
    raw, place_t, output_t = pin(raw, place, blocks[1][4])
    own_a = prepare_attend(blocks[1][2], output_t)
    feed_t = prepare_feed(place_t, blocks[1][8], blocks[1][10])

    stream = stacked(raw, cross_x(raw))
    stream, near, both, p_far, own_a, feed_t, moved_grad = pin(
        stream, near, both, p_far, own_a, feed_t, moved_grad
    )
    near_s = norm_only(stream)
    gains_s, bias_s, hidden_s, gains_t, bias_t, hidden_t = unpack_vectors(
        (attend, far, near, both), place, local, blocks[0][3].shape, blocks[0][9].shape
    )
    far_s = cross_core(near_s)
    attend_s = (attend, far, near, both)
    e_two = stacked(feed[:, :half], p_far[:, :half])
    e_near = cross_near(e_two)
    r_far = cross_far(feed[:, 2 * half :])
    grad_out = times(
        y_order(jnp.where(y_index == 0, cotangent[0], cotangent[1]), moved_grad, y_index, 0),
        chooser,
        BF16,
    )
    moved_grad = cross_x(grad_out)
    sent, kept, *saved_s, near_s, far_s = attention_forward(
        near_s, far_s, attend_s, bias_s, context, doc_max, (gains_s,)
    )
    sent, e_near, r_far, moved_grad = pin(sent, e_near, r_far, moved_grad)
    e_s = stacked(e_two, e_near)
    e_other = cross_y(e_s)
    r_two = stacked(feed[:, half:], beside(p_far[:, half:], r_far))
    r_near = cross_near(r_two)
    a_far = cross_far(own_a)
    partial = core_sum(kept, cross_core(sent))
    middle_s, near_two_s = add_norm(stream, partial, cross_x(partial), gains_s, 2, gains_s, 3)
    near_two_s, e_other, r_near, a_far, feed_t = pin(near_two_s, e_other, r_near, a_far, feed_t)
    a_two = stacked(own_a, a_far)
    a_near = cross_near(a_two)
    te_far, tr_far = cross_far(feed_t[:, :half]), cross_far(feed_t[:, 2 * half :])
    far_two_s = cross_core(near_two_s)
    feed_s = (near_two_s, far_two_s), ((e_s, e_other), (r_two, r_near), hidden_s)
    sent, kept = feed_forward(*feed_s[0], *feed_s[1])
    partial = core_sum(kept, cross_core(sent))
    between, near_t = add_norm(middle_s, partial, cross_x(partial), gains_s, 5, gains_t, 0)

    near_t, a_near, te_far, tr_far, feed_t = pin(near_t, a_near, te_far, tr_far, feed_t)
    attend_t = (a_two, a_near)
    te_two = stacked(feed_t[:, :half], te_far)
    te_near = cross_near(te_two)
    tr_far_one = cross_far(feed_t[:, half : 2 * half])
    far_t = cross_core(near_t)
    sent, kept, *saved_t = attention_forward(near_t, far_t, attend_t, bias_t, context, doc_max)
    sent, te_near, tr_far_one = pin(sent, te_near, tr_far_one)
    te = stacked(te_two, te_near)
    te_other = cross_y(te)
    tr_two = stacked(feed_t[:, half:], beside(tr_far_one, tr_far))
    tr_near = cross_near(tr_two)
    branch = stacked(grad_out, moved_grad)
    branch_far = cross_core(branch)
    partial = core_sum(kept, cross_core(sent))
    middle_t, near_two_t = add_norm(between, partial, cross_x(partial), gains_t, 2, gains_t, 3)
    near_two_t, te_other, tr_near, branch_far = pin(near_two_t, te_other, tr_near, branch_far)
    far_two_t = cross_core(near_two_t)
    feed_t = (near_two_t, far_two_t), ((te, te_other), (tr_two, tr_near), hidden_t)

    sums = jnp.zeros((16, features), F32)
    sent, kept, active, grad_hidden, hidden_sum_t = feed_backward(
        *feed_t[0], branch, branch_far, *feed_t[1]
    )
    partial = core_sum(kept, cross_core(sent))
    part_r = times_down(stacked(branch, branch_far), active, BF16)
    part_r, partial = pin(part_r, partial)
    r_moved = send_rows(part_r, cross_near)
    part_e = times_down(stacked(near_two_t, far_two_t), grad_hidden, BF16)
    e_moved = send_columns(part_e, cross_y)
    late_t, _ = pin(near_two_t, part_e)
    final_sent, final_kept = feed_forward(late_t, far_two_t, *feed_t[1])
    grad_middle, near_grad, sums = norm_back_near(
        branch, partial, cross_x(partial), middle_t, gains_t, 3, sums, 9
    )
    near_grad, r_moved, e_moved, final_sent, final_kept = pin(
        near_grad, r_moved, e_moved, final_sent, final_kept
    )
    part_e, part_r = keep_columns(part_e, e_moved), keep_rows(part_r, r_moved)
    e_moved = send_rows(part_e, cross_near)
    far_grad = cross_core(near_grad)
    sent, kept, grad_qkv, qkv_sum_t = attention_backward(
        near_grad, far_grad, attend_t, context, saved_t, doc_max
    )
    sent, e_moved, part_r = pin(sent, e_moved, part_r)
    part_e = keep_rows(part_e, e_moved)
    e_moved, r_moved = send_rows(part_e, cross_far), send_rows(part_r, cross_far)
    partial = core_sum(kept, cross_core(sent))
    part_a = beside(
        times_down(stacked(near_t, far_t), grad_qkv, BF16),
        times_down(stacked(near_grad, far_grad), saved_t[1], BF16),
    )
    part_a, a_moved = column_halves(part_a, y_index)
    a_moved = cross_y(a_moved)
    grad_between, branch, sums = norm_back_near(
        grad_middle, partial, cross_x(partial), between, gains_t, 0, sums, 6
    )

    branch, e_moved, r_moved, a_moved = pin(branch, e_moved, r_moved, a_moved)
    part_e, part_r = keep_rows(part_e, e_moved), keep_rows(part_r, r_moved)
    part_a = part_a.astype(F32) + a_moved.astype(F32)
    branch_far = cross_core(branch)
    sent, kept, active, grad_hidden, hidden_sum_s = feed_backward(
        *feed_s[0], branch, branch_far, *feed_s[1]
    )
    partial = core_sum(kept, cross_core(sent))
    feed_r = times_down(stacked(branch, branch_far), active, BF16)
    feed_r, part_a, partial = pin(feed_r, part_a, partial)
    fr_moved, a_moved = send_rows(feed_r, cross_near), send_rows(part_a, cross_near)
    feed_e = times_down(stacked(near_two_s, far_two_s), grad_hidden, BF16)
    fe_moved = send_columns(feed_e, cross_y)
    grad_middle, near_grad, sums = norm_back_near(
        grad_between, partial, cross_x(partial), middle_s, gains_s, 3, sums, 3
    )
    near_grad, a_moved, fr_moved, fe_moved, part_e, part_r = pin(
        near_grad, a_moved, fr_moved, fe_moved, part_e, part_r
    )
    part_a, feed_r, feed_e = (
        keep_rows(part_a, a_moved),
        keep_rows(feed_r, fr_moved),
        keep_columns(feed_e, fe_moved),
    )
    a_moved, fe_moved = send_rows(part_a, cross_far), send_rows(feed_e, cross_near)
    mine_t = beside(part_e, part_r).astype(BF16)
    theirs_t = cross_y(
        beside(mine_t[:, :half], mine_t[:, 2 * half :], mine_t[:, half : 2 * half])
    )
    far_grad = cross_core(near_grad)
    sent, kept, grad_qkv, qkv_sum_s = attention_backward(
        near_grad, far_grad, attend_s, context, saved_s, doc_max
    )
    sent, a_moved, fe_moved, feed_r = pin(sent, a_moved, fe_moved, feed_r)
    mine_at, feed_e = keep_rows(part_a, a_moved), keep_rows(feed_e, fe_moved)
    fr_moved, fe_moved = send_rows(feed_r, cross_far), send_rows(feed_e, cross_far)
    arrived = cross_core(sent)
    across = cross_x(halves_added(kept, arrived))
    grad_a = beside(
        times_down(stacked(near_s, far_s), grad_qkv, BF16),
        times_down(stacked(near_grad, far_grad), saved_s[1], BF16),
    )
    grad_a, y_moved = column_halves(grad_a, y_index)
    y_moved = cross_y(y_moved)
    grad_in, _, sums = norm_back(
        grad_middle, (kept, arrived, across), stream, gains_s, 0, sums, 0
    )
    sums_moved = cross_core(sums)
    input_grad = lax.dot_general(
        grad_in,
        chooser.astype(F32),
        (((1,), (1,)), ((), ())),
        precision=lax.Precision.HIGHEST,
        preferred_element_type=F32,
    )

    def swapped(value):
        first, second = value[:tokens], value[tokens:]
        return cross_y(jnp.where(y_index == 0, second, first))

    def restore(value, received):
        kept = jnp.where(y_index == 0, value[:tokens], value[tokens:])
        return jnp.where(y_index == 0, jnp.stack([kept, received]), jnp.stack([received, kept]))

    grad_moved = swapped(input_grad.astype(BF16))
    y_moved, sums_moved, theirs_t = pin(y_moved, sums_moved, theirs_t)
    grad_a = grad_a.astype(F32) + y_moved.astype(F32)
    y_moved = send_rows(grad_a, cross_near)
    sums = sums + sums_moved
    sums_moved = cross_x(sums)
    final_arrived = cross_core(final_sent)
    fe_moved, fr_moved, mine_at, sums_moved, final_arrived, grad_moved = pin(
        fe_moved, fr_moved, mine_at, sums_moved, final_arrived, grad_moved
    )
    final_across = cross_x(halves_added(final_kept, final_arrived))
    pack = pack_grads(
        sums + sums_moved,
        (qkv_sum_s, qkv_sum_t),
        (hidden_sum_s, hidden_sum_t),
        place,
        local,
        params[3].shape,
        params[9].shape,
    )
    mine_s = beside(keep_rows(feed_e, fe_moved), keep_rows(feed_r, fr_moved), mine_at).astype(BF16)
    pack_moved = cross_y(pack)
    expand_grad_t, reduce_grad_t = finish_feed(mine_t, theirs_t, place, half)
    y_moved, mine_s = pin(y_moved, mine_s)
    theirs_s = cross_y(
        beside(
            mine_s[:, :half], mine_s[:, 2 * half : 3 * half], mine_s[:, half : 2 * half], mine_s[:, 3 * half :]
        )
    )
    grad_a = keep_rows(grad_a, y_moved)
    y_moved = send_rows(grad_a, cross_far)
    final_across, expand_grad_t = pin(final_across, expand_grad_t)
    rows = 2 * tokens
    final = middle_t[:rows] + gains_t[5:6] + final_kept[:rows] + final_across.astype(F32)
    final = final + final_arrived[:rows].astype(F32)
    final = times_across(final.astype(BF16), chooser, BF16)
    y_moved, pack_moved, final = pin(y_moved, pack_moved, final)
    pack = pack + pack_moved
    pack_near = cross_near(pack[2 * ROWS :])
    mine_a = keep_rows(grad_a, y_moved).astype(BF16)
    theirs_a = cross_y(mine_a)
    final_moved = swapped(final)
    merged_grad_t, output_grad_t = finish_attend(
        (), mine_s[:, 3 * half :], theirs_s[:, 3 * half :], place
    )
    expand_grad_s, reduce_grad_s = finish_feed(
        mine_s[:, : 3 * half], theirs_s[:, : 3 * half], place, half
    )
    pack_near, pack = pin(pack_near, pack)
    pack = pack[: 2 * ROWS] + pack_near
    pack_far = cross_far(pack[ROWS:])
    theirs_a, final_moved, pack_far, output_grad_t, expand_grad_s = pin(
        theirs_a, final_moved, pack_far, output_grad_t, expand_grad_s
    )
    grad_moved = grad_moved.astype(F32)
    merged_grad_s, output_grad_s = finish_attend((), mine_a, theirs_a, place)
    vectors = unpack_grads(pack, pack_far, local, params[3].shape, params[9].shape)
    outputs = [restore(final, final_moved), restore(input_grad, grad_moved)]
    for vector, merged, output, expand, reduce in (
        (vectors[:8], merged_grad_s, output_grad_s, expand_grad_s, reduce_grad_s),
        (vectors[8:], merged_grad_t, output_grad_t, expand_grad_t, reduce_grad_t),
    ):
        outputs += [
            vector[0],
            vector[1],
            merged,
            vector[6],
            output,
            vector[2],
            vector[3],
            vector[4],
            expand,
            vector[7],
            reduce,
            vector[5],
        ]
    return tuple(outputs)


def solution(mesh):
    quick = (mesh.shape["dp"], mesh.shape["ctx"], mesh.shape["tp"]) == (4, 2, 4)
    placed = (
        P("dp", ("ctx", "tp"), None),
        P("dp", "ctx"),
        P("dp", ("ctx", "tp"), None),
        P("dp"),
        P("dp"),
        P("dp", None, "tp"),
        P(None, "tp", "dp"),
        P("tp", "dp"),
        P("dp"),
        P("dp"),
        P("dp"),
        P("dp", "tp"),
        P("tp", "dp"),
        P("tp", "dp"),
        P("dp"),
        P("dp"),
        P("dp"),
        P("dp", None, "tp"),
        P(None, "tp", "dp"),
        P("tp", "dp"),
        P("dp"),
        P("dp"),
        P("dp"),
        P("dp", "tp"),
        P("tp", "dp"),
        P("tp", "dp"),
        P("dp"),
    )
    return jax.shard_map(
        fast_shards if quick else general_shards,
        mesh=mesh,
        in_specs=placed,
        out_specs=(
            P("dp", ("ctx", "tp"), None),
            P("dp", ("ctx", "tp"), None),
            P("dp"),
            P("dp"),
            P("dp", None, "tp"),
            P(None, "tp", "dp"),
            P("tp", "dp"),
            P("dp"),
            P("dp"),
            P("dp"),
            P("dp", "tp"),
            P("tp", "dp"),
            P("tp", "dp"),
            P("dp"),
            P("dp"),
            P("dp"),
            P("dp", None, "tp"),
            P(None, "tp", "dp"),
            P("tp", "dp"),
            P("dp"),
            P("dp"),
            P("dp"),
            P("dp", "tp"),
            P("tp", "dp"),
            P("tp", "dp"),
            P("dp"),
        ),
        check_vma=False,
    )
```

```python
import jax
import jax.numpy as jnp
from jax import lax
from jax.experimental import pallas as pl
from jax.experimental.layout import Layout, with_layout_constraint
from jax.experimental.pallas import tpu as pltpu
from jax.sharding import PartitionSpec as P

HD = 64
DOC_MAX = 2000


EPSILON = 1e-05
GELU_SCALE = 0.7978845608028654


def from_behind(block, axis, distance):
    devices = range(lax.axis_size(axis))
    route = [(i - distance, i) for i in devices if i - distance in devices]
    return lax.ppermute(block, axis, route)


def layer_norm(values, norm_gain, norm_shift):
    center = values - jnp.mean(values, axis=-1, keepdims=True)
    spread = jnp.mean(center * center, axis=-1, keepdims=True)
    return center * lax.rsqrt(spread + EPSILON) * norm_gain + norm_shift


def gelu_tanh(values):
    return (
        0.5 * values * (1.0 + jnp.tanh(GELU_SCALE * (values + 0.044715 * values * values * values)))
    )


def spread_rows(row_block):
    return lax.all_gather(row_block, "tp", axis=1, tiled=True)


def gather_sums(partial_value):
    return lax.psum_scatter(
        partial_value.astype(jnp.bfloat16), "tp", scatter_dimension=1, tiled=True
    ).astype(jnp.float32)


def to_items(tensor, head_count):
    batches, length, features = tensor.shape
    head_size = features // head_count
    return (
        tensor.reshape(batches, length, head_count, head_size)
        .transpose(0, 2, 1, 3)
        .reshape(batches * head_count, length, head_size)
    )


def from_items(tensor, head_count):
    item_count, length, head_size = tensor.shape
    batches = item_count // head_count
    return (
        tensor.reshape(batches, head_count, length, head_size)
        .transpose(0, 2, 1, 3)
        .reshape(batches, length, head_count * head_size)
    )


def masked_scores(query_rows, key_rows, query_docs, key_docs, allowed):
    raw_scores = (
        jnp.einsum("qd,kd->qk", query_rows, key_rows, preferred_element_type=jnp.float32) * 0.125
    )
    keep_mask = allowed & (key_docs[None, :] == query_docs[:, None])
    return (jnp.where(keep_mask, raw_scores, -1e30), keep_mask)


def attend_forward(allowed):

    def attend_item(packed):
        query_rows, key_rows, value_rows, query_docs, key_docs = packed
        scores, keep_mask = masked_scores(query_rows, key_rows, query_docs, key_docs, allowed)
        row_top = jnp.max(scores, axis=-1, keepdims=True)
        raised = jnp.exp(scores - row_top)
        row_total = jnp.sum(raised, axis=-1, keepdims=True)
        weights = (raised / row_total).astype(jnp.bfloat16)
        mixed_rows = jnp.dot(weights, value_rows, preferred_element_type=jnp.float32).astype(
            jnp.bfloat16
        )
        return (mixed_rows, row_top[:, 0] + jnp.log(row_total[:, 0]))

    return attend_item


def attend_backward(allowed):

    def attend_item(packed):
        query_rows, key_rows, value_rows, query_docs, key_docs, log_total, grad_rows = packed
        scores, keep_mask = masked_scores(query_rows, key_rows, query_docs, key_docs, allowed)
        weights = jnp.where(keep_mask, jnp.exp(scores - log_total[:, None]), 0.0)
        grad_values = jnp.einsum(
            "qk,qd->kd", weights.astype(jnp.bfloat16), grad_rows, preferred_element_type=jnp.float32
        )
        grad_weights = jnp.einsum(
            "qd,kd->qk", grad_rows, value_rows, preferred_element_type=jnp.float32
        )
        centered = jnp.sum(weights * grad_weights, axis=-1, keepdims=True)
        grad_scores = (weights * (grad_weights - centered)).astype(jnp.bfloat16)
        grad_query = jnp.dot(grad_scores, key_rows, preferred_element_type=jnp.float32) * 0.125
        grad_keys = (
            jnp.einsum("qk,qd->kd", grad_scores, query_rows, preferred_element_type=jnp.float32)
            * 0.125
        )
        return (grad_query, grad_keys, grad_values)

    return attend_item


def layer_forward(stream, params, segments, key_docs, allowed, cycle_steps):
    (
        first_gain,
        first_shift,
        merged_weight,
        merged_bias,
        output_weight,
        output_bias,
        second_gain,
        second_shift,
        expand_weight,
        expand_bias,
        reduce_weight,
        reduce_bias,
    ) = params
    fetched = (
        lax.all_gather(first_gain, "dp", axis=0, tiled=True),
        lax.all_gather(first_shift, "dp", axis=0, tiled=True),
        lax.all_gather(merged_weight, "dp", axis=0, tiled=True),
        lax.all_gather(merged_bias, "dp", axis=2, tiled=True),
        lax.all_gather(output_weight, "dp", axis=1, tiled=True),
        lax.all_gather(output_bias, "dp", axis=0, tiled=True),
        lax.all_gather(second_gain, "dp", axis=0, tiled=True),
        lax.all_gather(second_shift, "dp", axis=0, tiled=True),
        lax.all_gather(expand_weight, "dp", axis=0, tiled=True),
        lax.all_gather(expand_bias, "dp", axis=1, tiled=True),
        lax.all_gather(reduce_weight, "dp", axis=1, tiled=True),
        lax.all_gather(reduce_bias, "dp", axis=0, tiled=True),
    )
    (
        first_gain,
        first_shift,
        merged_weight,
        merged_bias,
        output_weight,
        output_bias,
        second_gain,
        second_shift,
        expand_weight,
        expand_bias,
        reduce_weight,
        reduce_bias,
    ) = fetched
    head_count = merged_weight.shape[2] // HD
    normed = layer_norm(
        stream, first_gain.astype(jnp.float32), first_shift.astype(jnp.float32)
    ).astype(jnp.bfloat16)
    first_rows = spread_rows(normed)
    merged_out = jnp.einsum(
        "std,dkf->stkf", first_rows, merged_weight, preferred_element_type=jnp.float32
    )
    bias_pair = merged_bias.astype(jnp.float32).reshape(2, -1)
    query_rows = (merged_out[:, :, 0] + bias_pair[0]).astype(jnp.bfloat16)
    key_rows = merged_out[:, :, 1].astype(jnp.bfloat16)
    value_rows = (merged_out[:, :, 2] + bias_pair[1]).astype(jnp.bfloat16)
    key_list = [key_rows]
    value_list = [value_rows]
    moving = (key_rows, value_rows)
    for offset in range(cycle_steps):
        moving = from_behind((moving[0], moving[1]), "ctx", 1)
        key_list.insert(0, moving[0])
        value_list.insert(0, moving[1])
    query_items = to_items(query_rows, head_count)
    key_items = to_items(jnp.concatenate(key_list, axis=1), head_count)
    value_items = to_items(jnp.concatenate(value_list, axis=1), head_count)
    query_docs = jnp.repeat(segments, head_count, axis=0)
    window_docs = jnp.repeat(key_docs, head_count, axis=0)
    mixed_items, log_total = lax.map(
        attend_forward(allowed), (query_items, key_items, value_items, query_docs, window_docs)
    )
    mixed = from_items(mixed_items, head_count)
    attn_part = jnp.einsum("stf,fd->std", mixed, output_weight, preferred_element_type=jnp.float32)
    middle = stream + gather_sums(attn_part) + output_bias.astype(jnp.float32)
    normed_two = layer_norm(
        middle, second_gain.astype(jnp.float32), second_shift.astype(jnp.float32)
    ).astype(jnp.bfloat16)
    second_rows = spread_rows(normed_two)
    hidden = jnp.einsum(
        "std,df->stf", second_rows, expand_weight, preferred_element_type=jnp.float32
    ) + expand_bias.astype(jnp.float32).reshape(-1)
    activated = gelu_tanh(hidden).astype(jnp.bfloat16)
    mlp_part = jnp.einsum(
        "stf,fd->std", activated, reduce_weight, preferred_element_type=jnp.float32
    )
    result = middle + gather_sums(mlp_part) + reduce_bias.astype(jnp.float32)
    saved_state = (
        fetched,
        stream,
        first_rows,
        query_items,
        key_items,
        value_items,
        query_docs,
        window_docs,
        log_total,
        mixed,
        middle,
        second_rows,
        hidden,
        activated,
    )
    return (result, saved_state)


def reduce_grads(fresh):
    (
        gain_one,
        shift_one,
        merged_weights,
        merged_biases,
        output_weights,
        output_biases,
        gain_two,
        shift_two,
        expand_weights,
        expand_biases,
        reduce_weights,
        reduce_biases,
    ) = fresh
    summed = (
        lax.psum(gain_one.astype(jnp.bfloat16), "ctx").astype(jnp.float32),
        lax.psum(shift_one.astype(jnp.bfloat16), "ctx").astype(jnp.float32),
        lax.psum(merged_weights.astype(jnp.bfloat16), "ctx").astype(jnp.float32),
        lax.psum(merged_biases.astype(jnp.bfloat16), "ctx").astype(jnp.float32),
        lax.psum(output_weights.astype(jnp.bfloat16), "ctx").astype(jnp.float32),
        lax.psum(output_biases.astype(jnp.bfloat16), "ctx").astype(jnp.float32),
        lax.psum(gain_two.astype(jnp.bfloat16), "ctx").astype(jnp.float32),
        lax.psum(shift_two.astype(jnp.bfloat16), "ctx").astype(jnp.float32),
        lax.psum(expand_weights.astype(jnp.bfloat16), "ctx").astype(jnp.float32),
        lax.psum(expand_biases.astype(jnp.bfloat16), "ctx").astype(jnp.float32),
        lax.psum(reduce_weights.astype(jnp.bfloat16), "ctx").astype(jnp.float32),
        lax.psum(reduce_biases.astype(jnp.bfloat16), "ctx").astype(jnp.float32),
    )
    (
        gain_one,
        shift_one,
        merged_weights,
        merged_biases,
        output_weights,
        output_biases,
        gain_two,
        shift_two,
        expand_weights,
        expand_biases,
        reduce_weights,
        reduce_biases,
    ) = summed
    return (
        lax.psum_scatter(
            gain_one.astype(jnp.bfloat16), "dp", scatter_dimension=0, tiled=True
        ).astype(jnp.float32),
        lax.psum_scatter(
            shift_one.astype(jnp.bfloat16), "dp", scatter_dimension=0, tiled=True
        ).astype(jnp.float32),
        lax.psum_scatter(
            merged_weights.astype(jnp.bfloat16), "dp", scatter_dimension=0, tiled=True
        ).astype(jnp.float32),
        lax.psum_scatter(
            merged_biases.astype(jnp.bfloat16), "dp", scatter_dimension=2, tiled=True
        ).astype(jnp.float32),
        lax.psum_scatter(
            output_weights.astype(jnp.bfloat16), "dp", scatter_dimension=1, tiled=True
        ).astype(jnp.float32),
        lax.psum_scatter(
            output_biases.astype(jnp.bfloat16), "dp", scatter_dimension=0, tiled=True
        ).astype(jnp.float32),
        lax.psum_scatter(
            gain_two.astype(jnp.bfloat16), "dp", scatter_dimension=0, tiled=True
        ).astype(jnp.float32),
        lax.psum_scatter(
            shift_two.astype(jnp.bfloat16), "dp", scatter_dimension=0, tiled=True
        ).astype(jnp.float32),
        lax.psum_scatter(
            expand_weights.astype(jnp.bfloat16), "dp", scatter_dimension=0, tiled=True
        ).astype(jnp.float32),
        lax.psum_scatter(
            expand_biases.astype(jnp.bfloat16), "dp", scatter_dimension=1, tiled=True
        ).astype(jnp.float32),
        lax.psum_scatter(
            reduce_weights.astype(jnp.bfloat16), "dp", scatter_dimension=1, tiled=True
        ).astype(jnp.float32),
        lax.psum_scatter(
            reduce_biases.astype(jnp.bfloat16), "dp", scatter_dimension=0, tiled=True
        ).astype(jnp.float32),
    )


def layer_backward(grad_out, saved_state, allowed, cycle_steps, token_count):
    (
        fetched,
        stream,
        first_rows,
        query_items,
        key_items,
        value_items,
        query_docs,
        window_docs,
        log_total,
        mixed,
        middle,
        second_rows,
        hidden,
        activated,
    ) = saved_state
    (
        first_gain,
        first_shift,
        merged_weight,
        merged_bias,
        output_weight,
        output_bias,
        second_gain,
        second_shift,
        expand_weight,
        expand_bias,
        reduce_weight,
        reduce_bias,
    ) = fetched
    head_count = merged_weight.shape[2] // HD
    grad_branch = spread_rows(grad_out.astype(jnp.bfloat16))
    grad_reduce = jnp.einsum(
        "stf,std->fd", activated, grad_branch, preferred_element_type=jnp.float32
    )
    grad_active = jnp.einsum(
        "std,fd->stf", grad_branch, reduce_weight, preferred_element_type=jnp.float32
    )
    _, gelu_pull = jax.vjp(gelu_tanh, hidden)
    grad_hidden = gelu_pull(grad_active)[0].astype(jnp.bfloat16)
    grad_expand_bias = jnp.sum(grad_hidden, axis=(0, 1), dtype=jnp.float32).reshape(
        expand_bias.shape
    )
    grad_expand = jnp.einsum(
        "std,stf->df", second_rows, grad_hidden, preferred_element_type=jnp.float32
    )
    grad_second = gather_sums(
        jnp.einsum("stf,df->std", grad_hidden, expand_weight, preferred_element_type=jnp.float32)
    )
    _, second_pull = jax.vjp(
        layer_norm, middle, second_gain.astype(jnp.float32), second_shift.astype(jnp.float32)
    )
    grad_norm_mid, grad_second_gain, grad_second_shift = second_pull(grad_second)
    grad_middle = grad_out + grad_norm_mid
    grad_reduce_bias = jnp.sum(grad_out, axis=(0, 1))
    grad_attend = spread_rows(grad_middle.astype(jnp.bfloat16))
    grad_output = jnp.einsum("stf,std->fd", mixed, grad_attend, preferred_element_type=jnp.float32)
    grad_mixed = jnp.einsum(
        "std,fd->stf", grad_attend, output_weight, preferred_element_type=jnp.float32
    ).astype(jnp.bfloat16)
    grad_query_items, grad_key_items, grad_value_items = lax.map(
        attend_backward(allowed),
        (
            query_items,
            key_items,
            value_items,
            query_docs,
            window_docs,
            log_total,
            to_items(grad_mixed, head_count),
        ),
    )
    grad_query = from_items(grad_query_items, head_count)
    window_keys = from_items(grad_key_items, head_count)
    window_values = from_items(grad_value_items, head_count)
    local_keys = window_keys[:, cycle_steps * token_count :]
    local_values = window_values[:, cycle_steps * token_count :]
    carried = None
    for offset in range(cycle_steps, 0, -1):
        start_row = (cycle_steps - offset) * token_count
        block_keys = window_keys[:, start_row : start_row + token_count]
        block_values = window_values[:, start_row : start_row + token_count]
        if carried is not None:
            block_keys = block_keys + carried[0]
            block_values = block_values + carried[1]
        carried = (
            from_behind(block_keys.astype(jnp.bfloat16), "ctx", -1).astype(block_keys.dtype),
            from_behind(block_values.astype(jnp.bfloat16), "ctx", -1).astype(block_values.dtype),
        )
    local_keys = local_keys + carried[0]
    local_values = local_values + carried[1]
    grad_merged = jnp.stack([grad_query, local_keys, local_values], axis=2).astype(jnp.bfloat16)
    grad_merged_bias = jnp.stack(
        [
            jnp.sum(grad_merged[:, :, 0], axis=(0, 1), dtype=jnp.float32),
            jnp.sum(grad_merged[:, :, 2], axis=(0, 1), dtype=jnp.float32),
        ]
    ).reshape(merged_bias.shape)
    grad_merged_weight = jnp.einsum(
        "std,stkf->dkf", first_rows, grad_merged, preferred_element_type=jnp.float32
    )
    grad_first = gather_sums(
        jnp.einsum("stkf,dkf->std", grad_merged, merged_weight, preferred_element_type=jnp.float32)
    )
    _, first_pull = jax.vjp(
        layer_norm, stream, first_gain.astype(jnp.float32), first_shift.astype(jnp.float32)
    )
    grad_norm_in, grad_first_gain, grad_first_shift = first_pull(grad_first)
    grad_input = grad_middle + grad_norm_in
    grad_output_bias = jnp.sum(grad_middle, axis=(0, 1))
    vector_grads = lax.psum(
        (
            grad_first_gain,
            grad_first_shift,
            grad_second_gain,
            grad_second_shift,
            grad_output_bias,
            grad_reduce_bias,
        ),
        "tp",
    )
    fresh = (
        vector_grads[0],
        vector_grads[1],
        grad_merged_weight,
        grad_merged_bias,
        grad_output,
        vector_grads[4],
        vector_grads[2],
        vector_grads[3],
        grad_expand,
        grad_expand_bias,
        grad_reduce,
        vector_grads[5],
    )
    return (grad_input, reduce_grads(fresh))


def general_shards(
    inputs,
    segments,
    cotangent,
    student_first_gain,
    student_first_shift,
    student_merged_weight,
    student_merged_bias,
    student_output_weight,
    student_output_bias,
    student_second_gain,
    student_second_shift,
    student_expand_weight,
    student_expand_bias,
    student_reduce_weight,
    student_reduce_bias,
    teacher_first_gain,
    teacher_first_shift,
    teacher_merged_weight,
    teacher_merged_bias,
    teacher_output_weight,
    teacher_output_bias,
    teacher_second_gain,
    teacher_second_shift,
    teacher_expand_weight,
    teacher_expand_bias,
    teacher_reduce_weight,
    teacher_reduce_bias,
):
    student = (
        student_first_gain,
        student_first_shift,
        student_merged_weight,
        student_merged_bias,
        student_output_weight,
        student_output_bias,
        student_second_gain,
        student_second_shift,
        student_expand_weight,
        student_expand_bias,
        student_reduce_weight,
        student_reduce_bias,
    )
    teacher = (
        teacher_first_gain,
        teacher_first_shift,
        teacher_merged_weight,
        teacher_merged_bias,
        teacher_output_weight,
        teacher_output_bias,
        teacher_second_gain,
        teacher_second_shift,
        teacher_expand_weight,
        teacher_expand_bias,
        teacher_reduce_weight,
        teacher_reduce_bias,
    )
    token_count = segments.shape[1]
    context_size = lax.axis_size("ctx")
    context_index = lax.axis_index("ctx")
    doc_long = min(DOC_MAX, token_count * context_size // 2)
    cycle_steps = min((doc_long - 2) // token_count + 1, context_size - 1)
    doc_list = [segments]
    moving = segments
    for offset in range(cycle_steps):
        moving = from_behind(moving, "ctx", 1)
        doc_list.insert(0, moving)
    key_docs = jnp.concatenate(doc_list, axis=1)
    places = jnp.arange((cycle_steps + 1) * token_count, dtype=jnp.int32)
    relative = places - cycle_steps * token_count
    source = cycle_steps - places // token_count
    query_place = jnp.arange(token_count, dtype=jnp.int32)
    allowed = (relative[None, :] <= query_place[:, None]) & (source <= context_index)[None, :]
    stream = inputs.astype(jnp.float32)
    middle_stream, student_saved = layer_forward(
        stream, student, segments, key_docs, allowed, cycle_steps
    )
    final_stream, teacher_saved = layer_forward(
        middle_stream, teacher, segments, key_docs, allowed, cycle_steps
    )
    teacher_in_grad, teacher_grads = layer_backward(
        cotangent.astype(jnp.float32), teacher_saved, allowed, cycle_steps, token_count
    )
    input_grad, student_grads = layer_backward(
        teacher_in_grad, student_saved, allowed, cycle_steps, token_count
    )
    return (
        (final_stream.astype(jnp.bfloat16), input_grad)
        + tuple(student_grads)
        + tuple(teacher_grads)
    )


BF16 = jnp.bfloat16
F32 = jnp.float32
NEG = -1e30
TILE = 256
RELATIVE = (0, 2, 1, 3)


def row_major(value):
    return with_layout_constraint(value, Layout(major_to_minor=tuple(range(value.ndim))))


def swap(value, axis, bit):
    route = [(i, i ^ bit) for i in range(lax.axis_size(axis))]
    if value.ndim == 2:
        return row_major(lax.ppermute(row_major(value), axis, route))
    return lax.ppermute(value, axis, route)


def cross_core(value):
    return swap(value, "tp", 1)


def cross_x(value):
    return swap(value, "tp", 2)


def cross_y(value):
    return swap(value, "ctx", 1)


def cross_near(value):
    return swap(value, "dp", 1)


def cross_far(value):
    return swap(value, "dp", 2)


def cross_both(value):
    return swap(value, "dp", 3)


def stacked(*values):
    return jnp.concatenate(values, axis=0)


def beside(*values):
    return jnp.concatenate(values, axis=1)


def y_order(own, other, y_index, axis):
    return jnp.where(
        y_index == 0,
        jnp.concatenate([own, other], axis=axis),
        jnp.concatenate([other, own], axis=axis),
    )


def pin(*values):
    return lax.optimization_barrier(values)


def window_start(block, doc_max):
    return max(0, (block * TILE - doc_max + 1) // TILE) * TILE


def upright(line):
    size = line.shape[1]
    rows = lax.broadcasted_iota(jnp.int32, (size, size), 0)
    columns = lax.broadcasted_iota(jnp.int32, (size, size), 1)
    return jnp.sum(jnp.where(rows == columns, line, 0.0), axis=1, keepdims=True)


def join(pieces, whole):
    row, column = 0, 0
    most = whole.shape[0] * whole.shape[1] // sum(piece.shape[1] for piece in pieces)
    for piece in pieces:
        rows = min(piece.shape[0], most) if len(pieces) == 4 else piece.shape[0]
        whole[row : row + rows, column : column + piece.shape[1]] = piece[:rows, :]
        row += rows
        if row == whole.shape[0]:
            row, column = 0, column + piece.shape[1]


def dot_across(left, right):
    return lax.dot_general(left, right, (((1,), (1,)), ((), ())), preferred_element_type=F32)


def dot_down(left, right):
    return lax.dot_general(left, right, (((0,), (0,)), ((), ())), preferred_element_type=F32)


def token_place(me, member, half, rows):
    return pl.multiple_of((half * 4 + (me ^ (2 * (member & 1) + (member >> 1)))) * rows, rows)


def flat(column):
    size = column.shape[0]
    rows = lax.broadcasted_iota(jnp.int32, (size, size), 0)
    columns = lax.broadcasted_iota(jnp.int32, (size, size), 1)
    return jnp.sum(jnp.where(rows == columns, column, 0.0), axis=0, keepdims=True)


def fill_masks_across(docs, masks, doc_max):
    for block in range(docs.shape[1] // TILE):
        start, stop = window_start(block, doc_max), (block + 1) * TILE
        here = slice(block * TILE, stop)
        rows = block * TILE + lax.broadcasted_iota(jnp.int32, (TILE, stop - start), 0)
        columns = start + lax.broadcasted_iota(jnp.int32, (TILE, stop - start), 1)
        same = upright(docs[:, here]) == docs[:, start:stop]
        masks[here, : stop - start] = jnp.where(same & (columns <= rows), 0.0, NEG)


def mask_columns(length, doc_max):
    return max((block + 1) * TILE - window_start(block, doc_max) for block in range(length // TILE))


def fill_masks(docs, masks, doc_max):
    at = 0
    for block in range(docs.shape[1] // TILE):
        start = window_start(block, doc_max)
        size = (block + 1) * TILE - start
        for first in range(0, size, TILE):
            keys = slice(start + first, start + first + TILE)
            same = upright(docs[:, keys]) == docs[:, block * TILE : (block + 1) * TILE]
            if start + first == block * TILE:
                rows = lax.broadcasted_iota(jnp.int32, (TILE, TILE), 0)
                columns = lax.broadcasted_iota(jnp.int32, (TILE, TILE), 1)
                same = same & (rows <= columns)
            masks[at : at + TILE, :] = jnp.where(same, 0.0, NEG)
            at += TILE


def mask_rows(length, doc_max):
    return sum(
        (block + 1) * TILE - window_start(block, doc_max) for block in range(length // TILE)
    )


def split_heads(value, target, first, me, member):
    rows = value.shape[0] // 2
    for half in range(2):
        place = pl.ds(token_place(me, member, half, rows), rows)
        for j in range(value.shape[1] // HD):
            target[first + j, place, :] = value[half * rows : (half + 1) * rows, j * HD : (j + 1) * HD]


def merge_heads(source, me, member, rows):
    return jnp.concatenate(
        [
            jnp.concatenate(
                [
                    source[j, pl.ds(token_place(me, member, half, rows), rows), :]
                    for j in range(source.shape[0])
                ],
                axis=1,
            )
            for half in range(2)
        ],
        axis=0,
    )


def by_member(count, step):
    for i in range(count):
        step(i)


def attention_forward_kernel(
    heads,
    doc_max,
    count,
    scaled,
    me_ref,
    near_ref,
    far_ref,
    bias_ref,
    docs,
    *refs,
):
    mixed, attend_ref, masks = refs[-3:]
    refs = refs[:-3]
    sources = (near_ref, far_ref)
    if scaled:
        gains, refs, normed = refs[0], refs[1:-2], refs[-2:]
        for source, target in zip(sources, normed):
            target[...] = (source[...].astype(F32) * gains[0:1, :] + gains[1:2, :]).astype(BF16)
        sources = normed
    pieces, (sent_ref, kept_ref, split_ref, mixed_ref, log_ref) = refs[:count], refs[count:]
    join(pieces, attend_ref)
    fill_masks_across(docs, masks, doc_max)
    me = me_ref[0]
    width = heads * HD
    size = near_ref.shape[0] // 2
    length = 4 * size
    for source, first in zip(sources, (0, 2)):

        def project(i, source=source, first=first):
            at = pl.ds(pl.multiple_of(i * size, size), size)
            value = jnp.dot(source[at, :], attend_ref[:, : 3 * width], preferred_element_type=F32)
            value = (value + bias_ref[...]).astype(BF16)
            split_heads(value[:, :width] * BF16(0.125), split_ref, 0, me, first + i)
            split_heads(value[:, width:], split_ref, heads, me, first + i)

        by_member(2, project)

    def attend(h):
        for block in range(length // TILE):
            start, stop = window_start(block, doc_max), (block + 1) * TILE
            here = slice(block * TILE, stop)
            key, value = split_ref[heads + h, start:stop, :], split_ref[2 * heads + h, start:stop, :]
            scores = dot_across(split_ref[h, here, :], key) + masks[here, : stop - start]
            top = jnp.max(scores, axis=1, keepdims=True)
            raised = jnp.exp(scores - top)
            total = jnp.sum(raised, axis=1, keepdims=True)
            product = jnp.dot(raised.astype(BF16), value, preferred_element_type=F32)
            mixed[h, here, :] = (product * (1.0 / total)).astype(BF16)
            log_ref[h, :, here] = flat(top + jnp.log(total))

    lax.fori_loop(0, heads, lambda h, carry: (attend(h), carry)[1], 0)
    for out, first in ((sent_ref, 2), (kept_ref, 0)):

        def finish(i, out=out, first=first):
            rows = merge_heads(mixed, me, first + i, size // 2)
            mixed_ref[pl.ds(pl.multiple_of((first + i) * size, size), size), :] = rows
            at = pl.ds(pl.multiple_of(i * size, size), size)
            out[at, :] = dot_across(rows, attend_ref[:, 3 * width :]).astype(out.dtype)

        by_member(2, finish)


def attention_backward_kernel(
    heads,
    doc_max,
    count,
    me_ref,
    near_ref,
    far_ref,
    docs,
    split_ref,
    log_ref,
    *refs,
):
    pieces, (sent_ref, kept_ref, out_ref, sum_ref) = refs[:count], refs[count:-4]
    grad, total, attend_ref, masks = refs[-4:]
    join(pieces, attend_ref)
    fill_masks(docs, masks, doc_max)
    me = me_ref[0]
    width = heads * HD
    size = near_ref.shape[0] // 2
    length = 4 * size
    for source, first in ((near_ref, 0), (far_ref, 2)):

        def project(i, source=source, first=first):
            at = pl.ds(pl.multiple_of(i * size, size), size)
            value = jnp.dot(source[at, :], attend_ref[:, 3 * width :], preferred_element_type=F32)
            split_heads(value.astype(BF16), grad, 0, me, first + i)

        by_member(2, project)

    def attend(h):
        total[heads + h] = jnp.zeros((length, HD), F32)
        total[2 * heads + h] = jnp.zeros((length, HD), F32)
        at = 0
        for block in range(length // TILE):
            start, stop = window_start(block, doc_max), (block + 1) * TILE
            here, window = slice(block * TILE, stop), slice(start, stop)
            query, key, value = (
                split_ref[h, here, :],
                split_ref[heads + h, window, :],
                split_ref[2 * heads + h, window, :],
            )
            grad_rows = grad[h, here, :]
            scores = dot_across(key, query) + masks[at : at + stop - start, :]
            at += stop - start
            weights = jnp.exp(scores - log_ref[h, :, here])
            weighted = weights * dot_across(value, grad_rows)
            centered = jnp.sum(weighted, axis=0, keepdims=True)
            grad_scores = (weighted - weights * centered).astype(BF16)
            total[2 * heads + h, window, :] += jnp.dot(
                weights.astype(BF16), grad_rows, preferred_element_type=F32
            )
            total[heads + h, window, :] += jnp.dot(
                grad_scores, query, preferred_element_type=F32
            )
            total[h, here, :] = dot_down(key, grad_scores).T * 0.125

    lax.fori_loop(0, heads, lambda h, carry: (attend(h), carry)[1], 0)
    sum_ref[...] = jnp.zeros_like(sum_ref)
    for out, first in ((sent_ref, 2), (kept_ref, 0)):

        def finish(i, out=out, first=first):
            rows = merge_heads(total, me, first + i, size // 2).astype(BF16)
            out_ref[pl.ds(pl.multiple_of((first + i) * size, size), size), :] = rows
            sum_ref[...] += jnp.sum(rows.astype(F32), axis=0, keepdims=True)
            at = pl.ds(pl.multiple_of(i * size, size), size)
            out[at, :] = dot_across(rows, attend_ref[:, : 3 * width]).astype(out.dtype)

        by_member(2, finish)


VMEM = pl.BlockSpec(memory_space=pltpu.VMEM)
SMEM = pl.BlockSpec(memory_space=pltpu.SMEM)


def call(body, name, inputs, outputs, scratch, flops, transcendentals, limit=24):
    size = sum(v.size * v.dtype.itemsize for v in list(inputs) + list(outputs))
    return pl.pallas_call(
        body,
        out_shape=tuple(outputs),
        in_specs=[SMEM if v.ndim == 1 else VMEM for v in inputs],
        out_specs=tuple(VMEM for _ in outputs),
        scratch_shapes=scratch,
        cost_estimate=pl.CostEstimate(
            flops=flops, transcendentals=transcendentals, bytes_accessed=size
        ),
        compiler_params=pltpu.CompilerParams(vmem_limit_bytes=limit << 20),
        name=name,
    )(*inputs)


def shaped(rows, columns, kind):
    return jax.ShapeDtypeStruct((rows, columns), kind)


def attention_forward(near, far, attend, bias, context, doc_max, gains=()):
    me, docs = context
    half, features = near.shape
    width = bias.shape[1] // 3
    heads = width // HD
    area = heads * 2 * half * half

    def body(*refs):
        attention_forward_kernel(heads, doc_max, len(attend), len(gains) > 0, *refs)

    return call(
        body,
        "attention_forward",
        (me, near, far, bias, docs) + tuple(gains) + tuple(attend),
        (
            shaped(half, features, BF16),
            shaped(half, features, F32),
            jax.ShapeDtypeStruct((3 * heads, 2 * half, HD), BF16),
            shaped(2 * half, width, BF16),
            jax.ShapeDtypeStruct((heads, 1, 2 * half), F32),
        )
        + (shaped(half, features, BF16),) * (2 * len(gains)),
        [
            pltpu.VMEM((heads, 2 * half, HD), BF16),
            pltpu.VMEM((features, 4 * width), BF16),
            pltpu.VMEM((2 * half, mask_columns(2 * half, doc_max)), F32),
        ],
        16 * HD * area,
        area,
    )


def attention_backward(near, far, attend, context, saved, doc_max):
    me, docs = context
    split, _, log_total = saved
    half, features = near.shape
    heads = split.shape[0] // 3
    width = heads * HD
    area = heads * 2 * half * half

    def body(*refs):
        attention_backward_kernel(heads, doc_max, len(attend), *refs)

    return call(
        body,
        "attention_backward",
        (me, near, far, docs, split, log_total) + tuple(attend),
        (
            shaped(half, features, BF16),
            shaped(half, features, F32),
            shaped(2 * half, 3 * width, BF16),
            shaped(1, 3 * width, F32),
        ),
        [
            pltpu.VMEM((heads, 2 * half, HD), BF16),
            pltpu.VMEM((3 * heads, 2 * half, HD), F32),
            pltpu.VMEM((features, 4 * width), BF16),
            pltpu.VMEM((mask_rows(2 * half, doc_max), TILE), F32),
        ],
        40 * HD * area,
        area,
    )


CHUNK = 256


def gelu_both(values):
    inner = GELU_SCALE * (values + 0.044715 * values * values * values)
    bent = jnp.tanh(inner)
    value = 0.5 * values * (1.0 + bent)
    slope = 0.5 * (1.0 + bent) + 0.5 * values * (1.0 - bent * bent) * GELU_SCALE * (
        1.0 + 3.0 * 0.044715 * values * values
    )
    return value, slope


def feed_forward_kernel(count, piece, bias_ref, *refs):
    out, expand_ref, reduce_ref = refs[-3:]
    join(refs[:count], expand_ref)
    join(refs[count:-3], reduce_ref)

    for first in range(0, piece.shape[0], CHUNK):
        at = slice(first, first + CHUNK)
        hidden = jnp.dot(piece[at, :], expand_ref[...], preferred_element_type=F32)
        active = gelu_tanh(hidden + bias_ref[...]).astype(BF16)
        out[at, :] = dot_across(active, reduce_ref[...]).astype(out.dtype)


def feed_rows(piece, weights, kind):
    expand, reduce, bias = weights
    rows, features = piece.shape
    hidden = bias.shape[1]

    def body(*refs):
        feed_forward_kernel(len(expand), *refs)

    return call(
        body,
        "feed_forward",
        (piece, bias) + tuple(expand) + tuple(reduce),
        (shaped(rows, features, kind),),
        [pltpu.VMEM((features, hidden), BF16), pltpu.VMEM((features, hidden), BF16)],
        4 * rows * features * hidden,
        rows * hidden,
    )[0]


def feed_forward(near, far, expand, reduce, bias):
    weights = expand, reduce, bias
    return feed_rows(far, weights, BF16), feed_rows(near, weights, F32)


def feed_backward_kernel(count, piece, grads, bias_ref, *refs):
    out, active_ref, hidden_ref, sum_ref, expand_ref, reduce_ref = refs[-6:]
    join(refs[:count], expand_ref)
    join(refs[count:-6], reduce_ref)
    sum_ref[...] = jnp.zeros_like(sum_ref)

    for first in range(0, piece.shape[0], CHUNK):
        at = slice(first, first + CHUNK)
        hidden = jnp.dot(piece[at, :], expand_ref[...], preferred_element_type=F32)
        value, slope = gelu_both(hidden + bias_ref[...])
        active_ref[at, :] = value.astype(BF16)
        grad_active = jnp.dot(grads[at, :], reduce_ref[...], preferred_element_type=F32)
        grad_hidden = (grad_active * slope).astype(BF16)
        hidden_ref[at, :] = grad_hidden
        sum_ref[...] += jnp.sum(grad_hidden.astype(F32), axis=0, keepdims=True)
        out[at, :] = dot_across(grad_hidden, expand_ref[...]).astype(out.dtype)


def feed_back_rows(piece, grads, weights, kind):
    expand, reduce, bias = weights
    rows, features = piece.shape
    hidden = bias.shape[1]

    def body(*refs):
        feed_backward_kernel(len(expand), *refs)

    return call(
        body,
        "feed_backward",
        (piece, grads, bias) + tuple(expand) + tuple(reduce),
        (
            shaped(rows, features, kind),
            shaped(rows, hidden, BF16),
            shaped(rows, hidden, BF16),
            shaped(1, hidden, F32),
        ),
        [pltpu.VMEM((features, hidden), BF16), pltpu.VMEM((features, hidden), BF16)],
        6 * rows * features * hidden,
        rows * hidden,
    )


def feed_backward(near, far, near_grad, far_grad, expand, reduce, bias):
    weights = expand, reduce, bias
    sent, far_active, far_hidden, far_sum = feed_back_rows(far, far_grad, weights, BF16)
    kept, active, hidden, sums = feed_back_rows(near, near_grad, weights, F32)
    return (
        sent,
        kept,
        jnp.concatenate([active, far_active], axis=0),
        jnp.concatenate([hidden, far_hidden], axis=0),
        sums + far_sum,
    )


def row_block(rows, columns):
    return pl.BlockSpec((rows, columns), lambda i: (0, 0))


def row_call(body, name, inputs, rows, outputs):
    specs = [row_block(v.shape[0] if v.shape[0] <= 16 else rows, v.shape[1]) for v in inputs]
    size = sum(rows * v.shape[1] * v.dtype.itemsize for v in inputs)
    return pl.pallas_call(
        body,
        grid=(1,),
        out_shape=tuple(outputs),
        in_specs=specs,
        out_specs=tuple(row_block(*v.shape) for v in outputs),
        cost_estimate=pl.CostEstimate(
            flops=20 * rows * inputs[0].shape[1], transcendentals=rows, bytes_accessed=2 * size
        ),
        compiler_params=pltpu.CompilerParams(vmem_limit_bytes=18 << 20),
        name=name,
    )(*inputs)


STEP = 128


def add_norm(base, partial, across, vectors, bias_at, norm_vectors, norm_at):
    rows, columns = base.shape

    def body(base_ref, bias_ref, vector_ref, partial_ref, across_ref, sum_ref, norm_ref):
        bias = bias_ref[bias_at : bias_at + 1, :]
        gain, shift = vector_ref[norm_at : norm_at + 1, :], vector_ref[norm_at + 1 : norm_at + 2, :]

        def step(i, carry):
            here = pl.ds(pl.multiple_of(i * STEP, STEP), STEP)
            there = pl.ds(pl.multiple_of((i * STEP + rows // 2) % rows, STEP), STEP)
            total = partial_ref[here, :].astype(F32) + across_ref[there, :].astype(F32)
            total = base_ref[here, :].astype(F32) + bias + total
            sum_ref[here, :] = total
            norm_ref[here, :] = (normalize(total)[0] * gain + shift).astype(BF16)
            return carry

        lax.fori_loop(0, rows // STEP, step, 0)

    return row_call(
        body,
        "add_norm",
        [base, vectors, norm_vectors, partial, across],
        rows,
        (shaped(rows, columns, F32), shaped(rows, columns, BF16)),
    )


def norm_back_near(skip, partial, across, value, vectors, norm_at, sums, sums_at):
    rows, columns = skip.shape

    def body(skip_ref, value_ref, vector_ref, old_ref, partial_ref, across_ref, *outs):
        grad_ref, low_ref, sum_ref = outs
        gain = vector_ref[norm_at : norm_at + 1, :]
        sum_ref[...] = old_ref[...]

        def step(i, own):
            here = pl.ds(pl.multiple_of(i * STEP, STEP), STEP)
            there = pl.ds(pl.multiple_of((i * STEP + rows // 2) % rows, STEP), STEP)
            grad = partial_ref[here, :].astype(F32) + across_ref[there, :].astype(F32)
            unit, scale = normalize(value_ref[here, :].astype(F32))
            skipped = skip_ref[here, :].astype(F32)
            if own:
                for j, each in enumerate((grad * unit, grad, skipped)):
                    sum_ref[sums_at + j : sums_at + j + 1, :] += jnp.sum(each, axis=0, keepdims=True)
            total = skipped + norm_pullback(grad, unit, scale, gain)
            grad_ref[here, :] = total
            low_ref[here, :] = total.astype(BF16)

        count = rows // STEP // 2
        lax.fori_loop(0, count, lambda i, carry: (step(i, True), carry)[1], 0)
        lax.fori_loop(count, 2 * count, lambda i, carry: (step(i, False), carry)[1], 0)

    return row_call(
        body,
        "norm_back_near",
        [skip, value, vectors, sums, partial, across],
        rows,
        (shaped(rows, columns, F32), shaped(rows, columns, BF16), shaped(16, columns, F32)),
    )


def norm_only(values):
    rows, columns = values.shape

    def body(value_ref, unit_ref):
        unit_ref[...] = normalize(value_ref[...].astype(F32))[0].astype(BF16)

    return row_call(body, "norm_only", [values], rows, (shaped(rows, columns, BF16),))[0]


def norm_back(skip, addends, value, vectors, norm_at, sums, sums_at):
    rows, columns = addends[-1].shape

    def body(*refs):
        skip_ref, value_ref, vector_ref, old_ref = refs[:4]
        parts, (grad_ref, low_ref, sum_ref) = refs[4:-3], refs[-3:]
        grad = parts[0][...].astype(F32)
        for part in parts[1:]:
            grad = grad + part[...].astype(F32)
        unit, scale = normalize(value_ref[...].astype(F32))
        skipped = skip_ref[...]
        sum_ref[...] = old_ref[...]
        for i, each in enumerate((grad * unit, grad, skipped)):
            sum_ref[sums_at + i : sums_at + i + 1, :] = jnp.sum(each, axis=0, keepdims=True)
        total = skipped + norm_pullback(grad, unit, scale, vector_ref[norm_at : norm_at + 1, :])
        grad_ref[...] = total
        low_ref[...] = total.astype(BF16)

    return row_call(
        body,
        "norm_back",
        [skip, value, vectors, sums] + list(addends),
        rows,
        (shaped(rows, columns, F32), shaped(rows, columns, BF16), shaped(16, columns, F32)),
    )


def normalize(values):
    center = values - jnp.mean(values, axis=-1, keepdims=True)
    spread = jnp.mean(center * center, axis=-1, keepdims=True)
    scale = lax.rsqrt(spread + EPSILON)
    return center * scale, scale


def norm_rows(values, gain, shift):
    return (normalize(values)[0] * gain + shift).astype(BF16)


def norm_pullback(grad, unit, scale, gain):
    inner = grad * gain
    return scale * (
        inner
        - jnp.mean(inner, axis=-1, keepdims=True)
        - unit * jnp.mean(inner * unit, axis=-1, keepdims=True)
    )


def times(left, right, kind=F32):
    return jnp.dot(left, right, preferred_element_type=F32).astype(kind)


def times_across(left, right, kind=F32):
    return dot_across(left, right).astype(kind)


def times_down(left, right, kind=F32):
    return row_major(dot_down(left, right).astype(kind))


def gather_rows(rows):
    near = stacked(rows, cross_x(rows))
    return near, cross_core(near)


def add_half(value, cross):
    middle = value.shape[0] // 2
    return value[:middle].astype(F32) + cross(value[middle:].astype(BF16)).astype(F32)


def add_columns(value, cross):
    middle = value.shape[1] // 2
    return value[:, :middle].astype(F32) + cross(value[:, middle:].astype(BF16)).astype(F32)


def column_halves(shard, y_index):
    middle = shard.shape[1] // 2
    own = jnp.where(y_index == 0, shard[:, :middle], shard[:, middle:])
    other = jnp.where(y_index == 0, shard[:, middle:], shard[:, :middle])
    return own, other


def natural_columns(own, other, y_index):
    return jnp.where(y_index == 0, beside(own, other), beside(other, own))


def order_matrix(width, z_index):
    rows = width // 4
    natural = lax.broadcasted_iota(jnp.int32, (width, width), 0)
    place = lax.broadcasted_iota(jnp.int32, (width, width), 1)
    step, inner = place // rows, place % rows
    distance = 2 * (step & 1) + (step >> 1)
    return (natural == (z_index ^ distance) * rows + inner).astype(BF16)


def my_rows(pair, y_index):
    own = jnp.where(y_index == 0, pair[0], pair[1])
    sent = jnp.where(y_index == 0, pair[1], pair[0])
    return y_order(own, cross_y(sent), y_index, 0)


ROWS = 64
SPARE = ROWS // 4


def turn(value):
    size = value.shape[0]
    eye = (
        lax.broadcasted_iota(jnp.int32, (size, size), 0)
        == lax.broadcasted_iota(jnp.int32, (size, size), 1)
    ).astype(BF16)
    return dot_down(value, eye)


def pack_vectors(blocks, place):
    flat = []
    for gains, merged_bias, expand_bias in blocks:
        flat += list(gains) + [merged_bias.transpose(1, 0, 2), expand_bias]

    number = len(flat)

    def body(*refs):
        refs = refs[1:]
        out, part, sem = refs[number], refs[number + 1 : -1], refs[-1]
        copies = [
            pltpu.make_async_copy(refs[i], part[i], sem.at[i]) for i in range(number)
        ]
        for copy in copies:
            copy.start()
        out[...] = jnp.zeros_like(out)
        for copy in copies:
            copy.wait()
        for b in range(2):
            vectors, merged_bias, expand_bias = part[8 * b : 8 * b + 6], part[8 * b + 6], part[8 * b + 7]
            for i in range(6):
                local = vectors[i].shape[0]
                out[6 * b + i : 6 * b + i + 1, :local] = vectors[i][...].astype(F32).reshape(1, local)
            for h in range(merged_bias.shape[0]):
                value = merged_bias[h].astype(F32)
                out[16 + 8 * b + 2 * h : 18 + 8 * b + 2 * h, : value.shape[1]] = value
            value = expand_bias[...].astype(F32)
            out[32 + 16 * b : 32 + 16 * b + value.shape[0], : value.shape[1]] = value

    return pl.pallas_call(
        body,
        out_shape=shaped(ROWS, 256, F32),
        in_specs=[SMEM] + [pl.BlockSpec(memory_space=pltpu.HBM)] * number,
        out_specs=VMEM,
        scratch_shapes=[pltpu.VMEM(v.shape, v.dtype) for v in flat]
        + [pltpu.SemaphoreType.DMA((number,))],
        compiler_params=pltpu.CompilerParams(vmem_limit_bytes=60 << 20),
        name="pack_vectors",
    )(place, *flat)


def prepare_first(place, merged, output, blocks):
    flat = []
    for gains, merged_bias, expand_bias in blocks:
        flat += list(gains) + [merged_bias.transpose(1, 0, 2), expand_bias]
    flat += [merged.transpose(1, 0, 2), output]
    number = len(flat)
    local = output.shape[1]

    def body(*refs):
        out, part, small, sem = refs[number], refs[number + 1 : -2], refs[-2], refs[-1]
        copies = [pltpu.make_async_copy(refs[i], part[i], sem.at[i]) for i in range(number)]
        for copy in copies:
            copy.start()
        small[...] = jnp.zeros_like(small)
        for copy in copies:
            copy.wait()
        for b in range(2):
            vectors, merged_bias, expand_bias = part[8 * b : 8 * b + 6], part[8 * b + 6], part[8 * b + 7]
            for i in range(6):
                small[6 * b + i : 6 * b + i + 1, :local] = (
                    vectors[i][...].astype(F32).reshape(1, local)
                )
            for h in range(merged_bias.shape[0]):
                value = merged_bias[h].astype(F32)
                small[16 + 8 * b + 2 * h : 18 + 8 * b + 2 * h, : value.shape[1]] = value
            value = expand_bias[...].astype(F32)
            small[32 + 16 * b : 32 + 16 * b + value.shape[0], : value.shape[1]] = value
        merged_ref, output_ref = part[-2:]
        pieces = [merged_ref[k] for k in range(3)] + [turn(output_ref[...]).astype(BF16)]
        out[:local, :] = jnp.concatenate(pieces, axis=1)
        for i in range(4):
            out[local:, local * i : local * (i + 1)] = small[
                SPARE * i : SPARE * (i + 1), :local
            ].astype(BF16)

    return pl.pallas_call(
        body,
        out_shape=shaped(local + SPARE, 4 * local, BF16),
        in_specs=[pl.BlockSpec(memory_space=pltpu.HBM)] * number,
        out_specs=VMEM,
        scratch_shapes=[pltpu.VMEM(v.shape, v.dtype) for v in flat]
        + [pltpu.VMEM((ROWS, 256), F32), pltpu.SemaphoreType.DMA((number,))],
        compiler_params=pltpu.CompilerParams(vmem_limit_bytes=60 << 20),
        name="prepare_first",
    )(*flat)


def unpack_vectors(pieces, place, local, merged_shape, expand_shape):
    heads, few = merged_shape[1], merged_shape[2]
    groups = expand_shape[0]
    width = heads * 4 * few

    def body(place_ref, *refs):
        pieces, outs, pieces_ref = refs[:4], refs[4:-1], refs[-1]
        for k in range(4):
            for i in range(4):
                pieces_ref[k * ROWS + i * SPARE : k * ROWS + (i + 1) * SPARE, :local] = pieces[k][
                    local:, local * i : local * (i + 1)
                ].astype(F32)
        y, z = place_ref[0], place_ref[1]
        for b in range(2):
            gains, bias, hidden = outs[3 * b : 3 * b + 3]
            for k in range(4):
                gains[0:6, k * local : (k + 1) * local] = pieces_ref[
                    k * ROWS + 6 * b : k * ROWS + 6 * b + 6, :local
                ]
            bias[...] = jnp.zeros_like(bias)
            for natural in range(4):
                distance = z ^ natural
                base = (2 * (distance & 1) + (distance >> 1)) * ROWS
                part = pieces_ref[pl.ds(pl.multiple_of(base, ROWS), ROWS), :128]
                for i in range(2):
                    for h in range(heads):
                        line = 16 + 8 * b + 2 * h + i
                        at = 2 * i * width + h * 4 * few + natural * few
                        bias[:, at : at + few] = part[line : line + 1, :few]
                lines = part[32 + 16 * b : 32 + 16 * b + groups]
                half = groups // 2
                lines = jnp.where(
                    y == 0, lines, jnp.concatenate([lines[half:], lines[:half]], axis=0)
                )
                for p in range(groups):
                    at = p * 4 * few + natural * few
                    hidden[:, at : at + few] = lines[p : p + 1, :few]

    one = (
        shaped(8, 4 * local, F32),
        shaped(1, 3 * width, F32),
        shaped(1, groups * 4 * few, F32),
    )
    return pl.pallas_call(
        body,
        out_shape=one + one,
        in_specs=[SMEM] + [VMEM] * 4,
        out_specs=(VMEM,) * 6,
        scratch_shapes=[pltpu.VMEM((4 * ROWS, 256), F32)],
        compiler_params=pltpu.CompilerParams(vmem_limit_bytes=8 << 20),
        name="unpack_vectors",
    )(place, *pieces)


def prepare_attend(merged, output):
    local = output.shape[1]

    def body(merged_ref, output_ref, attend):
        pieces = [merged_ref[k] for k in range(3)] + [turn(output_ref[...]).astype(BF16)]
        attend[...] = jnp.concatenate(pieces, axis=1)

    return pl.pallas_call(
        body,
        out_shape=shaped(local, 4 * local, BF16),
        in_specs=[VMEM, VMEM],
        out_specs=VMEM,
        compiler_params=pltpu.CompilerParams(vmem_limit_bytes=12 << 20),
        name="prepare_attend",
    )(merged.transpose(1, 0, 2), output)


def prepare_feed(place, expand, reduce):
    local, half = expand.shape[0], expand.shape[1] // 2

    def body(place_ref, expand_ref, reduce_ref, feed):
        y = place_ref[0]
        first, second = reduce_ref[:, :half], reduce_ref[:, half:]
        feed[:, :half] = jnp.where(y == 0, expand_ref[:, :half], expand_ref[:, half:])
        feed[:, half : 2 * half] = jnp.where(y == 0, first, second)
        feed[:, 2 * half :] = jnp.where(y == 0, second, first)

    return pl.pallas_call(
        body,
        out_shape=shaped(local, 3 * half, BF16),
        in_specs=[SMEM, VMEM, VMEM],
        out_specs=VMEM,
        compiler_params=pltpu.CompilerParams(vmem_limit_bytes=12 << 20),
        name="prepare_feed",
    )(place, expand, reduce.T)


def pack_grads(sums, biases, hiddens, place, local, merged_shape, expand_shape):
    heads, few = merged_shape[1], merged_shape[2]
    groups = expand_shape[0]
    width = heads * 4 * few

    def body(place_ref, sum_ref, bias_s, bias_t, hidden_s, hidden_t, out):
        y, z = place_ref[0], place_ref[1]
        out[...] = jnp.zeros_like(out)
        for k in range(4):
            out[k * ROWS : k * ROWS + 12, :local] = sum_ref[0:12, k * local : (k + 1) * local]
        for natural in range(4):
            distance = z ^ natural
            base = pl.multiple_of((2 * (distance & 1) + (distance >> 1)) * ROWS, ROWS)
            lines = []
            for bias in (bias_s, bias_t):
                for h in range(heads):
                    for i in range(2):
                        at = 2 * i * width + h * 4 * few + natural * few
                        lines.append(bias[:, at : at + few])
                lines.append(jnp.zeros((2, few), F32))
            for hidden in (hidden_s, hidden_t):
                rows = [
                    hidden[:, p * 4 * few + natural * few : p * 4 * few + natural * few + few]
                    for p in range(groups)
                ]
                first, second = rows[: groups // 2], rows[groups // 2 :]
                first, second = jnp.concatenate(first, axis=0), jnp.concatenate(second, axis=0)
                lines.append(jnp.where(y == 0, first, second))
                lines.append(jnp.where(y == 0, second, first))
                lines.append(jnp.zeros((16 - groups, few), F32))
            out[pl.ds(pl.multiple_of(base + 16, 16), ROWS - 16), :few] = jnp.concatenate(lines, axis=0)

    return pl.pallas_call(
        body,
        out_shape=shaped(4 * ROWS, 256, F32),
        in_specs=[SMEM] + [VMEM] * 5,
        out_specs=VMEM,
        compiler_params=pltpu.CompilerParams(vmem_limit_bytes=4 << 20),
        name="pack_grads",
    )(place, sums, *biases, *hiddens)


def unpack_grads(mine, arrived, local, merged_shape, expand_shape):
    heads, few = merged_shape[1], merged_shape[2]
    groups = expand_shape[0]

    def body(mine_ref, arrived_ref, *outs):
        total = mine_ref[0:ROWS, :] + arrived_ref[...]
        for b in range(2):
            vectors, merged_bias, expand_bias = outs[8 * b : 8 * b + 6], outs[8 * b + 6], outs[8 * b + 7]
            for i in range(6):
                vectors[i][...] = total[6 * b + i : 6 * b + i + 1, :local].reshape(local)
            for h in range(heads):
                merged_bias[h] = total[16 + 8 * b + 2 * h : 18 + 8 * b + 2 * h, :few]
            expand_bias[...] = total[32 + 16 * b : 32 + 16 * b + groups, :few]

    one = [jax.ShapeDtypeStruct((local,), F32)] * 6 + [
        jax.ShapeDtypeStruct((heads, 2, few), F32),
        jax.ShapeDtypeStruct(expand_shape, F32),
    ]
    values = pl.pallas_call(
        body,
        out_shape=tuple(one + one),
        in_specs=[VMEM] * 2,
        out_specs=(VMEM,) * 16,
        compiler_params=pltpu.CompilerParams(vmem_limit_bytes=4 << 20),
        name="unpack_grads",
    )(mine, arrived)
    return [v.transpose(1, 0, 2) if v.ndim == 3 else v for v in values]


def finish_feed(mine, theirs, place, half):
    local = mine.shape[0]
    whole = mine.shape[1] == 3 * half

    def body(place_ref, mine_ref, theirs_ref, expand, reduce):
        y = place_ref[0]
        own, other = mine_ref[:, :half].astype(F32), theirs_ref[:, :half].astype(F32)
        expand[:, :half] = jnp.where(y == 0, own, other)
        expand[:, half:] = jnp.where(y == 0, other, own)
        if whole:
            total = mine_ref[:, half:].astype(F32) + theirs_ref[:, half:].astype(F32)
            own, other = total[:, :half], total[:, half:]
        else:
            own, other = mine_ref[:, half:].astype(F32), theirs_ref[:, half:].astype(F32)
        reduce[:, :half] = jnp.where(y == 0, own, other)
        reduce[:, half:] = jnp.where(y == 0, other, own)

    expand, reduce = pl.pallas_call(
        body,
        out_shape=(shaped(local, 2 * half, F32), shaped(local, 2 * half, F32)),
        in_specs=[SMEM, VMEM, VMEM],
        out_specs=(VMEM, VMEM),
        compiler_params=pltpu.CompilerParams(vmem_limit_bytes=12 << 20),
        name="finish_feed",
    )(place, mine, theirs)
    return expand, reduce.T


def finish_attend(added, mine, theirs, place):
    local = mine.shape[0]

    def body(place_ref, *refs):
        mine_ref, theirs_ref, merged, output = refs[-4:]
        y = place_ref[0]
        own, other = mine_ref[...], theirs_ref[...]
        split = jnp.concatenate(
            [jnp.where(y == 0, own, other), jnp.where(y == 0, other, own)], axis=1
        )
        output[...] = turn(split[:, -local:])
        whole = split.astype(F32)
        if added:
            total = refs[0][...].astype(F32) + refs[1][...].astype(F32)
            whole = jnp.concatenate([total, whole], axis=1)
        for k in range(3):
            merged[k] = whole[:, k * local : (k + 1) * local]

    merged, output = pl.pallas_call(
        body,
        out_shape=(jax.ShapeDtypeStruct((3, local, local), F32), shaped(local, local, F32)),
        in_specs=[SMEM] + [VMEM] * (2 + len(added)),
        out_specs=(VMEM, VMEM),
        compiler_params=pltpu.CompilerParams(vmem_limit_bytes=12 << 20),
        name="finish_attend",
    )(place, *added, mine, theirs)
    return merged.transpose(1, 0, 2), output


def halves_added(kept, arrived):
    middle = kept.shape[0] // 2
    return (kept[middle:] + arrived[middle:].astype(F32)).astype(BF16)


def core_sum(kept, arrived):
    return (kept + arrived.astype(F32)).astype(BF16)


def added(first, second):
    return (first.astype(F32) + second.astype(F32)).astype(BF16)


def send_columns(value, cross):
    middle = value.shape[1] // 2
    return cross(value[:, middle:].astype(BF16))


def keep_columns(value, arrived):
    return value[:, : value.shape[1] // 2].astype(F32) + arrived.astype(F32)


def send_rows(value, cross):
    middle = value.shape[0] // 2
    return cross(value[middle:].astype(BF16))


def keep_rows(value, arrived):
    return value[: value.shape[0] // 2].astype(F32) + arrived.astype(F32)


def fast_shards(inputs, segments, cotangent, *params):
    y_index = lax.axis_index("ctx")
    z_index = lax.axis_index("dp")
    me = lax.axis_index("tp")
    tokens, features = inputs.shape[1], inputs.shape[2]
    length = segments.shape[1] * 2
    doc_max = min(DOC_MAX, length // 2)
    blocks = (params[:12], params[12:])
    local = features // 4
    half = local * 2

    small = [((p[0], p[1], p[5], p[6], p[7], p[11]), p[3], p[9]) for p in blocks]
    place = jnp.stack([y_index, z_index]).astype(jnp.int32)
    p = blocks[0]
    attend = prepare_first(place, p[2], p[4], small)
    inputs, attend = pin(inputs, attend)
    far = cross_far(attend)
    sent_rows = jnp.where(y_index == 0, inputs[1], inputs[0])
    sent_rows, late = pin(sent_rows, attend)
    near = cross_near(late)
    sent_docs = jnp.where(y_index == 0, segments[1:2], segments[0:1]).astype(BF16)
    sent_docs = jnp.pad(sent_docs, ((0, 15), (0, features - sent_docs.shape[1])))
    moved = cross_y(stacked(sent_rows, sent_docs))
    kept_rows = jnp.where(y_index == 0, inputs[0], inputs[1])
    kept_docs = jnp.where(y_index == 0, segments[0:1], segments[1:2]).astype(F32)
    chooser = order_matrix(features, z_index)
    raw = times(y_order(kept_rows, moved[:tokens], y_index, 0), chooser, BF16)
    docs = y_order(
        kept_docs, moved[tokens : tokens + 1, : kept_docs.shape[1]].astype(F32), y_index, 1
    )
    context = (me.astype(jnp.int32).reshape(1), docs)
    both = cross_near(far)
    feed = prepare_feed(place, blocks[0][8], blocks[0][10])
    feed, far = pin(feed, far)
    p_far = cross_far(feed[:, : 2 * half])
    moved_grad = cross_y(jnp.where(y_index == 0, cotangent[1], cotangent[0]))
    raw, place_t, output_t = pin(raw, place, blocks[1][4])
    own_a = prepare_attend(blocks[1][2], output_t)
    feed_t = prepare_feed(place_t, blocks[1][8], blocks[1][10])

    stream = stacked(raw, cross_x(raw))
    stream, near, both, p_far, own_a, feed_t, moved_grad = pin(
        stream, near, both, p_far, own_a, feed_t, moved_grad
    )
    near_s = norm_only(stream)
    gains_s, bias_s, hidden_s, gains_t, bias_t, hidden_t = unpack_vectors(
        (attend, far, near, both), place, local, blocks[0][3].shape, blocks[0][9].shape
    )
    far_s = cross_core(near_s)
    attend_s = (attend, far, near, both)
    e_two = stacked(feed[:, :half], p_far[:, :half])
    e_near = cross_near(e_two)
    r_far = cross_far(feed[:, 2 * half :])
    grad_out = times(
        y_order(jnp.where(y_index == 0, cotangent[0], cotangent[1]), moved_grad, y_index, 0),
        chooser,
        BF16,
    )
    moved_grad = cross_x(grad_out)
    sent, kept, *saved_s, near_s, far_s = attention_forward(
        near_s, far_s, attend_s, bias_s, context, doc_max, (gains_s,)
    )
    sent, e_near, r_far, moved_grad = pin(sent, e_near, r_far, moved_grad)
    e_s = stacked(e_two, e_near)
    e_other = cross_y(e_s)
    r_two = stacked(feed[:, half:], beside(p_far[:, half:], r_far))
    r_near = cross_near(r_two)
    a_far = cross_far(own_a)
    partial = core_sum(kept, cross_core(sent))
    middle_s, near_two_s = add_norm(stream, partial, cross_x(partial), gains_s, 2, gains_s, 3)
    near_two_s, e_other, r_near, a_far, feed_t = pin(near_two_s, e_other, r_near, a_far, feed_t)
    a_two = stacked(own_a, a_far)
    a_near = cross_near(a_two)
    te_far, tr_far = cross_far(feed_t[:, :half]), cross_far(feed_t[:, 2 * half :])
    far_two_s = cross_core(near_two_s)
    feed_s = (near_two_s, far_two_s), ((e_s, e_other), (r_two, r_near), hidden_s)
    sent, kept = feed_forward(*feed_s[0], *feed_s[1])
    partial = core_sum(kept, cross_core(sent))
    between, near_t = add_norm(middle_s, partial, cross_x(partial), gains_s, 5, gains_t, 0)

    near_t, a_near, te_far, tr_far, feed_t = pin(near_t, a_near, te_far, tr_far, feed_t)
    attend_t = (a_two, a_near)
    te_two = stacked(feed_t[:, :half], te_far)
    te_near = cross_near(te_two)
    tr_far_one = cross_far(feed_t[:, half : 2 * half])
    far_t = cross_core(near_t)
    sent, kept, *saved_t = attention_forward(near_t, far_t, attend_t, bias_t, context, doc_max)
    sent, te_near, tr_far_one = pin(sent, te_near, tr_far_one)
    te = stacked(te_two, te_near)
    te_other = cross_y(te)
    tr_two = stacked(feed_t[:, half:], beside(tr_far_one, tr_far))
    tr_near = cross_near(tr_two)
    branch = stacked(grad_out, moved_grad)
    branch_far = cross_core(branch)
    partial = core_sum(kept, cross_core(sent))
    middle_t, near_two_t = add_norm(between, partial, cross_x(partial), gains_t, 2, gains_t, 3)
    near_two_t, te_other, tr_near, branch_far = pin(near_two_t, te_other, tr_near, branch_far)
    far_two_t = cross_core(near_two_t)
    feed_t = (near_two_t, far_two_t), ((te, te_other), (tr_two, tr_near), hidden_t)

    sums = jnp.zeros((16, features), F32)
    sent, kept, active, grad_hidden, hidden_sum_t = feed_backward(
        *feed_t[0], branch, branch_far, *feed_t[1]
    )
    partial = core_sum(kept, cross_core(sent))
    part_r = times_down(stacked(branch, branch_far), active, BF16)
    part_r, partial = pin(part_r, partial)
    r_moved = send_rows(part_r, cross_near)
    part_e = times_down(stacked(near_two_t, far_two_t), grad_hidden, BF16)
    e_moved = send_columns(part_e, cross_y)
    late_t, _ = pin(near_two_t, part_e)
    final_sent, final_kept = feed_forward(late_t, far_two_t, *feed_t[1])
    grad_middle, near_grad, sums = norm_back_near(
        branch, partial, cross_x(partial), middle_t, gains_t, 3, sums, 9
    )
    near_grad, r_moved, e_moved, final_sent, final_kept = pin(
        near_grad, r_moved, e_moved, final_sent, final_kept
    )
    part_e, part_r = keep_columns(part_e, e_moved), keep_rows(part_r, r_moved)
    e_moved = send_rows(part_e, cross_near)
    far_grad = cross_core(near_grad)
    sent, kept, grad_qkv, qkv_sum_t = attention_backward(
        near_grad, far_grad, attend_t, context, saved_t, doc_max
    )
    sent, e_moved, part_r = pin(sent, e_moved, part_r)
    part_e = keep_rows(part_e, e_moved)
    e_moved, r_moved = send_rows(part_e, cross_far), send_rows(part_r, cross_far)
    partial = core_sum(kept, cross_core(sent))
    part_a = beside(
        times_down(stacked(near_t, far_t), grad_qkv, BF16),
        times_down(stacked(near_grad, far_grad), saved_t[1], BF16),
    )
    part_a, a_moved = column_halves(part_a, y_index)
    a_moved = cross_y(a_moved)
    grad_between, branch, sums = norm_back_near(
        grad_middle, partial, cross_x(partial), between, gains_t, 0, sums, 6
    )

    branch, e_moved, r_moved, a_moved = pin(branch, e_moved, r_moved, a_moved)
    part_e, part_r = keep_rows(part_e, e_moved), keep_rows(part_r, r_moved)
    part_a = part_a.astype(F32) + a_moved.astype(F32)
    branch_far = cross_core(branch)
    sent, kept, active, grad_hidden, hidden_sum_s = feed_backward(
        *feed_s[0], branch, branch_far, *feed_s[1]
    )
    partial = core_sum(kept, cross_core(sent))
    feed_r = times_down(stacked(branch, branch_far), active, BF16)
    feed_r, part_a, partial = pin(feed_r, part_a, partial)
    fr_moved, a_moved = send_rows(feed_r, cross_near), send_rows(part_a, cross_near)
    feed_e = times_down(stacked(near_two_s, far_two_s), grad_hidden, BF16)
    fe_moved = send_columns(feed_e, cross_y)
    grad_middle, near_grad, sums = norm_back_near(
        grad_between, partial, cross_x(partial), middle_s, gains_s, 3, sums, 3
    )
    near_grad, a_moved, fr_moved, fe_moved, part_e, part_r = pin(
        near_grad, a_moved, fr_moved, fe_moved, part_e, part_r
    )
    part_a, feed_r, feed_e = (
        keep_rows(part_a, a_moved),
        keep_rows(feed_r, fr_moved),
        keep_columns(feed_e, fe_moved),
    )
    a_moved, fe_moved = send_rows(part_a, cross_far), send_rows(feed_e, cross_near)
    mine_t = beside(part_e, part_r).astype(BF16)
    theirs_t = cross_y(
        beside(mine_t[:, :half], mine_t[:, 2 * half :], mine_t[:, half : 2 * half])
    )
    far_grad = cross_core(near_grad)
    sent, kept, grad_qkv, qkv_sum_s = attention_backward(
        near_grad, far_grad, attend_s, context, saved_s, doc_max
    )
    sent, a_moved, fe_moved, feed_r = pin(sent, a_moved, fe_moved, feed_r)
    mine_at, feed_e = keep_rows(part_a, a_moved), keep_rows(feed_e, fe_moved)
    fr_moved, fe_moved = send_rows(feed_r, cross_far), send_rows(feed_e, cross_far)
    arrived = cross_core(sent)
    across = cross_x(halves_added(kept, arrived))
    grad_a = beside(
        times_down(stacked(near_s, far_s), grad_qkv, BF16),
        times_down(stacked(near_grad, far_grad), saved_s[1], BF16),
    )
    grad_a, y_moved = column_halves(grad_a, y_index)
    y_moved = cross_y(y_moved)
    grad_in, _, sums = norm_back(
        grad_middle, (kept, arrived, across), stream, gains_s, 0, sums, 0
    )
    sums_moved = cross_core(sums)
    input_grad = lax.dot_general(
        grad_in,
        chooser.astype(F32),
        (((1,), (1,)), ((), ())),
        precision=lax.Precision.HIGHEST,
        preferred_element_type=F32,
    )

    def swapped(value):
        first, second = value[:tokens], value[tokens:]
        return cross_y(jnp.where(y_index == 0, second, first))

    def restore(value, received):
        kept = jnp.where(y_index == 0, value[:tokens], value[tokens:])
        return jnp.where(y_index == 0, jnp.stack([kept, received]), jnp.stack([received, kept]))

    grad_moved = swapped(input_grad.astype(BF16))
    y_moved, sums_moved, theirs_t = pin(y_moved, sums_moved, theirs_t)
    grad_a = grad_a.astype(F32) + y_moved.astype(F32)
    y_moved = send_rows(grad_a, cross_near)
    sums = sums + sums_moved
    sums_moved = cross_x(sums)
    final_arrived = cross_core(final_sent)
    sums_moved, final_arrived, grad_moved = pin(sums_moved, final_arrived, grad_moved)
    final_across = cross_x(halves_added(final_kept, final_arrived))
    pack = pack_grads(
        sums + sums_moved,
        (qkv_sum_s, qkv_sum_t),
        (hidden_sum_s, hidden_sum_t),
        place,
        local,
        params[3].shape,
        params[9].shape,
    )
    pack_moved = cross_y(pack)
    fe_moved, fr_moved, mine_at, pack = pin(fe_moved, fr_moved, mine_at, pack)
    mine_s = beside(keep_rows(feed_e, fe_moved), keep_rows(feed_r, fr_moved), mine_at).astype(BF16)
    theirs_s = cross_y(
        beside(
            mine_s[:, :half], mine_s[:, 2 * half : 3 * half], mine_s[:, half : 2 * half], mine_s[:, 3 * half :]
        )
    )
    late, _ = pin(mine_t, mine_s)
    expand_grad_t, reduce_grad_t = finish_feed(late, theirs_t, place, half)
    grad_a = keep_rows(grad_a, y_moved)
    y_moved = send_rows(grad_a, cross_far)
    final_across, expand_grad_t = pin(final_across, expand_grad_t)
    rows = 2 * tokens
    final = middle_t[:rows] + gains_t[5:6] + final_kept[:rows] + final_across.astype(F32)
    final = final + final_arrived[:rows].astype(F32)
    final = times_across(final.astype(BF16), chooser, BF16)
    y_moved, pack_moved, final = pin(y_moved, pack_moved, final)
    pack = pack + pack_moved
    pack_near = cross_near(pack[2 * ROWS :])
    mine_a = keep_rows(grad_a, y_moved).astype(BF16)
    theirs_a = cross_y(mine_a)
    final_moved = swapped(final)
    merged_grad_t, output_grad_t = finish_attend(
        (), mine_s[:, 3 * half :], theirs_s[:, 3 * half :], place
    )
    expand_grad_s, reduce_grad_s = finish_feed(
        mine_s[:, : 3 * half], theirs_s[:, : 3 * half], place, half
    )
    pack_near, pack = pin(pack_near, pack)
    pack = pack[: 2 * ROWS] + pack_near
    pack_far = cross_far(pack[ROWS:])
    vectors = unpack_grads(pack, pack_far, local, params[3].shape, params[9].shape)
    final = restore(final, final_moved)
    theirs_a, final, first, output_grad_t, expand_grad_s = pin(
        theirs_a, final, vectors[0], output_grad_t, expand_grad_s
    )
    vectors[0] = first
    merged_grad_s, output_grad_s = finish_attend((), mine_a, theirs_a, place)
    outputs = [final, restore(input_grad, grad_moved.astype(F32))]
    for vector, merged, output, expand, reduce in (
        (vectors[:8], merged_grad_s, output_grad_s, expand_grad_s, reduce_grad_s),
        (vectors[8:], merged_grad_t, output_grad_t, expand_grad_t, reduce_grad_t),
    ):
        outputs += [
            vector[0],
            vector[1],
            merged,
            vector[6],
            output,
            vector[2],
            vector[3],
            vector[4],
            expand,
            vector[7],
            reduce,
            vector[5],
        ]
    return tuple(outputs)


def solution(mesh):
    quick = (mesh.shape["dp"], mesh.shape["ctx"], mesh.shape["tp"]) == (4, 2, 4)
    placed = (
        P("dp", ("ctx", "tp"), None),
        P("dp", "ctx"),
        P("dp", ("ctx", "tp"), None),
        P("dp"),
        P("dp"),
        P("dp", None, "tp"),
        P(None, "tp", "dp"),
        P("tp", "dp"),
        P("dp"),
        P("dp"),
        P("dp"),
        P("dp", "tp"),
        P("tp", "dp"),
        P("tp", "dp"),
        P("dp"),
        P("dp"),
        P("dp"),
        P("dp", None, "tp"),
        P(None, "tp", "dp"),
        P("tp", "dp"),
        P("dp"),
        P("dp"),
        P("dp"),
        P("dp", "tp"),
        P("tp", "dp"),
        P("tp", "dp"),
        P("dp"),
    )
    return jax.shard_map(
        fast_shards if quick else general_shards,
        mesh=mesh,
        in_specs=placed,
        out_specs=(
            P("dp", ("ctx", "tp"), None),
            P("dp", ("ctx", "tp"), None),
            P("dp"),
            P("dp"),
            P("dp", None, "tp"),
            P(None, "tp", "dp"),
            P("tp", "dp"),
            P("dp"),
            P("dp"),
            P("dp"),
            P("dp", "tp"),
            P("tp", "dp"),
            P("tp", "dp"),
            P("dp"),
            P("dp"),
            P("dp"),
            P("dp", None, "tp"),
            P(None, "tp", "dp"),
            P("tp", "dp"),
            P("dp"),
            P("dp"),
            P("dp"),
            P("dp", "tp"),
            P("tp", "dp"),
            P("tp", "dp"),
            P("dp"),
        ),
        check_vma=False,
    )
```

```python
import jax
import jax.numpy as jnp
from jax import lax
from jax.experimental import pallas as pl
from jax.experimental.layout import Layout, with_layout_constraint
from jax.experimental.pallas import tpu as pltpu
from jax.sharding import PartitionSpec as P

HD = 64
DOC_MAX = 2000


EPSILON = 1e-05
GELU_SCALE = 0.7978845608028654


def from_behind(block, axis, distance):
    devices = range(lax.axis_size(axis))
    route = [(i - distance, i) for i in devices if i - distance in devices]
    return lax.ppermute(block, axis, route)


def layer_norm(values, norm_gain, norm_shift):
    center = values - jnp.mean(values, axis=-1, keepdims=True)
    spread = jnp.mean(center * center, axis=-1, keepdims=True)
    return center * lax.rsqrt(spread + EPSILON) * norm_gain + norm_shift


def gelu_tanh(values):
    return (
        0.5 * values * (1.0 + jnp.tanh(GELU_SCALE * (values + 0.044715 * values * values * values)))
    )


def spread_rows(row_block):
    return lax.all_gather(row_block, "tp", axis=1, tiled=True)


def gather_sums(partial_value):
    return lax.psum_scatter(
        partial_value.astype(jnp.bfloat16), "tp", scatter_dimension=1, tiled=True
    ).astype(jnp.float32)


def to_items(tensor, head_count):
    batches, length, features = tensor.shape
    head_size = features // head_count
    return (
        tensor.reshape(batches, length, head_count, head_size)
        .transpose(0, 2, 1, 3)
        .reshape(batches * head_count, length, head_size)
    )


def from_items(tensor, head_count):
    item_count, length, head_size = tensor.shape
    batches = item_count // head_count
    return (
        tensor.reshape(batches, head_count, length, head_size)
        .transpose(0, 2, 1, 3)
        .reshape(batches, length, head_count * head_size)
    )


def masked_scores(query_rows, key_rows, query_docs, key_docs, allowed):
    raw_scores = (
        jnp.einsum("qd,kd->qk", query_rows, key_rows, preferred_element_type=jnp.float32) * 0.125
    )
    keep_mask = allowed & (key_docs[None, :] == query_docs[:, None])
    return (jnp.where(keep_mask, raw_scores, -1e30), keep_mask)


def attend_forward(allowed):

    def attend_item(packed):
        query_rows, key_rows, value_rows, query_docs, key_docs = packed
        scores, keep_mask = masked_scores(query_rows, key_rows, query_docs, key_docs, allowed)
        row_top = jnp.max(scores, axis=-1, keepdims=True)
        raised = jnp.exp(scores - row_top)
        row_total = jnp.sum(raised, axis=-1, keepdims=True)
        weights = (raised / row_total).astype(jnp.bfloat16)
        mixed_rows = jnp.dot(weights, value_rows, preferred_element_type=jnp.float32).astype(
            jnp.bfloat16
        )
        return (mixed_rows, row_top[:, 0] + jnp.log(row_total[:, 0]))

    return attend_item


def attend_backward(allowed):

    def attend_item(packed):
        query_rows, key_rows, value_rows, query_docs, key_docs, log_total, grad_rows = packed
        scores, keep_mask = masked_scores(query_rows, key_rows, query_docs, key_docs, allowed)
        weights = jnp.where(keep_mask, jnp.exp(scores - log_total[:, None]), 0.0)
        grad_values = jnp.einsum(
            "qk,qd->kd", weights.astype(jnp.bfloat16), grad_rows, preferred_element_type=jnp.float32
        )
        grad_weights = jnp.einsum(
            "qd,kd->qk", grad_rows, value_rows, preferred_element_type=jnp.float32
        )
        centered = jnp.sum(weights * grad_weights, axis=-1, keepdims=True)
        grad_scores = (weights * (grad_weights - centered)).astype(jnp.bfloat16)
        grad_query = jnp.dot(grad_scores, key_rows, preferred_element_type=jnp.float32) * 0.125
        grad_keys = (
            jnp.einsum("qk,qd->kd", grad_scores, query_rows, preferred_element_type=jnp.float32)
            * 0.125
        )
        return (grad_query, grad_keys, grad_values)

    return attend_item


def layer_forward(stream, params, segments, key_docs, allowed, cycle_steps):
    (
        first_gain,
        first_shift,
        merged_weight,
        merged_bias,
        output_weight,
        output_bias,
        second_gain,
        second_shift,
        expand_weight,
        expand_bias,
        reduce_weight,
        reduce_bias,
    ) = params
    fetched = (
        lax.all_gather(first_gain, "dp", axis=0, tiled=True),
        lax.all_gather(first_shift, "dp", axis=0, tiled=True),
        lax.all_gather(merged_weight, "dp", axis=0, tiled=True),
        lax.all_gather(merged_bias, "dp", axis=2, tiled=True),
        lax.all_gather(output_weight, "dp", axis=1, tiled=True),
        lax.all_gather(output_bias, "dp", axis=0, tiled=True),
        lax.all_gather(second_gain, "dp", axis=0, tiled=True),
        lax.all_gather(second_shift, "dp", axis=0, tiled=True),
        lax.all_gather(expand_weight, "dp", axis=0, tiled=True),
        lax.all_gather(expand_bias, "dp", axis=1, tiled=True),
        lax.all_gather(reduce_weight, "dp", axis=1, tiled=True),
        lax.all_gather(reduce_bias, "dp", axis=0, tiled=True),
    )
    (
        first_gain,
        first_shift,
        merged_weight,
        merged_bias,
        output_weight,
        output_bias,
        second_gain,
        second_shift,
        expand_weight,
        expand_bias,
        reduce_weight,
        reduce_bias,
    ) = fetched
    head_count = merged_weight.shape[2] // HD
    normed = layer_norm(
        stream, first_gain.astype(jnp.float32), first_shift.astype(jnp.float32)
    ).astype(jnp.bfloat16)
    first_rows = spread_rows(normed)
    merged_out = jnp.einsum(
        "std,dkf->stkf", first_rows, merged_weight, preferred_element_type=jnp.float32
    )
    bias_pair = merged_bias.astype(jnp.float32).reshape(2, -1)
    query_rows = (merged_out[:, :, 0] + bias_pair[0]).astype(jnp.bfloat16)
    key_rows = merged_out[:, :, 1].astype(jnp.bfloat16)
    value_rows = (merged_out[:, :, 2] + bias_pair[1]).astype(jnp.bfloat16)
    key_list = [key_rows]
    value_list = [value_rows]
    moving = (key_rows, value_rows)
    for offset in range(cycle_steps):
        moving = from_behind((moving[0], moving[1]), "ctx", 1)
        key_list.insert(0, moving[0])
        value_list.insert(0, moving[1])
    query_items = to_items(query_rows, head_count)
    key_items = to_items(jnp.concatenate(key_list, axis=1), head_count)
    value_items = to_items(jnp.concatenate(value_list, axis=1), head_count)
    query_docs = jnp.repeat(segments, head_count, axis=0)
    window_docs = jnp.repeat(key_docs, head_count, axis=0)
    mixed_items, log_total = lax.map(
        attend_forward(allowed), (query_items, key_items, value_items, query_docs, window_docs)
    )
    mixed = from_items(mixed_items, head_count)
    attn_part = jnp.einsum("stf,fd->std", mixed, output_weight, preferred_element_type=jnp.float32)
    middle = stream + gather_sums(attn_part) + output_bias.astype(jnp.float32)
    normed_two = layer_norm(
        middle, second_gain.astype(jnp.float32), second_shift.astype(jnp.float32)
    ).astype(jnp.bfloat16)
    second_rows = spread_rows(normed_two)
    hidden = jnp.einsum(
        "std,df->stf", second_rows, expand_weight, preferred_element_type=jnp.float32
    ) + expand_bias.astype(jnp.float32).reshape(-1)
    activated = gelu_tanh(hidden).astype(jnp.bfloat16)
    mlp_part = jnp.einsum(
        "stf,fd->std", activated, reduce_weight, preferred_element_type=jnp.float32
    )
    result = middle + gather_sums(mlp_part) + reduce_bias.astype(jnp.float32)
    saved_state = (
        fetched,
        stream,
        first_rows,
        query_items,
        key_items,
        value_items,
        query_docs,
        window_docs,
        log_total,
        mixed,
        middle,
        second_rows,
        hidden,
        activated,
    )
    return (result, saved_state)


def reduce_grads(fresh):
    (
        gain_one,
        shift_one,
        merged_weights,
        merged_biases,
        output_weights,
        output_biases,
        gain_two,
        shift_two,
        expand_weights,
        expand_biases,
        reduce_weights,
        reduce_biases,
    ) = fresh
    summed = (
        lax.psum(gain_one.astype(jnp.bfloat16), "ctx").astype(jnp.float32),
        lax.psum(shift_one.astype(jnp.bfloat16), "ctx").astype(jnp.float32),
        lax.psum(merged_weights.astype(jnp.bfloat16), "ctx").astype(jnp.float32),
        lax.psum(merged_biases.astype(jnp.bfloat16), "ctx").astype(jnp.float32),
        lax.psum(output_weights.astype(jnp.bfloat16), "ctx").astype(jnp.float32),
        lax.psum(output_biases.astype(jnp.bfloat16), "ctx").astype(jnp.float32),
        lax.psum(gain_two.astype(jnp.bfloat16), "ctx").astype(jnp.float32),
        lax.psum(shift_two.astype(jnp.bfloat16), "ctx").astype(jnp.float32),
        lax.psum(expand_weights.astype(jnp.bfloat16), "ctx").astype(jnp.float32),
        lax.psum(expand_biases.astype(jnp.bfloat16), "ctx").astype(jnp.float32),
        lax.psum(reduce_weights.astype(jnp.bfloat16), "ctx").astype(jnp.float32),
        lax.psum(reduce_biases.astype(jnp.bfloat16), "ctx").astype(jnp.float32),
    )
    (
        gain_one,
        shift_one,
        merged_weights,
        merged_biases,
        output_weights,
        output_biases,
        gain_two,
        shift_two,
        expand_weights,
        expand_biases,
        reduce_weights,
        reduce_biases,
    ) = summed
    return (
        lax.psum_scatter(
            gain_one.astype(jnp.bfloat16), "dp", scatter_dimension=0, tiled=True
        ).astype(jnp.float32),
        lax.psum_scatter(
            shift_one.astype(jnp.bfloat16), "dp", scatter_dimension=0, tiled=True
        ).astype(jnp.float32),
        lax.psum_scatter(
            merged_weights.astype(jnp.bfloat16), "dp", scatter_dimension=0, tiled=True
        ).astype(jnp.float32),
        lax.psum_scatter(
            merged_biases.astype(jnp.bfloat16), "dp", scatter_dimension=2, tiled=True
        ).astype(jnp.float32),
        lax.psum_scatter(
            output_weights.astype(jnp.bfloat16), "dp", scatter_dimension=1, tiled=True
        ).astype(jnp.float32),
        lax.psum_scatter(
            output_biases.astype(jnp.bfloat16), "dp", scatter_dimension=0, tiled=True
        ).astype(jnp.float32),
        lax.psum_scatter(
            gain_two.astype(jnp.bfloat16), "dp", scatter_dimension=0, tiled=True
        ).astype(jnp.float32),
        lax.psum_scatter(
            shift_two.astype(jnp.bfloat16), "dp", scatter_dimension=0, tiled=True
        ).astype(jnp.float32),
        lax.psum_scatter(
            expand_weights.astype(jnp.bfloat16), "dp", scatter_dimension=0, tiled=True
        ).astype(jnp.float32),
        lax.psum_scatter(
            expand_biases.astype(jnp.bfloat16), "dp", scatter_dimension=1, tiled=True
        ).astype(jnp.float32),
        lax.psum_scatter(
            reduce_weights.astype(jnp.bfloat16), "dp", scatter_dimension=1, tiled=True
        ).astype(jnp.float32),
        lax.psum_scatter(
            reduce_biases.astype(jnp.bfloat16), "dp", scatter_dimension=0, tiled=True
        ).astype(jnp.float32),
    )


def layer_backward(grad_out, saved_state, allowed, cycle_steps, token_count):
    (
        fetched,
        stream,
        first_rows,
        query_items,
        key_items,
        value_items,
        query_docs,
        window_docs,
        log_total,
        mixed,
        middle,
        second_rows,
        hidden,
        activated,
    ) = saved_state
    (
        first_gain,
        first_shift,
        merged_weight,
        merged_bias,
        output_weight,
        output_bias,
        second_gain,
        second_shift,
        expand_weight,
        expand_bias,
        reduce_weight,
        reduce_bias,
    ) = fetched
    head_count = merged_weight.shape[2] // HD
    grad_branch = spread_rows(grad_out.astype(jnp.bfloat16))
    grad_reduce = jnp.einsum(
        "stf,std->fd", activated, grad_branch, preferred_element_type=jnp.float32
    )
    grad_active = jnp.einsum(
        "std,fd->stf", grad_branch, reduce_weight, preferred_element_type=jnp.float32
    )
    _, gelu_pull = jax.vjp(gelu_tanh, hidden)
    grad_hidden = gelu_pull(grad_active)[0].astype(jnp.bfloat16)
    grad_expand_bias = jnp.sum(grad_hidden, axis=(0, 1), dtype=jnp.float32).reshape(
        expand_bias.shape
    )
    grad_expand = jnp.einsum(
        "std,stf->df", second_rows, grad_hidden, preferred_element_type=jnp.float32
    )
    grad_second = gather_sums(
        jnp.einsum("stf,df->std", grad_hidden, expand_weight, preferred_element_type=jnp.float32)
    )
    _, second_pull = jax.vjp(
        layer_norm, middle, second_gain.astype(jnp.float32), second_shift.astype(jnp.float32)
    )
    grad_norm_mid, grad_second_gain, grad_second_shift = second_pull(grad_second)
    grad_middle = grad_out + grad_norm_mid
    grad_reduce_bias = jnp.sum(grad_out, axis=(0, 1))
    grad_attend = spread_rows(grad_middle.astype(jnp.bfloat16))
    grad_output = jnp.einsum("stf,std->fd", mixed, grad_attend, preferred_element_type=jnp.float32)
    grad_mixed = jnp.einsum(
        "std,fd->stf", grad_attend, output_weight, preferred_element_type=jnp.float32
    ).astype(jnp.bfloat16)
    grad_query_items, grad_key_items, grad_value_items = lax.map(
        attend_backward(allowed),
        (
            query_items,
            key_items,
            value_items,
            query_docs,
            window_docs,
            log_total,
            to_items(grad_mixed, head_count),
        ),
    )
    grad_query = from_items(grad_query_items, head_count)
    window_keys = from_items(grad_key_items, head_count)
    window_values = from_items(grad_value_items, head_count)
    local_keys = window_keys[:, cycle_steps * token_count :]
    local_values = window_values[:, cycle_steps * token_count :]
    carried = None
    for offset in range(cycle_steps, 0, -1):
        start_row = (cycle_steps - offset) * token_count
        block_keys = window_keys[:, start_row : start_row + token_count]
        block_values = window_values[:, start_row : start_row + token_count]
        if carried is not None:
            block_keys = block_keys + carried[0]
            block_values = block_values + carried[1]
        carried = (
            from_behind(block_keys.astype(jnp.bfloat16), "ctx", -1).astype(block_keys.dtype),
            from_behind(block_values.astype(jnp.bfloat16), "ctx", -1).astype(block_values.dtype),
        )
    local_keys = local_keys + carried[0]
    local_values = local_values + carried[1]
    grad_merged = jnp.stack([grad_query, local_keys, local_values], axis=2).astype(jnp.bfloat16)
    grad_merged_bias = jnp.stack(
        [
            jnp.sum(grad_merged[:, :, 0], axis=(0, 1), dtype=jnp.float32),
            jnp.sum(grad_merged[:, :, 2], axis=(0, 1), dtype=jnp.float32),
        ]
    ).reshape(merged_bias.shape)
    grad_merged_weight = jnp.einsum(
        "std,stkf->dkf", first_rows, grad_merged, preferred_element_type=jnp.float32
    )
    grad_first = gather_sums(
        jnp.einsum("stkf,dkf->std", grad_merged, merged_weight, preferred_element_type=jnp.float32)
    )
    _, first_pull = jax.vjp(
        layer_norm, stream, first_gain.astype(jnp.float32), first_shift.astype(jnp.float32)
    )
    grad_norm_in, grad_first_gain, grad_first_shift = first_pull(grad_first)
    grad_input = grad_middle + grad_norm_in
    grad_output_bias = jnp.sum(grad_middle, axis=(0, 1))
    vector_grads = lax.psum(
        (
            grad_first_gain,
            grad_first_shift,
            grad_second_gain,
            grad_second_shift,
            grad_output_bias,
            grad_reduce_bias,
        ),
        "tp",
    )
    fresh = (
        vector_grads[0],
        vector_grads[1],
        grad_merged_weight,
        grad_merged_bias,
        grad_output,
        vector_grads[4],
        vector_grads[2],
        vector_grads[3],
        grad_expand,
        grad_expand_bias,
        grad_reduce,
        vector_grads[5],
    )
    return (grad_input, reduce_grads(fresh))


def general_shards(
    inputs,
    segments,
    cotangent,
    student_first_gain,
    student_first_shift,
    student_merged_weight,
    student_merged_bias,
    student_output_weight,
    student_output_bias,
    student_second_gain,
    student_second_shift,
    student_expand_weight,
    student_expand_bias,
    student_reduce_weight,
    student_reduce_bias,
    teacher_first_gain,
    teacher_first_shift,
    teacher_merged_weight,
    teacher_merged_bias,
    teacher_output_weight,
    teacher_output_bias,
    teacher_second_gain,
    teacher_second_shift,
    teacher_expand_weight,
    teacher_expand_bias,
    teacher_reduce_weight,
    teacher_reduce_bias,
):
    student = (
        student_first_gain,
        student_first_shift,
        student_merged_weight,
        student_merged_bias,
        student_output_weight,
        student_output_bias,
        student_second_gain,
        student_second_shift,
        student_expand_weight,
        student_expand_bias,
        student_reduce_weight,
        student_reduce_bias,
    )
    teacher = (
        teacher_first_gain,
        teacher_first_shift,
        teacher_merged_weight,
        teacher_merged_bias,
        teacher_output_weight,
        teacher_output_bias,
        teacher_second_gain,
        teacher_second_shift,
        teacher_expand_weight,
        teacher_expand_bias,
        teacher_reduce_weight,
        teacher_reduce_bias,
    )
    token_count = segments.shape[1]
    context_size = lax.axis_size("ctx")
    context_index = lax.axis_index("ctx")
    doc_long = min(DOC_MAX, token_count * context_size // 2)
    cycle_steps = min((doc_long - 2) // token_count + 1, context_size - 1)
    doc_list = [segments]
    moving = segments
    for offset in range(cycle_steps):
        moving = from_behind(moving, "ctx", 1)
        doc_list.insert(0, moving)
    key_docs = jnp.concatenate(doc_list, axis=1)
    places = jnp.arange((cycle_steps + 1) * token_count, dtype=jnp.int32)
    relative = places - cycle_steps * token_count
    source = cycle_steps - places // token_count
    query_place = jnp.arange(token_count, dtype=jnp.int32)
    allowed = (relative[None, :] <= query_place[:, None]) & (source <= context_index)[None, :]
    stream = inputs.astype(jnp.float32)
    middle_stream, student_saved = layer_forward(
        stream, student, segments, key_docs, allowed, cycle_steps
    )
    final_stream, teacher_saved = layer_forward(
        middle_stream, teacher, segments, key_docs, allowed, cycle_steps
    )
    teacher_in_grad, teacher_grads = layer_backward(
        cotangent.astype(jnp.float32), teacher_saved, allowed, cycle_steps, token_count
    )
    input_grad, student_grads = layer_backward(
        teacher_in_grad, student_saved, allowed, cycle_steps, token_count
    )
    return (
        (final_stream.astype(jnp.bfloat16), input_grad)
        + tuple(student_grads)
        + tuple(teacher_grads)
    )


BF16 = jnp.bfloat16
F32 = jnp.float32
NEG = -1e30
TILE = 256
RELATIVE = (0, 2, 1, 3)


def row_major(value):
    return with_layout_constraint(value, Layout(major_to_minor=tuple(range(value.ndim))))


def swap(value, axis, bit):
    route = [(i, i ^ bit) for i in range(lax.axis_size(axis))]
    if value.ndim == 2:
        return row_major(lax.ppermute(row_major(value), axis, route))
    return lax.ppermute(value, axis, route)


def cross_core(value):
    return swap(value, "tp", 1)


def cross_x(value):
    return swap(value, "tp", 2)


def cross_y(value):
    return swap(value, "ctx", 1)


def cross_near(value):
    return swap(value, "dp", 1)


def cross_far(value):
    return swap(value, "dp", 2)


def cross_both(value):
    return swap(value, "dp", 3)


def stacked(*values):
    return jnp.concatenate(values, axis=0)


def beside(*values):
    return jnp.concatenate(values, axis=1)


def y_order(own, other, y_index, axis):
    return jnp.where(
        y_index == 0,
        jnp.concatenate([own, other], axis=axis),
        jnp.concatenate([other, own], axis=axis),
    )


def pin(*values):
    return lax.optimization_barrier(values)


def window_start(block, doc_max):
    return max(0, (block * TILE - doc_max + 1) // TILE) * TILE


def upright(line):
    size = line.shape[1]
    rows = lax.broadcasted_iota(jnp.int32, (size, size), 0)
    columns = lax.broadcasted_iota(jnp.int32, (size, size), 1)
    return jnp.sum(jnp.where(rows == columns, line, 0.0), axis=1, keepdims=True)


def join(pieces, whole):
    row, column = 0, 0
    most = whole.shape[0] * whole.shape[1] // sum(piece.shape[1] for piece in pieces)
    for piece in pieces:
        rows = min(piece.shape[0], most) if len(pieces) == 4 else piece.shape[0]
        whole[row : row + rows, column : column + piece.shape[1]] = piece[:rows, :]
        row += rows
        if row == whole.shape[0]:
            row, column = 0, column + piece.shape[1]


def dot_across(left, right):
    return lax.dot_general(left, right, (((1,), (1,)), ((), ())), preferred_element_type=F32)


def dot_down(left, right):
    return lax.dot_general(left, right, (((0,), (0,)), ((), ())), preferred_element_type=F32)


def token_place(me, member, half, rows):
    return pl.multiple_of((half * 4 + (me ^ (2 * (member & 1) + (member >> 1)))) * rows, rows)


def flat(column):
    size = column.shape[0]
    rows = lax.broadcasted_iota(jnp.int32, (size, size), 0)
    columns = lax.broadcasted_iota(jnp.int32, (size, size), 1)
    return jnp.sum(jnp.where(rows == columns, column, 0.0), axis=0, keepdims=True)


def fill_masks_across(docs, masks, doc_max):
    for block in range(docs.shape[1] // TILE):
        start, stop = window_start(block, doc_max), (block + 1) * TILE
        here = slice(block * TILE, stop)
        rows = block * TILE + lax.broadcasted_iota(jnp.int32, (TILE, stop - start), 0)
        columns = start + lax.broadcasted_iota(jnp.int32, (TILE, stop - start), 1)
        same = upright(docs[:, here]) == docs[:, start:stop]
        masks[here, : stop - start] = jnp.where(same & (columns <= rows), 0.0, NEG)


def mask_columns(length, doc_max):
    return max((block + 1) * TILE - window_start(block, doc_max) for block in range(length // TILE))


def fill_masks(docs, masks, doc_max):
    at = 0
    for block in range(docs.shape[1] // TILE):
        start = window_start(block, doc_max)
        size = (block + 1) * TILE - start
        for first in range(0, size, TILE):
            keys = slice(start + first, start + first + TILE)
            same = upright(docs[:, keys]) == docs[:, block * TILE : (block + 1) * TILE]
            if start + first == block * TILE:
                rows = lax.broadcasted_iota(jnp.int32, (TILE, TILE), 0)
                columns = lax.broadcasted_iota(jnp.int32, (TILE, TILE), 1)
                same = same & (rows <= columns)
            masks[at : at + TILE, :] = jnp.where(same, 0.0, NEG)
            at += TILE


def mask_rows(length, doc_max):
    return sum(
        (block + 1) * TILE - window_start(block, doc_max) for block in range(length // TILE)
    )


def split_heads(value, target, first, me, member):
    rows = value.shape[0] // 2
    for half in range(2):
        place = pl.ds(token_place(me, member, half, rows), rows)
        for j in range(value.shape[1] // HD):
            target[first + j, place, :] = value[half * rows : (half + 1) * rows, j * HD : (j + 1) * HD]


def merge_heads(source, me, member, rows):
    return jnp.concatenate(
        [
            jnp.concatenate(
                [
                    source[j, pl.ds(token_place(me, member, half, rows), rows), :]
                    for j in range(source.shape[0])
                ],
                axis=1,
            )
            for half in range(2)
        ],
        axis=0,
    )


def by_member(count, step):
    for i in range(count):
        step(i)


def attention_forward_kernel(
    heads,
    doc_max,
    count,
    scaled,
    me_ref,
    near_ref,
    far_ref,
    bias_ref,
    docs,
    *refs,
):
    mixed, attend_ref, masks = refs[-3:]
    refs = refs[:-3]
    sources = (near_ref, far_ref)
    if scaled:
        gains, refs, normed = refs[0], refs[1:-2], refs[-2:]
        for source, target in zip(sources, normed):
            target[...] = (source[...].astype(F32) * gains[0:1, :] + gains[1:2, :]).astype(BF16)
        sources = normed
    pieces, (sent_ref, kept_ref, split_ref, mixed_ref, log_ref) = refs[:count], refs[count:]
    join(pieces, attend_ref)
    fill_masks_across(docs, masks, doc_max)
    me = me_ref[0]
    width = heads * HD
    size = near_ref.shape[0] // 2
    length = 4 * size
    for source, first in zip(sources, (0, 2)):

        def project(i, source=source, first=first):
            at = pl.ds(pl.multiple_of(i * size, size), size)
            value = jnp.dot(source[at, :], attend_ref[:, : 3 * width], preferred_element_type=F32)
            value = (value + bias_ref[...]).astype(BF16)
            split_heads(value[:, :width] * BF16(0.125), split_ref, 0, me, first + i)
            split_heads(value[:, width:], split_ref, heads, me, first + i)

        by_member(2, project)

    def attend(h):
        for block in range(length // TILE):
            start, stop = window_start(block, doc_max), (block + 1) * TILE
            here = slice(block * TILE, stop)
            key, value = split_ref[heads + h, start:stop, :], split_ref[2 * heads + h, start:stop, :]
            scores = dot_across(split_ref[h, here, :], key) + masks[here, : stop - start]
            top = jnp.max(scores, axis=1, keepdims=True)
            raised = jnp.exp(scores - top)
            total = jnp.sum(raised, axis=1, keepdims=True)
            product = jnp.dot(raised.astype(BF16), value, preferred_element_type=F32)
            mixed[h, here, :] = (product * (1.0 / total)).astype(BF16)
            log_ref[h, :, here] = flat(top + jnp.log(total))

    lax.fori_loop(0, heads, lambda h, carry: (attend(h), carry)[1], 0)
    for out, first in ((sent_ref, 2), (kept_ref, 0)):

        def finish(i, out=out, first=first):
            rows = merge_heads(mixed, me, first + i, size // 2)
            mixed_ref[pl.ds(pl.multiple_of((first + i) * size, size), size), :] = rows
            at = pl.ds(pl.multiple_of(i * size, size), size)
            out[at, :] = dot_across(rows, attend_ref[:, 3 * width :]).astype(out.dtype)

        by_member(2, finish)


def attention_backward_kernel(
    heads,
    doc_max,
    count,
    me_ref,
    near_ref,
    far_ref,
    docs,
    split_ref,
    log_ref,
    *refs,
):
    pieces, (sent_ref, kept_ref, out_ref, sum_ref) = refs[:count], refs[count:-4]
    grad, total, attend_ref, masks = refs[-4:]
    join(pieces, attend_ref)
    fill_masks(docs, masks, doc_max)
    me = me_ref[0]
    width = heads * HD
    size = near_ref.shape[0] // 2
    length = 4 * size
    for source, first in ((near_ref, 0), (far_ref, 2)):

        def project(i, source=source, first=first):
            at = pl.ds(pl.multiple_of(i * size, size), size)
            value = jnp.dot(source[at, :], attend_ref[:, 3 * width :], preferred_element_type=F32)
            split_heads(value.astype(BF16), grad, 0, me, first + i)

        by_member(2, project)

    def attend(h):
        total[heads + h] = jnp.zeros((length, HD), F32)
        total[2 * heads + h] = jnp.zeros((length, HD), F32)
        at = 0
        for block in range(length // TILE):
            start, stop = window_start(block, doc_max), (block + 1) * TILE
            here, window = slice(block * TILE, stop), slice(start, stop)
            query, key, value = (
                split_ref[h, here, :],
                split_ref[heads + h, window, :],
                split_ref[2 * heads + h, window, :],
            )
            grad_rows = grad[h, here, :]
            scores = dot_across(key, query) + masks[at : at + stop - start, :]
            at += stop - start
            weights = jnp.exp(scores - log_ref[h, :, here])
            weighted = weights * dot_across(value, grad_rows)
            centered = jnp.sum(weighted, axis=0, keepdims=True)
            grad_scores = (weighted - weights * centered).astype(BF16)
            total[2 * heads + h, window, :] += jnp.dot(
                weights.astype(BF16), grad_rows, preferred_element_type=F32
            )
            total[heads + h, window, :] += jnp.dot(
                grad_scores, query, preferred_element_type=F32
            )
            total[h, here, :] = dot_down(key, grad_scores).T * 0.125

    lax.fori_loop(0, heads, lambda h, carry: (attend(h), carry)[1], 0)
    sum_ref[...] = jnp.zeros_like(sum_ref)
    for out, first in ((sent_ref, 2), (kept_ref, 0)):

        def finish(i, out=out, first=first):
            rows = merge_heads(total, me, first + i, size // 2).astype(BF16)
            out_ref[pl.ds(pl.multiple_of((first + i) * size, size), size), :] = rows
            sum_ref[...] += jnp.sum(rows.astype(F32), axis=0, keepdims=True)
            at = pl.ds(pl.multiple_of(i * size, size), size)
            out[at, :] = dot_across(rows, attend_ref[:, : 3 * width]).astype(out.dtype)

        by_member(2, finish)


VMEM = pl.BlockSpec(memory_space=pltpu.VMEM)
SMEM = pl.BlockSpec(memory_space=pltpu.SMEM)


def call(body, name, inputs, outputs, scratch, flops, transcendentals, limit=24):
    size = sum(v.size * v.dtype.itemsize for v in list(inputs) + list(outputs))
    return pl.pallas_call(
        body,
        out_shape=tuple(outputs),
        in_specs=[SMEM if v.ndim == 1 else VMEM for v in inputs],
        out_specs=tuple(VMEM for _ in outputs),
        scratch_shapes=scratch,
        cost_estimate=pl.CostEstimate(
            flops=flops, transcendentals=transcendentals, bytes_accessed=size
        ),
        compiler_params=pltpu.CompilerParams(vmem_limit_bytes=limit << 20),
        name=name,
    )(*inputs)


def shaped(rows, columns, kind):
    return jax.ShapeDtypeStruct((rows, columns), kind)


def attention_forward(near, far, attend, bias, context, doc_max, gains=()):
    me, docs = context
    half, features = near.shape
    width = bias.shape[1] // 3
    heads = width // HD
    area = heads * 2 * half * half

    def body(*refs):
        attention_forward_kernel(heads, doc_max, len(attend), len(gains) > 0, *refs)

    return call(
        body,
        "attention_forward",
        (me, near, far, bias, docs) + tuple(gains) + tuple(attend),
        (
            shaped(half, features, BF16),
            shaped(half, features, F32),
            jax.ShapeDtypeStruct((3 * heads, 2 * half, HD), BF16),
            shaped(2 * half, width, BF16),
            jax.ShapeDtypeStruct((heads, 1, 2 * half), F32),
        )
        + (shaped(half, features, BF16),) * (2 * len(gains)),
        [
            pltpu.VMEM((heads, 2 * half, HD), BF16),
            pltpu.VMEM((features, 4 * width), BF16),
            pltpu.VMEM((2 * half, mask_columns(2 * half, doc_max)), F32),
        ],
        16 * HD * area,
        area,
    )


def attention_backward(near, far, attend, context, saved, doc_max):
    me, docs = context
    split, _, log_total = saved
    half, features = near.shape
    heads = split.shape[0] // 3
    width = heads * HD
    area = heads * 2 * half * half

    def body(*refs):
        attention_backward_kernel(heads, doc_max, len(attend), *refs)

    return call(
        body,
        "attention_backward",
        (me, near, far, docs, split, log_total) + tuple(attend),
        (
            shaped(half, features, BF16),
            shaped(half, features, F32),
            shaped(2 * half, 3 * width, BF16),
            shaped(1, 3 * width, F32),
        ),
        [
            pltpu.VMEM((heads, 2 * half, HD), BF16),
            pltpu.VMEM((3 * heads, 2 * half, HD), F32),
            pltpu.VMEM((features, 4 * width), BF16),
            pltpu.VMEM((mask_rows(2 * half, doc_max), TILE), F32),
        ],
        40 * HD * area,
        area,
    )


CHUNK = 256


def gelu_both(values):
    inner = GELU_SCALE * (values + 0.044715 * values * values * values)
    bent = jnp.tanh(inner)
    value = 0.5 * values * (1.0 + bent)
    slope = 0.5 * (1.0 + bent) + 0.5 * values * (1.0 - bent * bent) * GELU_SCALE * (
        1.0 + 3.0 * 0.044715 * values * values
    )
    return value, slope


def feed_forward_kernel(count, piece, bias_ref, *refs):
    out, expand_ref, reduce_ref = refs[-3:]
    join(refs[:count], expand_ref)
    join(refs[count:-3], reduce_ref)

    for first in range(0, piece.shape[0], CHUNK):
        at = slice(first, first + CHUNK)
        hidden = jnp.dot(piece[at, :], expand_ref[...], preferred_element_type=F32)
        active = gelu_tanh(hidden + bias_ref[...]).astype(BF16)
        out[at, :] = dot_across(active, reduce_ref[...]).astype(out.dtype)


def feed_rows(piece, weights, kind):
    expand, reduce, bias = weights
    rows, features = piece.shape
    hidden = bias.shape[1]

    def body(*refs):
        feed_forward_kernel(len(expand), *refs)

    return call(
        body,
        "feed_forward",
        (piece, bias) + tuple(expand) + tuple(reduce),
        (shaped(rows, features, kind),),
        [pltpu.VMEM((features, hidden), BF16), pltpu.VMEM((features, hidden), BF16)],
        4 * rows * features * hidden,
        rows * hidden,
    )[0]


def feed_forward(near, far, expand, reduce, bias):
    weights = expand, reduce, bias
    return feed_rows(far, weights, BF16), feed_rows(near, weights, F32)


def feed_backward_kernel(count, piece, grads, bias_ref, *refs):
    out, active_ref, hidden_ref, sum_ref, expand_ref, reduce_ref = refs[-6:]
    join(refs[:count], expand_ref)
    join(refs[count:-6], reduce_ref)
    sum_ref[...] = jnp.zeros_like(sum_ref)

    for first in range(0, piece.shape[0], CHUNK):
        at = slice(first, first + CHUNK)
        hidden = jnp.dot(piece[at, :], expand_ref[...], preferred_element_type=F32)
        value, slope = gelu_both(hidden + bias_ref[...])
        active_ref[at, :] = value.astype(BF16)
        grad_active = jnp.dot(grads[at, :], reduce_ref[...], preferred_element_type=F32)
        grad_hidden = (grad_active * slope).astype(BF16)
        hidden_ref[at, :] = grad_hidden
        sum_ref[...] += jnp.sum(grad_hidden.astype(F32), axis=0, keepdims=True)
        out[at, :] = dot_across(grad_hidden, expand_ref[...]).astype(out.dtype)


def feed_back_rows(piece, grads, weights, kind):
    expand, reduce, bias = weights
    rows, features = piece.shape
    hidden = bias.shape[1]

    def body(*refs):
        feed_backward_kernel(len(expand), *refs)

    return call(
        body,
        "feed_backward",
        (piece, grads, bias) + tuple(expand) + tuple(reduce),
        (
            shaped(rows, features, kind),
            shaped(rows, hidden, BF16),
            shaped(rows, hidden, BF16),
            shaped(1, hidden, F32),
        ),
        [pltpu.VMEM((features, hidden), BF16), pltpu.VMEM((features, hidden), BF16)],
        6 * rows * features * hidden,
        rows * hidden,
    )


def feed_backward(near, far, near_grad, far_grad, expand, reduce, bias):
    weights = expand, reduce, bias
    sent, far_active, far_hidden, far_sum = feed_back_rows(far, far_grad, weights, BF16)
    kept, active, hidden, sums = feed_back_rows(near, near_grad, weights, F32)
    return (
        sent,
        kept,
        jnp.concatenate([active, far_active], axis=0),
        jnp.concatenate([hidden, far_hidden], axis=0),
        sums + far_sum,
    )


def row_block(rows, columns):
    return pl.BlockSpec((rows, columns), lambda i: (0, 0))


def row_call(body, name, inputs, rows, outputs):
    specs = [row_block(v.shape[0] if v.shape[0] <= 16 else rows, v.shape[1]) for v in inputs]
    size = sum(rows * v.shape[1] * v.dtype.itemsize for v in inputs)
    return pl.pallas_call(
        body,
        grid=(1,),
        out_shape=tuple(outputs),
        in_specs=specs,
        out_specs=tuple(row_block(*v.shape) for v in outputs),
        cost_estimate=pl.CostEstimate(
            flops=20 * rows * inputs[0].shape[1], transcendentals=rows, bytes_accessed=2 * size
        ),
        compiler_params=pltpu.CompilerParams(vmem_limit_bytes=18 << 20),
        name=name,
    )(*inputs)


STEP = 128


def add_norm(base, partial, across, vectors, bias_at, norm_vectors, norm_at):
    rows, columns = base.shape

    def body(base_ref, bias_ref, vector_ref, partial_ref, across_ref, sum_ref, norm_ref):
        bias = bias_ref[bias_at : bias_at + 1, :]
        gain, shift = vector_ref[norm_at : norm_at + 1, :], vector_ref[norm_at + 1 : norm_at + 2, :]

        def step(i, carry):
            here = pl.ds(pl.multiple_of(i * STEP, STEP), STEP)
            there = pl.ds(pl.multiple_of((i * STEP + rows // 2) % rows, STEP), STEP)
            total = partial_ref[here, :].astype(F32) + across_ref[there, :].astype(F32)
            total = base_ref[here, :].astype(F32) + bias + total
            sum_ref[here, :] = total
            norm_ref[here, :] = (normalize(total)[0] * gain + shift).astype(BF16)
            return carry

        lax.fori_loop(0, rows // STEP, step, 0)

    return row_call(
        body,
        "add_norm",
        [base, vectors, norm_vectors, partial, across],
        rows,
        (shaped(rows, columns, F32), shaped(rows, columns, BF16)),
    )


def norm_back_near(skip, partial, across, value, vectors, norm_at, sums, sums_at):
    rows, columns = skip.shape

    def body(skip_ref, value_ref, vector_ref, old_ref, partial_ref, across_ref, *outs):
        grad_ref, low_ref, sum_ref = outs
        gain = vector_ref[norm_at : norm_at + 1, :]
        sum_ref[...] = old_ref[...]

        def step(i, own):
            here = pl.ds(pl.multiple_of(i * STEP, STEP), STEP)
            there = pl.ds(pl.multiple_of((i * STEP + rows // 2) % rows, STEP), STEP)
            grad = partial_ref[here, :].astype(F32) + across_ref[there, :].astype(F32)
            unit, scale = normalize(value_ref[here, :].astype(F32))
            skipped = skip_ref[here, :].astype(F32)
            if own:
                for j, each in enumerate((grad * unit, grad, skipped)):
                    sum_ref[sums_at + j : sums_at + j + 1, :] += jnp.sum(each, axis=0, keepdims=True)
            total = skipped + norm_pullback(grad, unit, scale, gain)
            grad_ref[here, :] = total
            low_ref[here, :] = total.astype(BF16)

        count = rows // STEP // 2
        lax.fori_loop(0, count, lambda i, carry: (step(i, True), carry)[1], 0)
        lax.fori_loop(count, 2 * count, lambda i, carry: (step(i, False), carry)[1], 0)

    return row_call(
        body,
        "norm_back_near",
        [skip, value, vectors, sums, partial, across],
        rows,
        (shaped(rows, columns, F32), shaped(rows, columns, BF16), shaped(16, columns, F32)),
    )


def norm_only(values):
    rows, columns = values.shape

    def body(value_ref, unit_ref):
        unit_ref[...] = normalize(value_ref[...].astype(F32))[0].astype(BF16)

    return row_call(body, "norm_only", [values], rows, (shaped(rows, columns, BF16),))[0]


def norm_back(skip, addends, value, vectors, norm_at, sums, sums_at):
    rows, columns = addends[-1].shape

    def body(*refs):
        skip_ref, value_ref, vector_ref, old_ref = refs[:4]
        parts, (grad_ref, low_ref, sum_ref) = refs[4:-3], refs[-3:]
        grad = parts[0][...].astype(F32)
        for part in parts[1:]:
            grad = grad + part[...].astype(F32)
        unit, scale = normalize(value_ref[...].astype(F32))
        skipped = skip_ref[...]
        sum_ref[...] = old_ref[...]
        for i, each in enumerate((grad * unit, grad, skipped)):
            sum_ref[sums_at + i : sums_at + i + 1, :] = jnp.sum(each, axis=0, keepdims=True)
        total = skipped + norm_pullback(grad, unit, scale, vector_ref[norm_at : norm_at + 1, :])
        grad_ref[...] = total
        low_ref[...] = total.astype(BF16)

    return row_call(
        body,
        "norm_back",
        [skip, value, vectors, sums] + list(addends),
        rows,
        (shaped(rows, columns, F32), shaped(rows, columns, BF16), shaped(16, columns, F32)),
    )


def normalize(values):
    center = values - jnp.mean(values, axis=-1, keepdims=True)
    spread = jnp.mean(center * center, axis=-1, keepdims=True)
    scale = lax.rsqrt(spread + EPSILON)
    return center * scale, scale


def norm_rows(values, gain, shift):
    return (normalize(values)[0] * gain + shift).astype(BF16)


def norm_pullback(grad, unit, scale, gain):
    inner = grad * gain
    return scale * (
        inner
        - jnp.mean(inner, axis=-1, keepdims=True)
        - unit * jnp.mean(inner * unit, axis=-1, keepdims=True)
    )


def times(left, right, kind=F32):
    return jnp.dot(left, right, preferred_element_type=F32).astype(kind)


def times_across(left, right, kind=F32):
    return dot_across(left, right).astype(kind)


def times_down(left, right, kind=F32):
    return row_major(dot_down(left, right).astype(kind))


def gather_rows(rows):
    near = stacked(rows, cross_x(rows))
    return near, cross_core(near)


def add_half(value, cross):
    middle = value.shape[0] // 2
    return value[:middle].astype(F32) + cross(value[middle:].astype(BF16)).astype(F32)


def add_columns(value, cross):
    middle = value.shape[1] // 2
    return value[:, :middle].astype(F32) + cross(value[:, middle:].astype(BF16)).astype(F32)


def column_halves(shard, y_index):
    middle = shard.shape[1] // 2
    own = jnp.where(y_index == 0, shard[:, :middle], shard[:, middle:])
    other = jnp.where(y_index == 0, shard[:, middle:], shard[:, :middle])
    return own, other


def natural_columns(own, other, y_index):
    return jnp.where(y_index == 0, beside(own, other), beside(other, own))


def order_matrix(width, z_index):
    rows = width // 4
    natural = lax.broadcasted_iota(jnp.int32, (width, width), 0)
    place = lax.broadcasted_iota(jnp.int32, (width, width), 1)
    step, inner = place // rows, place % rows
    distance = 2 * (step & 1) + (step >> 1)
    return (natural == (z_index ^ distance) * rows + inner).astype(BF16)


def my_rows(pair, y_index):
    own = jnp.where(y_index == 0, pair[0], pair[1])
    sent = jnp.where(y_index == 0, pair[1], pair[0])
    return y_order(own, cross_y(sent), y_index, 0)


ROWS = 64
SPARE = ROWS // 4


def turn(value):
    size = value.shape[0]
    eye = (
        lax.broadcasted_iota(jnp.int32, (size, size), 0)
        == lax.broadcasted_iota(jnp.int32, (size, size), 1)
    ).astype(BF16)
    return dot_down(value, eye)


def pack_vectors(blocks, place):
    flat = []
    for gains, merged_bias, expand_bias in blocks:
        flat += list(gains) + [merged_bias.transpose(1, 0, 2), expand_bias]

    number = len(flat)

    def body(*refs):
        refs = refs[1:]
        out, part, sem = refs[number], refs[number + 1 : -1], refs[-1]
        copies = [
            pltpu.make_async_copy(refs[i], part[i], sem.at[i]) for i in range(number)
        ]
        for copy in copies:
            copy.start()
        out[...] = jnp.zeros_like(out)
        for copy in copies:
            copy.wait()
        for b in range(2):
            vectors, merged_bias, expand_bias = part[8 * b : 8 * b + 6], part[8 * b + 6], part[8 * b + 7]
            for i in range(6):
                local = vectors[i].shape[0]
                out[6 * b + i : 6 * b + i + 1, :local] = vectors[i][...].astype(F32).reshape(1, local)
            for h in range(merged_bias.shape[0]):
                value = merged_bias[h].astype(F32)
                out[16 + 8 * b + 2 * h : 18 + 8 * b + 2 * h, : value.shape[1]] = value
            value = expand_bias[...].astype(F32)
            out[32 + 16 * b : 32 + 16 * b + value.shape[0], : value.shape[1]] = value

    return pl.pallas_call(
        body,
        out_shape=shaped(ROWS, 256, F32),
        in_specs=[SMEM] + [pl.BlockSpec(memory_space=pltpu.HBM)] * number,
        out_specs=VMEM,
        scratch_shapes=[pltpu.VMEM(v.shape, v.dtype) for v in flat]
        + [pltpu.SemaphoreType.DMA((number,))],
        compiler_params=pltpu.CompilerParams(vmem_limit_bytes=60 << 20),
        name="pack_vectors",
    )(place, *flat)


def prepare_first(place, merged, output, blocks):
    flat = []
    for gains, merged_bias, expand_bias in blocks:
        flat += list(gains) + [merged_bias.transpose(1, 0, 2), expand_bias]
    flat += [merged.transpose(1, 0, 2), output]
    number = len(flat)
    local = output.shape[1]

    def body(*refs):
        out, part, small, sem = refs[number], refs[number + 1 : -2], refs[-2], refs[-1]
        copies = [pltpu.make_async_copy(refs[i], part[i], sem.at[i]) for i in range(number)]
        for copy in copies:
            copy.start()
        small[...] = jnp.zeros_like(small)
        for copy in copies:
            copy.wait()
        for b in range(2):
            vectors, merged_bias, expand_bias = part[8 * b : 8 * b + 6], part[8 * b + 6], part[8 * b + 7]
            for i in range(6):
                small[6 * b + i : 6 * b + i + 1, :local] = (
                    vectors[i][...].astype(F32).reshape(1, local)
                )
            for h in range(merged_bias.shape[0]):
                value = merged_bias[h].astype(F32)
                small[16 + 8 * b + 2 * h : 18 + 8 * b + 2 * h, : value.shape[1]] = value
            value = expand_bias[...].astype(F32)
            small[32 + 16 * b : 32 + 16 * b + value.shape[0], : value.shape[1]] = value
        merged_ref, output_ref = part[-2:]
        pieces = [merged_ref[k] for k in range(3)] + [turn(output_ref[...]).astype(BF16)]
        out[:local, :] = jnp.concatenate(pieces, axis=1)
        for i in range(4):
            out[local:, local * i : local * (i + 1)] = small[
                SPARE * i : SPARE * (i + 1), :local
            ].astype(BF16)

    return pl.pallas_call(
        body,
        out_shape=shaped(local + SPARE, 4 * local, BF16),
        in_specs=[pl.BlockSpec(memory_space=pltpu.HBM)] * number,
        out_specs=VMEM,
        scratch_shapes=[pltpu.VMEM(v.shape, v.dtype) for v in flat]
        + [pltpu.VMEM((ROWS, 256), F32), pltpu.SemaphoreType.DMA((number,))],
        compiler_params=pltpu.CompilerParams(vmem_limit_bytes=60 << 20),
        name="prepare_first",
    )(*flat)


def unpack_vectors(pieces, place, local, merged_shape, expand_shape):
    heads, few = merged_shape[1], merged_shape[2]
    groups = expand_shape[0]
    width = heads * 4 * few

    def body(place_ref, *refs):
        pieces, outs, pieces_ref = refs[:4], refs[4:-1], refs[-1]
        for k in range(4):
            for i in range(4):
                pieces_ref[k * ROWS + i * SPARE : k * ROWS + (i + 1) * SPARE, :local] = pieces[k][
                    local:, local * i : local * (i + 1)
                ].astype(F32)
        y, z = place_ref[0], place_ref[1]
        for b in range(2):
            gains, bias, hidden = outs[3 * b : 3 * b + 3]
            for k in range(4):
                gains[0:6, k * local : (k + 1) * local] = pieces_ref[
                    k * ROWS + 6 * b : k * ROWS + 6 * b + 6, :local
                ]
            bias[...] = jnp.zeros_like(bias)
            for natural in range(4):
                distance = z ^ natural
                base = (2 * (distance & 1) + (distance >> 1)) * ROWS
                part = pieces_ref[pl.ds(pl.multiple_of(base, ROWS), ROWS), :128]
                for i in range(2):
                    for h in range(heads):
                        line = 16 + 8 * b + 2 * h + i
                        at = 2 * i * width + h * 4 * few + natural * few
                        bias[:, at : at + few] = part[line : line + 1, :few]
                lines = part[32 + 16 * b : 32 + 16 * b + groups]
                half = groups // 2
                lines = jnp.where(
                    y == 0, lines, jnp.concatenate([lines[half:], lines[:half]], axis=0)
                )
                for p in range(groups):
                    at = p * 4 * few + natural * few
                    hidden[:, at : at + few] = lines[p : p + 1, :few]

    one = (
        shaped(8, 4 * local, F32),
        shaped(1, 3 * width, F32),
        shaped(1, groups * 4 * few, F32),
    )
    return pl.pallas_call(
        body,
        out_shape=one + one,
        in_specs=[SMEM] + [VMEM] * 4,
        out_specs=(VMEM,) * 6,
        scratch_shapes=[pltpu.VMEM((4 * ROWS, 256), F32)],
        compiler_params=pltpu.CompilerParams(vmem_limit_bytes=8 << 20),
        name="unpack_vectors",
    )(place, *pieces)


def prepare_attend(merged, output):
    local = output.shape[1]

    def body(merged_ref, output_ref, attend):
        pieces = [merged_ref[k] for k in range(3)] + [turn(output_ref[...]).astype(BF16)]
        attend[...] = jnp.concatenate(pieces, axis=1)

    return pl.pallas_call(
        body,
        out_shape=shaped(local, 4 * local, BF16),
        in_specs=[VMEM, VMEM],
        out_specs=VMEM,
        compiler_params=pltpu.CompilerParams(vmem_limit_bytes=12 << 20),
        name="prepare_attend",
    )(merged.transpose(1, 0, 2), output)


def prepare_feed(place, expand, reduce):
    local, half = expand.shape[0], expand.shape[1] // 2

    def body(place_ref, expand_ref, reduce_ref, feed):
        y = place_ref[0]
        first, second = reduce_ref[:, :half], reduce_ref[:, half:]
        feed[:, :half] = jnp.where(y == 0, expand_ref[:, :half], expand_ref[:, half:])
        feed[:, half : 2 * half] = jnp.where(y == 0, first, second)
        feed[:, 2 * half :] = jnp.where(y == 0, second, first)

    return pl.pallas_call(
        body,
        out_shape=shaped(local, 3 * half, BF16),
        in_specs=[SMEM, VMEM, VMEM],
        out_specs=VMEM,
        compiler_params=pltpu.CompilerParams(vmem_limit_bytes=12 << 20),
        name="prepare_feed",
    )(place, expand, reduce.T)


def pack_grads(sums, biases, hiddens, place, local, merged_shape, expand_shape):
    heads, few = merged_shape[1], merged_shape[2]
    groups = expand_shape[0]
    width = heads * 4 * few

    def body(place_ref, sum_ref, bias_s, bias_t, hidden_s, hidden_t, out):
        y, z = place_ref[0], place_ref[1]
        out[...] = jnp.zeros_like(out)
        for k in range(4):
            out[k * ROWS : k * ROWS + 12, :local] = sum_ref[0:12, k * local : (k + 1) * local]
        for natural in range(4):
            distance = z ^ natural
            base = pl.multiple_of((2 * (distance & 1) + (distance >> 1)) * ROWS, ROWS)
            lines = []
            for bias in (bias_s, bias_t):
                for h in range(heads):
                    for i in range(2):
                        at = 2 * i * width + h * 4 * few + natural * few
                        lines.append(bias[:, at : at + few])
                lines.append(jnp.zeros((2, few), F32))
            for hidden in (hidden_s, hidden_t):
                rows = [
                    hidden[:, p * 4 * few + natural * few : p * 4 * few + natural * few + few]
                    for p in range(groups)
                ]
                first, second = rows[: groups // 2], rows[groups // 2 :]
                first, second = jnp.concatenate(first, axis=0), jnp.concatenate(second, axis=0)
                lines.append(jnp.where(y == 0, first, second))
                lines.append(jnp.where(y == 0, second, first))
                lines.append(jnp.zeros((16 - groups, few), F32))
            out[pl.ds(pl.multiple_of(base + 16, 16), ROWS - 16), :few] = jnp.concatenate(lines, axis=0)

    return pl.pallas_call(
        body,
        out_shape=shaped(4 * ROWS, 256, F32),
        in_specs=[SMEM] + [VMEM] * 5,
        out_specs=VMEM,
        compiler_params=pltpu.CompilerParams(vmem_limit_bytes=4 << 20),
        name="pack_grads",
    )(place, sums, *biases, *hiddens)


def unpack_grads(mine, arrived, local, merged_shape, expand_shape):
    heads, few = merged_shape[1], merged_shape[2]
    groups = expand_shape[0]

    def body(mine_ref, arrived_ref, *outs):
        total = mine_ref[0:ROWS, :] + arrived_ref[...]
        for b in range(2):
            vectors, merged_bias, expand_bias = outs[8 * b : 8 * b + 6], outs[8 * b + 6], outs[8 * b + 7]
            for i in range(6):
                vectors[i][...] = total[6 * b + i : 6 * b + i + 1, :local].reshape(local)
            for h in range(heads):
                merged_bias[h] = total[16 + 8 * b + 2 * h : 18 + 8 * b + 2 * h, :few]
            expand_bias[...] = total[32 + 16 * b : 32 + 16 * b + groups, :few]

    one = [jax.ShapeDtypeStruct((local,), F32)] * 6 + [
        jax.ShapeDtypeStruct((heads, 2, few), F32),
        jax.ShapeDtypeStruct(expand_shape, F32),
    ]
    values = pl.pallas_call(
        body,
        out_shape=tuple(one + one),
        in_specs=[VMEM] * 2,
        out_specs=(VMEM,) * 16,
        compiler_params=pltpu.CompilerParams(vmem_limit_bytes=4 << 20),
        name="unpack_grads",
    )(mine, arrived)
    return [v.transpose(1, 0, 2) if v.ndim == 3 else v for v in values]


def finish_feed(mine, theirs, place, half):
    local = mine.shape[0]
    whole = mine.shape[1] == 3 * half

    def body(place_ref, mine_ref, theirs_ref, expand, reduce):
        y = place_ref[0]
        own, other = mine_ref[:, :half].astype(F32), theirs_ref[:, :half].astype(F32)
        expand[:, :half] = jnp.where(y == 0, own, other)
        expand[:, half:] = jnp.where(y == 0, other, own)
        if whole:
            total = mine_ref[:, half:].astype(F32) + theirs_ref[:, half:].astype(F32)
            own, other = total[:, :half], total[:, half:]
        else:
            own, other = mine_ref[:, half:].astype(F32), theirs_ref[:, half:].astype(F32)
        reduce[:, :half] = jnp.where(y == 0, own, other)
        reduce[:, half:] = jnp.where(y == 0, other, own)

    expand, reduce = pl.pallas_call(
        body,
        out_shape=(shaped(local, 2 * half, F32), shaped(local, 2 * half, F32)),
        in_specs=[SMEM, VMEM, VMEM],
        out_specs=(VMEM, VMEM),
        compiler_params=pltpu.CompilerParams(vmem_limit_bytes=12 << 20),
        name="finish_feed",
    )(place, mine, theirs)
    return expand, reduce.T


def finish_attend(added, mine, theirs, place):
    local = mine.shape[0]

    def body(place_ref, *refs):
        mine_ref, theirs_ref, merged, output = refs[-4:]
        y = place_ref[0]
        own, other = mine_ref[...], theirs_ref[...]
        split = jnp.concatenate(
            [jnp.where(y == 0, own, other), jnp.where(y == 0, other, own)], axis=1
        )
        output[...] = turn(split[:, -local:])
        whole = split.astype(F32)
        if added:
            total = refs[0][...].astype(F32) + refs[1][...].astype(F32)
            whole = jnp.concatenate([total, whole], axis=1)
        for k in range(3):
            merged[k] = whole[:, k * local : (k + 1) * local]

    merged, output = pl.pallas_call(
        body,
        out_shape=(jax.ShapeDtypeStruct((3, local, local), F32), shaped(local, local, F32)),
        in_specs=[SMEM] + [VMEM] * (2 + len(added)),
        out_specs=(VMEM, VMEM),
        compiler_params=pltpu.CompilerParams(vmem_limit_bytes=12 << 20),
        name="finish_attend",
    )(place, *added, mine, theirs)
    return merged.transpose(1, 0, 2), output


def halves_added(kept, arrived):
    middle = kept.shape[0] // 2
    return (kept[middle:] + arrived[middle:].astype(F32)).astype(BF16)


def core_sum(kept, arrived):
    return (kept + arrived.astype(F32)).astype(BF16)


def added(first, second):
    return (first.astype(F32) + second.astype(F32)).astype(BF16)


def send_columns(value, cross):
    middle = value.shape[1] // 2
    return cross(value[:, middle:].astype(BF16))


def keep_columns(value, arrived):
    return value[:, : value.shape[1] // 2].astype(F32) + arrived.astype(F32)


def send_rows(value, cross):
    middle = value.shape[0] // 2
    return cross(value[middle:].astype(BF16))


def keep_rows(value, arrived):
    return value[: value.shape[0] // 2].astype(F32) + arrived.astype(F32)


def fast_shards(inputs, segments, cotangent, *params):
    y_index = lax.axis_index("ctx")
    z_index = lax.axis_index("dp")
    me = lax.axis_index("tp")
    tokens, features = inputs.shape[1], inputs.shape[2]
    length = segments.shape[1] * 2
    doc_max = min(DOC_MAX, length // 2)
    blocks = (params[:12], params[12:])
    local = features // 4
    half = local * 2

    small = [((p[0], p[1], p[5], p[6], p[7], p[11]), p[3], p[9]) for p in blocks]
    place = jnp.stack([y_index, z_index]).astype(jnp.int32)
    p = blocks[0]
    attend = prepare_first(place, p[2], p[4], small)
    inputs, attend = pin(inputs, attend)
    far = cross_far(attend)
    sent_rows = jnp.where(y_index == 0, inputs[1], inputs[0])
    sent_rows, late = pin(sent_rows, attend)
    near = cross_near(late)
    sent_docs = jnp.where(y_index == 0, segments[1:2], segments[0:1]).astype(BF16)
    sent_docs = jnp.pad(sent_docs, ((0, 15), (0, features - sent_docs.shape[1])))
    moved = cross_y(stacked(sent_rows, sent_docs))
    kept_rows = jnp.where(y_index == 0, inputs[0], inputs[1])
    kept_docs = jnp.where(y_index == 0, segments[0:1], segments[1:2]).astype(F32)
    chooser = order_matrix(features, z_index)
    raw = times(y_order(kept_rows, moved[:tokens], y_index, 0), chooser, BF16)
    docs = y_order(
        kept_docs, moved[tokens : tokens + 1, : kept_docs.shape[1]].astype(F32), y_index, 1
    )
    context = (me.astype(jnp.int32).reshape(1), docs)
    both = cross_near(far)
    feed = prepare_feed(place, blocks[0][8], blocks[0][10])
    feed, far = pin(feed, far)
    p_far = cross_far(feed[:, : 2 * half])
    moved_grad = cross_y(jnp.where(y_index == 0, cotangent[1], cotangent[0]))
    raw, place_t, output_t = pin(raw, place, blocks[1][4])
    own_a = prepare_attend(blocks[1][2], output_t)
    feed_t = prepare_feed(place_t, blocks[1][8], blocks[1][10])

    stream = stacked(raw, cross_x(raw))
    stream, near, both, p_far, own_a, feed_t, moved_grad = pin(
        stream, near, both, p_far, own_a, feed_t, moved_grad
    )
    near_s = norm_only(stream)
    gains_s, bias_s, hidden_s, gains_t, bias_t, hidden_t = unpack_vectors(
        (attend, far, near, both), place, local, blocks[0][3].shape, blocks[0][9].shape
    )
    far_s = cross_core(near_s)
    attend_s = (attend, far, near, both)
    e_two = stacked(feed[:, :half], p_far[:, :half])
    e_near = cross_near(e_two)
    r_far = cross_far(feed[:, 2 * half :])
    grad_out = times(
        y_order(jnp.where(y_index == 0, cotangent[0], cotangent[1]), moved_grad, y_index, 0),
        chooser,
        BF16,
    )
    moved_grad = cross_x(grad_out)
    sent, kept, *saved_s, near_s, far_s = attention_forward(
        near_s, far_s, attend_s, bias_s, context, doc_max, (gains_s,)
    )
    sent, e_near, r_far, moved_grad = pin(sent, e_near, r_far, moved_grad)
    e_s = stacked(e_two, e_near)
    e_other = cross_y(e_s)
    r_two = stacked(feed[:, half:], beside(p_far[:, half:], r_far))
    r_near = cross_near(r_two)
    a_far = cross_far(own_a)
    partial = core_sum(kept, cross_core(sent))
    middle_s, near_two_s = add_norm(stream, partial, cross_x(partial), gains_s, 2, gains_s, 3)
    near_two_s, e_other, r_near, a_far, feed_t = pin(near_two_s, e_other, r_near, a_far, feed_t)
    a_two = stacked(own_a, a_far)
    a_near = cross_near(a_two)
    te_far, tr_far = cross_far(feed_t[:, :half]), cross_far(feed_t[:, 2 * half :])
    far_two_s = cross_core(near_two_s)
    feed_s = (near_two_s, far_two_s), ((e_s, e_other), (r_two, r_near), hidden_s)
    sent, kept = feed_forward(*feed_s[0], *feed_s[1])
    partial = core_sum(kept, cross_core(sent))
    between, near_t = add_norm(middle_s, partial, cross_x(partial), gains_s, 5, gains_t, 0)

    near_t, a_near, te_far, tr_far, feed_t = pin(near_t, a_near, te_far, tr_far, feed_t)
    attend_t = (a_two, a_near)
    te_two = stacked(feed_t[:, :half], te_far)
    te_near = cross_near(te_two)
    tr_far_one = cross_far(feed_t[:, half : 2 * half])
    far_t = cross_core(near_t)
    sent, kept, *saved_t = attention_forward(near_t, far_t, attend_t, bias_t, context, doc_max)
    sent, te_near, tr_far_one = pin(sent, te_near, tr_far_one)
    te = stacked(te_two, te_near)
    te_other = cross_y(te)
    tr_two = stacked(feed_t[:, half:], beside(tr_far_one, tr_far))
    tr_near = cross_near(tr_two)
    branch = stacked(grad_out, moved_grad)
    branch_far = cross_core(branch)
    partial = core_sum(kept, cross_core(sent))
    middle_t, near_two_t = add_norm(between, partial, cross_x(partial), gains_t, 2, gains_t, 3)
    near_two_t, te_other, tr_near, branch_far = pin(near_two_t, te_other, tr_near, branch_far)
    far_two_t = cross_core(near_two_t)
    feed_t = (near_two_t, far_two_t), ((te, te_other), (tr_two, tr_near), hidden_t)

    sums = jnp.zeros((16, features), F32)
    sent, kept, active, grad_hidden, hidden_sum_t = feed_backward(
        *feed_t[0], branch, branch_far, *feed_t[1]
    )
    partial = core_sum(kept, cross_core(sent))
    part_r = times_down(stacked(branch, branch_far), active, BF16)
    part_r, partial = pin(part_r, partial)
    r_moved = send_rows(part_r, cross_near)
    part_e = times_down(stacked(near_two_t, far_two_t), grad_hidden, BF16)
    e_moved = send_columns(part_e, cross_y)
    late_t, _ = pin(near_two_t, part_e)
    final_sent, final_kept = feed_forward(late_t, far_two_t, *feed_t[1])
    grad_middle, near_grad, sums = norm_back_near(
        branch, partial, cross_x(partial), middle_t, gains_t, 3, sums, 9
    )
    near_grad, r_moved, e_moved, final_sent, final_kept = pin(
        near_grad, r_moved, e_moved, final_sent, final_kept
    )
    part_e, part_r = keep_columns(part_e, e_moved), keep_rows(part_r, r_moved)
    e_moved = send_rows(part_e, cross_near)
    far_grad = cross_core(near_grad)
    sent, kept, grad_qkv, qkv_sum_t = attention_backward(
        near_grad, far_grad, attend_t, context, saved_t, doc_max
    )
    sent, e_moved, part_r = pin(sent, e_moved, part_r)
    part_e = keep_rows(part_e, e_moved)
    e_moved, r_moved = send_rows(part_e, cross_far), send_rows(part_r, cross_far)
    partial = core_sum(kept, cross_core(sent))
    part_a = beside(
        times_down(stacked(near_t, far_t), grad_qkv, BF16),
        times_down(stacked(near_grad, far_grad), saved_t[1], BF16),
    )
    part_a, a_moved = column_halves(part_a, y_index)
    a_moved = cross_y(a_moved)
    grad_between, branch, sums = norm_back_near(
        grad_middle, partial, cross_x(partial), between, gains_t, 0, sums, 6
    )

    branch, e_moved, r_moved, a_moved = pin(branch, e_moved, r_moved, a_moved)
    part_e, part_r = keep_rows(part_e, e_moved), keep_rows(part_r, r_moved)
    part_a = part_a.astype(F32) + a_moved.astype(F32)
    branch_far = cross_core(branch)
    sent, kept, active, grad_hidden, hidden_sum_s = feed_backward(
        *feed_s[0], branch, branch_far, *feed_s[1]
    )
    partial = core_sum(kept, cross_core(sent))
    feed_r = times_down(stacked(branch, branch_far), active, BF16)
    feed_r, part_a, partial = pin(feed_r, part_a, partial)
    fr_moved, a_moved = send_rows(feed_r, cross_near), send_rows(part_a, cross_near)
    feed_e = times_down(stacked(near_two_s, far_two_s), grad_hidden, BF16)
    fe_moved = send_columns(feed_e, cross_y)
    grad_middle, near_grad, sums = norm_back_near(
        grad_between, partial, cross_x(partial), middle_s, gains_s, 3, sums, 3
    )
    near_grad, a_moved, fr_moved, fe_moved, part_e, part_r = pin(
        near_grad, a_moved, fr_moved, fe_moved, part_e, part_r
    )
    part_a, feed_r, feed_e = (
        keep_rows(part_a, a_moved),
        keep_rows(feed_r, fr_moved),
        keep_columns(feed_e, fe_moved),
    )
    a_moved, fe_moved = send_rows(part_a, cross_far), send_rows(feed_e, cross_near)
    mine_t = beside(part_e, part_r).astype(BF16)
    theirs_t = cross_y(
        beside(mine_t[:, :half], mine_t[:, 2 * half :], mine_t[:, half : 2 * half])
    )
    far_grad = cross_core(near_grad)
    sent, kept, grad_qkv, qkv_sum_s = attention_backward(
        near_grad, far_grad, attend_s, context, saved_s, doc_max
    )
    sent, a_moved, fe_moved, feed_r = pin(sent, a_moved, fe_moved, feed_r)
    mine_at, feed_e = keep_rows(part_a, a_moved), keep_rows(feed_e, fe_moved)
    fr_moved, fe_moved = send_rows(feed_r, cross_far), send_rows(feed_e, cross_far)
    arrived = cross_core(sent)
    across = cross_x(halves_added(kept, arrived))
    grad_a = beside(
        times_down(stacked(near_s, far_s), grad_qkv, BF16),
        times_down(stacked(near_grad, far_grad), saved_s[1], BF16),
    )
    grad_a, y_moved = column_halves(grad_a, y_index)
    y_moved = cross_y(y_moved)
    grad_in, _, sums = norm_back(
        grad_middle, (kept, arrived, across), stream, gains_s, 0, sums, 0
    )
    sums_moved = cross_core(sums)
    input_grad = lax.dot_general(
        grad_in,
        chooser.astype(F32),
        (((1,), (1,)), ((), ())),
        precision=lax.Precision.HIGHEST,
        preferred_element_type=F32,
    )

    def swapped(value):
        first, second = value[:tokens], value[tokens:]
        return cross_y(jnp.where(y_index == 0, second, first))

    def restore(value, received):
        kept = jnp.where(y_index == 0, value[:tokens], value[tokens:])
        return jnp.where(y_index == 0, jnp.stack([kept, received]), jnp.stack([received, kept]))

    grad_moved = swapped(input_grad.astype(BF16))
    y_moved, sums_moved, theirs_t = pin(y_moved, sums_moved, theirs_t)
    grad_a = grad_a.astype(F32) + y_moved.astype(F32)
    y_moved = send_rows(grad_a, cross_near)
    sums = sums + sums_moved
    sums_moved = cross_x(sums)
    final_arrived = cross_core(final_sent)
    sums_moved, final_arrived, grad_moved = pin(sums_moved, final_arrived, grad_moved)
    final_across = cross_x(halves_added(final_kept, final_arrived))
    pack = pack_grads(
        sums + sums_moved,
        (qkv_sum_s, qkv_sum_t),
        (hidden_sum_s, hidden_sum_t),
        place,
        local,
        params[3].shape,
        params[9].shape,
    )
    pack_moved = cross_y(pack)
    fe_moved, fr_moved, mine_at, pack = pin(fe_moved, fr_moved, mine_at, pack)
    mine_s = beside(keep_rows(feed_e, fe_moved), keep_rows(feed_r, fr_moved), mine_at).astype(BF16)
    theirs_s = cross_y(
        beside(
            mine_s[:, :half], mine_s[:, 2 * half : 3 * half], mine_s[:, half : 2 * half], mine_s[:, 3 * half :]
        )
    )
    y_moved, theirs_t = pin(y_moved, theirs_t)
    grad_a = keep_rows(grad_a, y_moved)
    y_moved = send_rows(grad_a, cross_far)
    grad_a, pack_moved = pin(grad_a, pack_moved)
    pack = pack + pack_moved
    pack_near = cross_near(pack[2 * ROWS :])
    expand_grad_t, reduce_grad_t = finish_feed(mine_t, theirs_t, place, half)
    final_across, expand_grad_t = pin(final_across, expand_grad_t)
    rows = 2 * tokens
    final = middle_t[:rows] + gains_t[5:6] + final_kept[:rows] + final_across.astype(F32)
    final = final + final_arrived[:rows].astype(F32)
    final = times_across(final.astype(BF16), chooser, BF16)
    y_moved, pack_near, final = pin(y_moved, pack_near, final)
    mine_a = keep_rows(grad_a, y_moved).astype(BF16)
    theirs_a = cross_y(mine_a)
    final_moved = swapped(final)
    merged_grad_t, output_grad_t = finish_attend(
        (), mine_s[:, 3 * half :], theirs_s[:, 3 * half :], place
    )
    expand_grad_s, reduce_grad_s = finish_feed(
        mine_s[:, : 3 * half], theirs_s[:, : 3 * half], place, half
    )
    pack = pack[: 2 * ROWS] + pack_near
    pack_far = cross_far(pack[ROWS:])
    vectors = unpack_grads(pack, pack_far, local, params[3].shape, params[9].shape)
    final = restore(final, final_moved)
    theirs_a, final, first, output_grad_t, expand_grad_s = pin(
        theirs_a, final, vectors[0], output_grad_t, expand_grad_s
    )
    vectors[0] = first
    merged_grad_s, output_grad_s = finish_attend((), mine_a, theirs_a, place)
    outputs = [final, restore(input_grad, grad_moved.astype(F32))]
    for vector, merged, output, expand, reduce in (
        (vectors[:8], merged_grad_s, output_grad_s, expand_grad_s, reduce_grad_s),
        (vectors[8:], merged_grad_t, output_grad_t, expand_grad_t, reduce_grad_t),
    ):
        outputs += [
            vector[0],
            vector[1],
            merged,
            vector[6],
            output,
            vector[2],
            vector[3],
            vector[4],
            expand,
            vector[7],
            reduce,
            vector[5],
        ]
    return tuple(outputs)


def solution(mesh):
    quick = (mesh.shape["dp"], mesh.shape["ctx"], mesh.shape["tp"]) == (4, 2, 4)
    placed = (
        P("dp", ("ctx", "tp"), None),
        P("dp", "ctx"),
        P("dp", ("ctx", "tp"), None),
        P("dp"),
        P("dp"),
        P("dp", None, "tp"),
        P(None, "tp", "dp"),
        P("tp", "dp"),
        P("dp"),
        P("dp"),
        P("dp"),
        P("dp", "tp"),
        P("tp", "dp"),
        P("tp", "dp"),
        P("dp"),
        P("dp"),
        P("dp"),
        P("dp", None, "tp"),
        P(None, "tp", "dp"),
        P("tp", "dp"),
        P("dp"),
        P("dp"),
        P("dp"),
        P("dp", "tp"),
        P("tp", "dp"),
        P("tp", "dp"),
        P("dp"),
    )
    return jax.shard_map(
        fast_shards if quick else general_shards,
        mesh=mesh,
        in_specs=placed,
        out_specs=(
            P("dp", ("ctx", "tp"), None),
            P("dp", ("ctx", "tp"), None),
            P("dp"),
            P("dp"),
            P("dp", None, "tp"),
            P(None, "tp", "dp"),
            P("tp", "dp"),
            P("dp"),
            P("dp"),
            P("dp"),
            P("dp", "tp"),
            P("tp", "dp"),
            P("tp", "dp"),
            P("dp"),
            P("dp"),
            P("dp"),
            P("dp", None, "tp"),
            P(None, "tp", "dp"),
            P("tp", "dp"),
            P("dp"),
            P("dp"),
            P("dp"),
            P("dp", "tp"),
            P("tp", "dp"),
            P("tp", "dp"),
            P("dp"),
        ),
        check_vma=False,
    )
```
